32 devices in a mesh: seq: 8 (over z, x), tp: 4 (over y, core).
Axes of the slice: x: 2, y: 2, z: 4, core: 2. Of those that a mesh axis runs over, the one named last changes fastest.
Arguments:
- inputs: bfloat16 [8192, 2048], P(('seq', 'tp')), may hold values from -6 to 6
- lengths: int32 [3], replicated, may hold values from 512 to 7168, as said below
- gain_attn: float32 [2048], P('seq'), may hold values from 0.5 to 1.5
- w_query: float32 [2048, 256], P('seq', 'tp'), may hold values from -0.25 to 0.25
- w_key: float32 [2048, 256], P('seq', 'tp'), may hold values from -0.25 to 0.25
- w_value: float32 [2048, 2048], P('seq', 'tp'), may hold values from -0.125 to 0.125
- w_out: float32 [2048, 2048], P('tp', 'seq'), may hold values from -0.5 to 0.5
- gain_mlp: float32 [2048], P('seq'), may hold values from 0.5 to 1.5
- w_gate: float32 [2048, 5504], P('seq', 'tp'), may hold values from -0.125 to 0.125
- w_up: float32 [2048, 5504], P('seq', 'tp'), may hold values from -0.125 to 0.125
- w_down: float32 [5504, 2048], P('tp', 'seq'), may hold values from -0.078125 to 0.078125
- cotangent: bfloat16 [8192, 2048], P(('seq', 'tp')), may hold values from -6 to 6
Outputs:
- block_output: bfloat16 [8192, 2048], P(('seq', 'tp'))
- input_grad: float32 [8192, 2048], P(('seq', 'tp'))
- grad_gain_attn: float32 [2048], P('seq')
- grad_w_query: float32 [2048, 256], P('seq', 'tp')
- grad_w_key: float32 [2048, 256], P('seq', 'tp')
- grad_w_value: float32 [2048, 2048], P('seq', 'tp')
- grad_w_out: float32 [2048, 2048], P('tp', 'seq')
- grad_gain_mlp: float32 [2048], P('seq')
- grad_w_gate: float32 [2048, 5504], P('seq', 'tp')
- grad_w_up: float32 [2048, 5504], P('seq', 'tp')
- grad_w_down: float32 [5504, 2048], P('tp', 'seq')
The draws below stay inside these ranges and needn't reach their ends.
Inputs may be any that keep to these rules, and one draw needn't show every extreme that they name: `lengths`: 3 rows laid end to end from token 0: 2 of 512 tokens and one of 7168; the long row is the second of them, and it starts in the first block of 1024 tokens and ends in the last.
All inputs are finite; a program needn't handle non-finite values.
Results may differ from the reference program's by a relative error of at most 0.022.
Values may be sent and summed in bfloat16 or wider, within the bound.
A program may use at most 256 MiB of HBM per device.

```python
from functools import partial
import jax
import jax.numpy as jnp
from jax import lax

D = 2048
HEADS = 16
FEAT = 16
VHEAD = 128
FF = 5504
TOK_DEV = 1024
SHORT = 512
ROWS = 3
NFEAT = 273
TOKENS = 8192


def draw_lengths(key, part):
    long_slot = jax.random.randint(key, (), 0, ROWS)
    spans_all = (long_slot * SHORT < TOK_DEV) & ((ROWS - 1 - long_slot) * SHORT < TOK_DEV)
    long_slot = jnp.where(spans_all, long_slot, (ROWS - 1) // 2)
    row_slots = jnp.arange(ROWS)
    return jnp.where(row_slots == long_slot, TOKENS - (ROWS - 1) * SHORT, SHORT).astype(jnp.int32)


def strengthened(values, stream_key, source, target, shards_of, factor):
    owner, partner = [(jnp.arange(values.shape[position]) // (values.shape[position] // shards_of)).reshape([-1 if axis == position else 1 for axis in range(values.ndim)]) for position in (source, target)]
    chosen = jax.random.permutation(stream_key, shards_of)[partner]
    strong = (owner == chosen) | (owner == (partner + shards_of // 2) % shards_of)
    return jnp.where(strong, factor * values, values)


def steps_of(key, shape, shards, smallest, top_value):
    def one(axis_at, shards_of):
        heights = jax.random.uniform(jax.random.fold_in(jax.random.fold_in(key, 6), axis_at), (shards_of,), jnp.float32, smallest / len(shards), top_value / len(shards))
        return jnp.repeat(jnp.exp(heights), shape[axis_at] // shards_of).reshape((-1,) + (1,) * (len(shape) - axis_at - 1))

    level = one(*shards[0])
    for cut in shards[1:]:
        level = level * one(*cut)
    return level


def scatter_about(rng, extent, deviation, reach, split=(), held_as=jnp.bfloat16):
    drawn = deviation * jax.random.normal(rng, extent, jnp.float32)
    if split:
        drawn = drawn * steps_of(rng, extent, split, -0.22, 0.18)
    return jnp.clip(drawn, -reach, reach).astype(held_as)


def bell_draw_with(rng, shape, deviation, bound, cuts, heavy, kind=jnp.bfloat16):
    values = deviation * jax.random.normal(rng, shape, jnp.float32)
    if cuts:
        values = values * steps_of(rng, shape, cuts, -0.22, 0.18)
    return jnp.clip(strengthened(values, jax.random.fold_in(rng, 3), *heavy), -bound, bound).astype(kind)


def setup_inputs(seed: int = 0) -> dict:
    key_list = jax.random.split(jax.random.key(seed), 13)
    inputs = bell_draw_with(key_list[0], (TOKENS, D), 1.0, 6.0, ((0, 32),), (0, 1, 32, 2.75))
    lengths = draw_lengths(jax.random.fold_in(key_list[12], 71), 0)
    gain_attn = jnp.clip(1.0 + 0.1 * jax.random.normal(key_list[2], (D,), jnp.float32), 0.5, 1.5)
    w_query = scatter_about(key_list[3], (D, HEADS * FEAT), (D // 4) ** -0.5, 0.25, ((0, 8), (1, 4)), jnp.float32)
    w_key = scatter_about(key_list[4], (D, HEADS * FEAT), (D // 4) ** -0.5, 0.25, ((0, 8), (1, 4)), jnp.float32)
    w_value = scatter_about(key_list[5], (D, D), D ** -0.5, 0.125, ((0, 8), (1, 4)), jnp.float32)
    w_out = scatter_about(key_list[6], (D, D), (D // 16) ** -0.5, 0.5, ((0, 4), (1, 8)), jnp.float32)
    gain_mlp = jnp.clip(1.0 + 0.1 * jax.random.normal(key_list[7], (D,), jnp.float32), 0.5, 1.5)
    w_gate = scatter_about(key_list[8], (D, FF), D ** -0.5, 0.125, ((0, 8), (1, 4)), jnp.float32)
    w_up = scatter_about(key_list[9], (D, FF), D ** -0.5, 0.125, ((0, 8), (1, 4)), jnp.float32)
    w_down = scatter_about(key_list[10], (FF, D), FF ** -0.5, 0.078125, ((0, 4), (1, 8)), jnp.float32)
    cotangent = bell_draw_with(key_list[11], (TOKENS, D), 1.0, 6.0, ((0, 32),), (0, 1, 32, 2.75))
    return {"inputs": inputs, "lengths": lengths, "gain_attn": gain_attn, "w_query": w_query, "w_key": w_key, "w_value": w_value, "w_out": w_out, "gain_mlp": gain_mlp, "w_gate": w_gate, "w_up": w_up, "w_down": w_down, "cotangent": cotangent}


epsilon = 1e-05
linear_coef = 0.5
square_coef = 0.17677669529663687
highest = lax.Precision.HIGHEST

@jax.custom_vjp
def low(v):
    return lax.optimization_barrier(v.astype(jnp.bfloat16)).astype(jnp.float32)

@jax.custom_vjp
def low_back(v):
    return v

def low_keep(v):
    return (low(v), None)

def low_pass(kept, grad):
    return (grad,)

def back_keep(v):
    return (v, None)

def back_low(kept, grad):
    return (low(grad),)
low.defvjp(low_keep, low_pass)
low_back.defvjp(back_keep, back_low)

def features(vector):
    squares = (vector[..., :, None] * vector[..., None, :]).reshape(vector.shape[:-1] + (vector.shape[-1] * vector.shape[-1],))
    return jnp.concatenate([jnp.ones_like(vector[..., :1]), vector * linear_coef, squares * square_coef], axis=-1)

def segment_masks(anchor, starts, length):
    positions = anchor + jnp.arange(length, dtype=jnp.int32)
    start_le = starts[None, :] <= positions[:, None]
    row_ids = lax.optimization_barrier(jnp.sum(start_le.astype(jnp.int32), axis=1))
    inside = (starts >= anchor) & (starts < anchor + length)
    carried = lax.optimization_barrier(jnp.sum(((starts[None, :] >= anchor) & start_le).astype(jnp.int32), axis=1)) == 0
    after_last = lax.optimization_barrier(jnp.sum(((starts[None, :] > positions[:, None]) & inside[None, :]).astype(jnp.int32), axis=1)) == 0
    resets = jnp.sum(inside.astype(jnp.int32)) > 0
    return (positions, row_ids, carried, after_last, resets)

def block_step(carried_in, inputs, starts):
    state_sum, key_total = carried_in
    query_block, key_block, value_block, anchor = inputs
    positions, row_ids, carried, after_last, resets = segment_masks(anchor, starts, TOK_DEV)
    allowed = ((row_ids[:, None] == row_ids[None, :]) & (positions[None, :] <= positions[:, None])).astype(jnp.float32)
    scores = low_back(jnp.einsum('thf,shf->hts', query_block, key_block, precision=highest) * 0.25)
    kernel = (1.0 + scores + 0.5 * scores * scores) * allowed[None]
    numerator = jnp.einsum('hts,shv->thv', low(kernel), value_block, precision=highest)
    denominator = lax.optimization_barrier(jnp.sum(kernel, axis=-1)).T
    carry_weight = carried.astype(jnp.float32)[:, None]
    query_feat = features(query_block)
    numerator = low_back(numerator + jnp.einsum('thn,hnv->thv', query_feat, state_sum, precision=highest) * carry_weight[:, :, None])
    denominator = denominator + jnp.einsum('thn,hn->th', query_feat, key_total, precision=highest) * carry_weight
    attended = numerator / denominator[:, :, None]
    key_feat = features(key_block) * after_last.astype(jnp.float32)[:, None, None]
    persist = 1.0 - resets.astype(jnp.float32)
    new_state = jnp.einsum('thn,thv->hnv', key_feat, value_block, precision=highest) + persist * state_sum
    new_total = lax.optimization_barrier(jnp.sum(key_feat, axis=0)) + persist * key_total
    return ((new_state, new_total), attended)

def attention(queries, key_rows, value_rows, starts):
    blocks = queries.shape[0] // TOK_DEV
    query_blocks = queries.reshape(blocks, TOK_DEV, HEADS, FEAT)
    key_blocks = key_rows.reshape(blocks, TOK_DEV, HEADS, FEAT)
    value_blocks = value_rows.reshape(blocks, TOK_DEV, HEADS, VHEAD)
    anchors = (jnp.arange(blocks) * TOK_DEV).astype(jnp.int32)
    initial = (jnp.zeros((HEADS, NFEAT, VHEAD), jnp.float32), jnp.zeros((HEADS, NFEAT), jnp.float32))
    block_fn = jax.checkpoint(partial(block_step, starts=starts))
    unused, outputs = lax.scan(block_fn, initial, (query_blocks, key_blocks, value_blocks, anchors))
    return outputs.reshape(queries.shape[0], HEADS * VHEAD)

def product(left, right):
    return jnp.dot(left, right, precision=highest)

def rms_scale(values):
    return lax.rsqrt(lax.optimization_barrier(jnp.mean(values * values, axis=-1, keepdims=True)) + epsilon)

def reference(inputs, lengths, gain_attn, w_query, w_key, w_value, w_out, gain_mlp, w_gate, w_up, w_down, cotangent):
    starts = (jnp.cumsum(lengths) - lengths).astype(jnp.int32)

    def forward(tokens, gain_first, query_w, key_w, value_w, out_w, gain_second, gate_w, up_w, down_w):
        normed_first = tokens * rms_scale(tokens)
        hidden_first = low(normed_first * low(gain_first))
        queries = low_back(low(product(hidden_first, low(query_w))))
        key_rows = low_back(low(product(hidden_first, low(key_w))))
        value_rows = low_back(low(product(hidden_first, low(value_w))))
        attended = attention(queries, key_rows, value_rows, starts)
        branch = low_back(product(low(attended), low(out_w)))
        middle = tokens + branch
        hidden_second = low(middle * rms_scale(middle) * low(gain_second))
        gate_value = low_back(product(hidden_second, low(gate_w)))
        upward = low_back(product(hidden_second, low(up_w)))
        mixed_rows = low_back(low(jax.nn.silu(gate_value) * upward))
        return middle + product(mixed_rows, low(down_w))
    primals = (inputs.astype(jnp.float32), gain_attn, w_query, w_key, w_value, w_out, gain_mlp, w_gate, w_up, w_down)
    result, pullback = jax.vjp(forward, *primals)
    grads = pullback(cotangent.astype(jnp.float32))
    return (result.astype(jnp.bfloat16), grads[0], grads[1], grads[2], grads[3], grads[4], grads[5], grads[6], grads[7], grads[8], grads[9])
```

```python
import jax
import jax.numpy as jnp
from jax import lax
from jax.sharding import PartitionSpec as P

FEAT = 16
VHEAD = 128


epsilon = 1e-05
linear_coef = 0.5
square_coef = 0.17677669529663687
highest = lax.Precision.HIGHEST
f32 = jnp.float32
bf16 = jnp.bfloat16


def ring_order(count):
    planes = 4 if count % 4 == 0 else 2
    columns = count // planes
    order = [z * columns for z in range(planes)]
    for z in reversed(range(planes)):
        xs = list(range(1, columns))
        if (planes - 1 - z) % 2:
            xs.reverse()
        order += [z * columns + x for x in xs]
    return order


def relative_list(count):
    half = count // 2
    out = []
    for j in range(1, half):
        out += [j, count - j]
    return out + [half, 0]


def ring_perms(count):
    ring = ring_order(count)
    fwd = [(ring[i], ring[(i + 1) % count]) for i in range(count)]
    return fwd, [(b, a) for a, b in fwd]


def ring_gather(own, half_rows):
    count = lax.axis_size("seq")
    fwd, bwd = ring_perms(count)
    half = count // 2
    got = {0: own}
    ahead = back = own
    for step in range(1, half):
        ahead = lax.ppermute(ahead, "seq", fwd)
        back = lax.ppermute(back, "seq", bwd)
        got[step] = ahead
        got[count - step] = back
    ahead = lax.ppermute(ahead[:half_rows], "seq", fwd)
    back = lax.ppermute(back[half_rows:], "seq", bwd)
    got[half] = jnp.concatenate([ahead, back], axis=0)
    return got


def ring_scatter(chunks):
    count = lax.axis_size("seq")
    fwd, bwd = ring_perms(count)
    half = chunks[0].shape[0] // 2
    ahead = chunks[1][:half]
    back = chunks[count - 1][half:]
    for step in range(count - 1):
        ahead = lax.ppermute(ahead, "seq", fwd).astype(f32)
        back = lax.ppermute(back, "seq", bwd).astype(f32)
        last = step == count - 2
        ahead = ahead + chunks[0 if last else 2 + step][:half].astype(f32)
        back = back + chunks[0 if last else count - 2 - step][half:].astype(f32)
        if not last:
            ahead = ahead.astype(bf16)
            back = back.astype(bf16)
    return jnp.concatenate([ahead, back], axis=0)


def to_relative(array, index_row, chunk):
    return jnp.concatenate(
        [lax.dynamic_slice_in_dim(array, i * chunk, chunk, 1) for i in index_row], axis=1
    )


def tp_perms(count):
    ys = count // 2
    core = [(i, i ^ 1) for i in range(count)]
    shift = [
        [(i, (((i // 2) + d) % ys) * 2 + i % 2) for i in range(count)] for d in range(ys)
    ]
    return core, shift


def tp_gather(own):
    count = lax.axis_size("tp")
    ys = count // 2
    place = lax.axis_index("tp")
    y, c = place // 2, place % 2
    core, shift = tp_perms(count)
    parts = [own] + [lax.ppermute(own, "tp", shift[d]) for d in range(1, ys)]
    mine = jnp.stack([lax.select_n((y - at + ys) % ys, *parts) for at in range(ys)])
    other = lax.ppermute(mine, "tp", core)
    full = jnp.stack([jnp.where(c == 0, mine, other), jnp.where(c == 0, other, mine)], axis=1)
    return full.reshape((count * own.shape[0],) + own.shape[1:])


def tp_scatter(partial):
    count = lax.axis_size("tp")
    ys = count // 2
    place = lax.axis_index("tp")
    y, c = place // 2, place % 2
    core, shift = tp_perms(count)
    blocks = partial.reshape((ys, 2, partial.shape[0] // count) + partial.shape[1:])
    sent = lax.dynamic_index_in_dim(blocks, 1 - c, 1, False)
    kept = lax.dynamic_index_in_dim(blocks, c, 1, False)
    pair = kept.astype(f32) + lax.ppermute(sent, "tp", core).astype(f32)
    low = pair.astype(bf16)
    own = lax.dynamic_index_in_dim(pair, y, 0, False)
    for d in range(1, ys):
        away = lax.dynamic_index_in_dim(low, (y + d) % ys, 0, False)
        own = own + lax.ppermute(away, "tp", shift[d]).astype(f32)
    return own


def tp_sum(vector):
    count = lax.axis_size("tp")
    core, shift = tp_perms(count)
    vector = vector + lax.ppermute(vector, "tp", core)
    return vector + sum(lax.ppermute(vector, "tp", shift[d]) for d in range(1, count // 2))


def carried(arrays, resets, step):
    count = lax.axis_size("seq")
    place = lax.axis_index("seq")

    def from_near(a, d):
        perm = [(i, i + d * step) for i in range(count) if 0 <= i + d * step < count]
        return lax.ppermute(a.astype(bf16), "seq", perm).astype(f32)

    def reset_within(d):
        at = jnp.arange(count)
        away = (place - at) * step
        return jnp.sum(jnp.where((away >= 1) & (away <= d), resets, 0)) > 0

    arrays = [from_near(a, 1) for a in arrays]
    d = 1
    while d < count - 1:
        keep = 1.0 - reset_within(d).astype(f32)
        arrays = [a + keep * from_near(a, d) for a in arrays]
        d *= 2
    return arrays


def features(vector):
    squares = (vector[..., :, None] * vector[..., None, :]).reshape(
        vector.shape[:-1] + (vector.shape[-1] * vector.shape[-1],)
    )
    return jnp.concatenate(
        [jnp.ones_like(vector[..., :1]), vector * linear_coef, squares * square_coef], axis=-1
    )


def feature_grad(vector, grad_feat):
    feat_width = vector.shape[-1]
    linear_part = grad_feat[..., 1 : 1 + feat_width]
    square_part = grad_feat[..., 1 + feat_width :].reshape(vector.shape + (feat_width,))
    mixed_part = jnp.sum(square_part * vector[..., None, :], axis=-1) + jnp.sum(
        square_part * vector[..., :, None], axis=-2
    )
    return linear_coef * linear_part + square_coef * mixed_part


def segment_masks(anchor, starts, length):
    positions = anchor + jnp.arange(length, dtype=jnp.int32)
    start_le = starts[None, :] <= positions[:, None]
    row_ids = jnp.sum(start_le.astype(jnp.int32), axis=1)
    inside = (starts >= anchor) & (starts < anchor + length)
    carry = jnp.sum(((starts[None, :] >= anchor) & start_le).astype(jnp.int32), axis=1) == 0
    after_last = (
        jnp.sum(
            ((starts[None, :] > positions[:, None]) & inside[None, :]).astype(jnp.int32), axis=1
        )
        == 0
    )
    return (positions, row_ids, carry, after_last)


def rms_scale(values):
    return lax.rsqrt(jnp.mean(values * values, axis=-1, keepdims=True) + epsilon)


def norm_back(grad_out, normed, scale, gain):
    grad_normed = grad_out * gain
    return scale * (grad_normed - normed * jnp.mean(grad_normed * normed, axis=-1, keepdims=True))


def pair_block(query_part, key_heads, row_ids, positions, first_row, span_rows):
    scores = (
        jnp.einsum("thf,shf->hts", query_part, key_heads, preferred_element_type=f32) * 0.25
    )
    rows_here = row_ids[first_row : first_row + span_rows]
    place_here = positions[first_row : first_row + span_rows]
    allowed = (
        (rows_here[:, None] == row_ids[None, :]) & (positions[None, :] <= place_here[:, None])
    ).astype(f32)
    kernel = (1.0 + scores + 0.5 * scores * scores) * allowed[None]
    return (scores, allowed, kernel)


def dot(a, b):
    return jnp.dot(a, b, preferred_element_type=f32)


def dot_t(a, b):
    return lax.dot_general(a, b, (((1,), (1,)), ((), ())), preferred_element_type=f32)


def dot_tt(a, b):
    return lax.dot_general(a, b, (((0,), (0,)), ((), ())), preferred_element_type=f32)


def on_device(
    inputs,
    lengths,
    gain_attn,
    w_query,
    w_key,
    w_value,
    w_out,
    gain_mlp,
    w_gate,
    w_up,
    w_down,
    cotangent,
):
    seq_count = lax.axis_size("seq")
    tp_count = lax.axis_size("tp")
    seq_index = lax.axis_index("seq")
    rows_own, width = inputs.shape
    chunk = width // seq_count
    half = chunk // 2
    block_len = rows_own * tp_count
    anchor = seq_index * block_len
    relative = relative_list(seq_count)
    ring = ring_order(seq_count)
    place_of = [ring.index(s) for s in range(seq_count)]
    to_rel = jnp.array(
        [[ring[(place_of[s] - k) % seq_count] for k in relative] for s in range(seq_count)],
        jnp.int32,
    )[seq_index]
    to_abs = jnp.array(
        [
            [relative.index((place_of[s] - place_of[o]) % seq_count) for o in range(seq_count)]
            for s in range(seq_count)
        ],
        jnp.int32,
    )[seq_index]
    to_rel = [to_rel[j] for j in range(seq_count)]
    to_abs = [to_abs[j] for j in range(seq_count)]

    qk_cols, v_cols, ff_cols = w_query.shape[1], w_value.shape[1], w_gate.shape[1]
    gains = jnp.stack([gain_attn, gain_mlp]).astype(bf16)
    qkv_cols = 2 * qk_cols + v_cols
    qkv_own = jnp.concatenate([w_query, w_key, w_value], axis=1).astype(bf16)
    gain_rows = jnp.zeros((16, qkv_cols), bf16).at[:2, :chunk].set(gains)
    first_own = jnp.concatenate([qkv_own, gain_rows], axis=0)
    out_own = w_out.astype(bf16).T
    gate_up_own = jnp.concatenate([w_gate, w_up], axis=1).astype(bf16)
    down_own = w_down.astype(bf16).T

    first_got = ring_gather(first_own, half)
    out_got = ring_gather(out_own, half)
    gate_up_got = ring_gather(gate_up_own, half)
    down_got = ring_gather(down_own, half)
    w_qkv = jnp.concatenate([first_got[k][:chunk] for k in relative], axis=0)
    gain_first = jnp.concatenate([first_got[k][chunk, :chunk] for k in relative]).astype(f32)
    gain_second = jnp.concatenate([first_got[k][chunk + 1, :chunk] for k in relative]).astype(f32)
    w_out_t = jnp.concatenate([out_got[k] for k in relative], axis=0)
    w_gate_up = jnp.concatenate([gate_up_got[k] for k in relative], axis=0)
    w_down_t = jnp.concatenate([down_got[k] for k in relative], axis=0)

    at = jnp.arange(lengths.shape[0])
    starts = jnp.sum(jnp.where(at[None, :] < at[:, None], lengths[None, :], 0), axis=1)
    positions, row_ids, carry_in, after_last = segment_masks(anchor, starts, block_len)
    carry_mask = carry_in.astype(f32)
    last_mask = after_last.astype(f32)
    resets = (
        jnp.sum(
            ((starts // block_len)[None, :] == jnp.arange(seq_count)[:, None]).astype(jnp.int32),
            axis=1,
        )
        > 0
    ).astype(jnp.int32)

    inputs_own = to_relative(inputs, to_rel, chunk)
    grad_own = to_relative(cotangent, to_rel, chunk)
    inputs_full = tp_gather(inputs_own).astype(f32)
    grad_full = tp_gather(grad_own)
    inputs_own = inputs_own.astype(f32)
    hidden_first = (inputs_full * rms_scale(inputs_full) * gain_first).astype(bf16)
    qkv = dot(hidden_first, w_qkv).astype(bf16)
    queries = qkv[:, :qk_cols]
    key_flat = qkv[:, qk_cols : 2 * qk_cols]
    value_flat = qkv[:, 2 * qk_cols :]
    heads_local = qk_cols // FEAT
    query_heads = queries.reshape(block_len, heads_local, FEAT)
    key_heads = key_flat.reshape(block_len, heads_local, FEAT)
    value_heads = value_flat.reshape(block_len, heads_local, VHEAD)
    query_float = query_heads.astype(f32)
    key_float = key_heads.astype(f32)
    value_float = value_heads.astype(f32)
    key_feat = features(key_float) * last_mask[:, None, None]
    local_state = jnp.einsum("thn,thv->hnv", key_feat, value_float, precision=highest)
    local_sum = jnp.sum(key_feat, axis=0)
    carry_state, carry_sum = carried([local_state, local_sum], resets, 1)
    step_rows = 512
    query_feat = features(query_float)
    carry_weight = carry_mask[:, None]
    numer_parts = []
    denom_parts = []
    for first_row in range(0, block_len, step_rows):
        query_part = query_heads[first_row : first_row + step_rows]
        scores, allowed, kernel = pair_block(
            query_part, key_heads, row_ids, positions, first_row, step_rows
        )
        numer_parts.append(
            jnp.einsum("hts,shv->thv", kernel.astype(bf16), value_heads, preferred_element_type=f32)
        )
        denom_parts.append(jnp.sum(kernel, axis=-1).T)
    numerator = (
        jnp.concatenate(numer_parts, axis=0)
        + jnp.einsum("thn,hnv->thv", query_feat, carry_state, precision=highest)
        * carry_weight[:, :, None]
    )
    denominator = (
        jnp.concatenate(denom_parts, axis=0)
        + jnp.einsum("thn,hn->th", query_feat, carry_sum, precision=highest) * carry_weight
    )
    attended = numerator / denominator[:, :, None]
    attended_low = attended.reshape(block_len, heads_local * VHEAD).astype(bf16)
    attn_partial = dot_t(attended_low, w_out_t).astype(bf16)
    middle_own = inputs_own + tp_scatter(attn_partial)
    scale_second = rms_scale(middle_own)
    normed_second = middle_own * scale_second
    hidden_second = tp_gather((normed_second * gain_second).astype(bf16))
    gate_up = dot(hidden_second, w_gate_up)
    gate_value, upward = gate_up[:, :ff_cols], gate_up[:, ff_cols:]
    sigmoid_gate = jax.nn.sigmoid(gate_value)
    silu_gate = gate_value * sigmoid_gate
    mixed_rows = (silu_gate * upward).astype(bf16)
    grad_down_t = dot_tt(grad_full, mixed_rows).astype(bf16)

    def by_distance(stack):
        return {k: stack[j * chunk : (j + 1) * chunk] for j, k in enumerate(relative)}

    sum_down_t = ring_scatter(by_distance(grad_down_t))
    mlp_own = tp_scatter(dot_t(mixed_rows, w_down_t).astype(bf16))
    block_output = to_relative((middle_own + mlp_own).astype(bf16), to_abs, chunk)

    grad_mixed = dot(grad_full, w_down_t).astype(bf16).astype(f32)
    grad_gate = (
        grad_mixed * upward * sigmoid_gate * (1.0 + gate_value * (1.0 - sigmoid_gate))
    ).astype(bf16)
    grad_upward = (grad_mixed * silu_gate).astype(bf16)
    grad_gate_up = jnp.concatenate([grad_gate, grad_upward], axis=1)
    hidden_partial = dot_t(grad_gate_up, w_gate_up).astype(bf16)
    sum_gate_up = ring_scatter(by_distance(dot_tt(hidden_second, grad_gate_up).astype(bf16)))
    grad_hidden = tp_scatter(hidden_partial)
    grad_middle = grad_own.astype(f32) + norm_back(
        grad_hidden, normed_second, scale_second, gain_second
    )
    grad_branch = tp_gather(grad_middle.astype(bf16))
    sum_out_t = ring_scatter(by_distance(dot_tt(grad_branch, attended_low).astype(bf16)))
    grad_attended = dot(grad_branch, w_out_t).reshape(block_len, heads_local, VHEAD)
    grad_numer = (grad_attended / denominator[:, :, None]).astype(bf16)
    grad_denom = -jnp.sum(grad_attended * attended, axis=-1) / denominator
    grad_numer_carried = grad_numer.astype(f32) * carry_weight[:, :, None]
    grad_denom_carried = grad_denom * carry_weight
    grad_state_in = jnp.einsum("thn,thv->hnv", query_feat, grad_numer_carried, precision=highest)
    grad_sum_in = jnp.einsum("thn,th->hn", query_feat, grad_denom_carried, precision=highest)
    grad_query_feat = (
        jnp.einsum("thv,hnv->thn", grad_numer_carried, carry_state, precision=highest)
        + grad_denom_carried[:, :, None] * carry_sum[None]
    )
    grad_state_out, grad_sum_out = carried([grad_state_in, grad_sum_in], resets, -1)
    grad_key_feat = (
        jnp.einsum("thv,hnv->thn", value_float, grad_state_out, precision=highest)
        + grad_sum_out[None]
    ) * last_mask[:, None, None]
    grad_value_state = jnp.einsum("thn,hnv->thv", key_feat, grad_state_out, precision=highest)
    grad_query_parts = []
    grad_key_inner = jnp.zeros((block_len, heads_local, FEAT), f32)
    grad_value_inner = jnp.zeros((block_len, heads_local, VHEAD), f32)
    for first_row in range(0, block_len, step_rows):
        query_part = query_heads[first_row : first_row + step_rows]
        scores, allowed, kernel = pair_block(
            query_part, key_heads, row_ids, positions, first_row, step_rows
        )
        numer_grad_part = grad_numer[first_row : first_row + step_rows]
        grad_weights = jnp.einsum(
            "thv,shv->hts", numer_grad_part, value_heads, preferred_element_type=f32
        )
        grad_scores = (
            (grad_weights + grad_denom[first_row : first_row + step_rows].T[:, :, None])
            * allowed[None]
            * (1.0 + scores)
        ).astype(bf16)
        grad_query_parts.append(
            jnp.einsum("hts,shf->thf", grad_scores, key_heads, preferred_element_type=f32) * 0.25
        )
        grad_key_inner = (
            grad_key_inner
            + jnp.einsum("hts,thf->shf", grad_scores, query_part, preferred_element_type=f32) * 0.25
        )
        grad_value_inner = grad_value_inner + jnp.einsum(
            "hts,thv->shv", kernel.astype(bf16), numer_grad_part, preferred_element_type=f32
        )
    grad_query = (
        jnp.concatenate(grad_query_parts, axis=0) + feature_grad(query_float, grad_query_feat)
    ).astype(bf16)
    grad_key = (grad_key_inner + feature_grad(key_float, grad_key_feat)).astype(bf16)
    grad_value = (grad_value_inner + grad_value_state).astype(bf16)
    grad_qkv = jnp.concatenate(
        [
            grad_query.reshape(block_len, heads_local * FEAT),
            grad_key.reshape(block_len, heads_local * FEAT),
            grad_value.reshape(block_len, heads_local * VHEAD),
        ],
        axis=1,
    )
    sum_qkv = ring_scatter(by_distance(dot_tt(hidden_first, grad_qkv).astype(bf16)))
    grad_hidden_first = tp_scatter(dot_t(grad_qkv, w_qkv).astype(bf16))
    scale_first = rms_scale(inputs_own)
    normed_first = inputs_own * scale_first
    grad_input = to_relative(
        grad_middle + norm_back(grad_hidden_first, normed_first, scale_first, gain_first),
        to_abs,
        chunk,
    )

    gain_terms = jnp.stack(
        [
            jnp.sum(qkv_own.astype(f32) * sum_qkv, axis=1),
            jnp.sum(gate_up_own.astype(f32) * sum_gate_up, axis=1),
        ]
    )
    gain_sums = tp_sum(gain_terms) / gains.astype(f32)
    return (
        block_output,
        grad_input,
        gain_sums[0],
        sum_qkv[:, :qk_cols],
        sum_qkv[:, qk_cols : 2 * qk_cols],
        sum_qkv[:, 2 * qk_cols :],
        sum_out_t.T,
        gain_sums[1],
        sum_gate_up[:, :ff_cols],
        sum_gate_up[:, ff_cols:],
        sum_down_t.T,
    )


def solution(mesh):
    in_specs = (
        P(("seq", "tp"), None),
        P(),
        P("seq"),
        P("seq", "tp"),
        P("seq", "tp"),
        P("seq", "tp"),
        P("tp", "seq"),
        P("seq"),
        P("seq", "tp"),
        P("seq", "tp"),
        P("tp", "seq"),
        P(("seq", "tp"), None),
    )
    out_specs = (
        P(("seq", "tp"), None),
        P(("seq", "tp"), None),
        P("seq"),
        P("seq", "tp"),
        P("seq", "tp"),
        P("seq", "tp"),
        P("tp", "seq"),
        P("seq"),
        P("seq", "tp"),
        P("seq", "tp"),
        P("tp", "seq"),
    )
    return jax.shard_map(
        on_device, mesh=mesh, in_specs=in_specs, out_specs=out_specs, check_vma=False
    )
```

```python
import jax
import jax.numpy as jnp
import numpy as np
from jax import lax
from jax.experimental import pallas as pl
from jax.experimental.pallas import tpu as pltpu
from jax.sharding import PartitionSpec as P

FEAT = 16
VHEAD = 128


epsilon = 1e-05
linear_coef = 0.5
square_coef = 0.17677669529663687
highest = lax.Precision.HIGHEST
f32 = jnp.float32
bf16 = jnp.bfloat16


def ring_order(count):
    planes = 4 if count % 4 == 0 else 2
    columns = count // planes
    order = [z * columns for z in range(planes)]
    for z in reversed(range(planes)):
        xs = list(range(1, columns))
        if (planes - 1 - z) % 2:
            xs.reverse()
        order += [z * columns + x for x in xs]
    return order


def relative_list(count):
    half = count // 2
    out = []
    for j in range(1, half):
        out += [j, count - j]
    return out + [half, 0]


def ring_perms(count):
    ring = ring_order(count)
    fwd = [(ring[i], ring[(i + 1) % count]) for i in range(count)]
    return fwd, [(b, a) for a, b in fwd]


def ring_gather(own, half_rows):
    count = lax.axis_size("seq")
    fwd, bwd = ring_perms(count)
    half = count // 2
    got = {0: own}
    ahead = back = own
    for step in range(1, half):
        ahead = lax.ppermute(ahead, "seq", fwd)
        back = lax.ppermute(back, "seq", bwd)
        got[step] = ahead
        got[count - step] = back
    ahead = lax.ppermute(ahead[:half_rows], "seq", fwd)
    back = lax.ppermute(back[half_rows:], "seq", bwd)
    got[half] = jnp.concatenate([ahead, back], axis=0)
    return got


def ring_scatter(chunks):
    count = lax.axis_size("seq")
    fwd, bwd = ring_perms(count)
    half = chunks[0].shape[0] // 2
    ahead = chunks[1][:half]
    back = chunks[count - 1][half:]
    for step in range(count - 1):
        ahead = lax.ppermute(ahead, "seq", fwd).astype(f32)
        back = lax.ppermute(back, "seq", bwd).astype(f32)
        last = step == count - 2
        ahead = ahead + chunks[0 if last else 2 + step][:half].astype(f32)
        back = back + chunks[0 if last else count - 2 - step][half:].astype(f32)
        if not last:
            ahead = ahead.astype(bf16)
            back = back.astype(bf16)
    return jnp.concatenate([ahead, back], axis=0)


def to_relative(array, index_row, chunk):
    return jnp.concatenate(
        [lax.dynamic_slice_in_dim(array, i * chunk, chunk, 1) for i in index_row], axis=1
    )


def tp_perms(count):
    ys = count // 2
    core = [(i, i ^ 1) for i in range(count)]
    shift = [
        [(i, (((i // 2) + d) % ys) * 2 + i % 2) for i in range(count)] for d in range(ys)
    ]
    return core, shift


def tp_gather(own):
    count = lax.axis_size("tp")
    ys = count // 2
    place = lax.axis_index("tp")
    y, c = place // 2, place % 2
    core, shift = tp_perms(count)
    parts = [own] + [lax.ppermute(own, "tp", shift[d]) for d in range(1, ys)]
    mine = jnp.stack([lax.select_n((y - at + ys) % ys, *parts) for at in range(ys)])
    other = lax.ppermute(mine, "tp", core)
    full = jnp.stack([jnp.where(c == 0, mine, other), jnp.where(c == 0, other, mine)], axis=1)
    return full.reshape((count * own.shape[0],) + own.shape[1:])


def tp_scatter(partial):
    count = lax.axis_size("tp")
    ys = count // 2
    place = lax.axis_index("tp")
    y, c = place // 2, place % 2
    core, shift = tp_perms(count)
    blocks = partial.reshape((ys, 2, partial.shape[0] // count) + partial.shape[1:])
    sent = lax.dynamic_index_in_dim(blocks, 1 - c, 1, False)
    kept = lax.dynamic_index_in_dim(blocks, c, 1, False)
    pair = kept.astype(f32) + lax.ppermute(sent, "tp", core).astype(f32)
    low = pair.astype(bf16)
    own = lax.dynamic_index_in_dim(pair, y, 0, False)
    for d in range(1, ys):
        away = lax.dynamic_index_in_dim(low, (y + d) % ys, 0, False)
        own = own + lax.ppermute(away, "tp", shift[d]).astype(f32)
    return own


def tp_sum(vector):
    count = lax.axis_size("tp")
    core, shift = tp_perms(count)
    vector = vector + lax.ppermute(vector, "tp", core)
    return vector + sum(lax.ppermute(vector, "tp", shift[d]) for d in range(1, count // 2))


def carried(arrays, resets, step):
    count = lax.axis_size("seq")
    place = lax.axis_index("seq")

    def from_near(a, d):
        perm = [(i, i + d * step) for i in range(count) if 0 <= i + d * step < count]
        return lax.ppermute(a.astype(bf16), "seq", perm).astype(f32)

    def reset_within(d):
        at = jnp.arange(count)
        away = (place - at) * step
        return jnp.sum(jnp.where((away >= 1) & (away <= d), resets, 0)) > 0

    arrays = [from_near(a, 1) for a in arrays]
    d = 1
    while d < count - 1:
        keep = 1.0 - reset_within(d).astype(f32)
        arrays = [a + keep * from_near(a, d) for a in arrays]
        d *= 2
    return arrays


def features(vector):
    squares = (vector[..., :, None] * vector[..., None, :]).reshape(
        vector.shape[:-1] + (vector.shape[-1] * vector.shape[-1],)
    )
    return jnp.concatenate(
        [jnp.ones_like(vector[..., :1]), vector * linear_coef, squares * square_coef], axis=-1
    )


def feature_grad(vector, grad_feat):
    feat_width = vector.shape[-1]
    linear_part = grad_feat[..., 1 : 1 + feat_width]
    square_part = grad_feat[..., 1 + feat_width :].reshape(vector.shape + (feat_width,))
    mixed_part = jnp.sum(square_part * vector[..., None, :], axis=-1) + jnp.sum(
        square_part * vector[..., :, None], axis=-2
    )
    return linear_coef * linear_part + square_coef * mixed_part


def segment_masks(anchor, starts, length):
    positions = anchor + jnp.arange(length, dtype=jnp.int32)
    start_le = starts[None, :] <= positions[:, None]
    row_ids = jnp.sum(start_le.astype(jnp.int32), axis=1)
    inside = (starts >= anchor) & (starts < anchor + length)
    carry = jnp.sum(((starts[None, :] >= anchor) & start_le).astype(jnp.int32), axis=1) == 0
    after_last = (
        jnp.sum(
            ((starts[None, :] > positions[:, None]) & inside[None, :]).astype(jnp.int32), axis=1
        )
        == 0
    )
    return (positions, row_ids, carry, after_last)


def rms_scale(values):
    return lax.rsqrt(jnp.mean(values * values, axis=-1, keepdims=True) + epsilon)


def norm_back(grad_out, normed, scale, gain):
    grad_normed = grad_out * gain
    return scale * (grad_normed - normed * jnp.mean(grad_normed * normed, axis=-1, keepdims=True))


def pair_block(query_part, key_heads, row_ids, positions, first_row, span_rows):
    scores = (
        jnp.einsum("thf,shf->hts", query_part, key_heads, preferred_element_type=f32) * 0.25
    )
    rows_here = row_ids[first_row : first_row + span_rows]
    place_here = positions[first_row : first_row + span_rows]
    allowed = (
        (rows_here[:, None] == row_ids[None, :]) & (positions[None, :] <= place_here[:, None])
    ).astype(f32)
    kernel = (1.0 + scores + 0.5 * scores * scores) * allowed[None]
    return (scores, allowed, kernel)


def dot(a, b):
    return jnp.dot(a, b, preferred_element_type=f32)


def dot_t(a, b):
    return lax.dot_general(a, b, (((1,), (1,)), ((), ())), preferred_element_type=f32)


def dot_tt(a, b):
    return lax.dot_general(a, b, (((0,), (0,)), ((), ())), preferred_element_type=f32)


def ring_place(seq):
    z, x = seq // 2, seq % 2
    return z + x * (7 - 2 * z)


def ring_seq(place):
    place = lax.rem(place + 8, 8)
    far = place // 4
    return (1 - far) * 2 * place + far * (15 - 2 * place)


class Sems:
    def __init__(self, ref):
        self.ref, self.used = ref, 0

    def take(self):
        self.used += 1
        return self.ref.at[self.used - 1]


class Links:
    def __init__(self, send, recv):
        self.send, self.recv, self.sent = Sems(send), Sems(recv), []

    def copy(self, src, dst, **to):
        return pltpu.make_async_remote_copy(
            src_ref=src,
            dst_ref=dst,
            send_sem=self.send.take(),
            recv_sem=self.recv.take(),
            device_id=to,
            device_id_type=pl.DeviceIdType.MESH,
        )

    def start(self, src, dst, **to):
        made = self.copy(src, dst, **to)
        made.start()
        self.sent.append(made)
        return made

    def sent_now(self, some):
        for made in some:
            made.wait_send()
        self.sent = [made for made in self.sent if all(made is not other for other in some)]

    def finish(self):
        for made in self.sent:
            made.wait_send()


class Gather:
    def __init__(self, links, arrays, split, nearby):
        self.links, self.arrays, self.split, self.nearby = links, arrays, split, nearby
        self.at = {k: j for j, k in enumerate(relative_list(8))}
        self.flying = {}
        self.events = [
            (a, step, way, part)
            for a in range(len(arrays))
            for step in (1, 2, 3, 4)
            for part in (0, 1)
            for way in (0, 1)
            if step < 4 or way == part
        ]
        self.done = 0
        for part in (0, 1):
            for way in (0, 1):
                self.go(0, 1, way, part)

    def rows(self, part):
        return pl.ds(part * self.split, self.split)

    def go(self, a, step, way, part):
        own, everyone = self.arrays[a]
        before, after = (step - 1, step) if way == 0 else ((9 - step) % 8, 8 - step)
        src = own if step == 1 else everyone.at[self.at[before]]
        self.flying[a, step, way, part] = self.links.start(
            src.at[self.rows(part)],
            everyone.at[self.at[after], self.rows(part)],
            seq=self.nearby[way],
        )

    def pump(self, upto):
        while self.done < min(upto, len(self.events)):
            a, step, way, part = self.events[self.done]
            self.flying[a, step, way, part].wait_recv()
            if step < 3 or (step == 3 and way == part):
                self.go(a, step + 1, way, part)
            if step == 3 and a + 1 < len(self.arrays):
                self.go(a + 1, 1, way, part)
            self.done += 1

    def pump_array(self, a):
        self.pump(14 * (a + 1))


def greet(peers):
    barrier = pltpu.get_barrier_semaphore()
    for peer in peers:
        pl.semaphore_signal(
            barrier, inc=1, device_id=peer, device_id_type=pl.DeviceIdType.MESH
        )
    pl.semaphore_wait(barrier, len(peers))


def places():
    seq, tp = lax.axis_index("seq"), lax.axis_index("tp")
    place = ring_place(seq)
    nearby = (ring_seq(place + 1), ring_seq(place - 1))
    over_y = lax.rem(tp + 2, 4)
    over_core = tp + 1 - 2 * (tp % 2)
    peers = [{"seq": ring_seq(place + k)} for k in range(1, 8)]
    peers += [{"tp": over_y}, {"tp": over_core}]
    return seq, tp, place, nearby, over_y, over_core, peers


class Rows:
    def __init__(self, links, own, everyone, tp, over_y, over_core, rows):
        self.links, self.all, self.tp = links, everyone, tp
        self.over_y, self.over_core, self.rows = over_y, over_core, rows
        half = rows // 2
        self.first = [
            links.start(
                own.at[pl.ds(i * half, half)], self.block(tp, i * half, half), tp=over_y
            )
            for i in (0, 1)
        ]
        self.near = links.start(own, self.block(tp, 0, rows), tp=over_core)
        self.last = []

    def block(self, owner, offset, size):
        return self.all.at[pl.ds(pl.multiple_of(owner * self.rows + offset, 16), size)]

    def forward(self, i):
        half = self.rows // 2
        self.first[i].wait_recv()
        came = self.block(self.over_y, i * half, half)
        self.last.append(self.links.start(came, came, tp=self.over_core))

    def finish(self):
        self.near.wait_recv()
        for made in self.last:
            made.wait_recv()


FEATS = 160


def phi(heads, h, select_a, select_b, lanes):
    a = dot(heads, select_a[h]) + lanes[0:1, :]
    b = dot(heads, select_b[h]) + lanes[1:2, :]
    return a, b


def fwd_kernel(
    x_ref, tok_ref, line_ref, sa_ref, sb_ref, lanes_ref, hm_ref, coef_ref,
    gain_ref, q_own, o_own, g_own, u_own, d_own, c_own,
    wq_all, wo_all, wg_all, wu_all, wd_all, c_all,
    h1_out, qkv_out, yb_out, den_out, x1_out, h2_out, gate_out, up_out, m_out, sin_out, gain_out,
    xg, h1, wq, wo, wg, wu, qkv, kq, num, den, yb, sc, rc, sy, ry, x1, h2, gate, up, mm,
    gains_all, gains, st, st_x, st_t, st_z, s_in, ho,
    send, recv, local,
):
    seq, tp, place, nearby, over_y, over_core, peers = places()
    z, x = seq // 2, seq % 2
    at = {k: j for j, k in enumerate(relative_list(8))}
    rows = x_ref.shape[0]
    total = 4 * rows
    links = Links(send, recv)
    locs = Sems(local)
    pending = []

    def store(src, dst):
        made = pltpu.make_async_copy(src, dst, locs.take())
        made.start()
        pending.append(made)

    def load(src, dst):
        made = pltpu.make_async_copy(src, dst, locs.take())
        made.start()
        return made

    greet(peers)
    gain_flying = [
        links.start(gain_ref, gains_all.at[at[k]], seq=ring_seq(place + k)) for k in range(1, 8)
    ]
    ring = Gather(
        links,
        [(q_own, wq_all), (o_own, wo_all), (g_own, wg_all), (u_own, wu_all), (d_own, wd_all)],
        128,
        nearby,
    )
    xrows = Rows(links, x_ref, xg, tp, over_y, over_core, rows)
    own_in = [
        load(x_ref, xrows.block(tp, 0, rows)),
        load(gain_ref, gains_all.at[at[0]]),
    ]
    own_kept = [load(own, everyone.at[at[0]]) for own, everyone in ring.arrays]
    store(c_own, c_all.at[pl.ds(pl.multiple_of(tp * rows, rows), rows)])

    ring.pump(6)
    xrows.forward(0)
    for made in gain_flying:
        made.wait_recv()
    for made in own_in:
        made.wait()
    for j in range(8):
        chunk = gains_all[j].astype(f32)
        gains[0:8, j * 256 : (j + 1) * 256] = chunk[0:8]
    ring.pump(10)
    xrows.forward(1)
    ring.pump_array(0)
    own_kept[0].wait()
    got = load_weights(load, wq_all, wq)
    xrows.finish()

    def norm_first(i, _):
        r = pl.ds(pl.multiple_of(i * 32, 32), 32)
        v = xg[r, :].astype(f32)
        s = lax.rsqrt(jnp.mean(v * v, axis=1, keepdims=True) + epsilon)
        h1[r, :] = (v * s * gains[0:1, :]).astype(bf16)
        return 0

    lax.fori_loop(0, total // 32, norm_first, 0)
    store(h1, h1_out)
    crows = Rows(links, c_own, c_all, tp, over_y, over_core, rows)
    ring.pump(15)
    for made in got:
        made.wait()

    def project(i, _):
        r = pl.ds(pl.multiple_of(i * 256, 256), 256)
        res = dot(h1[r, :], wq[...])
        qkv[r, :] = res.astype(bf16)
        kq[r, :] = pltpu.roll(res[:, :128], 64, 1).astype(bf16)
        return 0

    lax.fori_loop(0, total // 256, project, 0)
    store(qkv, qkv_out)
    ring.pump(17)

    heads = 4

    def head_v(h):
        return slice(128 + h * 128, 256 + h * 128)

    for h in range(heads):

        def state(i, c, h=h):
            s, zz = c
            r = pl.ds(pl.multiple_of(i * 256, 256), 256)
            a, b = phi(kq[r, :], h, sa_ref, sb_ref, lanes_ref)
            f = a * b * lanes_ref[2:3, :] * tok_ref[r, 2:3]
            s = s + dot_tt(f.astype(bf16), qkv[r, head_v(h)])
            return s, zz + jnp.sum(f, axis=0, keepdims=True)

        s, zz = lax.fori_loop(
            0, total // 256, state, (jnp.zeros((256, 128), f32), jnp.zeros((1, 256), f32))
        )
        pack_state(st, h, s, zz)
        ring.pump(18 + h)
    to_x = links.start(st, st_x, seq=seq + 1 - 2 * x)

    def local_head(h):
        for i in range(total // 256):
            r = slice(i * 256, (i + 1) * 256)
            span = (i + 1) * 256
            qm = (qkv[r, :128].astype(f32) * hm_ref[h : h + 1, :]).astype(bf16)
            u = dot_t(qm, kq[:span, :])
            keep = (line_ref[0:1, :span] >= tok_ref[r, 0:1]) & (
                line_ref[0:1, :span] <= tok_ref[r, 3:4]
            )
            kap = jnp.where(keep, (0.5 * u + 1.0) * u + 1.0, 0.0)
            den[r, h : h + 1] = jnp.sum(kap, axis=1, keepdims=True)
            num[r, h * 128 : (h + 1) * 128] = dot(kap.astype(bf16), qkv[:span, head_v(h)])

    local_head(0)
    ring.pump(23)
    local_head(1)
    ring.pump(25)
    to_x.wait_recv()
    for h in range(heads):
        mine, theirs = st[h].astype(f32), st_x[h].astype(f32)
        early = jnp.where(x == 0, mine, theirs)
        later = jnp.where(x == 0, theirs, mine)
        st_t[h] = (later + coef_ref[0:1, :] * early).astype(bf16)
    to_z = [links.copy(st_t, st_z.at[d - 1], seq=seq + 2 * d) for d in (1, 2, 3)]
    for d in (1, 2, 3):

        @pl.when(z + d < 4)
        def _(d=d):
            to_z[d - 1].start()

    local_head(2)
    ring.pump(27)
    local_head(3)
    ring.pump(28)
    own_kept[1].wait()
    got = load_weights(load, wo_all, wo)
    for h in range(heads):
        num_in = coef_ref[1:2, :] * st_x[h].astype(f32)
        s_in[h, 0:176, :] = num_in
        s_in[h, 176:256, :] = jnp.zeros((80, 128), f32)
    for d in (1, 2, 3):

        @pl.when(z >= d)
        def _(d=d):
            to_z[d - 1].wait_recv()
            for h in range(heads):
                s_in[h, 0:176, :] += coef_ref[1 + d : 2 + d, :] * st_z[d - 1, h].astype(f32)

    store(s_in, sin_out)
    for h in range(heads):
        z_row = jnp.concatenate([s_in[h, 160:161, :], s_in[h, 161:162, :]], axis=1)
        feat = jax.lax.broadcasted_iota(jnp.int32, (256, 128), 0)
        s_low = jnp.where(feat < FEATS, s_in[h], 0.0).astype(bf16)

        def carry(i, _, h=h, z_row=z_row, s_low=s_low):
            r = pl.ds(pl.multiple_of(i * 256, 256), 256)
            a, b = phi(qkv[r, 0:128], h, sa_ref, sb_ref, lanes_ref)
            f = a * b * lanes_ref[2:3, :] * tok_ref[r, 1:2]
            hv = slice(h * 128, (h + 1) * 128)
            top = num[r, hv] + dot(f.astype(bf16), s_low)
            low = den[r, h : h + 1] + jnp.sum(f * z_row, axis=1, keepdims=True)
            den[r, h : h + 1] = low
            y = top / low
            yb[r, hv] = y.astype(bf16)
            return 0

        lax.fori_loop(0, total // 256, carry, 0)
        ring.pump(29 + h)
    store(yb, yb_out)
    store(den, den_out)
    for made in got:
        made.wait()

    y_at, c_at = tp // 2, tp % 2

    def out_rows(block):
        return yb[pl.ds(pl.multiple_of(block * rows, rows), rows), :]

    cols = 512
    to_core = []
    for yy in (0, 1):

        def core_cols(i, _, yy=yy):
            c = pl.ds(pl.multiple_of(i * cols, cols), cols)
            sc[yy, :, c] = dot_t(out_rows(yy * 2 + 1 - c_at), wo[c, :]).astype(bf16)
            return 0

        lax.fori_loop(0, 2048 // cols, core_cols, 0)
        to_core.append(links.start(sc.at[yy], rc.at[yy], tp=over_core))
    for made in to_core:
        made.wait_recv()

    def away_cols(i, _):
        c = pl.ds(pl.multiple_of(i * cols, cols), cols)
        part = dot_t(out_rows((1 - y_at) * 2 + c_at), wo[c, :])
        sy[:, c] = (part + rc[1 - y_at, :, c].astype(f32)).astype(bf16)
        return 0

    lax.fori_loop(0, 2048 // cols, away_cols, 0)
    to_y = links.start(sy, ry, tp=over_y)

    def own_cols(i, _):
        c = pl.ds(pl.multiple_of(i * cols, cols), cols)
        x1[:, c] = (
            dot_t(out_rows(tp), wo[c, :]) + rc[y_at, :, c].astype(f32) + x_ref[:, c].astype(f32)
        )
        return 0

    lax.fori_loop(0, 2048 // cols, own_cols, 0)
    ring.pump(34)
    to_y.wait_recv()

    def norm_second(i, _):
        r = pl.ds(pl.multiple_of(i * 32, 32), 32)
        v = x1[r, :] + ry[r, :].astype(f32)
        x1[r, :] = v
        s = lax.rsqrt(jnp.mean(v * v, axis=1, keepdims=True) + epsilon)
        ho[r, :] = (v * s * gains[1:2, :]).astype(bf16)
        return 0

    lax.fori_loop(0, rows // 32, norm_second, 0)
    store(x1, x1_out)
    store(gains, gain_out)
    hrows = Rows(links, ho, h2, tp, over_y, over_core, rows)
    own_in = load(ho, hrows.block(tp, 0, rows))
    ring.pump(36)
    hrows.forward(0)
    ring.pump(37)
    hrows.forward(1)
    crows.forward(0)
    crows.forward(1)
    hrows.finish()
    crows.finish()
    own_in.wait()
    store(h2, h2_out)
    ring.pump_array(2)
    own_kept[2].wait()
    got = load_weights(load, wg_all, wg)
    ring.pump_array(3)
    own_kept[3].wait()
    got += load_weights(load, wu_all, wu)
    for made in got:
        made.wait()

    def gate_up(i, _):
        r = pl.ds(pl.multiple_of(i * 128, 128), 128)
        g = dot(h2[r, :], wg[...])
        uu = dot(h2[r, :], wu[...])
        gate[r, :] = g.astype(bf16)
        up[r, :] = uu.astype(bf16)
        mm[r, :] = (g * jax.nn.sigmoid(g) * uu).astype(bf16)
        return 0

    for quarter in range(4):
        lax.fori_loop(quarter * total // 512, (quarter + 1) * total // 512, gate_up, 0)
        ring.pump(58 + 2 * quarter)
    store(gate, gate_out)
    store(up, up_out)
    store(mm, m_out)
    ring.pump_array(4)
    own_kept[4].wait()
    for made in pending:
        made.wait()
    links.finish()
    for d in (1, 2, 3):

        @pl.when(z + d < 4)
        def _(d=d):
            to_z[d - 1].wait_send()


def pack_state(st, h, s, zz):
    st[h, 0:FEATS, :] = s[:FEATS].astype(bf16)
    tail = jnp.concatenate([zz[:, :128], zz[:, 128:], jnp.zeros((14, 128), f32)], axis=0)
    st[h, FEATS : FEATS + 16, :] = tail.astype(bf16)


def load_weights(load, everyone, flat):
    count, chunk = everyone.shape[0], everyone.shape[1]
    return [load(everyone.at[j], flat.at[pl.ds(j * chunk, chunk)]) for j in range(count)]


class Scatter:
    def __init__(self, slots, send, recv, nearby):
        self.slots, self.send, self.recv, self.nearby = slots, send, recv, nearby

    def copy(self, a, step, way, sub, src, slot, width):
        return pltpu.make_async_remote_copy(
            src_ref=src,
            dst_ref=self.piece(slot, way, sub, width),
            send_sem=self.send.at[a % 2, way, sub],
            recv_sem=self.recv.at[a % 2, way, sub, step],
            device_id={"seq": self.nearby[way]},
            device_id_type=pl.DeviceIdType.MESH,
        )

    def rows(self, way, sub, base=0):
        start = base + way * 128 + sub * 64
        return pl.ds(start if isinstance(start, int) else pl.multiple_of(start, 64), 64)

    def piece(self, slot, way, sub, width):
        return self.slots.at[slot, self.rows(way, sub), pl.ds(0, width)]

    def begin(self, a, own, width, column=0):
        for sub in (0, 1):
            for way in (0, 1):
                src = own.at[self.rows(way, sub, way * 256), pl.ds(column, width)]
                self.copy(a, 0, way, sub, src, 7 * (a % 2), width).start()

    def event(self, a, e, own, width, out, column=0):
        step, sub = e // 2, e % 2
        is_first, is_last = (6 - step) // 6, step // 6
        here = is_first * 7 * (a % 2) + (1 - is_first) * step
        far = (step + 1) // 4
        place0 = (1 - far) * 2 * (step + 1) + far * (11 - 2 * step) + is_last * 8
        far = (step + 2) // 4 - is_last
        place1 = (1 - far) * (3 + 2 * step) + far * (10 - 2 * step) + is_last * 9
        places = (place0, place1)
        for way in (0, 1):
            piece = self.piece(here, way, sub, width)
            came = self.copy(a, step, way, sub, piece, here, width)
            came.wait_recv()
            came.wait_send()

        def summed(way):
            mine = own[self.rows(way, sub, places[way] * 256), pl.ds(column, width)]
            came = self.slots[here, self.rows(way, sub), pl.ds(0, width)]
            return came.astype(f32) + mine.astype(f32)

        def on():
            for way in (0, 1):
                self.slots[here, self.rows(way, sub), pl.ds(0, width)] = summed(way).astype(bf16)
                piece = self.piece(here, way, sub, width)
                self.copy(a, step + 1, way, sub, piece, step + 1, width).start()

        def end():
            for way in (0, 1):
                out[self.rows(way, sub), pl.ds(0, width)] = summed(way)

        if isinstance(e, int):
            if step < 6:
                on()
            else:
                end()
        else:
            pl.when(step < 6)(on)
            pl.when(step == 6)(end)


class TpSum:
    def __init__(self, part, from_core, from_y, sems, credits, tp, over_y, over_core):
        self.part, self.from_core, self.from_y = part, from_core, from_y
        self.sems, self.credits = sems, credits
        self.tp, self.over_y, self.over_core = tp, over_y, over_core
        self.y, self.c = tp // 2, tp % 2

    def to_core(self, i, yy):
        return pltpu.make_async_remote_copy(
            src_ref=self.part.at[i, yy * 2 + 1 - self.c],
            dst_ref=self.from_core.at[i, yy],
            send_sem=self.sems.at[yy, i],
            recv_sem=self.sems.at[2 + yy, i],
            device_id={"tp": self.over_core},
            device_id_type=pl.DeviceIdType.MESH,
        )

    def to_y(self, i):
        return pltpu.make_async_remote_copy(
            src_ref=self.part.at[i, (1 - self.y) * 2 + self.c],
            dst_ref=self.from_y.at[i],
            send_sem=self.sems.at[4, i],
            recv_sem=self.sems.at[5, i],
            device_id={"tp": self.over_y},
            device_id_type=pl.DeviceIdType.MESH,
        )

    def sent(self, i):
        self.to_core(i, 0).wait_send()
        self.to_core(i, 1).wait_send()
        self.to_y(i).wait_send()

    def offer(self, i, turn, value):
        if turn > 0:
            self.sent(i)
        for block in range(4):
            self.part[i, block] = value[block * 256 : (block + 1) * 256].astype(bf16)
        if turn > 0:
            pl.semaphore_wait(self.credits.at[0], 1)
        for yy in (0, 1):
            self.to_core(i, yy).start()

    def pass_on(self, i, turn):
        for yy in (0, 1):
            self.to_core(i, yy).wait_recv()
        away = (1 - self.y) * 2 + self.c
        self.part[i, away] = (
            self.part[i, away].astype(f32) + self.from_core[i, 1 - self.y].astype(f32)
        ).astype(bf16)
        if turn > 0:
            pl.semaphore_wait(self.credits.at[1], 1)
        self.to_y(i).start()

    def take(self, i, turn, use):
        self.to_y(i).wait_recv()
        use(
            self.part[i, self.tp].astype(f32)
            + self.from_core[i, self.y].astype(f32)
            + self.from_y[i].astype(f32)
        )
        if turn < 2:
            for k, peer in ((0, self.over_core), (1, self.over_y)):
                pl.semaphore_signal(
                    self.credits.at[k],
                    inc=1,
                    device_id={"tp": peer},
                    device_id_type=pl.DeviceIdType.MESH,
                )


def col(i, width=256):
    return pl.ds(i * width if isinstance(i, int) else pl.multiple_of(i * width, width), width)


def bwd_kernel(
    tok_ref, line_ref, sa_ref, sb_ref, lanes_ref, hm_ref, coef_ref, gains, x_in, x1_in, s_in, den,
    wq_all, wo_all, wg_all, wu_all, wd_all, c_all, h1_all, qkv_all, yb_all, h2_all,
    gate_all, up_all, m_all,
    d_out, g_out, u_out, oq_out, block_out, input_out,
    slots, s1, s2, wo, stream, hs, rows_all, mm, dup, tiles, qkv, kq, yb, dnum, dden, dden_t, dqkv,
    dq, dk, part, from_core, from_y, acc, x1, bo, fout, st, st_x, st_t, st_z, s_back, own_rows,
    ring_send, ring_recv, tp_sems, credits, send, recv, local, tile_sems,
):
    seq, tp, place, nearby, over_y, over_core, peers = places()
    z, x = seq // 2, seq % 2
    rows, width = own_rows.shape
    total = 4 * rows
    ff = mm.shape[1]
    links = Links(send, recv)
    locs = Sems(local)

    def load(src, dst):
        made = pltpu.make_async_copy(src, dst, locs.take())
        made.start()
        return made

    def whole(everyone, flat):
        count, chunk = everyone.shape[0], everyone.shape[1]
        return [load(everyone.at[j], flat.at[pl.ds(j * chunk, chunk)]) for j in range(count)]

    got_c = load(c_all, rows_all)
    got_m = load(m_all, mm)
    got_wd = whole(wd_all, s2)
    greet(peers)
    got_x1 = load(x1_in, x1)
    got_qkv = [load(qkv_all, qkv), load(yb_all, yb)]
    got_wo = whole(wo_all, wo)
    ring = Scatter(slots, ring_send, ring_recv, nearby)
    sums = TpSum(part, from_core, from_y, tp_sems, credits, tp, over_y, over_core)

    def run(n, body, pumps=None, lookup=None):
        def step(i, _):
            body(i)
            if pumps:
                a, first, count = pumps
                every = n // count
                pl.when((i + 1) % every == 0)(lambda: event(a, first + (i + 1) // every - 1))
            return 0

        lax.fori_loop(0, n, step, 0)

    plan = {0: (s1, ff, 0), 1: (s2, ff, 0), 2: (s1, ff, 0), 3: (s2, 1152, 0)}

    def event(a, e):
        own, wide, column = plan[a]
        ring.event(a, e, own, wide, fout, column)

    def begin(a):
        own, wide, column = plan[a]
        ring.begin(a, own, wide, column)

    def events(a, first, last):
        lax.fori_loop(first, last, lambda e, _: (event(a, e), 0)[1], 0)

    def chunks_of(source, size, body, pumps=None, count=8):
        def copies(i, slot):
            return [
                pltpu.make_async_copy(a, b, tile_sems.at[k, slot])
                for k, (a, b) in enumerate(source(i, slot))
            ]

        for made in copies(0, 0):
            made.start()

        def step(i):
            slot = i % 2

            @pl.when(i + 1 < count)
            def _():
                for made in copies(i + 1, 1 - slot):
                    made.start()

            for made in copies(i, slot):
                made.wait()
            body(i, slot)

        run(count, step, pumps)

    got_c.wait()
    got_m.wait()

    def grad_down(j):
        s1[col(j), :] = dot_tt(rows_all[:, col(j)], mm[...]).astype(bf16)

    run(2, grad_down)
    begin(0)
    lax.fori_loop(2, 8, lambda j, _: (grad_down(j), 0)[1], 0)
    for made in got_wd:
        made.wait()
    events(0, 0, 1)

    def mlp(i):
        sums.offer(i, 0, dot_t(mm[...], s2[col(i), :]))
        pl.when(i > 0)(lambda: sums.pass_on(i - 1, 0))

    run(8, mlp, (0, 1, 2))
    sums.pass_on(7, 0)

    def gate_up_tiles(i, slot):
        r = col(i, 128)
        return [(gate_all.at[r], tiles.at[slot, 0]), (up_all.at[r], tiles.at[slot, 1])]

    def grad_gate_up(i, slot):
        r = col(i, 128)
        dm = dot(rows_all[r, :], s2[...]).astype(bf16).astype(f32)
        g = tiles[slot, 0].astype(f32)
        u = tiles[slot, 1].astype(f32)
        s = jax.nn.sigmoid(g)
        mm[r, :] = (dm * u * s * (1.0 + g * (1.0 - s))).astype(bf16)
        dup[r, :] = (dm * (g * s)).astype(bf16)

        def use(value):
            bo[:, col(i)] = (x1[:, col(i)] + value).astype(bf16)

        sums.take(i, 0, use)

    got_x1.wait()
    chunks_of(gate_up_tiles, 8, grad_gate_up, (0, 3, 4))
    pending = [load(bo, block_out)]

    def w_tiles(i, slot):
        return [(wg_all.at[i], stream.at[slot, 0]), (wu_all.at[i], stream.at[slot, 1])]

    def grad_hidden(i, slot):
        value = dot_t(mm[...], stream[slot, 0]) + dot_t(dup[...], stream[slot, 1])
        sums.offer(i, 1, value)
        pl.when(i > 0)(lambda: sums.pass_on(i - 1, 1))

    chunks_of(w_tiles, 8, grad_hidden, (0, 7, 2))
    sums.pass_on(7, 1)

    def h_tiles(everyone):
        return lambda i, slot: [(everyone.at[:, col(i)], hs.at[slot])]

    def grad_gate(i, slot):
        s2[col(i), :] = dot_tt(hs[slot], mm[...]).astype(bf16)

    chunks_of(h_tiles(h2_all), 8, grad_gate, (0, 9, 2))
    events(0, 11, 12)
    begin(1)

    def take_second(i):
        def use(value):
            acc[:, col(i)] = value

        sums.take(i, 1, use)

    run(8, take_second, (0, 12, 2))
    done = load(fout.at[:, pl.ds(0, ff)], d_out)

    def norm_back_second(i, _):
        r = pl.ds(pl.multiple_of(i * 32, 32), 32)
        v = x1[r, :]
        s = lax.rsqrt(jnp.mean(v * v, axis=1, keepdims=True) + epsilon)
        n = v * s
        dn = acc[r, :] * gains[1:2, :]
        own = pl.ds(pl.multiple_of(tp * rows + i * 32, 32), 32)
        back = rows_all[own, :].astype(f32) + s * (
            dn - n * jnp.mean(dn * n, axis=1, keepdims=True)
        )
        acc[r, :] = back
        own_rows[r, :] = back.astype(bf16)
        return 0

    lax.fori_loop(0, rows // 32, norm_back_second, 0)
    da = Rows(links, own_rows, rows_all, tp, over_y, over_core, rows)
    own_in = load(own_rows, da.block(tp, 0, rows))

    def grad_up(i, slot):
        s1[col(i), :] = dot_tt(hs[slot], dup[...]).astype(bf16)

    chunks_of(h_tiles(h2_all), 8, grad_up, (1, 0, 2))
    da.forward(0)
    events(1, 2, 5)
    da.forward(1)
    for made in got_qkv + got_wo:
        made.wait()
    da.finish()
    own_in.wait()
    links.sent_now(da.first + [da.near])
    got_x = load(x_in, own_rows)

    def head_v(h):
        return slice(128 + h * 128, 256 + h * 128)

    def grad_attended(i):
        r = col(i, 256)
        dy = dot(rows_all[r, :], wo[...])
        kq[r, :] = pltpu.roll(qkv[r, 0:128].astype(f32), 64, 1).astype(bf16)
        columns = []
        for h in range(4):
            hv = slice(h * 128, (h + 1) * 128)
            under = 1.0 / den[r, h : h + 1]
            part_h = dy[:, hv]
            dnum[r, hv] = (part_h * under).astype(bf16)
            low = jnp.sum(part_h * yb[r, hv].astype(f32), axis=1, keepdims=True)
            columns.append(-low * under)
        lane = lax.broadcasted_iota(jnp.int32, (256, 128), 1)
        packed = jnp.zeros((256, 128), f32)
        for h in range(4):
            packed = jnp.where(lane == h, columns[h], packed)
        dden[r, :] = packed
        dden_t[i] = packed.T[0:8, :]

    run(4, grad_attended)
    event(1, 5)

    for h in range(4):

        def state(i, c, h=h):
            s, zz = c
            r = col(i, 256)
            a, b = phi(qkv[r, 0:128], h, sa_ref, sb_ref, lanes_ref)
            f = a * b * lanes_ref[2:3, :] * tok_ref[r, 1:2]
            s = s + dot_tt(f.astype(bf16), dnum[r, h * 128 : (h + 1) * 128])
            return s, zz + jnp.sum(f * dden[r, h : h + 1], axis=0, keepdims=True)

        s, zz = lax.fori_loop(
            0, 4, state, (jnp.zeros((256, 128), f32), jnp.zeros((1, 256), f32))
        )
        pack_state(st, h, s, zz)
    to_x = links.start(st, st_x, seq=seq + 1 - 2 * x)
    event(1, 6)

    dq[...] = jnp.zeros(dq.shape, f32)

    def local_head(h):
        hm = hm_ref[h : h + 1, :]
        hv = slice(h * 128, (h + 1) * 128)
        for j in range(total // 256):
            k_rows = slice(j * 256, (j + 1) * 256)
            dv_s = jnp.zeros((256, 128), f32)
            dk_s = jnp.zeros((256, 128), f32)
            for i in range(j, total // 256):
                q_rows = slice(i * 256, (i + 1) * 256)
                qm = (qkv[q_rows, 0:128].astype(f32) * hm).astype(bf16)
                u = dot_t(kq[k_rows, :], qm)
                keep = tok_ref[k_rows, 3:4] >= line_ref[1:2, q_rows]
                if i == j:
                    keep = keep & (tok_ref[k_rows, 3:4] <= line_ref[0:1, q_rows])
                kap = jnp.where(keep, (0.5 * u + 1.0) * u + 1.0, 0.0).astype(bf16)
                dn = dnum[q_rows, hv]
                grad = dot_t(qkv[k_rows, head_v(h)], dn) + dden_t[i, h : h + 1, :]
                du = jnp.where(keep, grad * (1.0 + u), 0.0).astype(bf16)
                dv_s = dv_s + dot(kap, dn)
                dk_s = dk_s + dot(du, qm)
                dq[q_rows, :] += dot_tt(du, kq[k_rows, :]) * hm
            dqkv[k_rows, head_v(h)] = dv_s.astype(bf16)
            if h == 0:
                dk[k_rows, :] = dk_s
            else:
                dk[k_rows, :] += dk_s

    local_head(0)
    to_x.wait_recv()
    for h in range(4):
        mine, theirs = st[h].astype(f32), st_x[h].astype(f32)
        first = jnp.where(x == 0, mine, theirs)
        second = jnp.where(x == 0, theirs, mine)
        st_t[h] = (first + coef_ref[0:1, :] * second).astype(bf16)
    to_z = [links.copy(st_t, st_z.at[d - 1], seq=seq - 2 * d) for d in (1, 2, 3)]
    for d in (1, 2, 3):

        @pl.when(z >= d)
        def _(d=d):
            to_z[d - 1].start()

    events(1, 7, 8)
    local_head(1)
    events(1, 8, 9)
    local_head(2)
    events(1, 9, 10)
    local_head(3)
    events(1, 10, 12)
    begin(2)
    for h in range(4):
        s_back[h, 0:176, :] = coef_ref[1:2, :] * st_x[h].astype(f32)
        s_back[h, 176:256, :] = jnp.zeros((80, 128), f32)
    for d in (1, 2, 3):

        @pl.when(z + d < 4)
        def _(d=d):
            to_z[d - 1].wait_recv()
            for h in range(4):
                s_back[h, 0:176, :] += coef_ref[1 + d : 2 + d, :] * st_z[d - 1, h].astype(f32)

    def split_state(ref, h):
        z_row = jnp.concatenate([ref[h, 160:161, :], ref[h, 161:162, :]], axis=1)
        feat = lax.broadcasted_iota(jnp.int32, (256, 128), 0)
        return jnp.where(feat < FEATS, ref[h], 0.0).astype(bf16), z_row

    for h in range(4):
        s_q, z_q = split_state(s_in, h)
        s_k, z_k = split_state(s_back, h)
        hv = slice(h * 128, (h + 1) * 128)

        def through(grad, a, b, h=h):
            grad = grad * lanes_ref[2:3, :]
            return dot_t((grad * b).astype(bf16), sa_ref[h]) + dot_t(
                (grad * a).astype(bf16), sb_ref[h]
            )

        def carried_part(i, _, h=h, s_q=s_q, z_q=z_q, s_k=s_k, z_k=z_k, hv=hv, through=through):
            r = col(i, 256)
            a, b = phi(qkv[r, 0:128], h, sa_ref, sb_ref, lanes_ref)
            grad = dot_t(dnum[r, hv], s_q) + dden[r, h : h + 1] * z_q
            dq[r, :] += through(grad * tok_ref[r, 1:2], a, b)
            a, b = phi(kq[r, :], h, sa_ref, sb_ref, lanes_ref)
            last = tok_ref[r, 2:3]
            grad = dot_t(qkv[r, head_v(h)], s_k) + z_k
            dk[r, :] += through(grad * last, a, b)
            f = (a * b * lanes_ref[2:3, :] * last).astype(bf16)
            dqkv[r, head_v(h)] = (dqkv[r, head_v(h)].astype(f32) + dot(f, s_k)).astype(bf16)
            return 0

        lax.fori_loop(0, 4, carried_part, 0)

    def join(i):
        r = col(i, 256)
        dqkv[r, 0:128] = (dq[r, :] + pltpu.roll(dk[r, :], 64, 1)).astype(bf16)

    run(4, join)
    done.wait()
    events(1, 12, 14)
    done = load(fout.at[:, pl.ds(0, ff)], g_out)

    def wq_tiles(i, slot):
        return [(wq_all.at[i], stream.at[slot, 0, :, pl.ds(0, 640)])]

    def grad_hidden_first(i, slot):
        sums.offer(i, 2, dot_t(dqkv[...], stream[slot, 0, :, 0:640]))
        pl.when(i > 0)(lambda: sums.pass_on(i - 1, 2))

    chunks_of(wq_tiles, 8, grad_hidden_first, (2, 0, 2))
    sums.pass_on(7, 2)

    def grad_out_qkv(i, slot):
        s2[col(i), 0:512] = dot_tt(rows_all[:, col(i)], yb[...]).astype(bf16)
        s2[col(i), 512:1152] = dot_tt(hs[slot], dqkv[...]).astype(bf16)

    chunks_of(h_tiles(h1_all), 8, grad_out_qkv, (2, 2, 2))
    events(2, 4, 6)
    def take_first(i):
        def use(value):
            x1[:, col(i)] = value

        sums.take(i, 2, use)

    run(8, take_first, (2, 6, 2))
    got_x.wait()

    def norm_back_first(i, _):
        r = pl.ds(pl.multiple_of(i * 32, 32), 32)
        v = own_rows[r, :].astype(f32)
        s = lax.rsqrt(jnp.mean(v * v, axis=1, keepdims=True) + epsilon)
        n = v * s
        dn = x1[r, :] * gains[0:1, :]
        acc[r, :] += s * (dn - n * jnp.mean(dn * n, axis=1, keepdims=True))
        return 0

    lax.fori_loop(0, rows // 32, norm_back_first, 0)
    pending.append(load(acc, input_out))
    events(2, 8, 12)
    begin(3)
    done.wait()
    events(2, 12, 14)
    done = load(fout.at[:, pl.ds(0, ff)], u_out)
    events(3, 0, 12)
    done.wait()
    events(3, 12, 14)
    load(fout.at[:, pl.ds(0, 1152)], oq_out).wait()
    run(8, lambda i: sums.sent(i))
    for made in pending:
        made.wait()
    links.finish()
    for d in (1, 2, 3):

        @pl.when(z >= d)
        def _(d=d):
            to_z[d - 1].wait_send()


def feature_tables(heads):
    first = np.zeros((heads, 128, 256), np.float32)
    second = np.zeros((heads, 128, 256), np.float32)
    lanes = np.zeros((8, 256), np.float32)
    f = 0
    for i in range(FEAT):
        for j in range(i, FEAT):
            for h in range(heads):
                first[h, h * FEAT + i, f] = 1
                second[h, h * FEAT + j, f] = 1
            lanes[2, f] = square_coef if i == j else square_coef * 2**0.5
            f += 1
    for i in range(FEAT):
        for h in range(heads):
            first[h, h * FEAT + i, f] = 1
        lanes[1, f] = 1
        lanes[2, f] = linear_coef
        f += 1
    lanes[0, f] = lanes[1, f] = lanes[2, f] = 1
    mask = np.zeros((8, 128), np.float32)
    for h in range(heads):
        mask[h, h * FEAT : (h + 1) * FEAT] = 0.25
    return first, second, lanes, mask


def token_tables(lengths, seq_index, block_len, seq_count):
    at = jnp.arange(lengths.shape[0])
    starts = jnp.sum(jnp.where(at[None, :] < at[:, None], lengths[None, :], 0), axis=1)
    anchor = seq_index * block_len
    positions = anchor + jnp.arange(block_len, dtype=jnp.int32)
    begun = starts[None, :] <= positions[:, None]
    row_start = jnp.max(jnp.where(begun, starts[None, :], 0), axis=1)
    carry_in = row_start < anchor
    later = (starts[None, :] > positions[:, None]) & (starts[None, :] < anchor + block_len)
    after_last = jnp.sum(later.astype(jnp.int32), axis=1) == 0
    place = jnp.arange(block_len, dtype=jnp.int32)
    tok = jnp.stack(
        [
            jnp.maximum(row_start - anchor, 0).astype(f32),
            carry_in.astype(f32),
            after_last.astype(f32),
            place.astype(f32),
        ],
        axis=1,
    )
    line = jnp.concatenate([tok[:, 3][None], tok[:, 0][None], jnp.zeros((6, block_len), f32)])
    resets = (
        jnp.sum(
            ((starts // block_len)[None, :] == jnp.arange(seq_count)[:, None]).astype(jnp.int32),
            axis=1,
        )
        > 0
    ).astype(jnp.int32)

    def clear(first, last):
        blocks = jnp.arange(seq_count)
        inside = (blocks >= first) & (blocks <= last)
        return (jnp.sum(jnp.where(inside, resets, 0)) == 0).astype(f32)

    z, x = seq_index // 2, seq_index % 2
    coefs = [clear(2 * z + 1, 2 * z + 1), (x == 1).astype(f32)]
    coefs += [clear(2 * (z - d) + 2, seq_index - 1) for d in (1, 2, 3)]
    coefs += [jnp.zeros((), f32)] * 3
    back = [clear(2 * z, 2 * z), (x == 0).astype(f32)]
    back += [clear(seq_index + 1, 2 * (z + d) - 1) for d in (1, 2, 3)]
    back += [jnp.zeros((), f32)] * 3

    def wide(values):
        return jnp.broadcast_to(jnp.stack(values)[:, None], (8, 128))

    return tok, line, wide(coefs), wide(back)


def forward_pass(tables, x_own, c_own, gain_own, q_own, o_own, g_own, u_own, d_own):
    rows, width = x_own.shape
    total = 4 * rows
    ff = g_own.shape[1]
    hbm = pl.BlockSpec(memory_space=pl.ANY)
    vmem = pl.BlockSpec(memory_space=pltpu.VMEM)

    def shape(*dims, dtype=bf16):
        return jax.ShapeDtypeStruct(dims, dtype)

    outs = (
        shape(8, 256, q_own.shape[1]),
        shape(8, 256, o_own.shape[1]),
        shape(8, 256, ff),
        shape(8, 256, ff),
        shape(8, 256, ff),
        shape(total, width),
        shape(total, width),
        shape(total, q_own.shape[1]),
        shape(total, 512),
        shape(total, 128, dtype=f32),
        shape(rows, width, dtype=f32),
        shape(total, width),
        shape(total, ff),
        shape(total, ff),
        shape(total, ff),
        shape(4, 256, 128, dtype=f32),
        shape(8, width, dtype=f32),
    )
    scratch = [
        pltpu.VMEM((total, width), bf16),
        pltpu.VMEM((total, width), bf16),
        pltpu.VMEM((width, q_own.shape[1]), bf16),
        pltpu.VMEM((width, o_own.shape[1]), bf16),
        pltpu.VMEM((width, ff), bf16),
        pltpu.VMEM((width, ff), bf16),
        pltpu.VMEM((total, q_own.shape[1]), bf16),
        pltpu.VMEM((total, 128), bf16),
        pltpu.VMEM((total, 512), f32),
        pltpu.VMEM((total, 128), f32),
        pltpu.VMEM((total, 512), bf16),
        pltpu.VMEM((2, rows, width), bf16),
        pltpu.VMEM((2, rows, width), bf16),
        pltpu.VMEM((rows, width), bf16),
        pltpu.VMEM((rows, width), bf16),
        pltpu.VMEM((rows, width), f32),
        pltpu.VMEM((total, width), bf16),
        pltpu.VMEM((total, ff), bf16),
        pltpu.VMEM((total, ff), bf16),
        pltpu.VMEM((total, ff), bf16),
        pltpu.VMEM((8, 16, 256), bf16),
        pltpu.VMEM((8, width), f32),
        pltpu.VMEM((4, 176, 128), bf16),
        pltpu.VMEM((4, 176, 128), bf16),
        pltpu.VMEM((4, 176, 128), bf16),
        pltpu.VMEM((3, 4, 176, 128), bf16),
        pltpu.VMEM((4, 256, 128), f32),
        pltpu.VMEM((rows, width), bf16),
        pltpu.SemaphoreType.DMA((112,)),
        pltpu.SemaphoreType.DMA((112,)),
        pltpu.SemaphoreType.DMA((64,)),
    ]
    return pl.pallas_call(
        fwd_kernel,
        out_shape=outs,
        in_specs=[vmem] * 8 + [vmem] + [hbm] * 6,
        out_specs=(hbm,) * len(outs),
        scratch_shapes=scratch,
        compiler_params=pltpu.CompilerParams(
            collective_id=0, has_side_effects=True, vmem_limit_bytes=60 * 2**20
        ),
    )(
        x_own, *tables, gain_own, q_own, o_own, g_own, u_own, d_own, c_own,
    )


def backward_pass(tables, gains, x_own, x1, s_in, den, weights, c_all, acts):
    rows, width = x_own.shape
    total = 4 * rows
    ff = weights[2].shape[2]
    hbm = pl.BlockSpec(memory_space=pl.ANY)
    vmem = pl.BlockSpec(memory_space=pltpu.VMEM)

    def shape(*dims, dtype=f32):
        return jax.ShapeDtypeStruct(dims, dtype)

    outs = (
        shape(256, ff),
        shape(256, ff),
        shape(256, ff),
        shape(256, 1152),
        shape(rows, width, dtype=bf16),
        shape(rows, width),
    )
    scratch = [
        pltpu.VMEM((8, 256, ff), bf16),
        pltpu.VMEM((width, ff), bf16),
        pltpu.VMEM((width, ff), bf16),
        pltpu.VMEM((width, 512), bf16),
        pltpu.VMEM((2, 2, 256, ff), bf16),
        pltpu.VMEM((2, total, 256), bf16),
        pltpu.VMEM((total, width), bf16),
        pltpu.VMEM((total, ff), bf16),
        pltpu.VMEM((total, ff), bf16),
        pltpu.VMEM((2, 2, 128, ff), bf16),
        pltpu.VMEM((total, 640), bf16),
        pltpu.VMEM((total, 128), bf16),
        pltpu.VMEM((total, 512), bf16),
        pltpu.VMEM((total, 512), bf16),
        pltpu.VMEM((total, 128), f32),
        pltpu.VMEM((4, 8, 256), f32),
        pltpu.VMEM((total, 640), bf16),
        pltpu.VMEM((total, 128), f32),
        pltpu.VMEM((total, 128), f32),
        pltpu.VMEM((8, 4, 256, 256), bf16),
        pltpu.VMEM((8, 2, 256, 256), bf16),
        pltpu.VMEM((8, 256, 256), bf16),
        pltpu.VMEM((rows, width), f32),
        pltpu.VMEM((rows, width), f32),
        pltpu.VMEM((rows, width), bf16),
        pltpu.VMEM((256, ff), f32),
        pltpu.VMEM((4, 176, 128), bf16),
        pltpu.VMEM((4, 176, 128), bf16),
        pltpu.VMEM((4, 176, 128), bf16),
        pltpu.VMEM((3, 4, 176, 128), bf16),
        pltpu.VMEM((4, 256, 128), f32),
        pltpu.VMEM((rows, width), bf16),
        pltpu.SemaphoreType.DMA((2, 2, 2)),
        pltpu.SemaphoreType.DMA((2, 2, 2, 7)),
        pltpu.SemaphoreType.DMA((6, 8)),
        pltpu.SemaphoreType.REGULAR((2,)),
        pltpu.SemaphoreType.DMA((16,)),
        pltpu.SemaphoreType.DMA((16,)),
        pltpu.SemaphoreType.DMA((48,)),
        pltpu.SemaphoreType.DMA((2, 2)),
    ]
    return pl.pallas_call(
        bwd_kernel,
        out_shape=outs,
        in_specs=[vmem] * 8 + [hbm] * 2 + [vmem] * 2 + [hbm] * 13,
        out_specs=(hbm,) * len(outs),
        scratch_shapes=scratch,
        compiler_params=pltpu.CompilerParams(
            collective_id=1, has_side_effects=True, vmem_limit_bytes=62 * 2**20
        ),
    )(*tables, gains, x_own, x1, s_in, den, *weights, c_all, *acts)

def on_device_rings(
    inputs, lengths, gain_attn, w_query, w_key, w_value, w_out, gain_mlp, w_gate, w_up, w_down,
    cotangent,
):
    seq_count = 8
    seq_index = lax.axis_index("seq")
    rows, width = inputs.shape
    chunk = width // seq_count
    relative = relative_list(seq_count)
    ring = ring_order(seq_count)
    place_of = [ring.index(s) for s in range(seq_count)]
    to_rel = jnp.array(
        [[ring[(place_of[s] - k) % seq_count] for k in relative] for s in range(seq_count)],
        jnp.int32,
    )[seq_index]
    to_abs = jnp.array(
        [
            [relative.index((place_of[s] - place_of[o]) % seq_count) for o in range(seq_count)]
            for s in range(seq_count)
        ],
        jnp.int32,
    )[seq_index]
    to_rel = [to_rel[j] for j in range(seq_count)]
    to_abs = [to_abs[j] for j in range(seq_count)]

    gains = jnp.stack([gain_attn, gain_mlp]).astype(bf16)
    gain_own = jnp.zeros((16, chunk), bf16).at[:2].set(gains)
    qkv_own = jnp.concatenate([w_query, w_key, w_value], axis=1).astype(bf16)
    out_own = w_out.astype(bf16).T
    gate_own, up_own = w_gate.astype(bf16), w_up.astype(bf16)
    down_own = w_down.astype(bf16).T
    x_own = to_relative(inputs, to_rel, chunk)
    c_own = to_relative(cotangent, to_rel, chunk)

    tok, line, coefs, back = token_tables(lengths, seq_index, 4 * rows, seq_count)
    first, second, lanes, mask = feature_tables(4)
    tables = (
        tok, line, jnp.asarray(first, bf16), jnp.asarray(second, bf16), jnp.asarray(lanes),
        jnp.asarray(mask),
    )
    made = forward_pass(
        (*tables, coefs), x_own, c_own, gain_own, qkv_own, out_own, gate_own, up_own, down_own
    )
    weights, (c_all, h1, qkv, yb, den, x1, h2, gate, up, mixed, s_in, gain_all) = made[:5], made[5:]
    sum_down_t, sum_gate, sum_up, sum_oq, block, grad_input = backward_pass(
        (*tables, back), gain_all, x_own, x1, s_in, den, weights, c_all,
        (h1, qkv, yb, h2, gate, up, mixed),
    )

    sum_qkv = sum_oq[:, 512:]
    gain_terms = jnp.stack(
        [
            jnp.sum(qkv_own.astype(f32) * sum_qkv, axis=1),
            jnp.sum(gate_own.astype(f32) * sum_gate + up_own.astype(f32) * sum_up, axis=1),
        ]
    )
    gain_sums = tp_sum(gain_terms) / gains.astype(f32)
    qk_cols = w_query.shape[1]
    return (
        to_relative(block, to_abs, chunk),
        to_relative(grad_input, to_abs, chunk),
        gain_sums[0],
        sum_qkv[:, :qk_cols],
        sum_qkv[:, qk_cols : 2 * qk_cols],
        sum_qkv[:, 2 * qk_cols :],
        sum_oq[:, :512].T,
        gain_sums[1],
        sum_gate,
        sum_up,
        sum_down_t.T,
    )


def on_device(
    inputs,
    lengths,
    gain_attn,
    w_query,
    w_key,
    w_value,
    w_out,
    gain_mlp,
    w_gate,
    w_up,
    w_down,
    cotangent,
):
    seq_count = lax.axis_size("seq")
    tp_count = lax.axis_size("tp")
    seq_index = lax.axis_index("seq")
    rows_own, width = inputs.shape
    chunk = width // seq_count
    half = chunk // 2
    block_len = rows_own * tp_count
    anchor = seq_index * block_len
    relative = relative_list(seq_count)
    ring = ring_order(seq_count)
    place_of = [ring.index(s) for s in range(seq_count)]
    to_rel = jnp.array(
        [[ring[(place_of[s] - k) % seq_count] for k in relative] for s in range(seq_count)],
        jnp.int32,
    )[seq_index]
    to_abs = jnp.array(
        [
            [relative.index((place_of[s] - place_of[o]) % seq_count) for o in range(seq_count)]
            for s in range(seq_count)
        ],
        jnp.int32,
    )[seq_index]
    to_rel = [to_rel[j] for j in range(seq_count)]
    to_abs = [to_abs[j] for j in range(seq_count)]

    qk_cols, v_cols, ff_cols = w_query.shape[1], w_value.shape[1], w_gate.shape[1]
    gains = jnp.stack([gain_attn, gain_mlp]).astype(bf16)
    qkv_cols = 2 * qk_cols + v_cols
    qkv_own = jnp.concatenate([w_query, w_key, w_value], axis=1).astype(bf16)
    gain_rows = jnp.zeros((16, qkv_cols), bf16).at[:2, :chunk].set(gains)
    first_own = jnp.concatenate([qkv_own, gain_rows], axis=0)
    out_own = w_out.astype(bf16).T
    gate_up_own = jnp.concatenate([w_gate, w_up], axis=1).astype(bf16)
    down_own = w_down.astype(bf16).T

    first_got = ring_gather(first_own, half)
    out_got = ring_gather(out_own, half)
    gate_up_got = ring_gather(gate_up_own, half)
    down_got = ring_gather(down_own, half)
    w_qkv = jnp.concatenate([first_got[k][:chunk] for k in relative], axis=0)
    gain_first = jnp.concatenate([first_got[k][chunk, :chunk] for k in relative]).astype(f32)
    gain_second = jnp.concatenate([first_got[k][chunk + 1, :chunk] for k in relative]).astype(f32)
    w_out_t = jnp.concatenate([out_got[k] for k in relative], axis=0)
    w_gate_up = jnp.concatenate([gate_up_got[k] for k in relative], axis=0)
    w_down_t = jnp.concatenate([down_got[k] for k in relative], axis=0)

    at = jnp.arange(lengths.shape[0])
    starts = jnp.sum(jnp.where(at[None, :] < at[:, None], lengths[None, :], 0), axis=1)
    positions, row_ids, carry_in, after_last = segment_masks(anchor, starts, block_len)
    carry_mask = carry_in.astype(f32)
    last_mask = after_last.astype(f32)
    resets = (
        jnp.sum(
            ((starts // block_len)[None, :] == jnp.arange(seq_count)[:, None]).astype(jnp.int32),
            axis=1,
        )
        > 0
    ).astype(jnp.int32)

    inputs_own = to_relative(inputs, to_rel, chunk)
    grad_own = to_relative(cotangent, to_rel, chunk)
    inputs_full = tp_gather(inputs_own).astype(f32)
    grad_full = tp_gather(grad_own)
    inputs_own = inputs_own.astype(f32)
    hidden_first = (inputs_full * rms_scale(inputs_full) * gain_first).astype(bf16)
    qkv = dot(hidden_first, w_qkv).astype(bf16)
    queries = qkv[:, :qk_cols]
    key_flat = qkv[:, qk_cols : 2 * qk_cols]
    value_flat = qkv[:, 2 * qk_cols :]
    heads_local = qk_cols // FEAT
    query_heads = queries.reshape(block_len, heads_local, FEAT)
    key_heads = key_flat.reshape(block_len, heads_local, FEAT)
    value_heads = value_flat.reshape(block_len, heads_local, VHEAD)
    query_float = query_heads.astype(f32)
    key_float = key_heads.astype(f32)
    value_float = value_heads.astype(f32)
    key_feat = features(key_float) * last_mask[:, None, None]
    local_state = jnp.einsum("thn,thv->hnv", key_feat, value_float, precision=highest)
    local_sum = jnp.sum(key_feat, axis=0)
    carry_state, carry_sum = carried([local_state, local_sum], resets, 1)
    step_rows = 512
    query_feat = features(query_float)
    carry_weight = carry_mask[:, None]
    numer_parts = []
    denom_parts = []
    for first_row in range(0, block_len, step_rows):
        query_part = query_heads[first_row : first_row + step_rows]
        scores, allowed, kernel = pair_block(
            query_part, key_heads, row_ids, positions, first_row, step_rows
        )
        numer_parts.append(
            jnp.einsum("hts,shv->thv", kernel.astype(bf16), value_heads, preferred_element_type=f32)
        )
        denom_parts.append(jnp.sum(kernel, axis=-1).T)
    numerator = (
        jnp.concatenate(numer_parts, axis=0)
        + jnp.einsum("thn,hnv->thv", query_feat, carry_state, precision=highest)
        * carry_weight[:, :, None]
    )
    denominator = (
        jnp.concatenate(denom_parts, axis=0)
        + jnp.einsum("thn,hn->th", query_feat, carry_sum, precision=highest) * carry_weight
    )
    attended = numerator / denominator[:, :, None]
    attended_low = attended.reshape(block_len, heads_local * VHEAD).astype(bf16)
    attn_partial = dot_t(attended_low, w_out_t).astype(bf16)
    middle_own = inputs_own + tp_scatter(attn_partial)
    scale_second = rms_scale(middle_own)
    normed_second = middle_own * scale_second
    hidden_second = tp_gather((normed_second * gain_second).astype(bf16))
    gate_up = dot(hidden_second, w_gate_up)
    gate_value, upward = gate_up[:, :ff_cols], gate_up[:, ff_cols:]
    sigmoid_gate = jax.nn.sigmoid(gate_value)
    silu_gate = gate_value * sigmoid_gate
    mixed_rows = (silu_gate * upward).astype(bf16)
    grad_down_t = dot_tt(grad_full, mixed_rows).astype(bf16)

    def by_distance(stack):
        return {k: stack[j * chunk : (j + 1) * chunk] for j, k in enumerate(relative)}

    sum_down_t = ring_scatter(by_distance(grad_down_t))
    mlp_own = tp_scatter(dot_t(mixed_rows, w_down_t).astype(bf16))
    block_output = to_relative((middle_own + mlp_own).astype(bf16), to_abs, chunk)

    grad_mixed = dot(grad_full, w_down_t).astype(bf16).astype(f32)
    grad_gate = (
        grad_mixed * upward * sigmoid_gate * (1.0 + gate_value * (1.0 - sigmoid_gate))
    ).astype(bf16)
    grad_upward = (grad_mixed * silu_gate).astype(bf16)
    grad_gate_up = jnp.concatenate([grad_gate, grad_upward], axis=1)
    hidden_partial = dot_t(grad_gate_up, w_gate_up).astype(bf16)
    sum_gate_up = ring_scatter(by_distance(dot_tt(hidden_second, grad_gate_up).astype(bf16)))
    grad_hidden = tp_scatter(hidden_partial)
    grad_middle = grad_own.astype(f32) + norm_back(
        grad_hidden, normed_second, scale_second, gain_second
    )
    grad_branch = tp_gather(grad_middle.astype(bf16))
    sum_out_t = ring_scatter(by_distance(dot_tt(grad_branch, attended_low).astype(bf16)))
    grad_attended = dot(grad_branch, w_out_t).reshape(block_len, heads_local, VHEAD)
    grad_numer = (grad_attended / denominator[:, :, None]).astype(bf16)
    grad_denom = -jnp.sum(grad_attended * attended, axis=-1) / denominator
    grad_numer_carried = grad_numer.astype(f32) * carry_weight[:, :, None]
    grad_denom_carried = grad_denom * carry_weight
    grad_state_in = jnp.einsum("thn,thv->hnv", query_feat, grad_numer_carried, precision=highest)
    grad_sum_in = jnp.einsum("thn,th->hn", query_feat, grad_denom_carried, precision=highest)
    grad_query_feat = (
        jnp.einsum("thv,hnv->thn", grad_numer_carried, carry_state, precision=highest)
        + grad_denom_carried[:, :, None] * carry_sum[None]
    )
    grad_state_out, grad_sum_out = carried([grad_state_in, grad_sum_in], resets, -1)
    grad_key_feat = (
        jnp.einsum("thv,hnv->thn", value_float, grad_state_out, precision=highest)
        + grad_sum_out[None]
    ) * last_mask[:, None, None]
    grad_value_state = jnp.einsum("thn,hnv->thv", key_feat, grad_state_out, precision=highest)
    grad_query_parts = []
    grad_key_inner = jnp.zeros((block_len, heads_local, FEAT), f32)
    grad_value_inner = jnp.zeros((block_len, heads_local, VHEAD), f32)
    for first_row in range(0, block_len, step_rows):
        query_part = query_heads[first_row : first_row + step_rows]
        scores, allowed, kernel = pair_block(
            query_part, key_heads, row_ids, positions, first_row, step_rows
        )
        numer_grad_part = grad_numer[first_row : first_row + step_rows]
        grad_weights = jnp.einsum(
            "thv,shv->hts", numer_grad_part, value_heads, preferred_element_type=f32
        )
        grad_scores = (
            (grad_weights + grad_denom[first_row : first_row + step_rows].T[:, :, None])
            * allowed[None]
            * (1.0 + scores)
        ).astype(bf16)
        grad_query_parts.append(
            jnp.einsum("hts,shf->thf", grad_scores, key_heads, preferred_element_type=f32) * 0.25
        )
        grad_key_inner = (
            grad_key_inner
            + jnp.einsum("hts,thf->shf", grad_scores, query_part, preferred_element_type=f32) * 0.25
        )
        grad_value_inner = grad_value_inner + jnp.einsum(
            "hts,thv->shv", kernel.astype(bf16), numer_grad_part, preferred_element_type=f32
        )
    grad_query = (
        jnp.concatenate(grad_query_parts, axis=0) + feature_grad(query_float, grad_query_feat)
    ).astype(bf16)
    grad_key = (grad_key_inner + feature_grad(key_float, grad_key_feat)).astype(bf16)
    grad_value = (grad_value_inner + grad_value_state).astype(bf16)
    grad_qkv = jnp.concatenate(
        [
            grad_query.reshape(block_len, heads_local * FEAT),
            grad_key.reshape(block_len, heads_local * FEAT),
            grad_value.reshape(block_len, heads_local * VHEAD),
        ],
        axis=1,
    )
    sum_qkv = ring_scatter(by_distance(dot_tt(hidden_first, grad_qkv).astype(bf16)))
    grad_hidden_first = tp_scatter(dot_t(grad_qkv, w_qkv).astype(bf16))
    scale_first = rms_scale(inputs_own)
    normed_first = inputs_own * scale_first
    grad_input = to_relative(
        grad_middle + norm_back(grad_hidden_first, normed_first, scale_first, gain_first),
        to_abs,
        chunk,
    )

    gain_terms = jnp.stack(
        [
            jnp.sum(qkv_own.astype(f32) * sum_qkv, axis=1),
            jnp.sum(gate_up_own.astype(f32) * sum_gate_up, axis=1),
        ]
    )
    gain_sums = tp_sum(gain_terms) / gains.astype(f32)
    return (
        block_output,
        grad_input,
        gain_sums[0],
        sum_qkv[:, :qk_cols],
        sum_qkv[:, qk_cols : 2 * qk_cols],
        sum_qkv[:, 2 * qk_cols :],
        sum_out_t.T,
        gain_sums[1],
        sum_gate_up[:, :ff_cols],
        sum_gate_up[:, ff_cols:],
        sum_down_t.T,
    )


def solution(mesh):
    in_specs = (
        P(("seq", "tp"), None),
        P(),
        P("seq"),
        P("seq", "tp"),
        P("seq", "tp"),
        P("seq", "tp"),
        P("tp", "seq"),
        P("seq"),
        P("seq", "tp"),
        P("seq", "tp"),
        P("tp", "seq"),
        P(("seq", "tp"), None),
    )
    out_specs = (
        P(("seq", "tp"), None),
        P(("seq", "tp"), None),
        P("seq"),
        P("seq", "tp"),
        P("seq", "tp"),
        P("seq", "tp"),
        P("tp", "seq"),
        P("seq"),
        P("seq", "tp"),
        P("seq", "tp"),
        P("tp", "seq"),
    )
    small = mesh.shape["seq"] == 8 and mesh.shape["tp"] == 4
    body = on_device_rings if small else on_device
    return jax.shard_map(
        body, mesh=mesh, in_specs=in_specs, out_specs=out_specs, check_vma=False
    )
```

```python
import jax
import jax.numpy as jnp
import numpy as np
from jax import lax
from jax.experimental import pallas as pl
from jax.experimental.pallas import tpu as pltpu
from jax.sharding import PartitionSpec as P

FEAT = 16
VHEAD = 128


epsilon = 1e-05
linear_coef = 0.5
square_coef = 0.17677669529663687
highest = lax.Precision.HIGHEST
f32 = jnp.float32
bf16 = jnp.bfloat16


def ring_order(count):
    planes = 4 if count % 4 == 0 else 2
    columns = count // planes
    order = [z * columns for z in range(planes)]
    for z in reversed(range(planes)):
        xs = list(range(1, columns))
        if (planes - 1 - z) % 2:
            xs.reverse()
        order += [z * columns + x for x in xs]
    return order


def relative_list(count):
    half = count // 2
    out = []
    for j in range(1, half):
        out += [j, count - j]
    return out + [half, 0]


def ring_perms(count):
    ring = ring_order(count)
    fwd = [(ring[i], ring[(i + 1) % count]) for i in range(count)]
    return fwd, [(b, a) for a, b in fwd]


def ring_gather(own, half_rows):
    count = lax.axis_size("seq")
    fwd, bwd = ring_perms(count)
    half = count // 2
    got = {0: own}
    ahead = back = own
    for step in range(1, half):
        ahead = lax.ppermute(ahead, "seq", fwd)
        back = lax.ppermute(back, "seq", bwd)
        got[step] = ahead
        got[count - step] = back
    ahead = lax.ppermute(ahead[:half_rows], "seq", fwd)
    back = lax.ppermute(back[half_rows:], "seq", bwd)
    got[half] = jnp.concatenate([ahead, back], axis=0)
    return got


def ring_scatter(chunks):
    count = lax.axis_size("seq")
    fwd, bwd = ring_perms(count)
    half = chunks[0].shape[0] // 2
    ahead = chunks[1][:half]
    back = chunks[count - 1][half:]
    for step in range(count - 1):
        ahead = lax.ppermute(ahead, "seq", fwd).astype(f32)
        back = lax.ppermute(back, "seq", bwd).astype(f32)
        last = step == count - 2
        ahead = ahead + chunks[0 if last else 2 + step][:half].astype(f32)
        back = back + chunks[0 if last else count - 2 - step][half:].astype(f32)
        if not last:
            ahead = ahead.astype(bf16)
            back = back.astype(bf16)
    return jnp.concatenate([ahead, back], axis=0)


def to_relative(array, index_row, chunk):
    return jnp.concatenate(
        [lax.dynamic_slice_in_dim(array, i * chunk, chunk, 1) for i in index_row], axis=1
    )


def tp_perms(count):
    ys = count // 2
    core = [(i, i ^ 1) for i in range(count)]
    shift = [
        [(i, (((i // 2) + d) % ys) * 2 + i % 2) for i in range(count)] for d in range(ys)
    ]
    return core, shift


def tp_gather(own):
    count = lax.axis_size("tp")
    ys = count // 2
    place = lax.axis_index("tp")
    y, c = place // 2, place % 2
    core, shift = tp_perms(count)
    parts = [own] + [lax.ppermute(own, "tp", shift[d]) for d in range(1, ys)]
    mine = jnp.stack([lax.select_n((y - at + ys) % ys, *parts) for at in range(ys)])
    other = lax.ppermute(mine, "tp", core)
    full = jnp.stack([jnp.where(c == 0, mine, other), jnp.where(c == 0, other, mine)], axis=1)
    return full.reshape((count * own.shape[0],) + own.shape[1:])


def tp_scatter(partial):
    count = lax.axis_size("tp")
    ys = count // 2
    place = lax.axis_index("tp")
    y, c = place // 2, place % 2
    core, shift = tp_perms(count)
    blocks = partial.reshape((ys, 2, partial.shape[0] // count) + partial.shape[1:])
    sent = lax.dynamic_index_in_dim(blocks, 1 - c, 1, False)
    kept = lax.dynamic_index_in_dim(blocks, c, 1, False)
    pair = kept.astype(f32) + lax.ppermute(sent, "tp", core).astype(f32)
    low = pair.astype(bf16)
    own = lax.dynamic_index_in_dim(pair, y, 0, False)
    for d in range(1, ys):
        away = lax.dynamic_index_in_dim(low, (y + d) % ys, 0, False)
        own = own + lax.ppermute(away, "tp", shift[d]).astype(f32)
    return own


def tp_sum(vector):
    count = lax.axis_size("tp")
    core, shift = tp_perms(count)
    vector = vector + lax.ppermute(vector, "tp", core)
    return vector + sum(lax.ppermute(vector, "tp", shift[d]) for d in range(1, count // 2))


def carried(arrays, resets, step):
    count = lax.axis_size("seq")
    place = lax.axis_index("seq")

    def from_near(a, d):
        perm = [(i, i + d * step) for i in range(count) if 0 <= i + d * step < count]
        return lax.ppermute(a.astype(bf16), "seq", perm).astype(f32)

    def reset_within(d):
        at = jnp.arange(count)
        away = (place - at) * step
        return jnp.sum(jnp.where((away >= 1) & (away <= d), resets, 0)) > 0

    arrays = [from_near(a, 1) for a in arrays]
    d = 1
    while d < count - 1:
        keep = 1.0 - reset_within(d).astype(f32)
        arrays = [a + keep * from_near(a, d) for a in arrays]
        d *= 2
    return arrays


def features(vector):
    squares = (vector[..., :, None] * vector[..., None, :]).reshape(
        vector.shape[:-1] + (vector.shape[-1] * vector.shape[-1],)
    )
    return jnp.concatenate(
        [jnp.ones_like(vector[..., :1]), vector * linear_coef, squares * square_coef], axis=-1
    )


def feature_grad(vector, grad_feat):
    feat_width = vector.shape[-1]
    linear_part = grad_feat[..., 1 : 1 + feat_width]
    square_part = grad_feat[..., 1 + feat_width :].reshape(vector.shape + (feat_width,))
    mixed_part = jnp.sum(square_part * vector[..., None, :], axis=-1) + jnp.sum(
        square_part * vector[..., :, None], axis=-2
    )
    return linear_coef * linear_part + square_coef * mixed_part


def segment_masks(anchor, starts, length):
    positions = anchor + jnp.arange(length, dtype=jnp.int32)
    start_le = starts[None, :] <= positions[:, None]
    row_ids = jnp.sum(start_le.astype(jnp.int32), axis=1)
    inside = (starts >= anchor) & (starts < anchor + length)
    carry = jnp.sum(((starts[None, :] >= anchor) & start_le).astype(jnp.int32), axis=1) == 0
    after_last = (
        jnp.sum(
            ((starts[None, :] > positions[:, None]) & inside[None, :]).astype(jnp.int32), axis=1
        )
        == 0
    )
    return (positions, row_ids, carry, after_last)


def rms_scale(values):
    return lax.rsqrt(jnp.mean(values * values, axis=-1, keepdims=True) + epsilon)


def norm_back(grad_out, normed, scale, gain):
    grad_normed = grad_out * gain
    return scale * (grad_normed - normed * jnp.mean(grad_normed * normed, axis=-1, keepdims=True))


def pair_block(query_part, key_heads, row_ids, positions, first_row, span_rows):
    scores = (
        jnp.einsum("thf,shf->hts", query_part, key_heads, preferred_element_type=f32) * 0.25
    )
    rows_here = row_ids[first_row : first_row + span_rows]
    place_here = positions[first_row : first_row + span_rows]
    allowed = (
        (rows_here[:, None] == row_ids[None, :]) & (positions[None, :] <= place_here[:, None])
    ).astype(f32)
    kernel = (1.0 + scores + 0.5 * scores * scores) * allowed[None]
    return (scores, allowed, kernel)


def dot(a, b):
    return jnp.dot(a, b, preferred_element_type=f32)


def dot_t(a, b):
    return lax.dot_general(a, b, (((1,), (1,)), ((), ())), preferred_element_type=f32)


def dot_tt(a, b):
    return lax.dot_general(a, b, (((0,), (0,)), ((), ())), preferred_element_type=f32)


def ring_place(seq):
    z, x = seq // 2, seq % 2
    return z + x * (7 - 2 * z)


def ring_seq(place):
    place = lax.rem(place + 8, 8)
    far = place // 4
    return (1 - far) * 2 * place + far * (15 - 2 * place)


class Sems:
    def __init__(self, ref):
        self.ref, self.used = ref, 0

    def take(self):
        self.used += 1
        return self.ref.at[self.used - 1]


class Links:
    def __init__(self, send, recv):
        self.send, self.recv, self.sent = Sems(send), Sems(recv), []

    def copy(self, src, dst, **to):
        return pltpu.make_async_remote_copy(
            src_ref=src,
            dst_ref=dst,
            send_sem=self.send.take(),
            recv_sem=self.recv.take(),
            device_id=to,
            device_id_type=pl.DeviceIdType.MESH,
        )

    def start(self, src, dst, **to):
        made = self.copy(src, dst, **to)
        made.start()
        self.sent.append(made)
        return made

    def sent_now(self, some):
        for made in some:
            made.wait_send()
        self.sent = [made for made in self.sent if all(made is not other for other in some)]

    def finish(self):
        for made in self.sent:
            made.wait_send()


class Gather:
    def __init__(self, links, arrays, split, nearby):
        self.links, self.arrays, self.split, self.nearby = links, arrays, split, nearby
        self.at = {k: j for j, k in enumerate(relative_list(8))}
        self.flying = {}
        self.events = [
            (a, step, way, part)
            for a in range(len(arrays))
            for step in (1, 2, 3, 4)
            for part in (0, 1)
            for way in (0, 1)
            if step < 4 or way == part
        ]
        self.done = 0
        for part in (0, 1):
            for way in (0, 1):
                self.go(0, 1, way, part)

    def rows(self, part):
        return pl.ds(part * self.split, self.split)

    def go(self, a, step, way, part):
        own, everyone = self.arrays[a]
        before, after = (step - 1, step) if way == 0 else ((9 - step) % 8, 8 - step)
        src = own if step == 1 else everyone.at[self.at[before]]
        self.flying[a, step, way, part] = self.links.start(
            src.at[self.rows(part)],
            everyone.at[self.at[after], self.rows(part)],
            seq=self.nearby[way],
        )

    def pump(self, upto):
        while self.done < min(upto, len(self.events)):
            a, step, way, part = self.events[self.done]
            self.flying[a, step, way, part].wait_recv()
            if step < 3 or (step == 3 and way == part):
                self.go(a, step + 1, way, part)
            if step == 3 and a + 1 < len(self.arrays):
                self.go(a + 1, 1, way, part)
            self.done += 1

    def pump_array(self, a):
        self.pump(14 * (a + 1))


def greet(peers):
    barrier = pltpu.get_barrier_semaphore()
    for peer in peers:
        pl.semaphore_signal(
            barrier, inc=1, device_id=peer, device_id_type=pl.DeviceIdType.MESH
        )
    pl.semaphore_wait(barrier, len(peers))


def places():
    seq, tp = lax.axis_index("seq"), lax.axis_index("tp")
    place = ring_place(seq)
    nearby = (ring_seq(place + 1), ring_seq(place - 1))
    over_y = lax.rem(tp + 2, 4)
    over_core = tp + 1 - 2 * (tp % 2)
    peers = [{"seq": ring_seq(place + k)} for k in range(1, 8)]
    peers += [{"tp": over_y}, {"tp": over_core}]
    return seq, tp, place, nearby, over_y, over_core, peers


class Rows:
    def __init__(self, links, own, everyone, tp, over_y, over_core, rows):
        self.links, self.all, self.tp = links, everyone, tp
        self.over_y, self.over_core, self.rows = over_y, over_core, rows
        half = rows // 2
        self.first = [
            links.start(
                own.at[pl.ds(i * half, half)], self.block(tp, i * half, half), tp=over_y
            )
            for i in (0, 1)
        ]
        self.near = links.start(own, self.block(tp, 0, rows), tp=over_core)
        self.last = []

    def block(self, owner, offset, size):
        return self.all.at[pl.ds(pl.multiple_of(owner * self.rows + offset, 16), size)]

    def forward(self, i):
        half = self.rows // 2
        self.first[i].wait_recv()
        came = self.block(self.over_y, i * half, half)
        self.last.append(self.links.start(came, came, tp=self.over_core))

    def finish(self):
        self.near.wait_recv()
        for made in self.last:
            made.wait_recv()


FEATS = 160


def fill_tables(lengths, seq, tok, line, coefs, step):
    total = tok.shape[0]
    anchor = seq * total
    starts, at = [], 0
    for i in range(lengths.shape[0]):
        starts.append(at)
        at = at + lengths[i]

    def places_of(shape, axis):
        pos = lax.broadcasted_iota(jnp.int32, shape, axis)
        low = jnp.zeros(shape, jnp.int32) - anchor
        last = jnp.ones(shape, f32)
        for start in starts:
            here = start - anchor
            low = jnp.maximum(low, jnp.where(pos >= here, here, -anchor))
            last = jnp.where((pos < here) & (here < total), 0.0, last)
        return pos.astype(f32), low, last

    lane = lax.broadcasted_iota(jnp.int32, (total, 128), 1)
    pos, low, last = places_of((total, 128), 0)
    began = jnp.where(low < 0, 1.0, 0.0)
    first = jnp.maximum(low, 0).astype(f32)
    tok[...] = jnp.where(
        lane == 0, first, jnp.where(lane == 1, began, jnp.where(lane == 2, last, pos))
    )
    pos, low, last = places_of((8, total), 1)
    row = lax.broadcasted_iota(jnp.int32, (8, total), 0)
    line[...] = jnp.where(row == 0, pos, jnp.maximum(low, 0).astype(f32))

    def clear(lo, hi):
        free = jnp.ones((1, 128), f32)
        for start in starts:
            at = jnp.zeros((1, 128), jnp.int32) + start
            free = jnp.where((at >= lo * total) & (at < (hi + 1) * total), 0.0, free)
        return free

    z, x = seq // 2, seq % 2
    one = jnp.ones((1, 128), f32)
    if step > 0:
        rows = [clear(2 * z + 1, 2 * z + 1), one * x.astype(f32)]
        rows += [clear(2 * (z - d) + 2, seq - 1) for d in (1, 2, 3)]
    else:
        rows = [clear(2 * z, 2 * z), one * (1 - x).astype(f32)]
        rows += [clear(seq + 1, 2 * (z + d) - 1) for d in (1, 2, 3)]
    coefs[...] = jnp.concatenate(rows + [one * 0.0] * 3, axis=0)


def ring_columns(place):
    return [pl.ds(pl.multiple_of(ring_seq(place - k) * 256, 256), 256) for k in relative_list(8)]


def phi(heads, h, select_a, select_b, lanes):
    a = dot(heads, select_a[h]) + lanes[0:1, :]
    b = dot(heads, select_b[h]) + lanes[1:2, :]
    return a, b


def fwd_kernel(
    lengths, sa_ref, sb_ref, lanes_ref, hm_ref, gain_first, gain_second,
    x_in, wq_in, wk_in, wv_in, wo_in, wg_in, wu_in, wd_in, c_in,
    wq_all, wo_all, wg_all, wu_all, wd_all, c_all,
    h1_out, qkv_out, yb_out, den_out, x1_out, h2_out, gate_out, up_out, m_out, sin_out, gain_out,
    x_ref, tok_ref, line_ref, coef_ref, gain_ref, q_own, o_own, g_own, u_own, d_own,
    w_small, w_v, w_o, w_d, w_g,
    xg, h1, wq, wo, wg, wu, qkv, kq, num, den, yb, sc, rc, sy, ry, x1, gate, up, mm,
    gains_all, gains, st, st_x, st_t, st_z, s_in,
    send, recv, local,
):
    seq, tp, place, nearby, over_y, over_core, peers = places()
    z, x = seq // 2, seq % 2
    at = {k: j for j, k in enumerate(relative_list(8))}
    rows = x_ref.shape[0]
    total = 4 * rows
    links = Links(send, recv)
    locs = Sems(local)
    pending = []

    def store(src, dst):
        made = pltpu.make_async_copy(src, dst, locs.take())
        made.start()
        pending.append(made)

    def load(src, dst):
        made = pltpu.make_async_copy(src, dst, locs.take())
        made.start()
        return made

    got_qk = [load(wq_in, w_small.at[0:64]), load(wk_in, w_small.at[64:128]), load(wv_in, w_v)]
    columns = ring_columns(place)
    got_x = [load(x_in.at[:, c], x_ref.at[:, col(j)]) for j, c in enumerate(columns)]
    c_rows = pl.ds(pl.multiple_of(tp * rows, rows), rows)
    got_c = [load(c_in.at[:, c], c_all.at[c_rows, col(j)]) for j, c in enumerate(columns)]
    got_o = load(wo_in, w_o)
    ff = wd_in.shape[0]
    got_g = load(wg_in, w_g.at[pl.ds(0, ff)])
    got_d = load(wd_in, w_d.at[pl.ds(0, ff)])

    def turn(src, dst):
        for i in range(0, ff, 128):
            size = min(128, ff - i)
            dst[:, i : i + size] = src[i : i + 128, :].T[:, :size].astype(bf16)

    gain_ref[...] = jnp.concatenate(
        [gain_first[...], gain_second[...], jnp.zeros((14, 256), f32)], axis=0
    ).astype(bf16)
    greet(peers)
    gain_flying = [
        links.start(gain_ref, gains_all.at[at[k]], seq=ring_seq(place + k)) for k in range(1, 8)
    ]
    for made in got_x:
        made.wait()
    xrows = Rows(links, x_ref, xg, tp, over_y, over_core, rows)
    for made in got_qk:
        made.wait()
    q_own[:, 0:128] = w_small[...].T.astype(bf16)
    q_own[:, 128:640] = w_v[...].astype(bf16)
    ring = Gather(
        links,
        [(q_own, wq_all), (o_own, wo_all), (g_own, wg_all), (u_own, wu_all), (d_own, wd_all)],
        128,
        nearby,
    )
    own_in = [
        load(x_ref, xrows.block(tp, 0, rows)),
        load(gain_ref, gains_all.at[at[0]]),
    ]
    got_o.wait()
    o_own[...] = w_o[...].T.astype(bf16)
    ring.pump(2)
    got_g.wait()
    turn(w_g, g_own)
    got_u = load(wu_in, w_g.at[pl.ds(0, ff)])
    ring.pump(4)
    got_d.wait()
    turn(w_d, d_own)
    got_u.wait()
    turn(w_g, u_own)
    own_kept = [load(own, everyone.at[at[0]]) for own, everyone in ring.arrays]
    fill_tables(lengths, seq, tok_ref, line_ref, coef_ref, 1)

    ring.pump(6)
    xrows.forward(0)
    for made in gain_flying:
        made.wait_recv()
    for made in own_in:
        made.wait()
    for j in range(8):
        chunk = gains_all[j].astype(f32)
        gains[0:8, j * 256 : (j + 1) * 256] = chunk[0:8]
    ring.pump(10)
    xrows.forward(1)
    ring.pump_array(0)
    own_kept[0].wait()
    got = load_weights(load, wq_all, wq)
    xrows.finish()

    def norm_first(i, _):
        r = pl.ds(pl.multiple_of(i * 32, 32), 32)
        v = xg[r, :].astype(f32)
        s = lax.rsqrt(jnp.mean(v * v, axis=1, keepdims=True) + epsilon)
        h1[r, :] = (v * s * gains[0:1, :]).astype(bf16)
        return 0

    lax.fori_loop(0, total // 32, norm_first, 0)
    links.sent_now(xrows.last)
    store(h1, h1_out)
    for made in got_c:
        made.wait()
    crows = Rows(links, c_all.at[c_rows], c_all, tp, over_y, over_core, rows)
    ring.pump(15)
    for made in got:
        made.wait()

    def project(i, _):
        r = pl.ds(pl.multiple_of(i * 256, 256), 256)
        res = dot(h1[r, :], wq[...])
        qkv[r, :] = res.astype(bf16)
        kq[r, :] = pltpu.roll(res[:, :128], 64, 1).astype(bf16)
        return 0

    lax.fori_loop(0, total // 256, project, 0)
    store(qkv, qkv_out)
    ring.pump(17)

    heads = 4

    def head_v(h):
        return slice(128 + h * 128, 256 + h * 128)

    for h in range(heads):

        def state(i, c, h=h):
            s, zz = c
            r = pl.ds(pl.multiple_of(i * 256, 256), 256)
            a, b = phi(kq[r, :], h, sa_ref, sb_ref, lanes_ref)
            f = a * b * lanes_ref[2:3, :] * tok_ref[r, 2:3]
            s = s + dot_tt(f.astype(bf16), qkv[r, head_v(h)])
            return s, zz + jnp.sum(f, axis=0, keepdims=True)

        s, zz = lax.fori_loop(
            0, total // 256, state, (jnp.zeros((256, 128), f32), jnp.zeros((1, 256), f32))
        )
        pack_state(st, h, s, zz)
        ring.pump(18 + h)
    to_x = links.start(st, st_x, seq=seq + 1 - 2 * x)

    def local_head(h):
        for i in range(total // 256):
            r = slice(i * 256, (i + 1) * 256)
            span = (i + 1) * 256
            qm = (qkv[r, :128].astype(f32) * hm_ref[h : h + 1, :]).astype(bf16)
            u = dot_t(qm, kq[:span, :])
            keep = (line_ref[0:1, :span] >= tok_ref[r, 0:1]) & (
                line_ref[0:1, :span] <= tok_ref[r, 3:4]
            )
            kap = jnp.where(keep, (0.5 * u + 1.0) * u + 1.0, 0.0)
            den[r, h : h + 1] = jnp.sum(kap, axis=1, keepdims=True)
            num[r, h * 128 : (h + 1) * 128] = dot(kap.astype(bf16), qkv[:span, head_v(h)])

    local_head(0)
    ring.pump(23)
    local_head(1)
    ring.pump(25)
    to_x.wait_recv()
    for h in range(heads):
        mine, theirs = st[h].astype(f32), st_x[h].astype(f32)
        early = jnp.where(x == 0, mine, theirs)
        later = jnp.where(x == 0, theirs, mine)
        st_t[h] = (later + coef_ref[0:1, :] * early).astype(bf16)
    to_z = [links.copy(st_t, st_z.at[d - 1], seq=seq + 2 * d) for d in (1, 2, 3)]
    for d in (1, 2, 3):

        @pl.when(z + d < 4)
        def _(d=d):
            to_z[d - 1].start()

    local_head(2)
    ring.pump(27)
    local_head(3)
    ring.pump(28)
    own_kept[1].wait()
    got = load_weights(load, wo_all, wo)
    for h in range(heads):
        num_in = coef_ref[1:2, :] * st_x[h].astype(f32)
        s_in[h, 0:176, :] = num_in
        s_in[h, 176:256, :] = jnp.zeros((80, 128), f32)
    for d in (1, 2, 3):

        @pl.when(z >= d)
        def _(d=d):
            to_z[d - 1].wait_recv()
            for h in range(heads):
                s_in[h, 0:176, :] += coef_ref[1 + d : 2 + d, :] * st_z[d - 1, h].astype(f32)

    store(s_in, sin_out)
    for h in range(heads):
        z_row = jnp.concatenate([s_in[h, 160:161, :], s_in[h, 161:162, :]], axis=1)
        feat = jax.lax.broadcasted_iota(jnp.int32, (256, 128), 0)
        s_low = jnp.where(feat < FEATS, s_in[h], 0.0).astype(bf16)

        def carry(i, _, h=h, z_row=z_row, s_low=s_low):
            r = pl.ds(pl.multiple_of(i * 256, 256), 256)
            a, b = phi(qkv[r, 0:128], h, sa_ref, sb_ref, lanes_ref)
            f = a * b * lanes_ref[2:3, :] * tok_ref[r, 1:2]
            hv = slice(h * 128, (h + 1) * 128)
            top = num[r, hv] + dot(f.astype(bf16), s_low)
            low = den[r, h : h + 1] + jnp.sum(f * z_row, axis=1, keepdims=True)
            den[r, h : h + 1] = low
            y = top / low
            yb[r, hv] = y.astype(bf16)
            return 0

        lax.fori_loop(0, total // 256, carry, 0)
        ring.pump(29 + h)
    store(yb, yb_out)
    store(den, den_out)
    for made in got:
        made.wait()

    y_at, c_at = tp // 2, tp % 2

    def out_rows(block):
        return yb[pl.ds(pl.multiple_of(block * rows, rows), rows), :]

    cols = 512
    to_core = []
    for yy in (0, 1):

        def core_cols(i, _, yy=yy):
            c = pl.ds(pl.multiple_of(i * cols, cols), cols)
            sc[yy, :, c] = dot_t(out_rows(yy * 2 + 1 - c_at), wo[c, :]).astype(bf16)
            return 0

        lax.fori_loop(0, 2048 // cols, core_cols, 0)
        to_core.append(links.start(sc.at[yy], rc.at[yy], tp=over_core))
    for made in to_core:
        made.wait_recv()

    def away_cols(i, _):
        c = pl.ds(pl.multiple_of(i * cols, cols), cols)
        part = dot_t(out_rows((1 - y_at) * 2 + c_at), wo[c, :])
        sy[:, c] = (part + rc[1 - y_at, :, c].astype(f32)).astype(bf16)
        return 0

    lax.fori_loop(0, 2048 // cols, away_cols, 0)
    to_y = links.start(sy, ry, tp=over_y)

    def own_cols(i, _):
        c = pl.ds(pl.multiple_of(i * cols, cols), cols)
        x1[:, c] = (
            dot_t(out_rows(tp), wo[c, :]) + rc[y_at, :, c].astype(f32) + x_ref[:, c].astype(f32)
        )
        return 0

    lax.fori_loop(0, 2048 // cols, own_cols, 0)
    ring.pump(34)
    to_y.wait_recv()

    links.sent_now(xrows.first + [xrows.near])
    ho = x_ref

    def norm_second(i, _):
        r = pl.ds(pl.multiple_of(i * 32, 32), 32)
        v = x1[r, :] + ry[r, :].astype(f32)
        x1[r, :] = v
        s = lax.rsqrt(jnp.mean(v * v, axis=1, keepdims=True) + epsilon)
        ho[r, :] = (v * s * gains[1:2, :]).astype(bf16)
        return 0

    lax.fori_loop(0, rows // 32, norm_second, 0)
    store(x1, x1_out)
    store(gains, gain_out)
    h2 = xg
    hrows = Rows(links, ho, h2, tp, over_y, over_core, rows)
    own_in = load(ho, hrows.block(tp, 0, rows))
    ring.pump(36)
    hrows.forward(0)
    ring.pump(37)
    hrows.forward(1)
    crows.forward(0)
    crows.forward(1)
    hrows.finish()
    crows.finish()
    own_in.wait()
    store(h2, h2_out)
    ring.pump_array(2)
    own_kept[2].wait()
    got = load_weights(load, wg_all, wg)
    ring.pump_array(3)
    own_kept[3].wait()
    got += load_weights(load, wu_all, wu)
    for made in got:
        made.wait()

    def gate_up(i, _):
        r = pl.ds(pl.multiple_of(i * 128, 128), 128)
        g = dot(h2[r, :], wg[...])
        uu = dot(h2[r, :], wu[...])
        gate[r, :] = g.astype(bf16)
        up[r, :] = uu.astype(bf16)
        mm[r, :] = (g * jax.nn.sigmoid(g) * uu).astype(bf16)
        return 0

    for quarter in range(4):
        lax.fori_loop(quarter * total // 512, (quarter + 1) * total // 512, gate_up, 0)
        ring.pump(58 + 2 * quarter)
    store(gate, gate_out)
    store(up, up_out)
    store(mm, m_out)
    ring.pump_array(4)
    own_kept[4].wait()
    for made in pending:
        made.wait()
    links.finish()
    for d in (1, 2, 3):

        @pl.when(z + d < 4)
        def _(d=d):
            to_z[d - 1].wait_send()


def pack_state(st, h, s, zz):
    st[h, 0:FEATS, :] = s[:FEATS].astype(bf16)
    tail = jnp.concatenate([zz[:, :128], zz[:, 128:], jnp.zeros((14, 128), f32)], axis=0)
    st[h, FEATS : FEATS + 16, :] = tail.astype(bf16)


def load_weights(load, everyone, flat):
    count, chunk = everyone.shape[0], everyone.shape[1]
    return [load(everyone.at[j], flat.at[pl.ds(j * chunk, chunk)]) for j in range(count)]


class Scatter:
    def __init__(self, slots, send, recv, nearby):
        self.slots, self.send, self.recv, self.nearby = slots, send, recv, nearby

    def copy(self, a, step, way, sub, src, slot, width):
        return pltpu.make_async_remote_copy(
            src_ref=src,
            dst_ref=self.piece(slot, way, sub, width),
            send_sem=self.send.at[a % 2, way, sub],
            recv_sem=self.recv.at[a % 2, way, sub, step],
            device_id={"seq": self.nearby[way]},
            device_id_type=pl.DeviceIdType.MESH,
        )

    def rows(self, way, sub, base=0):
        start = base + way * 128 + sub * 64
        return pl.ds(start if isinstance(start, int) else pl.multiple_of(start, 64), 64)

    def piece(self, slot, way, sub, width):
        return self.slots.at[slot, self.rows(way, sub), pl.ds(0, width)]

    def begin(self, a, own, width, column=0):
        for sub in (0, 1):
            for way in (0, 1):
                src = own.at[self.rows(way, sub, way * 256), pl.ds(column, width)]
                self.copy(a, 0, way, sub, src, 7 * (a % 2), width).start()

    def event(self, a, e, own, width, out, column=0):
        step, sub = e // 2, e % 2
        is_first, is_last = (6 - step) // 6, step // 6
        here = is_first * 7 * (a % 2) + (1 - is_first) * step
        far = (step + 1) // 4
        place0 = (1 - far) * 2 * (step + 1) + far * (11 - 2 * step) + is_last * 8
        far = (step + 2) // 4 - is_last
        place1 = (1 - far) * (3 + 2 * step) + far * (10 - 2 * step) + is_last * 9
        places = (place0, place1)
        for way in (0, 1):
            piece = self.piece(here, way, sub, width)
            came = self.copy(a, step, way, sub, piece, here, width)
            came.wait_recv()
            came.wait_send()

        def summed(way):
            mine = own[self.rows(way, sub, places[way] * 256), pl.ds(column, width)]
            came = self.slots[here, self.rows(way, sub), pl.ds(0, width)]
            return came.astype(f32) + mine.astype(f32)

        def on():
            for way in (0, 1):
                self.slots[here, self.rows(way, sub), pl.ds(0, width)] = summed(way).astype(bf16)
                piece = self.piece(here, way, sub, width)
                self.copy(a, step + 1, way, sub, piece, step + 1, width).start()

        def end():
            for way in (0, 1):
                out[self.rows(way, sub), pl.ds(0, width)] = summed(way)

        if isinstance(e, int):
            if step < 6:
                on()
            else:
                end()
        else:
            pl.when(step < 6)(on)
            pl.when(step == 6)(end)


class TpSum:
    def __init__(self, part, from_core, from_y, sems, credits, tp, over_y, over_core):
        self.part, self.from_core, self.from_y = part, from_core, from_y
        self.sems, self.credits = sems, credits
        self.tp, self.over_y, self.over_core = tp, over_y, over_core
        self.y, self.c = tp // 2, tp % 2

    def to_core(self, i, yy):
        return pltpu.make_async_remote_copy(
            src_ref=self.part.at[i, yy * 2 + 1 - self.c],
            dst_ref=self.from_core.at[i, yy],
            send_sem=self.sems.at[yy, i],
            recv_sem=self.sems.at[2 + yy, i],
            device_id={"tp": self.over_core},
            device_id_type=pl.DeviceIdType.MESH,
        )

    def to_y(self, i):
        return pltpu.make_async_remote_copy(
            src_ref=self.part.at[i, (1 - self.y) * 2 + self.c],
            dst_ref=self.from_y.at[i],
            send_sem=self.sems.at[4, i],
            recv_sem=self.sems.at[5, i],
            device_id={"tp": self.over_y},
            device_id_type=pl.DeviceIdType.MESH,
        )

    def sent(self, i):
        self.to_core(i, 0).wait_send()
        self.to_core(i, 1).wait_send()
        self.to_y(i).wait_send()

    def offer(self, i, turn, value):
        if turn > 0:
            self.sent(i)
        for block in range(4):
            self.part[i, block] = value[block * 256 : (block + 1) * 256].astype(bf16)
        if turn > 0:
            pl.semaphore_wait(self.credits.at[0], 1)
        for yy in (0, 1):
            self.to_core(i, yy).start()

    def pass_on(self, i, turn):
        for yy in (0, 1):
            self.to_core(i, yy).wait_recv()
        away = (1 - self.y) * 2 + self.c
        self.part[i, away] = (
            self.part[i, away].astype(f32) + self.from_core[i, 1 - self.y].astype(f32)
        ).astype(bf16)
        if turn > 0:
            pl.semaphore_wait(self.credits.at[1], 1)
        self.to_y(i).start()

    def take(self, i, turn, use):
        self.to_y(i).wait_recv()
        use(
            self.part[i, self.tp].astype(f32)
            + self.from_core[i, self.y].astype(f32)
            + self.from_y[i].astype(f32)
        )
        if turn < 2:
            for k, peer in ((0, self.over_core), (1, self.over_y)):
                pl.semaphore_signal(
                    self.credits.at[k],
                    inc=1,
                    device_id={"tp": peer},
                    device_id_type=pl.DeviceIdType.MESH,
                )


def col(i, width=256):
    return pl.ds(i * width if isinstance(i, int) else pl.multiple_of(i * width, width), width)


def bwd_kernel(
    lengths, sa_ref, sb_ref, lanes_ref, hm_ref, gains, s_in, den, gain_first, gain_second,
    x_in, x1_in, wq_all, wo_all, wg_all, wu_all, wd_all, c_all, h1_all, qkv_all, yb_all, h2_all,
    gate_all, up_all, m_all,
    d_out, g_out, u_out, oq_out, block_out, input_out, gain_out,
    tok_ref, line_ref, coef_ref, terms, terms_core, terms_y,
    slots, s1, s2, wo, stream, hs, rows_all, mm, dup, tiles, qkv, kq, yb, dnum, dden, dden_t, dqkv,
    dq, dk, part, from_core, from_y, acc, x1, fout, st, st_x, st_t, st_z, s_back, own_rows,
    ring_send, ring_recv, tp_sems, credits, send, recv, local, tile_sems,
):
    seq, tp, place, nearby, over_y, over_core, peers = places()
    z, x = seq // 2, seq % 2
    rows, width = own_rows.shape
    total = 4 * rows
    ff = mm.shape[1]
    links = Links(send, recv)
    locs = Sems(local)

    def load(src, dst):
        made = pltpu.make_async_copy(src, dst, locs.take())
        made.start()
        return made

    def whole(everyone, flat):
        count, chunk = everyone.shape[0], everyone.shape[1]
        return [load(everyone.at[j], flat.at[pl.ds(j * chunk, chunk)]) for j in range(count)]

    got_c = load(c_all, rows_all)
    got_m = load(m_all, mm)
    got_wd = whole(wd_all, s2)
    greet(peers)
    got_x1 = load(x1_in, x1)
    fill_tables(lengths, seq, tok_ref, line_ref, coef_ref, -1)
    columns = ring_columns(place)
    got_qkv = [load(qkv_all, qkv), load(yb_all, yb)]
    got_wo = whole(wo_all, wo)
    ring = Scatter(slots, ring_send, ring_recv, nearby)
    sums = TpSum(part, from_core, from_y, tp_sems, credits, tp, over_y, over_core)

    def run(n, body, pumps=None, lookup=None):
        def step(i, _):
            body(i)
            if pumps:
                a, first, count = pumps
                every = n // count
                pl.when((i + 1) % every == 0)(lambda: event(a, first + (i + 1) // every - 1))
            return 0

        lax.fori_loop(0, n, step, 0)

    plan = {0: (s1, ff, 0), 1: (s2, ff, 0), 2: (s1, ff, 0), 3: (s2, 1152, 0)}

    def event(a, e):
        own, wide, column = plan[a]
        ring.event(a, e, own, wide, fout, column)

    def begin(a):
        own, wide, column = plan[a]
        ring.begin(a, own, wide, column)

    def events(a, first, last):
        lax.fori_loop(first, last, lambda e, _: (event(a, e), 0)[1], 0)

    def chunks_of(source, size, body, pumps=None, count=8):
        def copies(i, slot):
            return [
                pltpu.make_async_copy(a, b, tile_sems.at[k, slot])
                for k, (a, b) in enumerate(source(i, slot))
            ]

        for made in copies(0, 0):
            made.start()

        def step(i):
            slot = i % 2

            @pl.when(i + 1 < count)
            def _():
                for made in copies(i + 1, 1 - slot):
                    made.start()

            for made in copies(i, slot):
                made.wait()
            body(i, slot)

        run(count, step, pumps)

    got_c.wait()
    got_m.wait()

    def grad_down(j):
        s1[col(j), :] = dot_tt(rows_all[:, col(j)], mm[...]).astype(bf16)

    run(2, grad_down)
    begin(0)
    lax.fori_loop(2, 8, lambda j, _: (grad_down(j), 0)[1], 0)
    for made in got_wd:
        made.wait()
    events(0, 0, 1)

    def mlp(i):
        sums.offer(i, 0, dot_t(mm[...], s2[col(i), :]))
        pl.when(i > 0)(lambda: sums.pass_on(i - 1, 0))

    run(8, mlp, (0, 1, 2))
    sums.pass_on(7, 0)

    def gate_up_tiles(i, slot):
        r = col(i, 128)
        return [(gate_all.at[r], tiles.at[slot, 0]), (up_all.at[r], tiles.at[slot, 1])]

    def grad_gate_up(i, slot):
        r = col(i, 128)
        dm = dot(rows_all[r, :], s2[...]).astype(bf16).astype(f32)
        g = tiles[slot, 0].astype(f32)
        u = tiles[slot, 1].astype(f32)
        s = jax.nn.sigmoid(g)
        mm[r, :] = (dm * u * s * (1.0 + g * (1.0 - s))).astype(bf16)
        dup[r, :] = (dm * (g * s)).astype(bf16)

        def use(value):
            own_rows[:, col(i)] = (x1[:, col(i)] + value).astype(bf16)

        sums.take(i, 0, use)

    got_x1.wait()
    chunks_of(gate_up_tiles, 8, grad_gate_up, (0, 3, 4))
    kept = [load(own_rows.at[:, col(j)], block_out.at[:, c]) for j, c in enumerate(columns)]
    pending = []

    def w_tiles(i, slot):
        return [(wg_all.at[i], stream.at[slot, 0]), (wu_all.at[i], stream.at[slot, 1])]

    def grad_hidden(i, slot):
        value = dot_t(mm[...], stream[slot, 0]) + dot_t(dup[...], stream[slot, 1])
        sums.offer(i, 1, value)
        pl.when(i > 0)(lambda: sums.pass_on(i - 1, 1))

    chunks_of(w_tiles, 8, grad_hidden, (0, 7, 2))
    sums.pass_on(7, 1)

    def h_tiles(everyone):
        return lambda i, slot: [(everyone.at[:, col(i)], hs.at[slot])]

    def grad_gate(i, slot):
        s2[col(i), :] = dot_tt(hs[slot], mm[...]).astype(bf16)

    chunks_of(h_tiles(h2_all), 8, grad_gate, (0, 9, 2))
    events(0, 11, 12)
    begin(1)

    def take_second(i):
        def use(value):
            acc[:, col(i)] = value

        sums.take(i, 1, use)

    run(8, take_second, (0, 12, 2))
    done = load(fout.at[:, pl.ds(0, ff)], d_out)

    for made in kept:
        made.wait()

    def norm_back_second(i, _):
        r = pl.ds(pl.multiple_of(i * 32, 32), 32)
        v = x1[r, :]
        s = lax.rsqrt(jnp.mean(v * v, axis=1, keepdims=True) + epsilon)
        n = v * s
        dn = acc[r, :] * gains[1:2, :]
        own = pl.ds(pl.multiple_of(tp * rows + i * 32, 32), 32)
        back = rows_all[own, :].astype(f32) + s * (
            dn - n * jnp.mean(dn * n, axis=1, keepdims=True)
        )
        acc[r, :] = back
        own_rows[r, :] = back.astype(bf16)
        return 0

    lax.fori_loop(0, rows // 32, norm_back_second, 0)
    da = Rows(links, own_rows, rows_all, tp, over_y, over_core, rows)
    own_in = load(own_rows, da.block(tp, 0, rows))

    def grad_up(i, slot):
        s1[col(i), :] = dot_tt(hs[slot], dup[...]).astype(bf16)

    chunks_of(h_tiles(h2_all), 8, grad_up, (1, 0, 2))
    da.forward(0)
    events(1, 2, 5)
    da.forward(1)
    for made in got_qkv + got_wo:
        made.wait()
    da.finish()
    own_in.wait()
    links.sent_now(da.first + [da.near])
    got_x = [load(x_in.at[:, c], own_rows.at[:, col(j)]) for j, c in enumerate(columns)]

    def head_v(h):
        return slice(128 + h * 128, 256 + h * 128)

    def grad_attended(i):
        r = col(i, 256)
        dy = dot(rows_all[r, :], wo[...])
        kq[r, :] = pltpu.roll(qkv[r, 0:128].astype(f32), 64, 1).astype(bf16)
        columns = []
        for h in range(4):
            hv = slice(h * 128, (h + 1) * 128)
            under = 1.0 / den[r, h : h + 1]
            part_h = dy[:, hv]
            dnum[r, hv] = (part_h * under).astype(bf16)
            low = jnp.sum(part_h * yb[r, hv].astype(f32), axis=1, keepdims=True)
            columns.append(-low * under)
        lane = lax.broadcasted_iota(jnp.int32, (256, 128), 1)
        packed = jnp.zeros((256, 128), f32)
        for h in range(4):
            packed = jnp.where(lane == h, columns[h], packed)
        dden[r, :] = packed
        dden_t[i] = packed.T[0:8, :]

    run(4, grad_attended)
    event(1, 5)

    for h in range(4):

        def state(i, c, h=h):
            s, zz = c
            r = col(i, 256)
            a, b = phi(qkv[r, 0:128], h, sa_ref, sb_ref, lanes_ref)
            f = a * b * lanes_ref[2:3, :] * tok_ref[r, 1:2]
            s = s + dot_tt(f.astype(bf16), dnum[r, h * 128 : (h + 1) * 128])
            return s, zz + jnp.sum(f * dden[r, h : h + 1], axis=0, keepdims=True)

        s, zz = lax.fori_loop(
            0, 4, state, (jnp.zeros((256, 128), f32), jnp.zeros((1, 256), f32))
        )
        pack_state(st, h, s, zz)
    to_x = links.start(st, st_x, seq=seq + 1 - 2 * x)
    event(1, 6)

    dq[...] = jnp.zeros(dq.shape, f32)

    def local_head(h):
        hm = hm_ref[h : h + 1, :]
        hv = slice(h * 128, (h + 1) * 128)
        for j in range(total // 256):
            k_rows = slice(j * 256, (j + 1) * 256)
            dv_s = jnp.zeros((256, 128), f32)
            dk_s = jnp.zeros((256, 128), f32)
            for i in range(j, total // 256):
                q_rows = slice(i * 256, (i + 1) * 256)
                qm = (qkv[q_rows, 0:128].astype(f32) * hm).astype(bf16)
                u = dot_t(kq[k_rows, :], qm)
                keep = tok_ref[k_rows, 3:4] >= line_ref[1:2, q_rows]
                if i == j:
                    keep = keep & (tok_ref[k_rows, 3:4] <= line_ref[0:1, q_rows])
                kap = jnp.where(keep, (0.5 * u + 1.0) * u + 1.0, 0.0).astype(bf16)
                dn = dnum[q_rows, hv]
                grad = dot_t(qkv[k_rows, head_v(h)], dn) + dden_t[i, h : h + 1, :]
                du = jnp.where(keep, grad * (1.0 + u), 0.0).astype(bf16)
                dv_s = dv_s + dot(kap, dn)
                dk_s = dk_s + dot(du, qm)
                dq[q_rows, :] += dot_tt(du, kq[k_rows, :]) * hm
            dqkv[k_rows, head_v(h)] = dv_s.astype(bf16)
            if h == 0:
                dk[k_rows, :] = dk_s
            else:
                dk[k_rows, :] += dk_s

    local_head(0)
    to_x.wait_recv()
    for h in range(4):
        mine, theirs = st[h].astype(f32), st_x[h].astype(f32)
        first = jnp.where(x == 0, mine, theirs)
        second = jnp.where(x == 0, theirs, mine)
        st_t[h] = (first + coef_ref[0:1, :] * second).astype(bf16)
    to_z = [links.copy(st_t, st_z.at[d - 1], seq=seq - 2 * d) for d in (1, 2, 3)]
    for d in (1, 2, 3):

        @pl.when(z >= d)
        def _(d=d):
            to_z[d - 1].start()

    events(1, 7, 8)
    local_head(1)
    events(1, 8, 9)
    local_head(2)
    events(1, 9, 10)
    local_head(3)
    events(1, 10, 12)
    begin(2)
    for h in range(4):
        s_back[h, 0:176, :] = coef_ref[1:2, :] * st_x[h].astype(f32)
        s_back[h, 176:256, :] = jnp.zeros((80, 128), f32)
    for d in (1, 2, 3):

        @pl.when(z + d < 4)
        def _(d=d):
            to_z[d - 1].wait_recv()
            for h in range(4):
                s_back[h, 0:176, :] += coef_ref[1 + d : 2 + d, :] * st_z[d - 1, h].astype(f32)

    def split_state(ref, h):
        z_row = jnp.concatenate([ref[h, 160:161, :], ref[h, 161:162, :]], axis=1)
        feat = lax.broadcasted_iota(jnp.int32, (256, 128), 0)
        return jnp.where(feat < FEATS, ref[h], 0.0).astype(bf16), z_row

    for h in range(4):
        s_q, z_q = split_state(s_in, h)
        s_k, z_k = split_state(s_back, h)
        hv = slice(h * 128, (h + 1) * 128)

        def through(grad, a, b, h=h):
            grad = grad * lanes_ref[2:3, :]
            return dot_t((grad * b).astype(bf16), sa_ref[h]) + dot_t(
                (grad * a).astype(bf16), sb_ref[h]
            )

        def carried_part(i, _, h=h, s_q=s_q, z_q=z_q, s_k=s_k, z_k=z_k, hv=hv, through=through):
            r = col(i, 256)
            a, b = phi(qkv[r, 0:128], h, sa_ref, sb_ref, lanes_ref)
            grad = dot_t(dnum[r, hv], s_q) + dden[r, h : h + 1] * z_q
            dq[r, :] += through(grad * tok_ref[r, 1:2], a, b)
            a, b = phi(kq[r, :], h, sa_ref, sb_ref, lanes_ref)
            last = tok_ref[r, 2:3]
            grad = dot_t(qkv[r, head_v(h)], s_k) + z_k
            dk[r, :] += through(grad * last, a, b)
            f = (a * b * lanes_ref[2:3, :] * last).astype(bf16)
            dqkv[r, head_v(h)] = (dqkv[r, head_v(h)].astype(f32) + dot(f, s_k)).astype(bf16)
            return 0

        lax.fori_loop(0, 4, carried_part, 0)

    def join(i):
        r = col(i, 256)
        dqkv[r, 0:128] = (dq[r, :] + pltpu.roll(dk[r, :], 64, 1)).astype(bf16)

    run(4, join)
    done.wait()
    events(1, 12, 14)
    done = load(fout.at[:, pl.ds(0, ff)], g_out)
    own_w = load(wg_all.at[7], stream.at[0, 0])
    own_w.wait()
    gain_two = jnp.sum(fout[:, 0:ff] * stream[0, 0].astype(f32), axis=1, keepdims=True)

    def wq_tiles(i, slot):
        return [(wq_all.at[i], stream.at[slot, 0, :, pl.ds(0, 640)])]

    def grad_hidden_first(i, slot):
        sums.offer(i, 2, dot_t(dqkv[...], stream[slot, 0, :, 0:640]))
        pl.when(i > 0)(lambda: sums.pass_on(i - 1, 2))

    chunks_of(wq_tiles, 8, grad_hidden_first, (2, 0, 2))
    sums.pass_on(7, 2)

    def grad_out_qkv(i, slot):
        s2[col(i), 0:512] = dot_tt(rows_all[:, col(i)], yb[...]).astype(bf16)
        s2[col(i), 512:1152] = dot_tt(hs[slot], dqkv[...]).astype(bf16)

    chunks_of(h_tiles(h1_all), 8, grad_out_qkv, (2, 2, 2))
    events(2, 4, 6)
    def take_first(i):
        def use(value):
            x1[:, col(i)] = value

        sums.take(i, 2, use)

    run(8, take_first, (2, 6, 2))
    for made in got_x:
        made.wait()

    def norm_back_first(i, _):
        r = pl.ds(pl.multiple_of(i * 32, 32), 32)
        v = own_rows[r, :].astype(f32)
        s = lax.rsqrt(jnp.mean(v * v, axis=1, keepdims=True) + epsilon)
        n = v * s
        dn = x1[r, :] * gains[0:1, :]
        acc[r, :] += s * (dn - n * jnp.mean(dn * n, axis=1, keepdims=True))
        return 0

    lax.fori_loop(0, rows // 32, norm_back_first, 0)
    pending += [load(acc.at[:, col(j)], input_out.at[:, c]) for j, c in enumerate(columns)]
    events(2, 8, 12)
    begin(3)
    done.wait()
    events(2, 12, 14)
    done = load(fout.at[:, pl.ds(0, ff)], u_out)
    own_w = load(wu_all.at[7], stream.at[0, 0])
    own_q = load(wq_all.at[7], stream.at[1, 0, :, pl.ds(0, 640)])
    own_w.wait()
    own_q.wait()
    gain_two += jnp.sum(fout[:, 0:ff] * stream[0, 0].astype(f32), axis=1, keepdims=True)
    events(3, 0, 12)
    done.wait()
    events(3, 12, 14)
    pending.append(load(fout.at[:, pl.ds(0, 1152)], oq_out))
    gain_one = jnp.sum(fout[:, 512:1152] * stream[1, 0, :, 0:640].astype(f32), axis=1, keepdims=True)
    lane = lax.broadcasted_iota(jnp.int32, (256, 128), 1)
    both = jnp.where(lane == 0, gain_one, jnp.where(lane == 1, gain_two, 0.0)).T[0:8, :]
    terms[0] = both
    over = links.start(terms.at[0], terms_core, tp=over_core)
    over.wait_recv()
    both = both + terms_core[...]
    terms[1] = both
    over = links.start(terms.at[1], terms_y, tp=over_y)
    over.wait_recv()
    own_gains = jnp.concatenate(
        [gain_first[...], gain_second[...], jnp.ones((6, 256), f32)], axis=0
    ).astype(bf16)
    terms[2] = (both + terms_y[...]) / own_gains.astype(f32)
    pending.append(load(terms.at[2], gain_out))
    run(8, lambda i: sums.sent(i))
    for made in pending:
        made.wait()
    links.finish()
    for d in (1, 2, 3):

        @pl.when(z >= d)
        def _(d=d):
            to_z[d - 1].wait_send()


def feature_tables(heads):
    first = np.zeros((heads, 128, 256), np.float32)
    second = np.zeros((heads, 128, 256), np.float32)
    lanes = np.zeros((8, 256), np.float32)
    f = 0
    for i in range(FEAT):
        for j in range(i, FEAT):
            for h in range(heads):
                first[h, h * FEAT + i, f] = 1
                second[h, h * FEAT + j, f] = 1
            lanes[2, f] = square_coef if i == j else square_coef * 2**0.5
            f += 1
    for i in range(FEAT):
        for h in range(heads):
            first[h, h * FEAT + i, f] = 1
        lanes[1, f] = 1
        lanes[2, f] = linear_coef
        f += 1
    lanes[0, f] = lanes[1, f] = lanes[2, f] = 1
    mask = np.zeros((8, 128), np.float32)
    for h in range(heads):
        mask[h, h * FEAT : (h + 1) * FEAT] = 0.25
    return first, second, lanes, mask


def forward_pass(lengths, constants, gain_first, gain_second, x_in, weights, c_in):
    rows, width = x_in.shape
    total = 4 * rows
    ff = weights[4].shape[0]
    hbm = pl.BlockSpec(memory_space=pl.ANY)
    vmem = pl.BlockSpec(memory_space=pltpu.VMEM)

    def shape(*dims, dtype=bf16):
        return jax.ShapeDtypeStruct(dims, dtype)

    outs = (
        shape(8, 256, 640),
        shape(8, 256, 512),
        shape(8, 256, ff),
        shape(8, 256, ff),
        shape(8, 256, ff),
        shape(total, width),
        shape(total, width),
        shape(total, 640),
        shape(total, 512),
        shape(total, 128, dtype=f32),
        shape(rows, width, dtype=f32),
        shape(total, width),
        shape(total, ff),
        shape(total, ff),
        shape(total, ff),
        shape(4, 256, 128, dtype=f32),
        shape(8, width, dtype=f32),
    )
    scratch = [
        pltpu.VMEM((rows, width), bf16),
        pltpu.VMEM((total, 128), f32),
        pltpu.VMEM((8, total), f32),
        pltpu.VMEM((8, 128), f32),
        pltpu.VMEM((16, 256), bf16),
        pltpu.VMEM((256, 640), bf16),
        pltpu.VMEM((256, 512), bf16),
        pltpu.VMEM((256, ff), bf16),
        pltpu.VMEM((256, ff), bf16),
        pltpu.VMEM((256, ff), bf16),
        pltpu.VMEM((128, 256), f32),
        pltpu.VMEM((256, 512), f32),
        pltpu.VMEM((512, 256), f32),
        pltpu.VMEM((-(-ff // 128) * 128, 256), f32),
        pltpu.VMEM((-(-ff // 128) * 128, 256), f32),
        pltpu.VMEM((total, width), bf16),
        pltpu.VMEM((total, width), bf16),
        pltpu.VMEM((width, 640), bf16),
        pltpu.VMEM((width, 512), bf16),
        pltpu.VMEM((width, ff), bf16),
        pltpu.VMEM((width, ff), bf16),
        pltpu.VMEM((total, 640), bf16),
        pltpu.VMEM((total, 128), bf16),
        pltpu.VMEM((total, 512), f32),
        pltpu.VMEM((total, 128), f32),
        pltpu.VMEM((total, 512), bf16),
        pltpu.VMEM((2, rows, width), bf16),
        pltpu.VMEM((2, rows, width), bf16),
        pltpu.VMEM((rows, width), bf16),
        pltpu.VMEM((rows, width), bf16),
        pltpu.VMEM((rows, width), f32),
        pltpu.VMEM((total, ff), bf16),
        pltpu.VMEM((total, ff), bf16),
        pltpu.VMEM((total, ff), bf16),
        pltpu.VMEM((8, 16, 256), bf16),
        pltpu.VMEM((8, width), f32),
        pltpu.VMEM((4, 176, 128), bf16),
        pltpu.VMEM((4, 176, 128), bf16),
        pltpu.VMEM((4, 176, 128), bf16),
        pltpu.VMEM((3, 4, 176, 128), bf16),
        pltpu.VMEM((4, 256, 128), f32),
        pltpu.SemaphoreType.DMA((112,)),
        pltpu.SemaphoreType.DMA((112,)),
        pltpu.SemaphoreType.DMA((112,)),
    ]
    return pl.pallas_call(
        fwd_kernel,
        out_shape=outs,
        in_specs=[pl.BlockSpec(memory_space=pltpu.SMEM)] + [vmem] * 6 + [hbm] * 9,
        out_specs=(hbm,) * len(outs),
        scratch_shapes=scratch,
        compiler_params=pltpu.CompilerParams(
            collective_id=0, has_side_effects=True, vmem_limit_bytes=60 * 2**20
        ),
    )(lengths, *constants, gain_first, gain_second, x_in, *weights, c_in)


def backward_pass(lengths, constants, gains, s_in, den, gain_pair, x_in, x1, weights, c_all, acts):
    rows, width = x_in.shape
    total = 4 * rows
    ff = weights[2].shape[2]
    hbm = pl.BlockSpec(memory_space=pl.ANY)
    vmem = pl.BlockSpec(memory_space=pltpu.VMEM)

    def shape(*dims, dtype=f32):
        return jax.ShapeDtypeStruct(dims, dtype)

    outs = (
        shape(256, ff),
        shape(256, ff),
        shape(256, ff),
        shape(256, 1152),
        shape(rows, width, dtype=bf16),
        shape(rows, width),
        shape(8, 256),
    )
    scratch = [
        pltpu.VMEM((total, 128), f32),
        pltpu.VMEM((8, total), f32),
        pltpu.VMEM((8, 128), f32),
        pltpu.VMEM((3, 8, 256), f32),
        pltpu.VMEM((8, 256), f32),
        pltpu.VMEM((8, 256), f32),
        pltpu.VMEM((8, 256, ff), bf16),
        pltpu.VMEM((width, ff), bf16),
        pltpu.VMEM((width, ff), bf16),
        pltpu.VMEM((width, 512), bf16),
        pltpu.VMEM((2, 2, 256, ff), bf16),
        pltpu.VMEM((2, total, 256), bf16),
        pltpu.VMEM((total, width), bf16),
        pltpu.VMEM((total, ff), bf16),
        pltpu.VMEM((total, ff), bf16),
        pltpu.VMEM((2, 2, 128, ff), bf16),
        pltpu.VMEM((total, 640), bf16),
        pltpu.VMEM((total, 128), bf16),
        pltpu.VMEM((total, 512), bf16),
        pltpu.VMEM((total, 512), bf16),
        pltpu.VMEM((total, 128), f32),
        pltpu.VMEM((4, 8, 256), f32),
        pltpu.VMEM((total, 640), bf16),
        pltpu.VMEM((total, 128), f32),
        pltpu.VMEM((total, 128), f32),
        pltpu.VMEM((8, 4, 256, 256), bf16),
        pltpu.VMEM((8, 2, 256, 256), bf16),
        pltpu.VMEM((8, 256, 256), bf16),
        pltpu.VMEM((rows, width), f32),
        pltpu.VMEM((rows, width), f32),
        pltpu.VMEM((256, ff), f32),
        pltpu.VMEM((4, 176, 128), bf16),
        pltpu.VMEM((4, 176, 128), bf16),
        pltpu.VMEM((4, 176, 128), bf16),
        pltpu.VMEM((3, 4, 176, 128), bf16),
        pltpu.VMEM((4, 256, 128), f32),
        pltpu.VMEM((rows, width), bf16),
        pltpu.SemaphoreType.DMA((2, 2, 2)),
        pltpu.SemaphoreType.DMA((2, 2, 2, 7)),
        pltpu.SemaphoreType.DMA((6, 8)),
        pltpu.SemaphoreType.REGULAR((2,)),
        pltpu.SemaphoreType.DMA((16,)),
        pltpu.SemaphoreType.DMA((16,)),
        pltpu.SemaphoreType.DMA((80,)),
        pltpu.SemaphoreType.DMA((2, 2)),
    ]
    return pl.pallas_call(
        bwd_kernel,
        out_shape=outs,
        in_specs=[pl.BlockSpec(memory_space=pltpu.SMEM)] + [vmem] * 9 + [hbm] * 15,
        out_specs=(hbm,) * len(outs),
        scratch_shapes=scratch,
        compiler_params=pltpu.CompilerParams(
            collective_id=1, has_side_effects=True, vmem_limit_bytes=62 * 2**20
        ),
    )(lengths, *constants, gains, s_in, den, *gain_pair, x_in, x1, *weights, c_all, *acts)


def on_device_rings(
    inputs, lengths, gain_attn, w_query, w_key, w_value, w_out, gain_mlp, w_gate, w_up, w_down,
    cotangent,
):
    first, second, lanes, mask = feature_tables(4)
    constants = (
        jnp.asarray(first, bf16), jnp.asarray(second, bf16), jnp.asarray(lanes), jnp.asarray(mask),
    )
    gain_pair = (gain_attn.reshape(1, -1), gain_mlp.reshape(1, -1))
    made = forward_pass(
        lengths, constants, *gain_pair, inputs,
        (w_query.T, w_key.T, w_value, w_out, w_gate.T, w_up.T, w_down), cotangent,
    )
    weights, (c_all, h1, qkv, yb, den, x1, h2, gate, up, mixed, s_in, gain_all) = made[:5], made[5:]
    sum_down_t, sum_gate, sum_up, sum_oq, block, grad_input, gain_sums = backward_pass(
        lengths, constants, gain_all, s_in, den, gain_pair, inputs, x1, weights, c_all,
        (h1, qkv, yb, h2, gate, up, mixed),
    )
    return (
        block,
        grad_input,
        gain_sums[0],
        sum_oq[:, 512:576],
        sum_oq[:, 576:640],
        sum_oq[:, 640:],
        sum_oq[:, :512].T,
        gain_sums[1],
        sum_gate,
        sum_up,
        sum_down_t.T,
    )


def on_device(
    inputs,
    lengths,
    gain_attn,
    w_query,
    w_key,
    w_value,
    w_out,
    gain_mlp,
    w_gate,
    w_up,
    w_down,
    cotangent,
):
    seq_count = lax.axis_size("seq")
    tp_count = lax.axis_size("tp")
    seq_index = lax.axis_index("seq")
    rows_own, width = inputs.shape
    chunk = width // seq_count
    half = chunk // 2
    block_len = rows_own * tp_count
    anchor = seq_index * block_len
    relative = relative_list(seq_count)
    ring = ring_order(seq_count)
    place_of = [ring.index(s) for s in range(seq_count)]
    to_rel = jnp.array(
        [[ring[(place_of[s] - k) % seq_count] for k in relative] for s in range(seq_count)],
        jnp.int32,
    )[seq_index]
    to_abs = jnp.array(
        [
            [relative.index((place_of[s] - place_of[o]) % seq_count) for o in range(seq_count)]
            for s in range(seq_count)
        ],
        jnp.int32,
    )[seq_index]
    to_rel = [to_rel[j] for j in range(seq_count)]
    to_abs = [to_abs[j] for j in range(seq_count)]

    qk_cols, v_cols, ff_cols = w_query.shape[1], w_value.shape[1], w_gate.shape[1]
    gains = jnp.stack([gain_attn, gain_mlp]).astype(bf16)
    qkv_cols = 2 * qk_cols + v_cols
    qkv_own = jnp.concatenate([w_query, w_key, w_value], axis=1).astype(bf16)
    gain_rows = jnp.zeros((16, qkv_cols), bf16).at[:2, :chunk].set(gains)
    first_own = jnp.concatenate([qkv_own, gain_rows], axis=0)
    out_own = w_out.astype(bf16).T
    gate_up_own = jnp.concatenate([w_gate, w_up], axis=1).astype(bf16)
    down_own = w_down.astype(bf16).T

    first_got = ring_gather(first_own, half)
    out_got = ring_gather(out_own, half)
    gate_up_got = ring_gather(gate_up_own, half)
    down_got = ring_gather(down_own, half)
    w_qkv = jnp.concatenate([first_got[k][:chunk] for k in relative], axis=0)
    gain_first = jnp.concatenate([first_got[k][chunk, :chunk] for k in relative]).astype(f32)
    gain_second = jnp.concatenate([first_got[k][chunk + 1, :chunk] for k in relative]).astype(f32)
    w_out_t = jnp.concatenate([out_got[k] for k in relative], axis=0)
    w_gate_up = jnp.concatenate([gate_up_got[k] for k in relative], axis=0)
    w_down_t = jnp.concatenate([down_got[k] for k in relative], axis=0)

    at = jnp.arange(lengths.shape[0])
    starts = jnp.sum(jnp.where(at[None, :] < at[:, None], lengths[None, :], 0), axis=1)
    positions, row_ids, carry_in, after_last = segment_masks(anchor, starts, block_len)
    carry_mask = carry_in.astype(f32)
    last_mask = after_last.astype(f32)
    resets = (
        jnp.sum(
            ((starts // block_len)[None, :] == jnp.arange(seq_count)[:, None]).astype(jnp.int32),
            axis=1,
        )
        > 0
    ).astype(jnp.int32)

    inputs_own = to_relative(inputs, to_rel, chunk)
    grad_own = to_relative(cotangent, to_rel, chunk)
    inputs_full = tp_gather(inputs_own).astype(f32)
    grad_full = tp_gather(grad_own)
    inputs_own = inputs_own.astype(f32)
    hidden_first = (inputs_full * rms_scale(inputs_full) * gain_first).astype(bf16)
    qkv = dot(hidden_first, w_qkv).astype(bf16)
    queries = qkv[:, :qk_cols]
    key_flat = qkv[:, qk_cols : 2 * qk_cols]
    value_flat = qkv[:, 2 * qk_cols :]
    heads_local = qk_cols // FEAT
    query_heads = queries.reshape(block_len, heads_local, FEAT)
    key_heads = key_flat.reshape(block_len, heads_local, FEAT)
    value_heads = value_flat.reshape(block_len, heads_local, VHEAD)
    query_float = query_heads.astype(f32)
    key_float = key_heads.astype(f32)
    value_float = value_heads.astype(f32)
    key_feat = features(key_float) * last_mask[:, None, None]
    local_state = jnp.einsum("thn,thv->hnv", key_feat, value_float, precision=highest)
    local_sum = jnp.sum(key_feat, axis=0)
    carry_state, carry_sum = carried([local_state, local_sum], resets, 1)
    step_rows = 512
    query_feat = features(query_float)
    carry_weight = carry_mask[:, None]
    numer_parts = []
    denom_parts = []
    for first_row in range(0, block_len, step_rows):
        query_part = query_heads[first_row : first_row + step_rows]
        scores, allowed, kernel = pair_block(
            query_part, key_heads, row_ids, positions, first_row, step_rows
        )
        numer_parts.append(
            jnp.einsum("hts,shv->thv", kernel.astype(bf16), value_heads, preferred_element_type=f32)
        )
        denom_parts.append(jnp.sum(kernel, axis=-1).T)
    numerator = (
        jnp.concatenate(numer_parts, axis=0)
        + jnp.einsum("thn,hnv->thv", query_feat, carry_state, precision=highest)
        * carry_weight[:, :, None]
    )
    denominator = (
        jnp.concatenate(denom_parts, axis=0)
        + jnp.einsum("thn,hn->th", query_feat, carry_sum, precision=highest) * carry_weight
    )
    attended = numerator / denominator[:, :, None]
    attended_low = attended.reshape(block_len, heads_local * VHEAD).astype(bf16)
    attn_partial = dot_t(attended_low, w_out_t).astype(bf16)
    middle_own = inputs_own + tp_scatter(attn_partial)
    scale_second = rms_scale(middle_own)
    normed_second = middle_own * scale_second
    hidden_second = tp_gather((normed_second * gain_second).astype(bf16))
    gate_up = dot(hidden_second, w_gate_up)
    gate_value, upward = gate_up[:, :ff_cols], gate_up[:, ff_cols:]
    sigmoid_gate = jax.nn.sigmoid(gate_value)
    silu_gate = gate_value * sigmoid_gate
    mixed_rows = (silu_gate * upward).astype(bf16)
    grad_down_t = dot_tt(grad_full, mixed_rows).astype(bf16)

    def by_distance(stack):
        return {k: stack[j * chunk : (j + 1) * chunk] for j, k in enumerate(relative)}

    sum_down_t = ring_scatter(by_distance(grad_down_t))
    mlp_own = tp_scatter(dot_t(mixed_rows, w_down_t).astype(bf16))
    block_output = to_relative((middle_own + mlp_own).astype(bf16), to_abs, chunk)

    grad_mixed = dot(grad_full, w_down_t).astype(bf16).astype(f32)
    grad_gate = (
        grad_mixed * upward * sigmoid_gate * (1.0 + gate_value * (1.0 - sigmoid_gate))
    ).astype(bf16)
    grad_upward = (grad_mixed * silu_gate).astype(bf16)
    grad_gate_up = jnp.concatenate([grad_gate, grad_upward], axis=1)
    hidden_partial = dot_t(grad_gate_up, w_gate_up).astype(bf16)
    sum_gate_up = ring_scatter(by_distance(dot_tt(hidden_second, grad_gate_up).astype(bf16)))
    grad_hidden = tp_scatter(hidden_partial)
    grad_middle = grad_own.astype(f32) + norm_back(
        grad_hidden, normed_second, scale_second, gain_second
    )
    grad_branch = tp_gather(grad_middle.astype(bf16))
    sum_out_t = ring_scatter(by_distance(dot_tt(grad_branch, attended_low).astype(bf16)))
    grad_attended = dot(grad_branch, w_out_t).reshape(block_len, heads_local, VHEAD)
    grad_numer = (grad_attended / denominator[:, :, None]).astype(bf16)
    grad_denom = -jnp.sum(grad_attended * attended, axis=-1) / denominator
    grad_numer_carried = grad_numer.astype(f32) * carry_weight[:, :, None]
    grad_denom_carried = grad_denom * carry_weight
    grad_state_in = jnp.einsum("thn,thv->hnv", query_feat, grad_numer_carried, precision=highest)
    grad_sum_in = jnp.einsum("thn,th->hn", query_feat, grad_denom_carried, precision=highest)
    grad_query_feat = (
        jnp.einsum("thv,hnv->thn", grad_numer_carried, carry_state, precision=highest)
        + grad_denom_carried[:, :, None] * carry_sum[None]
    )
    grad_state_out, grad_sum_out = carried([grad_state_in, grad_sum_in], resets, -1)
    grad_key_feat = (
        jnp.einsum("thv,hnv->thn", value_float, grad_state_out, precision=highest)
        + grad_sum_out[None]
    ) * last_mask[:, None, None]
    grad_value_state = jnp.einsum("thn,hnv->thv", key_feat, grad_state_out, precision=highest)
    grad_query_parts = []
    grad_key_inner = jnp.zeros((block_len, heads_local, FEAT), f32)
    grad_value_inner = jnp.zeros((block_len, heads_local, VHEAD), f32)
    for first_row in range(0, block_len, step_rows):
        query_part = query_heads[first_row : first_row + step_rows]
        scores, allowed, kernel = pair_block(
            query_part, key_heads, row_ids, positions, first_row, step_rows
        )
        numer_grad_part = grad_numer[first_row : first_row + step_rows]
        grad_weights = jnp.einsum(
            "thv,shv->hts", numer_grad_part, value_heads, preferred_element_type=f32
        )
        grad_scores = (
            (grad_weights + grad_denom[first_row : first_row + step_rows].T[:, :, None])
            * allowed[None]
            * (1.0 + scores)
        ).astype(bf16)
        grad_query_parts.append(
            jnp.einsum("hts,shf->thf", grad_scores, key_heads, preferred_element_type=f32) * 0.25
        )
        grad_key_inner = (
            grad_key_inner
            + jnp.einsum("hts,thf->shf", grad_scores, query_part, preferred_element_type=f32) * 0.25
        )
        grad_value_inner = grad_value_inner + jnp.einsum(
            "hts,thv->shv", kernel.astype(bf16), numer_grad_part, preferred_element_type=f32
        )
    grad_query = (
        jnp.concatenate(grad_query_parts, axis=0) + feature_grad(query_float, grad_query_feat)
    ).astype(bf16)
    grad_key = (grad_key_inner + feature_grad(key_float, grad_key_feat)).astype(bf16)
    grad_value = (grad_value_inner + grad_value_state).astype(bf16)
    grad_qkv = jnp.concatenate(
        [
            grad_query.reshape(block_len, heads_local * FEAT),
            grad_key.reshape(block_len, heads_local * FEAT),
            grad_value.reshape(block_len, heads_local * VHEAD),
        ],
        axis=1,
    )
    sum_qkv = ring_scatter(by_distance(dot_tt(hidden_first, grad_qkv).astype(bf16)))
    grad_hidden_first = tp_scatter(dot_t(grad_qkv, w_qkv).astype(bf16))
    scale_first = rms_scale(inputs_own)
    normed_first = inputs_own * scale_first
    grad_input = to_relative(
        grad_middle + norm_back(grad_hidden_first, normed_first, scale_first, gain_first),
        to_abs,
        chunk,
    )

    gain_terms = jnp.stack(
        [
            jnp.sum(qkv_own.astype(f32) * sum_qkv, axis=1),
            jnp.sum(gate_up_own.astype(f32) * sum_gate_up, axis=1),
        ]
    )
    gain_sums = tp_sum(gain_terms) / gains.astype(f32)
    return (
        block_output,
        grad_input,
        gain_sums[0],
        sum_qkv[:, :qk_cols],
        sum_qkv[:, qk_cols : 2 * qk_cols],
        sum_qkv[:, 2 * qk_cols :],
        sum_out_t.T,
        gain_sums[1],
        sum_gate_up[:, :ff_cols],
        sum_gate_up[:, ff_cols:],
        sum_down_t.T,
    )


def solution(mesh):
    in_specs = (
        P(("seq", "tp"), None),
        P(),
        P("seq"),
        P("seq", "tp"),
        P("seq", "tp"),
        P("seq", "tp"),
        P("tp", "seq"),
        P("seq"),
        P("seq", "tp"),
        P("seq", "tp"),
        P("tp", "seq"),
        P(("seq", "tp"), None),
    )
    out_specs = (
        P(("seq", "tp"), None),
        P(("seq", "tp"), None),
        P("seq"),
        P("seq", "tp"),
        P("seq", "tp"),
        P("seq", "tp"),
        P("tp", "seq"),
        P("seq"),
        P("seq", "tp"),
        P("seq", "tp"),
        P("tp", "seq"),
    )
    small = mesh.shape["seq"] == 8 and mesh.shape["tp"] == 4
    body = on_device_rings if small else on_device
    return jax.shard_map(
        body, mesh=mesh, in_specs=in_specs, out_specs=out_specs, check_vma=False
    )
```

```python
import jax
import jax.numpy as jnp
import numpy as np
from jax import lax
from jax.experimental import pallas as pl
from jax.experimental.pallas import tpu as pltpu
from jax.sharding import PartitionSpec as P

FEAT = 16
VHEAD = 128


epsilon = 1e-05
linear_coef = 0.5
square_coef = 0.17677669529663687
highest = lax.Precision.HIGHEST
f32 = jnp.float32
bf16 = jnp.bfloat16


def ring_order(count):
    planes = 4 if count % 4 == 0 else 2
    columns = count // planes
    order = [z * columns for z in range(planes)]
    for z in reversed(range(planes)):
        xs = list(range(1, columns))
        if (planes - 1 - z) % 2:
            xs.reverse()
        order += [z * columns + x for x in xs]
    return order


def relative_list(count):
    half = count // 2
    out = []
    for j in range(1, half):
        out += [j, count - j]
    return out + [half, 0]


def ring_perms(count):
    ring = ring_order(count)
    fwd = [(ring[i], ring[(i + 1) % count]) for i in range(count)]
    return fwd, [(b, a) for a, b in fwd]


def ring_gather(own, half_rows):
    count = lax.axis_size("seq")
    fwd, bwd = ring_perms(count)
    half = count // 2
    got = {0: own}
    ahead = back = own
    for step in range(1, half):
        ahead = lax.ppermute(ahead, "seq", fwd)
        back = lax.ppermute(back, "seq", bwd)
        got[step] = ahead
        got[count - step] = back
    ahead = lax.ppermute(ahead[:half_rows], "seq", fwd)
    back = lax.ppermute(back[half_rows:], "seq", bwd)
    got[half] = jnp.concatenate([ahead, back], axis=0)
    return got


def ring_scatter(chunks):
    count = lax.axis_size("seq")
    fwd, bwd = ring_perms(count)
    half = chunks[0].shape[0] // 2
    ahead = chunks[1][:half]
    back = chunks[count - 1][half:]
    for step in range(count - 1):
        ahead = lax.ppermute(ahead, "seq", fwd).astype(f32)
        back = lax.ppermute(back, "seq", bwd).astype(f32)
        last = step == count - 2
        ahead = ahead + chunks[0 if last else 2 + step][:half].astype(f32)
        back = back + chunks[0 if last else count - 2 - step][half:].astype(f32)
        if not last:
            ahead = ahead.astype(bf16)
            back = back.astype(bf16)
    return jnp.concatenate([ahead, back], axis=0)


def to_relative(array, index_row, chunk):
    return jnp.concatenate(
        [lax.dynamic_slice_in_dim(array, i * chunk, chunk, 1) for i in index_row], axis=1
    )


def tp_perms(count):
    ys = count // 2
    core = [(i, i ^ 1) for i in range(count)]
    shift = [
        [(i, (((i // 2) + d) % ys) * 2 + i % 2) for i in range(count)] for d in range(ys)
    ]
    return core, shift


def tp_gather(own):
    count = lax.axis_size("tp")
    ys = count // 2
    place = lax.axis_index("tp")
    y, c = place // 2, place % 2
    core, shift = tp_perms(count)
    parts = [own] + [lax.ppermute(own, "tp", shift[d]) for d in range(1, ys)]
    mine = jnp.stack([lax.select_n((y - at + ys) % ys, *parts) for at in range(ys)])
    other = lax.ppermute(mine, "tp", core)
    full = jnp.stack([jnp.where(c == 0, mine, other), jnp.where(c == 0, other, mine)], axis=1)
    return full.reshape((count * own.shape[0],) + own.shape[1:])


def tp_scatter(partial):
    count = lax.axis_size("tp")
    ys = count // 2
    place = lax.axis_index("tp")
    y, c = place // 2, place % 2
    core, shift = tp_perms(count)
    blocks = partial.reshape((ys, 2, partial.shape[0] // count) + partial.shape[1:])
    sent = lax.dynamic_index_in_dim(blocks, 1 - c, 1, False)
    kept = lax.dynamic_index_in_dim(blocks, c, 1, False)
    pair = kept.astype(f32) + lax.ppermute(sent, "tp", core).astype(f32)
    low = pair.astype(bf16)
    own = lax.dynamic_index_in_dim(pair, y, 0, False)
    for d in range(1, ys):
        away = lax.dynamic_index_in_dim(low, (y + d) % ys, 0, False)
        own = own + lax.ppermute(away, "tp", shift[d]).astype(f32)
    return own


def tp_sum(vector):
    count = lax.axis_size("tp")
    core, shift = tp_perms(count)
    vector = vector + lax.ppermute(vector, "tp", core)
    return vector + sum(lax.ppermute(vector, "tp", shift[d]) for d in range(1, count // 2))


def carried(arrays, resets, step):
    count = lax.axis_size("seq")
    place = lax.axis_index("seq")

    def from_near(a, d):
        perm = [(i, i + d * step) for i in range(count) if 0 <= i + d * step < count]
        return lax.ppermute(a.astype(bf16), "seq", perm).astype(f32)

    def reset_within(d):
        at = jnp.arange(count)
        away = (place - at) * step
        return jnp.sum(jnp.where((away >= 1) & (away <= d), resets, 0)) > 0

    arrays = [from_near(a, 1) for a in arrays]
    d = 1
    while d < count - 1:
        keep = 1.0 - reset_within(d).astype(f32)
        arrays = [a + keep * from_near(a, d) for a in arrays]
        d *= 2
    return arrays


def features(vector):
    squares = (vector[..., :, None] * vector[..., None, :]).reshape(
        vector.shape[:-1] + (vector.shape[-1] * vector.shape[-1],)
    )
    return jnp.concatenate(
        [jnp.ones_like(vector[..., :1]), vector * linear_coef, squares * square_coef], axis=-1
    )


def feature_grad(vector, grad_feat):
    feat_width = vector.shape[-1]
    linear_part = grad_feat[..., 1 : 1 + feat_width]
    square_part = grad_feat[..., 1 + feat_width :].reshape(vector.shape + (feat_width,))
    mixed_part = jnp.sum(square_part * vector[..., None, :], axis=-1) + jnp.sum(
        square_part * vector[..., :, None], axis=-2
    )
    return linear_coef * linear_part + square_coef * mixed_part


def segment_masks(anchor, starts, length):
    positions = anchor + jnp.arange(length, dtype=jnp.int32)
    start_le = starts[None, :] <= positions[:, None]
    row_ids = jnp.sum(start_le.astype(jnp.int32), axis=1)
    inside = (starts >= anchor) & (starts < anchor + length)
    carry = jnp.sum(((starts[None, :] >= anchor) & start_le).astype(jnp.int32), axis=1) == 0
    after_last = (
        jnp.sum(
            ((starts[None, :] > positions[:, None]) & inside[None, :]).astype(jnp.int32), axis=1
        )
        == 0
    )
    return (positions, row_ids, carry, after_last)


def rms_scale(values):
    return lax.rsqrt(jnp.mean(values * values, axis=-1, keepdims=True) + epsilon)


def norm_back(grad_out, normed, scale, gain):
    grad_normed = grad_out * gain
    return scale * (grad_normed - normed * jnp.mean(grad_normed * normed, axis=-1, keepdims=True))


def pair_block(query_part, key_heads, row_ids, positions, first_row, span_rows):
    scores = (
        jnp.einsum("thf,shf->hts", query_part, key_heads, preferred_element_type=f32) * 0.25
    )
    rows_here = row_ids[first_row : first_row + span_rows]
    place_here = positions[first_row : first_row + span_rows]
    allowed = (
        (rows_here[:, None] == row_ids[None, :]) & (positions[None, :] <= place_here[:, None])
    ).astype(f32)
    kernel = (1.0 + scores + 0.5 * scores * scores) * allowed[None]
    return (scores, allowed, kernel)


def dot(a, b):
    return jnp.dot(a, b, preferred_element_type=f32)


def dot_t(a, b):
    return lax.dot_general(a, b, (((1,), (1,)), ((), ())), preferred_element_type=f32)


def dot_tt(a, b):
    return lax.dot_general(a, b, (((0,), (0,)), ((), ())), preferred_element_type=f32)


def ring_place(seq):
    z, x = seq // 2, seq % 2
    return z + x * (7 - 2 * z)


def ring_seq(place):
    place = lax.rem(place + 8, 8)
    far = place // 4
    return (1 - far) * 2 * place + far * (15 - 2 * place)


class Sems:
    def __init__(self, ref):
        self.ref, self.used = ref, 0

    def take(self):
        self.used += 1
        return self.ref.at[self.used - 1]


class Links:
    def __init__(self, send, recv):
        self.send, self.recv, self.sent = Sems(send), Sems(recv), []

    def copy(self, src, dst, **to):
        return pltpu.make_async_remote_copy(
            src_ref=src,
            dst_ref=dst,
            send_sem=self.send.take(),
            recv_sem=self.recv.take(),
            device_id=to,
            device_id_type=pl.DeviceIdType.MESH,
        )

    def start(self, src, dst, **to):
        made = self.copy(src, dst, **to)
        made.start()
        self.sent.append(made)
        return made

    def sent_now(self, some):
        for made in some:
            made.wait_send()
        self.sent = [made for made in self.sent if all(made is not other for other in some)]

    def finish(self):
        for made in self.sent:
            made.wait_send()


class Gather:
    def __init__(self, links, arrays, split, nearby, gangs):
        self.links, self.arrays, self.split, self.nearby = links, arrays, split, nearby
        self.at = {k: j for j, k in enumerate(relative_list(8))}
        self.flying, self.gangs, self.done = {}, gangs, 0
        self.gang_of = {a: i for i, gang in enumerate(gangs) for a in gang}
        self.events = [
            (a, step, way, part)
            for gang in gangs
            for step in (1, 2, 3, 4)
            for a in gang
            for part in (0, 1)
            for way in (0, 1)
            if step < 4 or way == part
        ]
        for a in gangs[0]:
            for part in (0, 1):
                for way in (0, 1):
                    self.go(a, 1, way, part)

    def rows(self, part):
        return pl.ds(part * self.split, self.split)

    def go(self, a, step, way, part):
        own, everyone = self.arrays[a]
        before, after = (step - 1, step) if way == 0 else ((9 - step) % 8, 8 - step)
        src = own if step == 1 else everyone.at[self.at[before]]
        self.flying[a, step, way, part] = self.links.start(
            src.at[self.rows(part)],
            everyone.at[self.at[after], self.rows(part)],
            seq=self.nearby[way],
        )

    def pump(self, upto):
        while self.done < min(upto, len(self.events)):
            a, step, way, part = self.events[self.done]
            self.flying[a, step, way, part].wait_recv()
            if step < 3 or (step == 3 and way == part):
                self.go(a, step + 1, way, part)
            i = self.gang_of[a]
            if step == 3 and i + 1 < len(self.gangs):
                mine, later = self.gangs[i].index(a), self.gangs[i + 1]
                if i == 0:
                    later = later + self.gangs[2]
                elif i == 1:
                    later = []
                last = mine == len(self.gangs[i]) - 1
                for other in later[mine:] if last else later[mine : mine + 1]:
                    self.go(other, 1, way, part)
            self.done += 1

    def pump_array(self, a):
        gang = self.gang_of[a]
        self.pump(14 * sum(len(g) for g in self.gangs[: gang + 1]))


def greet(peers):
    barrier = pltpu.get_barrier_semaphore()
    for peer in peers:
        pl.semaphore_signal(
            barrier, inc=1, device_id=peer, device_id_type=pl.DeviceIdType.MESH
        )
    pl.semaphore_wait(barrier, len(peers))


def places():
    seq, tp = lax.axis_index("seq"), lax.axis_index("tp")
    place = ring_place(seq)
    nearby = (ring_seq(place + 1), ring_seq(place - 1))
    over_y = lax.rem(tp + 2, 4)
    over_core = tp + 1 - 2 * (tp % 2)
    peers = [{"seq": ring_seq(place + k)} for k in range(1, 8)]
    peers += [{"tp": over_y}, {"tp": over_core}]
    return seq, tp, place, nearby, over_y, over_core, peers


class Rows:
    def __init__(self, links, own, everyone, tp, over_y, over_core, rows):
        self.links, self.all, self.tp = links, everyone, tp
        self.over_y, self.over_core, self.rows = over_y, over_core, rows
        half = rows // 2
        self.first = [
            links.start(
                own.at[pl.ds(i * half, half)], self.block(tp, i * half, half), tp=over_y
            )
            for i in (0, 1)
        ]
        self.near = links.start(own, self.block(tp, 0, rows), tp=over_core)
        self.last = []

    def block(self, owner, offset, size):
        return self.all.at[pl.ds(pl.multiple_of(owner * self.rows + offset, 16), size)]

    def forward(self, i):
        half = self.rows // 2
        self.first[i].wait_recv()
        came = self.block(self.over_y, i * half, half)
        self.last.append(self.links.start(came, came, tp=self.over_core))

    def finish(self):
        self.near.wait_recv()
        for made in self.last:
            made.wait_recv()


FEATS = 160


def fill_tables(lengths, seq, tok, line, coefs, step):
    total = tok.shape[0]
    anchor = seq * total
    starts, at = [], 0
    for i in range(lengths.shape[0]):
        starts.append(at)
        at = at + lengths[i]

    def places_of(shape, axis):
        pos = lax.broadcasted_iota(jnp.int32, shape, axis)
        low = jnp.zeros(shape, jnp.int32) - anchor
        last = jnp.ones(shape, f32)
        for start in starts:
            here = start - anchor
            low = jnp.maximum(low, jnp.where(pos >= here, here, -anchor))
            last = jnp.where((pos < here) & (here < total), 0.0, last)
        return pos.astype(f32), low, last

    lane = lax.broadcasted_iota(jnp.int32, (total, 128), 1)
    pos, low, last = places_of((total, 128), 0)
    began = jnp.where(low < 0, 1.0, 0.0)
    first = jnp.maximum(low, 0).astype(f32)
    tok[...] = jnp.where(
        lane == 0, first, jnp.where(lane == 1, began, jnp.where(lane == 2, last, pos))
    )
    pos, low, last = places_of((8, total), 1)
    row = lax.broadcasted_iota(jnp.int32, (8, total), 0)
    line[...] = jnp.where(row == 0, pos, jnp.maximum(low, 0).astype(f32))

    def clear(lo, hi):
        free = jnp.ones((1, 128), f32)
        for start in starts:
            at = jnp.zeros((1, 128), jnp.int32) + start
            free = jnp.where((at >= lo * total) & (at < (hi + 1) * total), 0.0, free)
        return free

    z, x = seq // 2, seq % 2
    one = jnp.ones((1, 128), f32)
    if step > 0:
        rows = [clear(2 * z + 1, 2 * z + 1), one * x.astype(f32), clear(2 * z, seq - 1)]
    else:
        rows = [clear(2 * z, 2 * z), one * (1 - x).astype(f32), clear(seq + 1, 2 * z + 1)]
    rows.append(clear(2 * z, 2 * z + 1))
    coefs[...] = jnp.concatenate(rows + [one * 0.0] * 4, axis=0)


class Chain:
    def __init__(self, links, st_t, st_z, coefs, seq, z, step):
        self.st_t, self.st_z, self.coefs = st_t, st_z, coefs
        self.turn = z if step > 0 else 3 - z
        self.hop = links.copy(st_t, st_z, seq=seq + 2 * step)

    def move(self, turn):
        @pl.when(self.turn == turn)
        def _():
            if turn > 0:
                self.hop.wait_recv()
            if turn < 3:
                if turn > 0:
                    for h in range(4):
                        own = self.st_t[h].astype(f32)
                        came = self.coefs[3:4, :] * self.st_z[h].astype(f32)
                        self.st_t[h] = (own + came).astype(bf16)
                self.hop.start()

    def use(self, states, near):
        for h in range(4):
            states[h, 0:176, :] = self.coefs[1:2, :] * near[h].astype(f32)
            states[h, 176:256, :] = jnp.zeros((80, 128), f32)

        @pl.when(self.turn > 0)
        def _():
            for h in range(4):
                states[h, 0:176, :] += self.coefs[2:3, :] * self.st_z[h].astype(f32)

    def finish(self):
        @pl.when(self.turn < 3)
        def _():
            self.hop.wait_send()


def ring_columns(place):
    return [pl.ds(pl.multiple_of(ring_seq(place - k) * 256, 256), 256) for k in relative_list(8)]


def phi(heads, h, select_a, select_b, lanes):
    a = dot(heads, select_a[h]) + lanes[0:1, :]
    b = dot(heads, select_b[h]) + lanes[1:2, :]
    return a, b


def fwd_kernel(
    lengths, sa_ref, sb_ref, lanes_ref, hm_ref, gain_first, gain_second,
    x_in, wq_in, wk_in, wv_in, wo_in, wg_in, wu_in, wd_in, c_in,
    wq_all, wo_all, wg_all, wu_all, wd_all, c_all,
    h1_out, qkv_out, yb_out, den_out, x1_out, h2_out, gate_out, up_out, m_out, sin_out, gain_out,
    x_ref, tok_ref, line_ref, coef_ref, gain_ref, q_own, o_own, g_own, u_own, d_own,
    w_small, w_v, w_o, w_d, w_g,
    xg, h1, wq, wo, wg, wu, qkv, kq, num, den, yb, sc, rc, sy, ry, x1, gate, up, mm,
    gains_all, gains, st, st_x, st_t, st_z, s_in,
    send, recv, local,
):
    seq, tp, place, nearby, over_y, over_core, peers = places()
    z, x = seq // 2, seq % 2
    at = {k: j for j, k in enumerate(relative_list(8))}
    rows = x_ref.shape[0]
    total = 4 * rows
    links = Links(send, recv)
    locs = Sems(local)
    pending = []

    def store(src, dst):
        made = pltpu.make_async_copy(src, dst, locs.take())
        made.start()
        pending.append(made)

    def load(src, dst):
        made = pltpu.make_async_copy(src, dst, locs.take())
        made.start()
        return made

    got_qk = [load(wq_in, w_small.at[0:64]), load(wk_in, w_small.at[64:128]), load(wv_in, w_v)]
    columns = ring_columns(place)
    got_x = [load(x_in.at[:, c], x_ref.at[:, col(j)]) for j, c in enumerate(columns)]
    c_rows = pl.ds(pl.multiple_of(tp * rows, rows), rows)
    got_c = [load(c_in.at[:, c], c_all.at[c_rows, col(j)]) for j, c in enumerate(columns)]
    got_o = load(wo_in, w_o)
    ff = wd_in.shape[0]
    got_g = load(wg_in, w_g.at[pl.ds(0, ff)])
    got_d = load(wd_in, w_d.at[pl.ds(0, ff)])

    def turn(src, dst):
        for i in range(0, ff, 128):
            size = min(128, ff - i)
            dst[:, i : i + size] = src[i : i + 128, :].T[:, :size].astype(bf16)

    gain_ref[...] = jnp.concatenate(
        [gain_first[...], gain_second[...], jnp.zeros((14, 256), f32)], axis=0
    ).astype(bf16)
    greet(peers)
    gain_flying = [
        links.start(gain_ref, gains_all.at[at[k]], seq=ring_seq(place + k)) for k in range(1, 8)
    ]
    for made in got_x:
        made.wait()
    xrows = Rows(links, x_ref, xg, tp, over_y, over_core, rows)
    for made in got_qk:
        made.wait()
    q_own[:, 0:128] = w_small[...].T.astype(bf16)
    q_own[:, 128:640] = w_v[...].astype(bf16)
    ring = Gather(
        links,
        [(q_own, wq_all), (o_own, wo_all), (g_own, wg_all), (u_own, wu_all), (d_own, wd_all)],
        128,
        nearby,
        [[0], [1], [2, 3], [4]],
    )
    own_in = [
        load(x_ref, xrows.block(tp, 0, rows)),
        load(gain_ref, gains_all.at[at[0]]),
    ]
    got_o.wait()
    o_own[...] = w_o[...].T.astype(bf16)
    ring.pump(2)
    got_g.wait()
    turn(w_g, g_own)
    got_u = load(wu_in, w_g.at[pl.ds(0, ff)])
    ring.pump(4)
    got_d.wait()
    turn(w_d, d_own)
    got_u.wait()
    turn(w_g, u_own)
    own_kept = [load(own, everyone.at[at[0]]) for own, everyone in ring.arrays]
    fill_tables(lengths, seq, tok_ref, line_ref, coef_ref, 1)

    ring.pump(6)
    xrows.forward(0)
    for made in gain_flying:
        made.wait_recv()
    for made in own_in:
        made.wait()
    for j in range(8):
        chunk = gains_all[j].astype(f32)
        gains[0:8, j * 256 : (j + 1) * 256] = chunk[0:8]
    ring.pump(10)
    xrows.forward(1)
    ring.pump_array(0)
    own_kept[0].wait()
    got = load_weights(load, wq_all, wq)
    xrows.finish()

    def norm_first(i, _):
        r = pl.ds(pl.multiple_of(i * 32, 32), 32)
        v = xg[r, :].astype(f32)
        s = lax.rsqrt(jnp.mean(v * v, axis=1, keepdims=True) + epsilon)
        h1[r, :] = (v * s * gains[0:1, :]).astype(bf16)
        return 0

    lax.fori_loop(0, total // 32, norm_first, 0)
    links.sent_now(xrows.last)
    store(h1, h1_out)
    for made in got_c:
        made.wait()
    crows = Rows(links, c_all.at[c_rows], c_all, tp, over_y, over_core, rows)
    ring.pump(15)
    for made in got:
        made.wait()

    def project(i, _):
        r = pl.ds(pl.multiple_of(i * 256, 256), 256)
        res = dot(h1[r, :], wq[...])
        qkv[r, :] = res.astype(bf16)
        kq[r, :] = pltpu.roll(res[:, :128], 64, 1).astype(bf16)
        return 0

    lax.fori_loop(0, total // 256, project, 0)
    store(qkv, qkv_out)
    ring.pump(16)

    heads = 4

    def head_v(h):
        return slice(128 + h * 128, 256 + h * 128)

    for h in range(heads):

        def state(i, c, h=h):
            s, zz = c
            r = pl.ds(pl.multiple_of(i * 256, 256), 256)
            a, b = phi(kq[r, :], h, sa_ref, sb_ref, lanes_ref)
            f = a * b * lanes_ref[2:3, :] * tok_ref[r, 2:3]
            s = s + dot_tt(f.astype(bf16), qkv[r, head_v(h)])
            return s, zz + jnp.sum(f, axis=0, keepdims=True)

        s, zz = lax.fori_loop(
            0, total // 256, state, (jnp.zeros((256, 128), f32), jnp.zeros((1, 256), f32))
        )
        pack_state(st, h, s, zz)
        ring.pump(16 + (h + 1) // 2)
    to_x = links.start(st, st_x, seq=seq + 1 - 2 * x)

    def local_head(h):
        for i in range(total // 256):
            r = slice(i * 256, (i + 1) * 256)
            span = (i + 1) * 256
            qm = (qkv[r, :128].astype(f32) * hm_ref[h : h + 1, :]).astype(bf16)
            u = dot_t(qm, kq[:span, :])
            keep = (line_ref[0:1, :span] >= tok_ref[r, 0:1]) & (
                line_ref[0:1, :span] <= tok_ref[r, 3:4]
            )
            kap = jnp.where(keep, (0.5 * u + 1.0) * u + 1.0, 0.0)
            den[r, h : h + 1] = jnp.sum(kap, axis=1, keepdims=True)
            num[r, h * 128 : (h + 1) * 128] = dot(kap.astype(bf16), qkv[:span, head_v(h)])

    local_head(0)
    ring.pump(19)
    to_x.wait_recv()
    for h in range(heads):
        mine, theirs = st[h].astype(f32), st_x[h].astype(f32)
        early = jnp.where(x == 0, mine, theirs)
        later = jnp.where(x == 0, theirs, mine)
        st_t[h] = (later + coef_ref[0:1, :] * early).astype(bf16)
    chain = Chain(links, st_t, st_z, coef_ref, seq, z, 1)
    chain.move(0)
    local_head(1)
    chain.move(1)
    ring.pump(20)
    local_head(2)
    chain.move(2)
    ring.pump(22)
    local_head(3)
    chain.move(3)
    ring.pump(24)
    chain.use(s_in, st_x)
    store(s_in, sin_out)
    for h in range(heads):
        z_row = jnp.concatenate([s_in[h, 160:161, :], s_in[h, 161:162, :]], axis=1)
        feat = jax.lax.broadcasted_iota(jnp.int32, (256, 128), 0)
        s_low = jnp.where(feat < FEATS, s_in[h], 0.0).astype(bf16)

        def carry(i, _, h=h, z_row=z_row, s_low=s_low):
            r = pl.ds(pl.multiple_of(i * 256, 256), 256)
            a, b = phi(qkv[r, 0:128], h, sa_ref, sb_ref, lanes_ref)
            f = a * b * lanes_ref[2:3, :] * tok_ref[r, 1:2]
            hv = slice(h * 128, (h + 1) * 128)
            top = num[r, hv] + dot(f.astype(bf16), s_low)
            low = den[r, h : h + 1] + jnp.sum(f * z_row, axis=1, keepdims=True)
            den[r, h : h + 1] = low
            y = top / low
            yb[r, hv] = y.astype(bf16)
            return 0

        lax.fori_loop(0, total // 256, carry, 0)
        ring.pump(25 + h)
    store(yb, yb_out)
    store(den, den_out)
    ring.pump_array(1)
    own_kept[1].wait()
    got = load_weights(load, wo_all, wo)
    for made in got:
        made.wait()

    y_at, c_at = tp // 2, tp % 2

    def out_rows(block):
        return yb[pl.ds(pl.multiple_of(block * rows, rows), rows), :]

    cols = 512
    to_core = []
    for yy in (0, 1):

        def core_cols(i, _, yy=yy):
            c = pl.ds(pl.multiple_of(i * cols, cols), cols)
            sc[yy, :, c] = dot_t(out_rows(yy * 2 + 1 - c_at), wo[c, :]).astype(bf16)
            return 0

        lax.fori_loop(0, 2048 // cols, core_cols, 0)
        to_core.append(links.start(sc.at[yy], rc.at[yy], tp=over_core))
    for made in to_core:
        made.wait_recv()
    ring.pump(32)

    def away_cols(i, _):
        c = pl.ds(pl.multiple_of(i * cols, cols), cols)
        part = dot_t(out_rows((1 - y_at) * 2 + c_at), wo[c, :])
        sy[:, c] = (part + rc[1 - y_at, :, c].astype(f32)).astype(bf16)
        return 0

    lax.fori_loop(0, 2048 // cols, away_cols, 0)
    to_y = links.start(sy, ry, tp=over_y)

    def own_cols(i, _):
        c = pl.ds(pl.multiple_of(i * cols, cols), cols)
        x1[:, c] = (
            dot_t(out_rows(tp), wo[c, :]) + rc[y_at, :, c].astype(f32) + x_ref[:, c].astype(f32)
        )
        return 0

    lax.fori_loop(0, 2048 // cols, own_cols, 0)
    ring.pump(34)
    to_y.wait_recv()
    ring.pump(37)

    links.sent_now(xrows.first + [xrows.near])
    ho = x_ref

    def norm_second(i, _):
        r = pl.ds(pl.multiple_of(i * 32, 32), 32)
        v = x1[r, :] + ry[r, :].astype(f32)
        x1[r, :] = v
        s = lax.rsqrt(jnp.mean(v * v, axis=1, keepdims=True) + epsilon)
        ho[r, :] = (v * s * gains[1:2, :]).astype(bf16)
        return 0

    lax.fori_loop(0, rows // 32, norm_second, 0)
    store(x1, x1_out)
    store(gains, gain_out)
    h2 = xg
    hrows = Rows(links, ho, h2, tp, over_y, over_core, rows)
    own_in = load(ho, hrows.block(tp, 0, rows))
    ring.pump(40)
    hrows.forward(0)
    ring.pump(43)
    hrows.forward(1)
    crows.forward(0)
    crows.forward(1)
    hrows.finish()
    crows.finish()
    own_in.wait()
    store(h2, h2_out)
    ring.pump_array(2)
    own_kept[2].wait()
    got = load_weights(load, wg_all, wg)
    ring.pump_array(3)
    own_kept[3].wait()
    got += load_weights(load, wu_all, wu)
    for made in got:
        made.wait()

    def gate_up(i, _):
        r = pl.ds(pl.multiple_of(i * 128, 128), 128)
        g = dot(h2[r, :], wg[...])
        uu = dot(h2[r, :], wu[...])
        gate[r, :] = g.astype(bf16)
        up[r, :] = uu.astype(bf16)
        mm[r, :] = (g * jax.nn.sigmoid(g) * uu).astype(bf16)
        return 0

    for quarter in range(4):
        lax.fori_loop(quarter * total // 512, (quarter + 1) * total // 512, gate_up, 0)
        ring.pump(58 + 2 * quarter)
    store(gate, gate_out)
    store(up, up_out)
    store(mm, m_out)
    ring.pump_array(4)
    own_kept[4].wait()
    for made in pending:
        made.wait()
    links.finish()
    chain.finish()


def pack_state(st, h, s, zz):
    st[h, 0:FEATS, :] = s[:FEATS].astype(bf16)
    tail = jnp.concatenate([zz[:, :128], zz[:, 128:], jnp.zeros((14, 128), f32)], axis=0)
    st[h, FEATS : FEATS + 16, :] = tail.astype(bf16)


def load_weights(load, everyone, flat):
    count, chunk = everyone.shape[0], everyone.shape[1]
    return [load(everyone.at[j], flat.at[pl.ds(j * chunk, chunk)]) for j in range(count)]


class Scatter:
    def __init__(self, slots, send, recv, nearby):
        self.slots, self.send, self.recv, self.nearby = slots, send, recv, nearby

    def copy(self, a, step, way, sub, src, slot, width):
        return pltpu.make_async_remote_copy(
            src_ref=src,
            dst_ref=self.piece(slot, way, sub, width),
            send_sem=self.send.at[a % 2, way, sub],
            recv_sem=self.recv.at[a % 2, way, sub, step],
            device_id={"seq": self.nearby[way]},
            device_id_type=pl.DeviceIdType.MESH,
        )

    def slot(self, a, step):
        return (a % 2) * 4 + (a // 2 * 7 + step) % 4

    def rows(self, way, sub, base=0):
        start = base + way * 128 + sub * 64
        return pl.ds(start if isinstance(start, int) else pl.multiple_of(start, 64), 64)

    def piece(self, slot, way, sub, width):
        return self.slots.at[slot, self.rows(way, sub), pl.ds(0, width)]

    def begin(self, a, own, width, column=0):
        for sub in (0, 1):
            for way in (0, 1):
                src = own.at[self.rows(way, sub, way * 256), pl.ds(column, width)]
                self.copy(a, 0, way, sub, src, self.slot(a, 0), width).start()

    def event(self, a, e, own, width, out, column=0):
        step, sub = e // 2, e % 2
        is_last = step // 6
        here = self.slot(a, step)
        far = (step + 1) // 4
        place0 = (1 - far) * 2 * (step + 1) + far * (11 - 2 * step) + is_last * 8
        far = (step + 2) // 4 - is_last
        place1 = (1 - far) * (3 + 2 * step) + far * (10 - 2 * step) + is_last * 9
        places = (place0, place1)
        for way in (0, 1):
            piece = self.piece(here, way, sub, width)
            came = self.copy(a, step, way, sub, piece, here, width)
            came.wait_recv()
            came.wait_send()

        def summed(way):
            mine = own[self.rows(way, sub, places[way] * 256), pl.ds(column, width)]
            came = self.slots[here, self.rows(way, sub), pl.ds(0, width)]
            return came.astype(f32) + mine.astype(f32)

        def on():
            for way in (0, 1):
                self.slots[here, self.rows(way, sub), pl.ds(0, width)] = summed(way).astype(bf16)
                piece = self.piece(here, way, sub, width)
                self.copy(a, step + 1, way, sub, piece, self.slot(a, step + 1), width).start()

        def end():
            for way in (0, 1):
                out[self.rows(way, sub), pl.ds(0, width)] = summed(way)

        if isinstance(e, int):
            if step < 6:
                on()
            else:
                end()
        else:
            pl.when(step < 6)(on)
            pl.when(step == 6)(end)


class TpSum:
    def __init__(self, part, from_core, from_y, sems, credits, tp, over_y, over_core):
        self.part, self.from_core, self.from_y = part, from_core, from_y
        self.sems, self.credits = sems, credits
        self.tp, self.over_y, self.over_core = tp, over_y, over_core
        self.y, self.c = tp // 2, tp % 2

    def to_core(self, i, yy):
        return pltpu.make_async_remote_copy(
            src_ref=self.part.at[i, yy * 2 + 1 - self.c],
            dst_ref=self.from_core.at[i, yy],
            send_sem=self.sems.at[yy, i],
            recv_sem=self.sems.at[2 + yy, i],
            device_id={"tp": self.over_core},
            device_id_type=pl.DeviceIdType.MESH,
        )

    def to_y(self, i):
        return pltpu.make_async_remote_copy(
            src_ref=self.part.at[i, (1 - self.y) * 2 + self.c],
            dst_ref=self.from_y.at[i],
            send_sem=self.sems.at[4, i],
            recv_sem=self.sems.at[5, i],
            device_id={"tp": self.over_y},
            device_id_type=pl.DeviceIdType.MESH,
        )

    def sent(self, i):
        self.to_core(i, 0).wait_send()
        self.to_core(i, 1).wait_send()
        self.to_y(i).wait_send()

    def offer(self, i, turn, value):
        if turn > 0:
            self.sent(i)
        for block in range(4):
            self.part[i, block] = value[block * 256 : (block + 1) * 256].astype(bf16)
        if turn > 0:
            pl.semaphore_wait(self.credits.at[0], 1)
        for yy in (0, 1):
            self.to_core(i, yy).start()

    def pass_on(self, i, turn):
        for yy in (0, 1):
            self.to_core(i, yy).wait_recv()
        away = (1 - self.y) * 2 + self.c
        self.part[i, away] = (
            self.part[i, away].astype(f32) + self.from_core[i, 1 - self.y].astype(f32)
        ).astype(bf16)
        if turn > 0:
            pl.semaphore_wait(self.credits.at[1], 1)
        self.to_y(i).start()

    def take(self, i, turn, use):
        self.to_y(i).wait_recv()
        use(
            self.part[i, self.tp].astype(f32)
            + self.from_core[i, self.y].astype(f32)
            + self.from_y[i].astype(f32)
        )
        if turn < 2:
            for k, peer in ((0, self.over_core), (1, self.over_y)):
                pl.semaphore_signal(
                    self.credits.at[k],
                    inc=1,
                    device_id={"tp": peer},
                    device_id_type=pl.DeviceIdType.MESH,
                )


def col(i, width=256):
    return pl.ds(i * width if isinstance(i, int) else pl.multiple_of(i * width, width), width)


def bwd_kernel(
    lengths, sa_ref, sb_ref, lanes_ref, hm_ref, gains, s_in, den, gain_first, gain_second,
    x_in, x1_in, wq_all, wo_all, wg_all, wu_all, wd_all, c_all, h1_all, qkv_all, yb_all, h2_all,
    gate_all, up_all, m_all,
    d_out, g_out, u_out, oq_out, block_out, input_out, gain_out, u_kept,
    tok_ref, line_ref, coef_ref, terms, terms_core, terms_y,
    slots, s1, s2, wo, stream, hs, rows_all, mm, dup, tiles, qkv, kq, yb, dnum, dden, dden_t, dqkv,
    dq, dk, part, from_core, from_y, acc, x1, fout, st, st_x, st_t, st_z, s_back, own_rows,
    ring_send, ring_recv, tp_sems, credits, send, recv, local, tile_sems,
):
    seq, tp, place, nearby, over_y, over_core, peers = places()
    z, x = seq // 2, seq % 2
    rows, width = own_rows.shape
    total = 4 * rows
    ff = mm.shape[1]
    links = Links(send, recv)
    locs = Sems(local)

    def load(src, dst):
        made = pltpu.make_async_copy(src, dst, locs.take())
        made.start()
        return made

    def whole(everyone, flat):
        count, chunk = everyone.shape[0], everyone.shape[1]
        return [load(everyone.at[j], flat.at[pl.ds(j * chunk, chunk)]) for j in range(count)]

    got_c = load(c_all, rows_all)
    got_m = load(m_all, mm)
    got_wd = whole(wd_all, s2)
    greet(peers)
    got_x1 = load(x1_in, x1)
    fill_tables(lengths, seq, tok_ref, line_ref, coef_ref, -1)
    columns = ring_columns(place)
    got_qkv = [load(qkv_all, qkv), load(yb_all, yb)]
    got_wo = whole(wo_all, wo)
    ring = Scatter(slots, ring_send, ring_recv, nearby)
    sums = TpSum(part, from_core, from_y, tp_sems, credits, tp, over_y, over_core)

    def run(n, body, pumps=None):
        def step(i, _):
            body(i)
            if pumps:
                a, first, count = pumps
                every = n // count
                pl.when((i + 1) % every == 0)(lambda: event(a, first + (i + 1) // every - 1))
            return 0

        lax.fori_loop(0, n, step, 0)

    plan = {0: (s1, ff, 0), 1: (s2, ff, 0), 2: (s1, ff, 0), 3: (s2, 1152, 0)}

    def event(a, e):
        own, wide, column = plan[a]
        ring.event(a, e, own, wide, fout, column)

    def begin(a):
        own, wide, column = plan[a]
        ring.begin(a, own, wide, column)

    def events(a, first, last):
        lax.fori_loop(first, last, lambda e, _: (event(a, e), 0)[1], 0)

    def both(a, first, b, second, count):
        def pair(i, _):
            event(a, first + i)
            event(b, second + i)
            return 0

        lax.fori_loop(0, count, pair, 0)

    def chunks_of(source, size, body, pumps=None, count=8):
        def copies(i, slot):
            return [
                pltpu.make_async_copy(a, b, tile_sems.at[k, slot])
                for k, (a, b) in enumerate(source(i, slot))
            ]

        for made in copies(0, 0):
            made.start()

        def step(i):
            slot = i % 2

            @pl.when(i + 1 < count)
            def _():
                for made in copies(i + 1, 1 - slot):
                    made.start()

            for made in copies(i, slot):
                made.wait()
            body(i, slot)

        run(count, step, pumps)

    got_c.wait()
    got_m.wait()

    def grad_down(j):
        s1[col(j), :] = dot_tt(rows_all[:, col(j)], mm[...]).astype(bf16)

    run(2, grad_down)
    begin(0)
    lax.fori_loop(2, 8, lambda j, _: (grad_down(j), 0)[1], 0)
    for made in got_wd:
        made.wait()
    events(0, 0, 1)

    def mlp(i):
        sums.offer(i, 0, dot_t(mm[...], s2[col(i), :]))
        pl.when(i > 0)(lambda: sums.pass_on(i - 1, 0))

    run(8, mlp, (0, 1, 2))
    sums.pass_on(7, 0)

    def gate_up_tiles(i, slot):
        r = col(i, 128)
        return [
            (gate_all.at[r], tiles.at[slot, pl.ds(0, 128)]),
            (up_all.at[r], tiles.at[slot, pl.ds(128, 128)]),
        ]

    def grad_gate_up(i, slot):
        r = col(i, 128)
        dm = dot(rows_all[r, :], s2[...]).astype(bf16).astype(f32)
        g = tiles[slot, 0:128].astype(f32)
        u = tiles[slot, 128:256].astype(f32)
        s = jax.nn.sigmoid(g)
        mm[r, :] = (dm * u * s * (1.0 + g * (1.0 - s))).astype(bf16)
        dup[r, :] = (dm * (g * s)).astype(bf16)

        pl.when(i >= 3)(lambda: take_block(i - 3))

    def take_block(i):
        def use(value):
            own_rows[:, col(i)] = (x1[:, col(i)] + value).astype(bf16)

        sums.take(i, 0, use)

    got_x1.wait()
    chunks_of(gate_up_tiles, 8, grad_gate_up, (0, 3, 4))

    def w_tiles(i, slot):
        return [(wg_all.at[i], stream.at[slot, 0]), (wu_all.at[i], stream.at[slot, 1])]

    def grad_hidden(i, slot):
        pl.when(i < 3)(lambda: take_block(5 + i))
        value = dot_t(mm[...], stream[slot, 0]) + dot_t(dup[...], stream[slot, 1])
        sums.offer(i, 1, value)
        pl.when(i > 0)(lambda: sums.pass_on(i - 1, 1))

    chunks_of(w_tiles, 8, grad_hidden, (0, 7, 2))
    kept = [load(own_rows.at[:, col(j)], block_out.at[:, c]) for j, c in enumerate(columns)]
    pending = []
    sums.pass_on(7, 1)

    def h_tiles(everyone):
        return lambda i, slot: [(everyone.at[:, col(i)], hs.at[slot])]

    def keep_up(i, slot):
        return pltpu.make_async_copy(tiles.at[slot], u_kept.at[col(i)], tile_sems.at[1, slot])

    def grads(i, slot):
        s2[col(i), :] = dot_tt(hs[slot], mm[...]).astype(bf16)
        pl.when(i >= 2)(lambda: keep_up(i - 2, slot).wait())
        tiles[slot] = dot_tt(hs[slot], dup[...]).astype(bf16)
        keep_up(i, slot).start()
        pl.when(i == 1)(lambda: begin(1))

    chunks_of(h_tiles(h2_all), 8, grads, (0, 9, 2))
    keep_up(6, 0).wait()
    keep_up(7, 1).wait()

    def take_second(i):
        def use(value):
            acc[:, col(i)] = value

        sums.take(i, 1, use)

    events(0, 11, 12)
    run(2, take_second)
    both(1, 0, 0, 12, 2)
    done = load(fout.at[:, pl.ds(0, ff)], d_out)
    got_up = load(u_kept, s1)
    lax.fori_loop(2, 5, lambda i, _: (take_second(i), 0)[1], 0)
    events(1, 2, 3)
    got_up.wait()
    begin(2)
    lax.fori_loop(5, 8, lambda i, _: (take_second(i), 0)[1], 0)
    both(1, 3, 2, 0, 1)

    for made in kept:
        made.wait()

    def norm_back_second(i, _):
        r = pl.ds(pl.multiple_of(i * 32, 32), 32)
        v = x1[r, :]
        s = lax.rsqrt(jnp.mean(v * v, axis=1, keepdims=True) + epsilon)
        n = v * s
        dn = acc[r, :] * gains[1:2, :]
        own = pl.ds(pl.multiple_of(tp * rows + i * 32, 32), 32)
        back = rows_all[own, :].astype(f32) + s * (
            dn - n * jnp.mean(dn * n, axis=1, keepdims=True)
        )
        acc[r, :] = back
        own_rows[r, :] = back.astype(bf16)
        return 0

    lax.fori_loop(0, rows // 32, norm_back_second, 0)
    da = Rows(links, own_rows, rows_all, tp, over_y, over_core, rows)
    own_in = load(own_rows, da.block(tp, 0, rows))

    both(1, 4, 2, 1, 1)
    da.forward(0)
    both(1, 5, 2, 2, 1)
    da.forward(1)
    for made in got_qkv + got_wo:
        made.wait()
    da.finish()
    own_in.wait()
    links.sent_now(da.first + [da.near])
    got_x = [load(x_in.at[:, c], own_rows.at[:, col(j)]) for j, c in enumerate(columns)]

    def head_v(h):
        return slice(128 + h * 128, 256 + h * 128)

    def grad_attended(i):
        r = col(i, 256)
        dy = dot(rows_all[r, :], wo[...])
        kq[r, :] = pltpu.roll(qkv[r, 0:128].astype(f32), 64, 1).astype(bf16)
        columns = []
        for h in range(4):
            hv = slice(h * 128, (h + 1) * 128)
            under = 1.0 / den[r, h : h + 1]
            part_h = dy[:, hv]
            dnum[r, hv] = (part_h * under).astype(bf16)
            low = jnp.sum(part_h * yb[r, hv].astype(f32), axis=1, keepdims=True)
            columns.append(-low * under)
        lane = lax.broadcasted_iota(jnp.int32, (256, 128), 1)
        packed = jnp.zeros((256, 128), f32)
        for h in range(4):
            packed = jnp.where(lane == h, columns[h], packed)
        dden[r, :] = packed
        dden_t[i] = packed.T[0:8, :]

    run(4, grad_attended)
    both(1, 6, 2, 3, 1)

    for h in range(4):

        def state(i, c, h=h):
            s, zz = c
            r = col(i, 256)
            a, b = phi(qkv[r, 0:128], h, sa_ref, sb_ref, lanes_ref)
            f = a * b * lanes_ref[2:3, :] * tok_ref[r, 1:2]
            s = s + dot_tt(f.astype(bf16), dnum[r, h * 128 : (h + 1) * 128])
            return s, zz + jnp.sum(f * dden[r, h : h + 1], axis=0, keepdims=True)

        s, zz = lax.fori_loop(
            0, 4, state, (jnp.zeros((256, 128), f32), jnp.zeros((1, 256), f32))
        )
        pack_state(st, h, s, zz)
    to_x = links.start(st, st_x, seq=seq + 1 - 2 * x)
    both(1, 7, 2, 4, 1)

    dq[...] = jnp.zeros(dq.shape, f32)

    def local_head(h):
        hm = hm_ref[h : h + 1, :]
        hv = slice(h * 128, (h + 1) * 128)
        for j in range(total // 256):
            k_rows = slice(j * 256, (j + 1) * 256)
            dv_s = jnp.zeros((256, 128), f32)
            dk_s = jnp.zeros((256, 128), f32)
            for i in range(j, total // 256):
                q_rows = slice(i * 256, (i + 1) * 256)
                qm = (qkv[q_rows, 0:128].astype(f32) * hm).astype(bf16)
                u = dot_t(kq[k_rows, :], qm)
                keep = tok_ref[k_rows, 3:4] >= line_ref[1:2, q_rows]
                if i == j:
                    keep = keep & (tok_ref[k_rows, 3:4] <= line_ref[0:1, q_rows])
                kap = jnp.where(keep, (0.5 * u + 1.0) * u + 1.0, 0.0).astype(bf16)
                dn = dnum[q_rows, hv]
                grad = dot_t(qkv[k_rows, head_v(h)], dn) + dden_t[i, h : h + 1, :]
                du = jnp.where(keep, grad * (1.0 + u), 0.0).astype(bf16)
                dv_s = dv_s + dot(kap, dn)
                dk_s = dk_s + dot(du, qm)
                dq[q_rows, :] += dot_tt(du, kq[k_rows, :]) * hm
            dqkv[k_rows, head_v(h)] = dv_s.astype(bf16)
            if h == 0:
                dk[k_rows, :] = dk_s
            else:
                dk[k_rows, :] += dk_s

    local_head(0)
    to_x.wait_recv()
    for h in range(4):
        mine, theirs = st[h].astype(f32), st_x[h].astype(f32)
        first = jnp.where(x == 0, mine, theirs)
        second = jnp.where(x == 0, theirs, mine)
        st_t[h] = (first + coef_ref[0:1, :] * second).astype(bf16)
    chain = Chain(links, st_t, st_z, coef_ref, seq, z, -1)
    chain.move(0)
    both(1, 8, 2, 5, 1)
    local_head(1)
    chain.move(1)
    both(1, 9, 2, 6, 1)
    local_head(2)
    chain.move(2)
    both(1, 10, 2, 7, 1)
    local_head(3)
    chain.move(3)
    both(1, 11, 2, 8, 1)
    chain.use(s_back, st_x)

    def split_state(ref, h):
        z_row = jnp.concatenate([ref[h, 160:161, :], ref[h, 161:162, :]], axis=1)
        feat = lax.broadcasted_iota(jnp.int32, (256, 128), 0)
        return jnp.where(feat < FEATS, ref[h], 0.0).astype(bf16), z_row

    for h in range(4):
        s_q, z_q = split_state(s_in, h)
        s_k, z_k = split_state(s_back, h)
        hv = slice(h * 128, (h + 1) * 128)

        def through(grad, a, b, h=h):
            grad = grad * lanes_ref[2:3, :]
            return dot_t((grad * b).astype(bf16), sa_ref[h]) + dot_t(
                (grad * a).astype(bf16), sb_ref[h]
            )

        def carried_part(i, _, h=h, s_q=s_q, z_q=z_q, s_k=s_k, z_k=z_k, hv=hv, through=through):
            r = col(i, 256)
            a, b = phi(qkv[r, 0:128], h, sa_ref, sb_ref, lanes_ref)
            grad = dot_t(dnum[r, hv], s_q) + dden[r, h : h + 1] * z_q
            dq[r, :] += through(grad * tok_ref[r, 1:2], a, b)
            a, b = phi(kq[r, :], h, sa_ref, sb_ref, lanes_ref)
            last = tok_ref[r, 2:3]
            grad = dot_t(qkv[r, head_v(h)], s_k) + z_k
            dk[r, :] += through(grad * last, a, b)
            f = (a * b * lanes_ref[2:3, :] * last).astype(bf16)
            dqkv[r, head_v(h)] = (dqkv[r, head_v(h)].astype(f32) + dot(f, s_k)).astype(bf16)
            return 0

        lax.fori_loop(0, 4, carried_part, 0)

    def join(i):
        r = col(i, 256)
        dqkv[r, 0:128] = (dq[r, :] + pltpu.roll(dk[r, :], 64, 1)).astype(bf16)

    run(4, join)
    done.wait()
    both(1, 12, 2, 9, 2)
    done = load(fout.at[:, pl.ds(0, ff)], g_out)
    own_w = load(wg_all.at[7], stream.at[0, 0])
    own_w.wait()
    gain_two = jnp.sum(fout[:, 0:ff] * stream[0, 0].astype(f32), axis=1, keepdims=True)

    def wq_tiles(i, slot):
        return [(wq_all.at[i], stream.at[slot, 0, :, pl.ds(0, 640)])]

    def grad_hidden_first(i, slot):
        sums.offer(i, 2, dot_t(dqkv[...], stream[slot, 0, :, 0:640]))
        pl.when(i > 0)(lambda: sums.pass_on(i - 1, 2))

    chunks_of(wq_tiles, 8, grad_hidden_first, (2, 11, 1))
    sums.pass_on(7, 2)

    def grad_out_qkv(i, slot):
        s2[col(i), 0:512] = dot_tt(rows_all[:, col(i)], yb[...]).astype(bf16)
        s2[col(i), 512:1152] = dot_tt(hs[slot], dqkv[...]).astype(bf16)

        pl.when(i == 1)(lambda: begin(3))

    chunks_of(h_tiles(h1_all), 8, grad_out_qkv, (3, 0, 1))
    done.wait()
    both(2, 12, 3, 1, 2)
    done = load(fout.at[:, pl.ds(0, ff)], u_out)
    def take_first(i):
        def use(value):
            x1[:, col(i)] = value

        sums.take(i, 2, use)

    run(8, take_first, (3, 3, 4))
    for made in got_x:
        made.wait()

    def norm_back_first(i, _):
        r = pl.ds(pl.multiple_of(i * 32, 32), 32)
        v = own_rows[r, :].astype(f32)
        s = lax.rsqrt(jnp.mean(v * v, axis=1, keepdims=True) + epsilon)
        n = v * s
        dn = x1[r, :] * gains[0:1, :]
        acc[r, :] += s * (dn - n * jnp.mean(dn * n, axis=1, keepdims=True))
        return 0

    lax.fori_loop(0, rows // 32, norm_back_first, 0)
    pending += [load(acc.at[:, col(j)], input_out.at[:, c]) for j, c in enumerate(columns)]
    own_w = load(wu_all.at[7], stream.at[0, 0])
    own_q = load(wq_all.at[7], stream.at[1, 0, :, pl.ds(0, 640)])
    own_w.wait()
    own_q.wait()
    gain_two += jnp.sum(fout[:, 0:ff] * stream[0, 0].astype(f32), axis=1, keepdims=True)
    events(3, 7, 12)
    done.wait()
    events(3, 12, 14)
    pending.append(load(fout.at[:, pl.ds(0, 1152)], oq_out))
    gain_one = jnp.sum(fout[:, 512:1152] * stream[1, 0, :, 0:640].astype(f32), axis=1, keepdims=True)
    lane = lax.broadcasted_iota(jnp.int32, (256, 128), 1)
    both = jnp.where(lane == 0, gain_one, jnp.where(lane == 1, gain_two, 0.0)).T[0:8, :]
    terms[0] = both
    over = links.start(terms.at[0], terms_core, tp=over_core)
    over.wait_recv()
    both = both + terms_core[...]
    terms[1] = both
    over = links.start(terms.at[1], terms_y, tp=over_y)
    over.wait_recv()
    own_gains = jnp.concatenate(
        [gain_first[...], gain_second[...], jnp.ones((6, 256), f32)], axis=0
    ).astype(bf16)
    terms[2] = (both + terms_y[...]) / own_gains.astype(f32)
    pending.append(load(terms.at[2], gain_out))
    run(8, lambda i: sums.sent(i))
    for made in pending:
        made.wait()
    links.finish()
    chain.finish()


def feature_tables(heads):
    first = np.zeros((heads, 128, 256), np.float32)
    second = np.zeros((heads, 128, 256), np.float32)
    lanes = np.zeros((8, 256), np.float32)
    f = 0
    for i in range(FEAT):
        for j in range(i, FEAT):
            for h in range(heads):
                first[h, h * FEAT + i, f] = 1
                second[h, h * FEAT + j, f] = 1
            lanes[2, f] = square_coef if i == j else square_coef * 2**0.5
            f += 1
    for i in range(FEAT):
        for h in range(heads):
            first[h, h * FEAT + i, f] = 1
        lanes[1, f] = 1
        lanes[2, f] = linear_coef
        f += 1
    lanes[0, f] = lanes[1, f] = lanes[2, f] = 1
    mask = np.zeros((8, 128), np.float32)
    for h in range(heads):
        mask[h, h * FEAT : (h + 1) * FEAT] = 0.25
    return first, second, lanes, mask


def forward_pass(lengths, constants, gain_first, gain_second, x_in, weights, c_in):
    rows, width = x_in.shape
    total = 4 * rows
    ff = weights[4].shape[0]
    hbm = pl.BlockSpec(memory_space=pl.ANY)
    vmem = pl.BlockSpec(memory_space=pltpu.VMEM)

    def shape(*dims, dtype=bf16):
        return jax.ShapeDtypeStruct(dims, dtype)

    outs = (
        shape(8, 256, 640),
        shape(8, 256, 512),
        shape(8, 256, ff),
        shape(8, 256, ff),
        shape(8, 256, ff),
        shape(total, width),
        shape(total, width),
        shape(total, 640),
        shape(total, 512),
        shape(total, 128, dtype=f32),
        shape(rows, width, dtype=f32),
        shape(total, width),
        shape(total, ff),
        shape(total, ff),
        shape(total, ff),
        shape(4, 256, 128, dtype=f32),
        shape(8, width, dtype=f32),
    )
    scratch = [
        pltpu.VMEM((rows, width), bf16),
        pltpu.VMEM((total, 128), f32),
        pltpu.VMEM((8, total), f32),
        pltpu.VMEM((8, 128), f32),
        pltpu.VMEM((16, 256), bf16),
        pltpu.VMEM((256, 640), bf16),
        pltpu.VMEM((256, 512), bf16),
        pltpu.VMEM((256, ff), bf16),
        pltpu.VMEM((256, ff), bf16),
        pltpu.VMEM((256, ff), bf16),
        pltpu.VMEM((128, 256), f32),
        pltpu.VMEM((256, 512), f32),
        pltpu.VMEM((512, 256), f32),
        pltpu.VMEM((-(-ff // 128) * 128, 256), f32),
        pltpu.VMEM((-(-ff // 128) * 128, 256), f32),
        pltpu.VMEM((total, width), bf16),
        pltpu.VMEM((total, width), bf16),
        pltpu.VMEM((width, 640), bf16),
        pltpu.VMEM((width, 512), bf16),
        pltpu.VMEM((width, ff), bf16),
        pltpu.VMEM((width, ff), bf16),
        pltpu.VMEM((total, 640), bf16),
        pltpu.VMEM((total, 128), bf16),
        pltpu.VMEM((total, 512), f32),
        pltpu.VMEM((total, 128), f32),
        pltpu.VMEM((total, 512), bf16),
        pltpu.VMEM((2, rows, width), bf16),
        pltpu.VMEM((2, rows, width), bf16),
        pltpu.VMEM((rows, width), bf16),
        pltpu.VMEM((rows, width), bf16),
        pltpu.VMEM((rows, width), f32),
        pltpu.VMEM((total, ff), bf16),
        pltpu.VMEM((total, ff), bf16),
        pltpu.VMEM((total, ff), bf16),
        pltpu.VMEM((8, 16, 256), bf16),
        pltpu.VMEM((8, width), f32),
        pltpu.VMEM((4, 176, 128), bf16),
        pltpu.VMEM((4, 176, 128), bf16),
        pltpu.VMEM((4, 176, 128), bf16),
        pltpu.VMEM((4, 176, 128), bf16),
        pltpu.VMEM((4, 256, 128), f32),
        pltpu.SemaphoreType.DMA((112,)),
        pltpu.SemaphoreType.DMA((112,)),
        pltpu.SemaphoreType.DMA((112,)),
    ]
    return pl.pallas_call(
        fwd_kernel,
        out_shape=outs,
        in_specs=[pl.BlockSpec(memory_space=pltpu.SMEM)] + [vmem] * 6 + [hbm] * 9,
        out_specs=(hbm,) * len(outs),
        scratch_shapes=scratch,
        compiler_params=pltpu.CompilerParams(
            collective_id=0, has_side_effects=True, vmem_limit_bytes=60 * 2**20
        ),
    )(lengths, *constants, gain_first, gain_second, x_in, *weights, c_in)


def backward_pass(lengths, constants, gains, s_in, den, gain_pair, x_in, x1, weights, c_all, acts):
    rows, width = x_in.shape
    total = 4 * rows
    ff = weights[2].shape[2]
    hbm = pl.BlockSpec(memory_space=pl.ANY)
    vmem = pl.BlockSpec(memory_space=pltpu.VMEM)

    def shape(*dims, dtype=f32):
        return jax.ShapeDtypeStruct(dims, dtype)

    outs = (
        shape(256, ff),
        shape(256, ff),
        shape(256, ff),
        shape(256, 1152),
        shape(rows, width, dtype=bf16),
        shape(rows, width),
        shape(8, 256),
        shape(width, ff, dtype=bf16),
    )
    scratch = [
        pltpu.VMEM((total, 128), f32),
        pltpu.VMEM((8, total), f32),
        pltpu.VMEM((8, 128), f32),
        pltpu.VMEM((3, 8, 256), f32),
        pltpu.VMEM((8, 256), f32),
        pltpu.VMEM((8, 256), f32),
        pltpu.VMEM((8, 256, ff), bf16),
        pltpu.VMEM((width, ff), bf16),
        pltpu.VMEM((width, ff), bf16),
        pltpu.VMEM((width, 512), bf16),
        pltpu.VMEM((2, 2, 256, ff), bf16),
        pltpu.VMEM((2, total, 256), bf16),
        pltpu.VMEM((total, width), bf16),
        pltpu.VMEM((total, ff), bf16),
        pltpu.VMEM((total, ff), bf16),
        pltpu.VMEM((2, 256, ff), bf16),
        pltpu.VMEM((total, 640), bf16),
        pltpu.VMEM((total, 128), bf16),
        pltpu.VMEM((total, 512), bf16),
        pltpu.VMEM((total, 512), bf16),
        pltpu.VMEM((total, 128), f32),
        pltpu.VMEM((4, 8, 256), f32),
        pltpu.VMEM((total, 640), bf16),
        pltpu.VMEM((total, 128), f32),
        pltpu.VMEM((total, 128), f32),
        pltpu.VMEM((8, 4, 256, 256), bf16),
        pltpu.VMEM((8, 2, 256, 256), bf16),
        pltpu.VMEM((8, 256, 256), bf16),
        pltpu.VMEM((rows, width), f32),
        pltpu.VMEM((rows, width), f32),
        pltpu.VMEM((256, ff), f32),
        pltpu.VMEM((4, 176, 128), bf16),
        pltpu.VMEM((4, 176, 128), bf16),
        pltpu.VMEM((4, 176, 128), bf16),
        pltpu.VMEM((4, 176, 128), bf16),
        pltpu.VMEM((4, 256, 128), f32),
        pltpu.VMEM((rows, width), bf16),
        pltpu.SemaphoreType.DMA((2, 2, 2)),
        pltpu.SemaphoreType.DMA((2, 2, 2, 7)),
        pltpu.SemaphoreType.DMA((6, 8)),
        pltpu.SemaphoreType.REGULAR((2,)),
        pltpu.SemaphoreType.DMA((16,)),
        pltpu.SemaphoreType.DMA((16,)),
        pltpu.SemaphoreType.DMA((80,)),
        pltpu.SemaphoreType.DMA((2, 2)),
    ]
    return pl.pallas_call(
        bwd_kernel,
        out_shape=outs,
        in_specs=[pl.BlockSpec(memory_space=pltpu.SMEM)] + [vmem] * 9 + [hbm] * 15,
        out_specs=(hbm,) * len(outs),
        scratch_shapes=scratch,
        compiler_params=pltpu.CompilerParams(
            collective_id=1, has_side_effects=True, vmem_limit_bytes=62 * 2**20
        ),
    )(lengths, *constants, gains, s_in, den, *gain_pair, x_in, x1, *weights, c_all, *acts)


def on_device_rings(
    inputs, lengths, gain_attn, w_query, w_key, w_value, w_out, gain_mlp, w_gate, w_up, w_down,
    cotangent,
):
    first, second, lanes, mask = feature_tables(4)
    constants = (
        jnp.asarray(first, bf16), jnp.asarray(second, bf16), jnp.asarray(lanes), jnp.asarray(mask),
    )
    gain_pair = (gain_attn.reshape(1, -1), gain_mlp.reshape(1, -1))
    made = forward_pass(
        lengths, constants, *gain_pair, inputs,
        (w_query.T, w_key.T, w_value, w_out, w_gate.T, w_up.T, w_down), cotangent,
    )
    weights, (c_all, h1, qkv, yb, den, x1, h2, gate, up, mixed, s_in, gain_all) = made[:5], made[5:]
    sum_down_t, sum_gate, sum_up, sum_oq, block, grad_input, gain_sums, _ = backward_pass(
        lengths, constants, gain_all, s_in, den, gain_pair, inputs, x1, weights, c_all,
        (h1, qkv, yb, h2, gate, up, mixed),
    )
    return (
        block,
        grad_input,
        gain_sums[0],
        sum_oq[:, 512:576],
        sum_oq[:, 576:640],
        sum_oq[:, 640:],
        sum_oq[:, :512].T,
        gain_sums[1],
        sum_gate,
        sum_up,
        sum_down_t.T,
    )


def on_device(
    inputs,
    lengths,
    gain_attn,
    w_query,
    w_key,
    w_value,
    w_out,
    gain_mlp,
    w_gate,
    w_up,
    w_down,
    cotangent,
):
    seq_count = lax.axis_size("seq")
    tp_count = lax.axis_size("tp")
    seq_index = lax.axis_index("seq")
    rows_own, width = inputs.shape
    chunk = width // seq_count
    half = chunk // 2
    block_len = rows_own * tp_count
    anchor = seq_index * block_len
    relative = relative_list(seq_count)
    ring = ring_order(seq_count)
    place_of = [ring.index(s) for s in range(seq_count)]
    to_rel = jnp.array(
        [[ring[(place_of[s] - k) % seq_count] for k in relative] for s in range(seq_count)],
        jnp.int32,
    )[seq_index]
    to_abs = jnp.array(
        [
            [relative.index((place_of[s] - place_of[o]) % seq_count) for o in range(seq_count)]
            for s in range(seq_count)
        ],
        jnp.int32,
    )[seq_index]
    to_rel = [to_rel[j] for j in range(seq_count)]
    to_abs = [to_abs[j] for j in range(seq_count)]

    qk_cols, v_cols, ff_cols = w_query.shape[1], w_value.shape[1], w_gate.shape[1]
    gains = jnp.stack([gain_attn, gain_mlp]).astype(bf16)
    qkv_cols = 2 * qk_cols + v_cols
    qkv_own = jnp.concatenate([w_query, w_key, w_value], axis=1).astype(bf16)
    gain_rows = jnp.zeros((16, qkv_cols), bf16).at[:2, :chunk].set(gains)
    first_own = jnp.concatenate([qkv_own, gain_rows], axis=0)
    out_own = w_out.astype(bf16).T
    gate_up_own = jnp.concatenate([w_gate, w_up], axis=1).astype(bf16)
    down_own = w_down.astype(bf16).T

    first_got = ring_gather(first_own, half)
    out_got = ring_gather(out_own, half)
    gate_up_got = ring_gather(gate_up_own, half)
    down_got = ring_gather(down_own, half)
    w_qkv = jnp.concatenate([first_got[k][:chunk] for k in relative], axis=0)
    gain_first = jnp.concatenate([first_got[k][chunk, :chunk] for k in relative]).astype(f32)
    gain_second = jnp.concatenate([first_got[k][chunk + 1, :chunk] for k in relative]).astype(f32)
    w_out_t = jnp.concatenate([out_got[k] for k in relative], axis=0)
    w_gate_up = jnp.concatenate([gate_up_got[k] for k in relative], axis=0)
    w_down_t = jnp.concatenate([down_got[k] for k in relative], axis=0)

    at = jnp.arange(lengths.shape[0])
    starts = jnp.sum(jnp.where(at[None, :] < at[:, None], lengths[None, :], 0), axis=1)
    positions, row_ids, carry_in, after_last = segment_masks(anchor, starts, block_len)
    carry_mask = carry_in.astype(f32)
    last_mask = after_last.astype(f32)
    resets = (
        jnp.sum(
            ((starts // block_len)[None, :] == jnp.arange(seq_count)[:, None]).astype(jnp.int32),
            axis=1,
        )
        > 0
    ).astype(jnp.int32)

    inputs_own = to_relative(inputs, to_rel, chunk)
    grad_own = to_relative(cotangent, to_rel, chunk)
    inputs_full = tp_gather(inputs_own).astype(f32)
    grad_full = tp_gather(grad_own)
    inputs_own = inputs_own.astype(f32)
    hidden_first = (inputs_full * rms_scale(inputs_full) * gain_first).astype(bf16)
    qkv = dot(hidden_first, w_qkv).astype(bf16)
    queries = qkv[:, :qk_cols]
    key_flat = qkv[:, qk_cols : 2 * qk_cols]
    value_flat = qkv[:, 2 * qk_cols :]
    heads_local = qk_cols // FEAT
    query_heads = queries.reshape(block_len, heads_local, FEAT)
    key_heads = key_flat.reshape(block_len, heads_local, FEAT)
    value_heads = value_flat.reshape(block_len, heads_local, VHEAD)
    query_float = query_heads.astype(f32)
    key_float = key_heads.astype(f32)
    value_float = value_heads.astype(f32)
    key_feat = features(key_float) * last_mask[:, None, None]
    local_state = jnp.einsum("thn,thv->hnv", key_feat, value_float, precision=highest)
    local_sum = jnp.sum(key_feat, axis=0)
    carry_state, carry_sum = carried([local_state, local_sum], resets, 1)
    step_rows = 512
    query_feat = features(query_float)
    carry_weight = carry_mask[:, None]
    numer_parts = []
    denom_parts = []
    for first_row in range(0, block_len, step_rows):
        query_part = query_heads[first_row : first_row + step_rows]
        scores, allowed, kernel = pair_block(
            query_part, key_heads, row_ids, positions, first_row, step_rows
        )
        numer_parts.append(
            jnp.einsum("hts,shv->thv", kernel.astype(bf16), value_heads, preferred_element_type=f32)
        )
        denom_parts.append(jnp.sum(kernel, axis=-1).T)
    numerator = (
        jnp.concatenate(numer_parts, axis=0)
        + jnp.einsum("thn,hnv->thv", query_feat, carry_state, precision=highest)
        * carry_weight[:, :, None]
    )
    denominator = (
        jnp.concatenate(denom_parts, axis=0)
        + jnp.einsum("thn,hn->th", query_feat, carry_sum, precision=highest) * carry_weight
    )
    attended = numerator / denominator[:, :, None]
    attended_low = attended.reshape(block_len, heads_local * VHEAD).astype(bf16)
    attn_partial = dot_t(attended_low, w_out_t).astype(bf16)
    middle_own = inputs_own + tp_scatter(attn_partial)
    scale_second = rms_scale(middle_own)
    normed_second = middle_own * scale_second
    hidden_second = tp_gather((normed_second * gain_second).astype(bf16))
    gate_up = dot(hidden_second, w_gate_up)
    gate_value, upward = gate_up[:, :ff_cols], gate_up[:, ff_cols:]
    sigmoid_gate = jax.nn.sigmoid(gate_value)
    silu_gate = gate_value * sigmoid_gate
    mixed_rows = (silu_gate * upward).astype(bf16)
    grad_down_t = dot_tt(grad_full, mixed_rows).astype(bf16)

    def by_distance(stack):
        return {k: stack[j * chunk : (j + 1) * chunk] for j, k in enumerate(relative)}

    sum_down_t = ring_scatter(by_distance(grad_down_t))
    mlp_own = tp_scatter(dot_t(mixed_rows, w_down_t).astype(bf16))
    block_output = to_relative((middle_own + mlp_own).astype(bf16), to_abs, chunk)

    grad_mixed = dot(grad_full, w_down_t).astype(bf16).astype(f32)
    grad_gate = (
        grad_mixed * upward * sigmoid_gate * (1.0 + gate_value * (1.0 - sigmoid_gate))
    ).astype(bf16)
    grad_upward = (grad_mixed * silu_gate).astype(bf16)
    grad_gate_up = jnp.concatenate([grad_gate, grad_upward], axis=1)
    hidden_partial = dot_t(grad_gate_up, w_gate_up).astype(bf16)
    sum_gate_up = ring_scatter(by_distance(dot_tt(hidden_second, grad_gate_up).astype(bf16)))
    grad_hidden = tp_scatter(hidden_partial)
    grad_middle = grad_own.astype(f32) + norm_back(
        grad_hidden, normed_second, scale_second, gain_second
    )
    grad_branch = tp_gather(grad_middle.astype(bf16))
    sum_out_t = ring_scatter(by_distance(dot_tt(grad_branch, attended_low).astype(bf16)))
    grad_attended = dot(grad_branch, w_out_t).reshape(block_len, heads_local, VHEAD)
    grad_numer = (grad_attended / denominator[:, :, None]).astype(bf16)
    grad_denom = -jnp.sum(grad_attended * attended, axis=-1) / denominator
    grad_numer_carried = grad_numer.astype(f32) * carry_weight[:, :, None]
    grad_denom_carried = grad_denom * carry_weight
    grad_state_in = jnp.einsum("thn,thv->hnv", query_feat, grad_numer_carried, precision=highest)
    grad_sum_in = jnp.einsum("thn,th->hn", query_feat, grad_denom_carried, precision=highest)
    grad_query_feat = (
        jnp.einsum("thv,hnv->thn", grad_numer_carried, carry_state, precision=highest)
        + grad_denom_carried[:, :, None] * carry_sum[None]
    )
    grad_state_out, grad_sum_out = carried([grad_state_in, grad_sum_in], resets, -1)
    grad_key_feat = (
        jnp.einsum("thv,hnv->thn", value_float, grad_state_out, precision=highest)
        + grad_sum_out[None]
    ) * last_mask[:, None, None]
    grad_value_state = jnp.einsum("thn,hnv->thv", key_feat, grad_state_out, precision=highest)
    grad_query_parts = []
    grad_key_inner = jnp.zeros((block_len, heads_local, FEAT), f32)
    grad_value_inner = jnp.zeros((block_len, heads_local, VHEAD), f32)
    for first_row in range(0, block_len, step_rows):
        query_part = query_heads[first_row : first_row + step_rows]
        scores, allowed, kernel = pair_block(
            query_part, key_heads, row_ids, positions, first_row, step_rows
        )
        numer_grad_part = grad_numer[first_row : first_row + step_rows]
        grad_weights = jnp.einsum(
            "thv,shv->hts", numer_grad_part, value_heads, preferred_element_type=f32
        )
        grad_scores = (
            (grad_weights + grad_denom[first_row : first_row + step_rows].T[:, :, None])
            * allowed[None]
            * (1.0 + scores)
        ).astype(bf16)
        grad_query_parts.append(
            jnp.einsum("hts,shf->thf", grad_scores, key_heads, preferred_element_type=f32) * 0.25
        )
        grad_key_inner = (
            grad_key_inner
            + jnp.einsum("hts,thf->shf", grad_scores, query_part, preferred_element_type=f32) * 0.25
        )
        grad_value_inner = grad_value_inner + jnp.einsum(
            "hts,thv->shv", kernel.astype(bf16), numer_grad_part, preferred_element_type=f32
        )
    grad_query = (
        jnp.concatenate(grad_query_parts, axis=0) + feature_grad(query_float, grad_query_feat)
    ).astype(bf16)
    grad_key = (grad_key_inner + feature_grad(key_float, grad_key_feat)).astype(bf16)
    grad_value = (grad_value_inner + grad_value_state).astype(bf16)
    grad_qkv = jnp.concatenate(
        [
            grad_query.reshape(block_len, heads_local * FEAT),
            grad_key.reshape(block_len, heads_local * FEAT),
            grad_value.reshape(block_len, heads_local * VHEAD),
        ],
        axis=1,
    )
    sum_qkv = ring_scatter(by_distance(dot_tt(hidden_first, grad_qkv).astype(bf16)))
    grad_hidden_first = tp_scatter(dot_t(grad_qkv, w_qkv).astype(bf16))
    scale_first = rms_scale(inputs_own)
    normed_first = inputs_own * scale_first
    grad_input = to_relative(
        grad_middle + norm_back(grad_hidden_first, normed_first, scale_first, gain_first),
        to_abs,
        chunk,
    )

    gain_terms = jnp.stack(
        [
            jnp.sum(qkv_own.astype(f32) * sum_qkv, axis=1),
            jnp.sum(gate_up_own.astype(f32) * sum_gate_up, axis=1),
        ]
    )
    gain_sums = tp_sum(gain_terms) / gains.astype(f32)
    return (
        block_output,
        grad_input,
        gain_sums[0],
        sum_qkv[:, :qk_cols],
        sum_qkv[:, qk_cols : 2 * qk_cols],
        sum_qkv[:, 2 * qk_cols :],
        sum_out_t.T,
        gain_sums[1],
        sum_gate_up[:, :ff_cols],
        sum_gate_up[:, ff_cols:],
        sum_down_t.T,
    )


def solution(mesh):
    in_specs = (
        P(("seq", "tp"), None),
        P(),
        P("seq"),
        P("seq", "tp"),
        P("seq", "tp"),
        P("seq", "tp"),
        P("tp", "seq"),
        P("seq"),
        P("seq", "tp"),
        P("seq", "tp"),
        P("tp", "seq"),
        P(("seq", "tp"), None),
    )
    out_specs = (
        P(("seq", "tp"), None),
        P(("seq", "tp"), None),
        P("seq"),
        P("seq", "tp"),
        P("seq", "tp"),
        P("seq", "tp"),
        P("tp", "seq"),
        P("seq"),
        P("seq", "tp"),
        P("seq", "tp"),
        P("tp", "seq"),
    )
    small = mesh.shape["seq"] == 8 and mesh.shape["tp"] == 4
    body = on_device_rings if small else on_device
    return jax.shard_map(
        body, mesh=mesh, in_specs=in_specs, out_specs=out_specs, check_vma=False
    )
```

```python
import jax
import jax.numpy as jnp
import numpy as np
from jax import lax
from jax.experimental import pallas as pl
from jax.experimental.pallas import tpu as pltpu
from jax.sharding import PartitionSpec as P

FEAT = 16
VHEAD = 128


epsilon = 1e-05
linear_coef = 0.5
square_coef = 0.17677669529663687
highest = lax.Precision.HIGHEST
f32 = jnp.float32
bf16 = jnp.bfloat16


def ring_order(count):
    planes = 4 if count % 4 == 0 else 2
    columns = count // planes
    order = [z * columns for z in range(planes)]
    for z in reversed(range(planes)):
        xs = list(range(1, columns))
        if (planes - 1 - z) % 2:
            xs.reverse()
        order += [z * columns + x for x in xs]
    return order


def relative_list(count):
    half = count // 2
    out = []
    for j in range(1, half):
        out += [j, count - j]
    return out + [half, 0]


def ring_perms(count):
    ring = ring_order(count)
    fwd = [(ring[i], ring[(i + 1) % count]) for i in range(count)]
    return fwd, [(b, a) for a, b in fwd]


def ring_gather(own, half_rows):
    count = lax.axis_size("seq")
    fwd, bwd = ring_perms(count)
    half = count // 2
    got = {0: own}
    ahead = back = own
    for step in range(1, half):
        ahead = lax.ppermute(ahead, "seq", fwd)
        back = lax.ppermute(back, "seq", bwd)
        got[step] = ahead
        got[count - step] = back
    ahead = lax.ppermute(ahead[:half_rows], "seq", fwd)
    back = lax.ppermute(back[half_rows:], "seq", bwd)
    got[half] = jnp.concatenate([ahead, back], axis=0)
    return got


def ring_scatter(chunks):
    count = lax.axis_size("seq")
    fwd, bwd = ring_perms(count)
    half = chunks[0].shape[0] // 2
    ahead = chunks[1][:half]
    back = chunks[count - 1][half:]
    for step in range(count - 1):
        ahead = lax.ppermute(ahead, "seq", fwd).astype(f32)
        back = lax.ppermute(back, "seq", bwd).astype(f32)
        last = step == count - 2
        ahead = ahead + chunks[0 if last else 2 + step][:half].astype(f32)
        back = back + chunks[0 if last else count - 2 - step][half:].astype(f32)
        if not last:
            ahead = ahead.astype(bf16)
            back = back.astype(bf16)
    return jnp.concatenate([ahead, back], axis=0)


def to_relative(array, index_row, chunk):
    return jnp.concatenate(
        [lax.dynamic_slice_in_dim(array, i * chunk, chunk, 1) for i in index_row], axis=1
    )


def tp_perms(count):
    ys = count // 2
    core = [(i, i ^ 1) for i in range(count)]
    shift = [
        [(i, (((i // 2) + d) % ys) * 2 + i % 2) for i in range(count)] for d in range(ys)
    ]
    return core, shift


def tp_gather(own):
    count = lax.axis_size("tp")
    ys = count // 2
    place = lax.axis_index("tp")
    y, c = place // 2, place % 2
    core, shift = tp_perms(count)
    parts = [own] + [lax.ppermute(own, "tp", shift[d]) for d in range(1, ys)]
    mine = jnp.stack([lax.select_n((y - at + ys) % ys, *parts) for at in range(ys)])
    other = lax.ppermute(mine, "tp", core)
    full = jnp.stack([jnp.where(c == 0, mine, other), jnp.where(c == 0, other, mine)], axis=1)
    return full.reshape((count * own.shape[0],) + own.shape[1:])


def tp_scatter(partial):
    count = lax.axis_size("tp")
    ys = count // 2
    place = lax.axis_index("tp")
    y, c = place // 2, place % 2
    core, shift = tp_perms(count)
    blocks = partial.reshape((ys, 2, partial.shape[0] // count) + partial.shape[1:])
    sent = lax.dynamic_index_in_dim(blocks, 1 - c, 1, False)
    kept = lax.dynamic_index_in_dim(blocks, c, 1, False)
    pair = kept.astype(f32) + lax.ppermute(sent, "tp", core).astype(f32)
    low = pair.astype(bf16)
    own = lax.dynamic_index_in_dim(pair, y, 0, False)
    for d in range(1, ys):
        away = lax.dynamic_index_in_dim(low, (y + d) % ys, 0, False)
        own = own + lax.ppermute(away, "tp", shift[d]).astype(f32)
    return own


def tp_sum(vector):
    count = lax.axis_size("tp")
    core, shift = tp_perms(count)
    vector = vector + lax.ppermute(vector, "tp", core)
    return vector + sum(lax.ppermute(vector, "tp", shift[d]) for d in range(1, count // 2))


def carried(arrays, resets, step):
    count = lax.axis_size("seq")
    place = lax.axis_index("seq")

    def from_near(a, d):
        perm = [(i, i + d * step) for i in range(count) if 0 <= i + d * step < count]
        return lax.ppermute(a.astype(bf16), "seq", perm).astype(f32)

    def reset_within(d):
        at = jnp.arange(count)
        away = (place - at) * step
        return jnp.sum(jnp.where((away >= 1) & (away <= d), resets, 0)) > 0

    arrays = [from_near(a, 1) for a in arrays]
    d = 1
    while d < count - 1:
        keep = 1.0 - reset_within(d).astype(f32)
        arrays = [a + keep * from_near(a, d) for a in arrays]
        d *= 2
    return arrays


def features(vector):
    squares = (vector[..., :, None] * vector[..., None, :]).reshape(
        vector.shape[:-1] + (vector.shape[-1] * vector.shape[-1],)
    )
    return jnp.concatenate(
        [jnp.ones_like(vector[..., :1]), vector * linear_coef, squares * square_coef], axis=-1
    )


def feature_grad(vector, grad_feat):
    feat_width = vector.shape[-1]
    linear_part = grad_feat[..., 1 : 1 + feat_width]
    square_part = grad_feat[..., 1 + feat_width :].reshape(vector.shape + (feat_width,))
    mixed_part = jnp.sum(square_part * vector[..., None, :], axis=-1) + jnp.sum(
        square_part * vector[..., :, None], axis=-2
    )
    return linear_coef * linear_part + square_coef * mixed_part


def segment_masks(anchor, starts, length):
    positions = anchor + jnp.arange(length, dtype=jnp.int32)
    start_le = starts[None, :] <= positions[:, None]
    row_ids = jnp.sum(start_le.astype(jnp.int32), axis=1)
    inside = (starts >= anchor) & (starts < anchor + length)
    carry = jnp.sum(((starts[None, :] >= anchor) & start_le).astype(jnp.int32), axis=1) == 0
    after_last = (
        jnp.sum(
            ((starts[None, :] > positions[:, None]) & inside[None, :]).astype(jnp.int32), axis=1
        )
        == 0
    )
    return (positions, row_ids, carry, after_last)


def rms_scale(values):
    return lax.rsqrt(jnp.mean(values * values, axis=-1, keepdims=True) + epsilon)


def norm_back(grad_out, normed, scale, gain):
    grad_normed = grad_out * gain
    return scale * (grad_normed - normed * jnp.mean(grad_normed * normed, axis=-1, keepdims=True))


def pair_block(query_part, key_heads, row_ids, positions, first_row, span_rows):
    scores = (
        jnp.einsum("thf,shf->hts", query_part, key_heads, preferred_element_type=f32) * 0.25
    )
    rows_here = row_ids[first_row : first_row + span_rows]
    place_here = positions[first_row : first_row + span_rows]
    allowed = (
        (rows_here[:, None] == row_ids[None, :]) & (positions[None, :] <= place_here[:, None])
    ).astype(f32)
    kernel = (1.0 + scores + 0.5 * scores * scores) * allowed[None]
    return (scores, allowed, kernel)


def dot(a, b):
    return jnp.dot(a, b, preferred_element_type=f32)


def dot_t(a, b):
    return lax.dot_general(a, b, (((1,), (1,)), ((), ())), preferred_element_type=f32)


def dot_tt(a, b):
    return lax.dot_general(a, b, (((0,), (0,)), ((), ())), preferred_element_type=f32)


def ring_place(seq):
    z, x = seq // 2, seq % 2
    return z + x * (7 - 2 * z)


def ring_seq(place):
    place = lax.rem(place + 8, 8)
    far = place // 4
    return (1 - far) * 2 * place + far * (15 - 2 * place)


class Sems:
    def __init__(self, ref):
        self.ref, self.used = ref, 0

    def take(self):
        self.used += 1
        return self.ref.at[self.used - 1]


class Links:
    def __init__(self, send, recv):
        self.send, self.recv, self.sent = Sems(send), Sems(recv), []

    def copy(self, src, dst, **to):
        return pltpu.make_async_remote_copy(
            src_ref=src,
            dst_ref=dst,
            send_sem=self.send.take(),
            recv_sem=self.recv.take(),
            device_id=to,
            device_id_type=pl.DeviceIdType.MESH,
        )

    def start(self, src, dst, **to):
        made = self.copy(src, dst, **to)
        made.start()
        self.sent.append(made)
        return made

    def sent_now(self, some):
        for made in some:
            made.wait_send()
        self.sent = [made for made in self.sent if all(made is not other for other in some)]

    def finish(self):
        for made in self.sent:
            made.wait_send()


class Gather:
    def __init__(self, links, arrays, split, nearby, gangs):
        self.links, self.arrays, self.split, self.nearby = links, arrays, split, nearby
        self.at = {k: j for j, k in enumerate(relative_list(8))}
        self.flying, self.gangs, self.done = {}, gangs, 0
        self.gang_of = {a: i for i, gang in enumerate(gangs) for a in gang}
        self.events = [
            (a, step, way, part)
            for gang in gangs
            for step in (1, 2, 3, 4)
            for a in gang
            for part in (0, 1)
            for way in (0, 1)
            if step < 4 or way == part
        ]
        for a in gangs[0]:
            for part in (0, 1):
                for way in (0, 1):
                    self.go(a, 1, way, part)

    def rows(self, part):
        return pl.ds(part * self.split, self.split)

    def go(self, a, step, way, part):
        own, everyone = self.arrays[a]
        before, after = (step - 1, step) if way == 0 else ((9 - step) % 8, 8 - step)
        src = own if step == 1 else everyone.at[self.at[before]]
        self.flying[a, step, way, part] = self.links.start(
            src.at[self.rows(part)],
            everyone.at[self.at[after], self.rows(part)],
            seq=self.nearby[way],
        )

    def pump(self, upto):
        while self.done < min(upto, len(self.events)):
            a, step, way, part = self.events[self.done]
            self.flying[a, step, way, part].wait_recv()
            if step < 3 or (step == 3 and way == part):
                self.go(a, step + 1, way, part)
            i = self.gang_of[a]
            if step == 3 and i + 1 < len(self.gangs):
                mine, later = self.gangs[i].index(a), self.gangs[i + 1]
                if i == 0:
                    later = later + self.gangs[2]
                elif i == 1:
                    later = []
                last = mine == len(self.gangs[i]) - 1
                for other in later[mine:] if last else later[mine : mine + 1]:
                    self.go(other, 1, way, part)
            self.done += 1

    def pump_array(self, a):
        gang = self.gang_of[a]
        self.pump(14 * sum(len(g) for g in self.gangs[: gang + 1]))


def greet(peers):
    barrier = pltpu.get_barrier_semaphore()
    for peer in peers:
        pl.semaphore_signal(
            barrier, inc=1, device_id=peer, device_id_type=pl.DeviceIdType.MESH
        )
    pl.semaphore_wait(barrier, len(peers))


def places():
    seq, tp = lax.axis_index("seq"), lax.axis_index("tp")
    place = ring_place(seq)
    nearby = (ring_seq(place + 1), ring_seq(place - 1))
    over_y = lax.rem(tp + 2, 4)
    over_core = tp + 1 - 2 * (tp % 2)
    peers = [{"seq": ring_seq(place + k)} for k in range(1, 8)]
    peers += [{"tp": over_y}, {"tp": over_core}]
    return seq, tp, place, nearby, over_y, over_core, peers


class Rows:
    def __init__(self, links, own, everyone, tp, over_y, over_core, rows):
        self.links, self.all, self.tp = links, everyone, tp
        self.over_y, self.over_core, self.rows = over_y, over_core, rows
        half = rows // 2
        self.first = [
            links.start(
                own.at[pl.ds(i * half, half)], self.block(tp, i * half, half), tp=over_y
            )
            for i in (0, 1)
        ]
        self.near = links.start(own, self.block(tp, 0, rows), tp=over_core)
        self.last = []

    def block(self, owner, offset, size):
        return self.all.at[pl.ds(pl.multiple_of(owner * self.rows + offset, 16), size)]

    def forward(self, i):
        half = self.rows // 2
        self.first[i].wait_recv()
        came = self.block(self.over_y, i * half, half)
        self.last.append(self.links.start(came, came, tp=self.over_core))

    def finish(self):
        self.near.wait_recv()
        for made in self.last:
            made.wait_recv()


FEATS = 160


def fill_tables(lengths, seq, tok, line, coefs, step):
    total = tok.shape[0]
    anchor = seq * total
    starts, at = [], 0
    for i in range(lengths.shape[0]):
        starts.append(at)
        at = at + lengths[i]

    def places_of(shape, axis):
        pos = lax.broadcasted_iota(jnp.int32, shape, axis)
        low = jnp.zeros(shape, jnp.int32) - anchor
        last = jnp.ones(shape, f32)
        for start in starts:
            here = start - anchor
            low = jnp.maximum(low, jnp.where(pos >= here, here, -anchor))
            last = jnp.where((pos < here) & (here < total), 0.0, last)
        return pos.astype(f32), low, last

    lane = lax.broadcasted_iota(jnp.int32, (total, 128), 1)
    pos, low, last = places_of((total, 128), 0)
    began = jnp.where(low < 0, 1.0, 0.0)
    first = jnp.maximum(low, 0).astype(f32)
    tok[...] = jnp.where(
        lane == 0, first, jnp.where(lane == 1, began, jnp.where(lane == 2, last, pos))
    )
    pos, low, last = places_of((8, total), 1)
    row = lax.broadcasted_iota(jnp.int32, (8, total), 0)
    line[...] = jnp.where(row == 0, pos, jnp.maximum(low, 0).astype(f32))

    def clear(lo, hi):
        free = jnp.ones((1, 128), f32)
        for start in starts:
            at = jnp.zeros((1, 128), jnp.int32) + start
            free = jnp.where((at >= lo * total) & (at < (hi + 1) * total), 0.0, free)
        return free

    z, x = seq // 2, seq % 2
    one = jnp.ones((1, 128), f32)
    if step > 0:
        rows = [clear(2 * z + 1, 2 * z + 1), one * x.astype(f32), clear(2 * z, seq - 1)]
    else:
        rows = [clear(2 * z, 2 * z), one * (1 - x).astype(f32), clear(seq + 1, 2 * z + 1)]
    rows.append(clear(2 * z, 2 * z + 1))
    coefs[...] = jnp.concatenate(rows + [one * 0.0] * 4, axis=0)


class Chain:
    def __init__(self, links, st_t, st_z, coefs, seq, z, step):
        self.st_t, self.st_z, self.coefs = st_t, st_z, coefs
        self.turn = z if step > 0 else 3 - z
        self.hop = links.copy(st_t, st_z, seq=seq + 2 * step)

    def move(self, turn):
        @pl.when(self.turn == turn)
        def _():
            if turn > 0:
                self.hop.wait_recv()
            if turn < 3:
                if turn > 0:
                    for h in range(4):
                        own = self.st_t[h].astype(f32)
                        came = self.coefs[3:4, :] * self.st_z[h].astype(f32)
                        self.st_t[h] = (own + came).astype(bf16)
                self.hop.start()

    def use(self, states, near):
        for h in range(4):
            states[h, 0:176, :] = self.coefs[1:2, :] * near[h].astype(f32)
            states[h, 176:256, :] = jnp.zeros((80, 128), f32)

        @pl.when(self.turn > 0)
        def _():
            for h in range(4):
                states[h, 0:176, :] += self.coefs[2:3, :] * self.st_z[h].astype(f32)

    def finish(self):
        @pl.when(self.turn < 3)
        def _():
            self.hop.wait_send()


def ring_columns(place):
    return [pl.ds(pl.multiple_of(ring_seq(place - k) * 256, 256), 256) for k in relative_list(8)]


def phi(heads, h, select_a, select_b, lanes):
    a = dot(heads, select_a[h]) + lanes[0:1, :]
    b = dot(heads, select_b[h]) + lanes[1:2, :]
    return a, b


def fwd_kernel(
    lengths, sa_ref, sb_ref, lanes_ref, hm_ref, gain_first, gain_second,
    x_in, wq_in, wk_in, wv_in, wo_in, wg_in, wu_in, wd_in, c_in,
    wq_all, wo_all, wg_all, wu_all, wd_all, c_all,
    h1_out, qkv_out, yb_out, den_out, x1_out, h2_out, gate_out, up_out, m_out, sin_out, gain_out, terms_out,
    x_ref, tok_ref, line_ref, coef_ref, gain_ref, q_own, o_own, g_own, u_own, d_own,
    w_small, w_v, w_o, w_d, w_g,
    xg, h1, wq, wo, wg, wu, qkv, kq, num, den, yb, sc, rc, sy, ry, x1, gate, up, mm,
    gains_all, gains, st, st_x, st_t, st_z, s_in,
    send, recv, local,
):
    seq, tp, place, nearby, over_y, over_core, peers = places()
    z, x = seq // 2, seq % 2
    at = {k: j for j, k in enumerate(relative_list(8))}
    rows = x_ref.shape[0]
    total = 4 * rows
    links = Links(send, recv)
    locs = Sems(local)
    pending = []

    def store(src, dst):
        made = pltpu.make_async_copy(src, dst, locs.take())
        made.start()
        pending.append(made)

    def load(src, dst):
        made = pltpu.make_async_copy(src, dst, locs.take())
        made.start()
        return made

    got_qk = [load(wq_in, w_small.at[0:64]), load(wk_in, w_small.at[64:128]), load(wv_in, w_v)]
    columns = ring_columns(place)
    got_x = [load(x_in.at[:, c], x_ref.at[:, col(j)]) for j, c in enumerate(columns)]
    c_rows = pl.ds(pl.multiple_of(tp * rows, rows), rows)
    got_c = [load(c_in.at[:, c], c_all.at[c_rows, col(j)]) for j, c in enumerate(columns)]
    got_o = load(wo_in, w_o)
    ff = wd_in.shape[0]
    got_g = load(wg_in, w_g.at[pl.ds(0, ff)])
    got_d = load(wd_in, w_d.at[pl.ds(0, ff)])

    def turn(src, dst):
        for i in range(0, ff, 128):
            size = min(128, ff - i)
            dst[:, i : i + size] = src[i : i + 128, :].T[:, :size].astype(bf16)

    gain_ref[...] = jnp.concatenate(
        [gain_first[...], gain_second[...], jnp.zeros((14, 256), f32)], axis=0
    ).astype(bf16)
    greet(peers)
    gain_flying = [
        links.start(gain_ref, gains_all.at[at[k]], seq=ring_seq(place + k)) for k in range(1, 8)
    ]
    for made in got_x:
        made.wait()
    xrows = Rows(links, x_ref, xg, tp, over_y, over_core, rows)
    for made in got_qk:
        made.wait()
    q_own[:, 0:128] = w_small[...].T.astype(bf16)
    q_own[:, 128:640] = w_v[...].astype(bf16)
    ring = Gather(
        links,
        [(q_own, wq_all), (o_own, wo_all), (g_own, wg_all), (u_own, wu_all), (d_own, wd_all)],
        128,
        nearby,
        [[0], [1], [2, 3], [4]],
    )
    own_in = [
        load(x_ref, xrows.block(tp, 0, rows)),
        load(gain_ref, gains_all.at[at[0]]),
    ]
    got_o.wait()
    o_own[...] = w_o[...].T.astype(bf16)
    ring.pump(2)
    got_g.wait()
    turn(w_g, g_own)
    got_u = load(wu_in, w_g.at[pl.ds(0, ff)])
    ring.pump(4)
    got_d.wait()
    turn(w_d, d_own)
    got_u.wait()
    turn(w_g, u_own)
    own_kept = [load(own, everyone.at[at[0]]) for own, everyone in ring.arrays]
    fill_tables(lengths, seq, tok_ref, line_ref, coef_ref, 1)

    ring.pump(6)
    xrows.forward(0)
    for made in gain_flying:
        made.wait_recv()
    for made in own_in:
        made.wait()
    for j in range(8):
        chunk = gains_all[j].astype(f32)
        gains[0:8, j * 256 : (j + 1) * 256] = chunk[0:8]
    ring.pump(10)
    xrows.forward(1)
    ring.pump_array(0)
    own_kept[0].wait()
    got = load_weights(load, wq_all, wq)
    xrows.finish()

    def norm_first(i, _):
        r = pl.ds(pl.multiple_of(i * 32, 32), 32)
        v = xg[r, :].astype(f32)
        s = lax.rsqrt(jnp.mean(v * v, axis=1, keepdims=True) + epsilon)
        h1[r, :] = (v * s * gains[0:1, :]).astype(bf16)
        return 0

    lax.fori_loop(0, total // 32, norm_first, 0)
    links.sent_now(xrows.last)
    kept_h1 = load(h1, h1_out)
    for made in got_c:
        made.wait()
    crows = Rows(links, c_all.at[c_rows], c_all, tp, over_y, over_core, rows)
    ring.pump(15)
    for made in got:
        made.wait()

    def project(i, _):
        r = pl.ds(pl.multiple_of(i * 256, 256), 256)
        res = dot(h1[r, :], wq[...])
        qkv[r, :] = res.astype(bf16)
        kq[r, :] = pltpu.roll(res[:, :128], 64, 1).astype(bf16)
        return 0

    lax.fori_loop(0, total // 256, project, 0)
    store(qkv, qkv_out)
    ring.pump(16)

    heads = 4

    def head_v(h):
        return slice(128 + h * 128, 256 + h * 128)

    for h in range(heads):

        def state(i, c, h=h):
            s, zz = c
            r = pl.ds(pl.multiple_of(i * 256, 256), 256)
            a, b = phi(kq[r, :], h, sa_ref, sb_ref, lanes_ref)
            f = a * b * lanes_ref[2:3, :] * tok_ref[r, 2:3]
            s = s + dot_tt(f.astype(bf16), qkv[r, head_v(h)])
            return s, zz + jnp.sum(f, axis=0, keepdims=True)

        s, zz = lax.fori_loop(
            0, total // 256, state, (jnp.zeros((256, 128), f32), jnp.zeros((1, 256), f32))
        )
        pack_state(st, h, s, zz)
        ring.pump(16 + (h + 1) // 2)
    to_x = links.start(st, st_x, seq=seq + 1 - 2 * x)

    def local_head(h):
        for i in range(total // 256):
            r = slice(i * 256, (i + 1) * 256)
            span = (i + 1) * 256
            qm = (qkv[r, :128].astype(f32) * hm_ref[h : h + 1, :]).astype(bf16)
            u = dot_t(qm, kq[:span, :])
            keep = (line_ref[0:1, :span] >= tok_ref[r, 0:1]) & (
                line_ref[0:1, :span] <= tok_ref[r, 3:4]
            )
            kap = jnp.where(keep, (0.5 * u + 1.0) * u + 1.0, 0.0)
            den[r, h : h + 1] = jnp.sum(kap, axis=1, keepdims=True)
            num[r, h * 128 : (h + 1) * 128] = dot(kap.astype(bf16), qkv[:span, head_v(h)])

    local_head(0)
    ring.pump(19)
    to_x.wait_recv()
    for h in range(heads):
        mine, theirs = st[h].astype(f32), st_x[h].astype(f32)
        early = jnp.where(x == 0, mine, theirs)
        later = jnp.where(x == 0, theirs, mine)
        st_t[h] = (later + coef_ref[0:1, :] * early).astype(bf16)
    chain = Chain(links, st_t, st_z, coef_ref, seq, z, 1)
    chain.move(0)
    local_head(1)
    chain.move(1)
    ring.pump(20)
    local_head(2)
    chain.move(2)
    ring.pump(22)
    local_head(3)
    chain.move(3)
    ring.pump(24)
    chain.use(s_in, st_x)
    store(s_in, sin_out)
    for h in range(heads):
        z_row = jnp.concatenate([s_in[h, 160:161, :], s_in[h, 161:162, :]], axis=1)
        feat = jax.lax.broadcasted_iota(jnp.int32, (256, 128), 0)
        s_low = jnp.where(feat < FEATS, s_in[h], 0.0).astype(bf16)

        def carry(i, _, h=h, z_row=z_row, s_low=s_low):
            r = pl.ds(pl.multiple_of(i * 256, 256), 256)
            a, b = phi(qkv[r, 0:128], h, sa_ref, sb_ref, lanes_ref)
            f = a * b * lanes_ref[2:3, :] * tok_ref[r, 1:2]
            hv = slice(h * 128, (h + 1) * 128)
            top = num[r, hv] + dot(f.astype(bf16), s_low)
            low = den[r, h : h + 1] + jnp.sum(f * z_row, axis=1, keepdims=True)
            den[r, h : h + 1] = low
            y = top / low
            yb[r, hv] = y.astype(bf16)
            return 0

        lax.fori_loop(0, total // 256, carry, 0)
        ring.pump(25 + h)
    store(yb, yb_out)
    store(den, den_out)
    ring.pump_array(1)
    own_kept[1].wait()
    got = load_weights(load, wo_all, wo)
    for made in got:
        made.wait()

    y_at, c_at = tp // 2, tp % 2

    def out_rows(block):
        return yb[pl.ds(pl.multiple_of(block * rows, rows), rows), :]

    cols = 512
    to_core = []
    for yy in (0, 1):

        def core_cols(i, _, yy=yy):
            c = pl.ds(pl.multiple_of(i * cols, cols), cols)
            sc[yy, :, c] = dot_t(out_rows(yy * 2 + 1 - c_at), wo[c, :]).astype(bf16)
            return 0

        lax.fori_loop(0, 2048 // cols, core_cols, 0)
        to_core.append(links.start(sc.at[yy], rc.at[yy], tp=over_core))
    for made in to_core:
        made.wait_recv()
    ring.pump(32)

    def away_cols(i, _):
        c = pl.ds(pl.multiple_of(i * cols, cols), cols)
        part = dot_t(out_rows((1 - y_at) * 2 + c_at), wo[c, :])
        sy[:, c] = (part + rc[1 - y_at, :, c].astype(f32)).astype(bf16)
        return 0

    lax.fori_loop(0, 2048 // cols, away_cols, 0)
    to_y = links.start(sy, ry, tp=over_y)

    def own_cols(i, _):
        c = pl.ds(pl.multiple_of(i * cols, cols), cols)
        x1[:, c] = (
            dot_t(out_rows(tp), wo[c, :]) + rc[y_at, :, c].astype(f32) + x_ref[:, c].astype(f32)
        )
        return 0

    lax.fori_loop(0, 2048 // cols, own_cols, 0)
    ring.pump(34)
    to_y.wait_recv()
    ring.pump(37)

    links.sent_now(xrows.first + [xrows.near])
    ho = x_ref

    def norm_second(i, _):
        r = pl.ds(pl.multiple_of(i * 32, 32), 32)
        v = x1[r, :] + ry[r, :].astype(f32)
        x1[r, :] = v
        s = lax.rsqrt(jnp.mean(v * v, axis=1, keepdims=True) + epsilon)
        ho[r, :] = (v * s * gains[1:2, :]).astype(bf16)
        return 0

    lax.fori_loop(0, rows // 32, norm_second, 0)
    store(x1, x1_out)
    store(gains, gain_out)
    h2 = xg
    hrows = Rows(links, ho, h2, tp, over_y, over_core, rows)
    own_in = load(ho, hrows.block(tp, 0, rows))
    ring.pump(40)
    hrows.forward(0)
    ring.pump(43)
    hrows.forward(1)
    crows.forward(0)
    crows.forward(1)
    hrows.finish()
    crows.finish()
    own_in.wait()
    store(h2, h2_out)
    kept_h1.wait()
    got_c = load(c_all, h1)
    ring.pump_array(2)
    own_kept[2].wait()
    got = load_weights(load, wg_all, wg)
    ring.pump_array(3)
    own_kept[3].wait()
    got += load_weights(load, wu_all, wu)
    for made in got:
        made.wait()

    def gate_up(i, _):
        r = pl.ds(pl.multiple_of(i * 128, 128), 128)
        g = dot(h2[r, :], wg[...])
        uu = dot(h2[r, :], wu[...])
        gate[r, :] = g.astype(bf16)
        up[r, :] = uu.astype(bf16)
        mm[r, :] = (g * jax.nn.sigmoid(g) * uu).astype(bf16)
        return 0

    for quarter in range(4):
        lax.fori_loop(quarter * total // 512, (quarter + 1) * total // 512, gate_up, 0)
        ring.pump(58 + 2 * quarter)
    store(gate, gate_out)
    store(up, up_out)
    store(mm, m_out)
    got_c.wait()
    links.sent_now([ring.flying[a, 1, way, part] for a in (2, 3) for way in (0, 1) for part in (0, 1)])
    out_sems = [locs.take(), locs.take()]
    buffers = [g_own, u_own]

    def keep_terms(j, k):
        return pltpu.make_async_copy(buffers[k], terms_out.at[col(j)], out_sems[k])

    def grad_down(i, _):
        for k in (0, 1):
            pl.when(i > 0)(lambda k=k: keep_terms(2 * i - 2 + k, k).wait())
            buffers[k][...] = dot_tt(h1[:, col(2 * i + k)], mm[...]).astype(bf16)
            keep_terms(2 * i + k, k).start()
        return 0

    lax.fori_loop(0, 2, grad_down, 0)
    ring.pump(66)
    lax.fori_loop(2, 4, grad_down, 0)
    for k in (0, 1):
        keep_terms(6 + k, k).wait()
    ring.pump_array(4)
    own_kept[4].wait()
    for made in pending:
        made.wait()
    links.finish()
    chain.finish()


def pack_state(st, h, s, zz):
    st[h, 0:FEATS, :] = s[:FEATS].astype(bf16)
    tail = jnp.concatenate([zz[:, :128], zz[:, 128:], jnp.zeros((14, 128), f32)], axis=0)
    st[h, FEATS : FEATS + 16, :] = tail.astype(bf16)


def load_weights(load, everyone, flat):
    count, chunk = everyone.shape[0], everyone.shape[1]
    return [load(everyone.at[j], flat.at[pl.ds(j * chunk, chunk)]) for j in range(count)]


class Scatter:
    def __init__(self, slots, send, recv, nearby):
        self.slots, self.send, self.recv, self.nearby = slots, send, recv, nearby

    def copy(self, a, step, way, sub, src, slot, width):
        return pltpu.make_async_remote_copy(
            src_ref=src,
            dst_ref=self.piece(slot, way, sub, width),
            send_sem=self.send.at[a % 2, way, sub],
            recv_sem=self.recv.at[a % 2, way, sub, step],
            device_id={"seq": self.nearby[way]},
            device_id_type=pl.DeviceIdType.MESH,
        )

    def slot(self, a, step):
        return (a % 2) * 4 + (a // 2 * 7 + step) % 4

    def rows(self, way, sub, base=0):
        start = base + way * 128 + sub * 64
        return pl.ds(start if isinstance(start, int) else pl.multiple_of(start, 64), 64)

    def piece(self, slot, way, sub, width):
        return self.slots.at[slot, self.rows(way, sub), pl.ds(0, width)]

    def begin(self, a, own, width, column=0):
        for sub in (0, 1):
            for way in (0, 1):
                src = own.at[self.rows(way, sub, way * 256), pl.ds(column, width)]
                self.copy(a, 0, way, sub, src, self.slot(a, 0), width).start()

    def event(self, a, e, own, width, out, column=0):
        step, sub = e // 2, e % 2
        is_last = step // 6
        here = self.slot(a, step)
        far = (step + 1) // 4
        place0 = (1 - far) * 2 * (step + 1) + far * (11 - 2 * step) + is_last * 8
        far = (step + 2) // 4 - is_last
        place1 = (1 - far) * (3 + 2 * step) + far * (10 - 2 * step) + is_last * 9
        places = (place0, place1)
        for way in (0, 1):
            piece = self.piece(here, way, sub, width)
            came = self.copy(a, step, way, sub, piece, here, width)
            came.wait_recv()
            came.wait_send()

        def summed(way):
            mine = own[self.rows(way, sub, places[way] * 256), pl.ds(column, width)]
            came = self.slots[here, self.rows(way, sub), pl.ds(0, width)]
            return came.astype(f32) + mine.astype(f32)

        def on():
            for way in (0, 1):
                self.slots[here, self.rows(way, sub), pl.ds(0, width)] = summed(way).astype(bf16)
                piece = self.piece(here, way, sub, width)
                self.copy(a, step + 1, way, sub, piece, self.slot(a, step + 1), width).start()

        def end():
            for way in (0, 1):
                out[self.rows(way, sub), pl.ds(0, width)] = summed(way)

        if isinstance(e, int):
            if step < 6:
                on()
            else:
                end()
        else:
            pl.when(step < 6)(on)
            pl.when(step == 6)(end)


class TpSum:
    def __init__(self, part, from_core, from_y, sems, credits, tp, over_y, over_core):
        self.part, self.from_core, self.from_y = part, from_core, from_y
        self.sems, self.credits = sems, credits
        self.tp, self.over_y, self.over_core = tp, over_y, over_core
        self.y, self.c = tp // 2, tp % 2

    def to_core(self, i, yy):
        return pltpu.make_async_remote_copy(
            src_ref=self.part.at[i, yy * 2 + 1 - self.c],
            dst_ref=self.from_core.at[i, yy],
            send_sem=self.sems.at[yy, i],
            recv_sem=self.sems.at[2 + yy, i],
            device_id={"tp": self.over_core},
            device_id_type=pl.DeviceIdType.MESH,
        )

    def to_y(self, i):
        return pltpu.make_async_remote_copy(
            src_ref=self.part.at[i, (1 - self.y) * 2 + self.c],
            dst_ref=self.from_y.at[i],
            send_sem=self.sems.at[4, i],
            recv_sem=self.sems.at[5, i],
            device_id={"tp": self.over_y},
            device_id_type=pl.DeviceIdType.MESH,
        )

    def sent(self, i):
        self.to_core(i, 0).wait_send()
        self.to_core(i, 1).wait_send()
        self.to_y(i).wait_send()

    def offer(self, i, turn, value):
        if turn > 0:
            self.sent(i)
        for block in range(4):
            self.part[i, block] = value[block * 256 : (block + 1) * 256].astype(bf16)
        if turn > 0:
            pl.semaphore_wait(self.credits.at[0], 1)
        for yy in (0, 1):
            self.to_core(i, yy).start()

    def pass_on(self, i, turn):
        for yy in (0, 1):
            self.to_core(i, yy).wait_recv()
        away = (1 - self.y) * 2 + self.c
        self.part[i, away] = (
            self.part[i, away].astype(f32) + self.from_core[i, 1 - self.y].astype(f32)
        ).astype(bf16)
        if turn > 0:
            pl.semaphore_wait(self.credits.at[1], 1)
        self.to_y(i).start()

    def take(self, i, turn, use):
        self.to_y(i).wait_recv()
        use(
            self.part[i, self.tp].astype(f32)
            + self.from_core[i, self.y].astype(f32)
            + self.from_y[i].astype(f32)
        )
        if turn < 2:
            for k, peer in ((0, self.over_core), (1, self.over_y)):
                pl.semaphore_signal(
                    self.credits.at[k],
                    inc=1,
                    device_id={"tp": peer},
                    device_id_type=pl.DeviceIdType.MESH,
                )


def col(i, width=256):
    return pl.ds(i * width if isinstance(i, int) else pl.multiple_of(i * width, width), width)


def bwd_kernel(
    lengths, sa_ref, sb_ref, lanes_ref, hm_ref, gains, s_in, den, gain_first, gain_second,
    x_in, x1_in, wq_all, wo_all, wg_all, wu_all, wd_all, c_all, h1_all, qkv_all, yb_all, h2_all,
    gate_all, up_all, m_all, terms_all,
    d_out, g_out, u_out, oq_out, block_out, input_out, gain_out, u_kept,
    tok_ref, line_ref, coef_ref, terms, terms_core, terms_y,
    slots, s1, s2, wo, stream, hs, rows_all, mm, dup, tiles, qkv, kq, yb, dnum, dden, dden_t, dqkv,
    dq, dk, part, from_core, from_y, acc, x1, fout, st, st_x, st_t, st_z, s_back, own_rows,
    ring_send, ring_recv, tp_sems, credits, send, recv, local, tile_sems,
):
    seq, tp, place, nearby, over_y, over_core, peers = places()
    z, x = seq // 2, seq % 2
    rows, width = own_rows.shape
    total = 4 * rows
    ff = mm.shape[1]
    links = Links(send, recv)
    locs = Sems(local)

    def load(src, dst):
        made = pltpu.make_async_copy(src, dst, locs.take())
        made.start()
        return made

    def whole(everyone, flat):
        count, chunk = everyone.shape[0], everyone.shape[1]
        return [load(everyone.at[j], flat.at[pl.ds(j * chunk, chunk)]) for j in range(count)]

    got_m = load(m_all, mm)
    got_wd = whole(wd_all, s2)
    got_terms = load(terms_all, s1)
    got_c = load(c_all, rows_all)
    greet(peers)
    ring = Scatter(slots, ring_send, ring_recv, nearby)
    ring.begin(0, terms_all, ff)
    got_x1 = load(x1_in, x1)
    fill_tables(lengths, seq, tok_ref, line_ref, coef_ref, -1)
    columns = ring_columns(place)
    got_qkv = [load(qkv_all, qkv), load(yb_all, yb)]
    got_wo = whole(wo_all, wo)
    sums = TpSum(part, from_core, from_y, tp_sems, credits, tp, over_y, over_core)

    def run(n, body, pumps=None):
        def step(i, _):
            body(i)
            if pumps:
                a, first, count = pumps
                every = n // count
                pl.when((i + 1) % every == 0)(lambda: event(a, first + (i + 1) // every - 1))
            return 0

        lax.fori_loop(0, n, step, 0)

    plan = {0: (s1, ff, 0), 1: (s2, ff, 0), 2: (s1, ff, 0), 3: (s2, 1152, 0)}

    def event(a, e):
        own, wide, column = plan[a]
        ring.event(a, e, own, wide, fout, column)

    def begin(a):
        own, wide, column = plan[a]
        ring.begin(a, own, wide, column)

    def events(a, first, last):
        lax.fori_loop(first, last, lambda e, _: (event(a, e), 0)[1], 0)

    def both(a, first, b, second, count):
        def pair(i, _):
            event(a, first + i)
            event(b, second + i)
            return 0

        lax.fori_loop(0, count, pair, 0)

    def chunks_of(source, size, body, pumps=None, count=8):
        def copies(i, slot):
            return [
                pltpu.make_async_copy(a, b, tile_sems.at[k, slot])
                for k, (a, b) in enumerate(source(i, slot))
            ]

        for made in copies(0, 0):
            made.start()

        def step(i):
            slot = i % 2

            @pl.when(i + 1 < count)
            def _():
                for made in copies(i + 1, 1 - slot):
                    made.start()

            for made in copies(i, slot):
                made.wait()
            body(i, slot)

        run(count, step, pumps)

    got_m.wait()
    for made in got_wd:
        made.wait()
    got_terms.wait()

    def mlp(i):
        sums.offer(i, 0, dot_t(mm[...], s2[col(i), :]))
        pl.when(i > 0)(lambda: sums.pass_on(i - 1, 0))

    run(8, mlp, (0, 0, 2))
    sums.pass_on(7, 0)

    def gate_up_tiles(i, slot):
        r = col(i, 128)
        return [
            (gate_all.at[r], tiles.at[slot, pl.ds(0, 128)]),
            (up_all.at[r], tiles.at[slot, pl.ds(128, 128)]),
        ]

    def grad_gate_up(i, slot):
        r = col(i, 128)
        dm = dot(rows_all[r, :], s2[...]).astype(bf16).astype(f32)
        g = tiles[slot, 0:128].astype(f32)
        u = tiles[slot, 128:256].astype(f32)
        s = jax.nn.sigmoid(g)
        mm[r, :] = (dm * u * s * (1.0 + g * (1.0 - s))).astype(bf16)
        dup[r, :] = (dm * (g * s)).astype(bf16)

        pl.when(i >= 3)(lambda: take_block(i - 3))

    def take_block(i):
        def use(value):
            own_rows[:, col(i)] = (x1[:, col(i)] + value).astype(bf16)

        sums.take(i, 0, use)

    got_x1.wait()
    got_c.wait()
    chunks_of(gate_up_tiles, 8, grad_gate_up, (0, 2, 4))

    def w_tiles(i, slot):
        return [(wg_all.at[i], stream.at[slot, 0]), (wu_all.at[i], stream.at[slot, 1])]

    def grad_hidden(i, slot):
        pl.when(i < 3)(lambda: take_block(5 + i))
        value = dot_t(mm[...], stream[slot, 0]) + dot_t(dup[...], stream[slot, 1])
        sums.offer(i, 1, value)
        pl.when(i > 0)(lambda: sums.pass_on(i - 1, 1))

    chunks_of(w_tiles, 8, grad_hidden, (0, 6, 4))
    kept = [load(own_rows.at[:, col(j)], block_out.at[:, c]) for j, c in enumerate(columns)]
    pending = []
    sums.pass_on(7, 1)

    def h_tiles(everyone):
        return lambda i, slot: [(everyone.at[:, col(i)], hs.at[slot])]

    def keep_up(i, slot):
        return pltpu.make_async_copy(tiles.at[slot], u_kept.at[col(i)], tile_sems.at[1, slot])

    def grads(i, slot):
        s2[col(i), :] = dot_tt(hs[slot], mm[...]).astype(bf16)
        pl.when(i >= 2)(lambda: keep_up(i - 2, slot).wait())
        tiles[slot] = dot_tt(hs[slot], dup[...]).astype(bf16)
        keep_up(i, slot).start()
        pl.when(i == 1)(lambda: begin(1))

    chunks_of(h_tiles(h2_all), 8, grads, (0, 10, 2))
    keep_up(6, 0).wait()
    keep_up(7, 1).wait()

    def take_second(i):
        def use(value):
            acc[:, col(i)] = value

        sums.take(i, 1, use)

    run(2, take_second)
    both(1, 0, 0, 12, 2)
    done = load(fout.at[:, pl.ds(0, ff)], d_out)
    got_up = load(u_kept, s1)
    lax.fori_loop(2, 5, lambda i, _: (take_second(i), 0)[1], 0)
    events(1, 2, 3)
    got_up.wait()
    begin(2)
    lax.fori_loop(5, 8, lambda i, _: (take_second(i), 0)[1], 0)
    both(1, 3, 2, 0, 1)

    for made in kept:
        made.wait()

    def norm_back_second(i, _):
        r = pl.ds(pl.multiple_of(i * 32, 32), 32)
        v = x1[r, :]
        s = lax.rsqrt(jnp.mean(v * v, axis=1, keepdims=True) + epsilon)
        n = v * s
        dn = acc[r, :] * gains[1:2, :]
        own = pl.ds(pl.multiple_of(tp * rows + i * 32, 32), 32)
        back = rows_all[own, :].astype(f32) + s * (
            dn - n * jnp.mean(dn * n, axis=1, keepdims=True)
        )
        acc[r, :] = back
        own_rows[r, :] = back.astype(bf16)
        return 0

    lax.fori_loop(0, rows // 32, norm_back_second, 0)
    da = Rows(links, own_rows, rows_all, tp, over_y, over_core, rows)
    own_in = load(own_rows, da.block(tp, 0, rows))

    both(1, 4, 2, 1, 1)
    da.forward(0)
    both(1, 5, 2, 2, 1)
    da.forward(1)
    for made in got_qkv + got_wo:
        made.wait()
    da.finish()
    own_in.wait()
    links.sent_now(da.first + [da.near])
    got_x = [load(x_in.at[:, c], own_rows.at[:, col(j)]) for j, c in enumerate(columns)]

    def head_v(h):
        return slice(128 + h * 128, 256 + h * 128)

    def grad_attended(i):
        r = col(i, 256)
        dy = dot(rows_all[r, :], wo[...])
        kq[r, :] = pltpu.roll(qkv[r, 0:128].astype(f32), 64, 1).astype(bf16)
        columns = []
        for h in range(4):
            hv = slice(h * 128, (h + 1) * 128)
            under = 1.0 / den[r, h : h + 1]
            part_h = dy[:, hv]
            dnum[r, hv] = (part_h * under).astype(bf16)
            low = jnp.sum(part_h * yb[r, hv].astype(f32), axis=1, keepdims=True)
            columns.append(-low * under)
        lane = lax.broadcasted_iota(jnp.int32, (256, 128), 1)
        packed = jnp.zeros((256, 128), f32)
        for h in range(4):
            packed = jnp.where(lane == h, columns[h], packed)
        dden[r, :] = packed
        dden_t[i] = packed.T[0:8, :]

    run(4, grad_attended)
    both(1, 6, 2, 3, 1)

    for h in range(4):

        def state(i, c, h=h):
            s, zz = c
            r = col(i, 256)
            a, b = phi(qkv[r, 0:128], h, sa_ref, sb_ref, lanes_ref)
            f = a * b * lanes_ref[2:3, :] * tok_ref[r, 1:2]
            s = s + dot_tt(f.astype(bf16), dnum[r, h * 128 : (h + 1) * 128])
            return s, zz + jnp.sum(f * dden[r, h : h + 1], axis=0, keepdims=True)

        s, zz = lax.fori_loop(
            0, 4, state, (jnp.zeros((256, 128), f32), jnp.zeros((1, 256), f32))
        )
        pack_state(st, h, s, zz)
    to_x = links.start(st, st_x, seq=seq + 1 - 2 * x)
    both(1, 7, 2, 4, 1)

    dq[...] = jnp.zeros(dq.shape, f32)

    def local_head(h):
        hm = hm_ref[h : h + 1, :]
        hv = slice(h * 128, (h + 1) * 128)
        for j in range(total // 256):
            k_rows = slice(j * 256, (j + 1) * 256)
            dv_s = jnp.zeros((256, 128), f32)
            dk_s = jnp.zeros((256, 128), f32)
            for i in range(j, total // 256):
                q_rows = slice(i * 256, (i + 1) * 256)
                qm = (qkv[q_rows, 0:128].astype(f32) * hm).astype(bf16)
                u = dot_t(kq[k_rows, :], qm)
                keep = tok_ref[k_rows, 3:4] >= line_ref[1:2, q_rows]
                if i == j:
                    keep = keep & (tok_ref[k_rows, 3:4] <= line_ref[0:1, q_rows])
                kap = jnp.where(keep, (0.5 * u + 1.0) * u + 1.0, 0.0).astype(bf16)
                dn = dnum[q_rows, hv]
                grad = dot_t(qkv[k_rows, head_v(h)], dn) + dden_t[i, h : h + 1, :]
                du = jnp.where(keep, grad * (1.0 + u), 0.0).astype(bf16)
                dv_s = dv_s + dot(kap, dn)
                dk_s = dk_s + dot(du, qm)
                dq[q_rows, :] += dot_tt(du, kq[k_rows, :]) * hm
            dqkv[k_rows, head_v(h)] = dv_s.astype(bf16)
            if h == 0:
                dk[k_rows, :] = dk_s
            else:
                dk[k_rows, :] += dk_s

    local_head(0)
    to_x.wait_recv()
    for h in range(4):
        mine, theirs = st[h].astype(f32), st_x[h].astype(f32)
        first = jnp.where(x == 0, mine, theirs)
        second = jnp.where(x == 0, theirs, mine)
        st_t[h] = (first + coef_ref[0:1, :] * second).astype(bf16)
    chain = Chain(links, st_t, st_z, coef_ref, seq, z, -1)
    chain.move(0)
    both(1, 8, 2, 5, 1)
    local_head(1)
    chain.move(1)
    both(1, 9, 2, 6, 1)
    local_head(2)
    chain.move(2)
    both(1, 10, 2, 7, 1)
    local_head(3)
    chain.move(3)
    both(1, 11, 2, 8, 1)
    chain.use(s_back, st_x)

    def split_state(ref, h):
        z_row = jnp.concatenate([ref[h, 160:161, :], ref[h, 161:162, :]], axis=1)
        feat = lax.broadcasted_iota(jnp.int32, (256, 128), 0)
        return jnp.where(feat < FEATS, ref[h], 0.0).astype(bf16), z_row

    for h in range(4):
        s_q, z_q = split_state(s_in, h)
        s_k, z_k = split_state(s_back, h)
        hv = slice(h * 128, (h + 1) * 128)

        def through(grad, a, b, h=h):
            grad = grad * lanes_ref[2:3, :]
            return dot_t((grad * b).astype(bf16), sa_ref[h]) + dot_t(
                (grad * a).astype(bf16), sb_ref[h]
            )

        def carried_part(i, _, h=h, s_q=s_q, z_q=z_q, s_k=s_k, z_k=z_k, hv=hv, through=through):
            r = col(i, 256)
            a, b = phi(qkv[r, 0:128], h, sa_ref, sb_ref, lanes_ref)
            grad = dot_t(dnum[r, hv], s_q) + dden[r, h : h + 1] * z_q
            dq[r, :] += through(grad * tok_ref[r, 1:2], a, b)
            a, b = phi(kq[r, :], h, sa_ref, sb_ref, lanes_ref)
            last = tok_ref[r, 2:3]
            grad = dot_t(qkv[r, head_v(h)], s_k) + z_k
            dk[r, :] += through(grad * last, a, b)
            f = (a * b * lanes_ref[2:3, :] * last).astype(bf16)
            dqkv[r, head_v(h)] = (dqkv[r, head_v(h)].astype(f32) + dot(f, s_k)).astype(bf16)
            return 0

        lax.fori_loop(0, 4, carried_part, 0)

    def join(i):
        r = col(i, 256)
        dqkv[r, 0:128] = (dq[r, :] + pltpu.roll(dk[r, :], 64, 1)).astype(bf16)

    run(4, join)
    done.wait()
    both(1, 12, 2, 9, 2)
    done = load(fout.at[:, pl.ds(0, ff)], g_out)
    own_w = load(wg_all.at[7], stream.at[0, 0])
    own_w.wait()
    gain_two = jnp.sum(fout[:, 0:ff] * stream[0, 0].astype(f32), axis=1, keepdims=True)

    def wq_tiles(i, slot):
        return [(wq_all.at[i], stream.at[slot, 0, :, pl.ds(0, 640)])]

    def grad_hidden_first(i, slot):
        sums.offer(i, 2, dot_t(dqkv[...], stream[slot, 0, :, 0:640]))
        pl.when(i > 0)(lambda: sums.pass_on(i - 1, 2))

    chunks_of(wq_tiles, 8, grad_hidden_first, (2, 11, 1))
    sums.pass_on(7, 2)

    def grad_out_qkv(i, slot):
        s2[col(i), 0:512] = dot_tt(rows_all[:, col(i)], yb[...]).astype(bf16)
        s2[col(i), 512:1152] = dot_tt(hs[slot], dqkv[...]).astype(bf16)

        pl.when(i == 1)(lambda: begin(3))

    chunks_of(h_tiles(h1_all), 8, grad_out_qkv, (3, 0, 1))
    done.wait()
    both(2, 12, 3, 1, 2)
    done = load(fout.at[:, pl.ds(0, ff)], u_out)
    def take_first(i):
        def use(value):
            x1[:, col(i)] = value

        sums.take(i, 2, use)

    run(8, take_first, (3, 3, 4))
    for made in got_x:
        made.wait()

    def norm_back_first(i, _):
        r = pl.ds(pl.multiple_of(i * 32, 32), 32)
        v = own_rows[r, :].astype(f32)
        s = lax.rsqrt(jnp.mean(v * v, axis=1, keepdims=True) + epsilon)
        n = v * s
        dn = x1[r, :] * gains[0:1, :]
        acc[r, :] += s * (dn - n * jnp.mean(dn * n, axis=1, keepdims=True))
        return 0

    lax.fori_loop(0, rows // 32, norm_back_first, 0)
    pending += [load(acc.at[:, col(j)], input_out.at[:, c]) for j, c in enumerate(columns)]
    own_w = load(wu_all.at[7], stream.at[0, 0])
    own_q = load(wq_all.at[7], stream.at[1, 0, :, pl.ds(0, 640)])
    own_w.wait()
    own_q.wait()
    gain_two += jnp.sum(fout[:, 0:ff] * stream[0, 0].astype(f32), axis=1, keepdims=True)
    events(3, 7, 12)
    done.wait()
    events(3, 12, 14)
    pending.append(load(fout.at[:, pl.ds(0, 1152)], oq_out))
    gain_one = jnp.sum(fout[:, 512:1152] * stream[1, 0, :, 0:640].astype(f32), axis=1, keepdims=True)
    lane = lax.broadcasted_iota(jnp.int32, (256, 128), 1)
    both = jnp.where(lane == 0, gain_one, jnp.where(lane == 1, gain_two, 0.0)).T[0:8, :]
    terms[0] = both
    over = links.start(terms.at[0], terms_core, tp=over_core)
    over.wait_recv()
    both = both + terms_core[...]
    terms[1] = both
    over = links.start(terms.at[1], terms_y, tp=over_y)
    over.wait_recv()
    own_gains = jnp.concatenate(
        [gain_first[...], gain_second[...], jnp.ones((6, 256), f32)], axis=0
    ).astype(bf16)
    terms[2] = (both + terms_y[...]) / own_gains.astype(f32)
    pending.append(load(terms.at[2], gain_out))
    run(8, lambda i: sums.sent(i))
    for made in pending:
        made.wait()
    links.finish()
    chain.finish()


def feature_tables(heads):
    first = np.zeros((heads, 128, 256), np.float32)
    second = np.zeros((heads, 128, 256), np.float32)
    lanes = np.zeros((8, 256), np.float32)
    f = 0
    for i in range(FEAT):
        for j in range(i, FEAT):
            for h in range(heads):
                first[h, h * FEAT + i, f] = 1
                second[h, h * FEAT + j, f] = 1
            lanes[2, f] = square_coef if i == j else square_coef * 2**0.5
            f += 1
    for i in range(FEAT):
        for h in range(heads):
            first[h, h * FEAT + i, f] = 1
        lanes[1, f] = 1
        lanes[2, f] = linear_coef
        f += 1
    lanes[0, f] = lanes[1, f] = lanes[2, f] = 1
    mask = np.zeros((8, 128), np.float32)
    for h in range(heads):
        mask[h, h * FEAT : (h + 1) * FEAT] = 0.25
    return first, second, lanes, mask


def forward_pass(lengths, constants, gain_first, gain_second, x_in, weights, c_in):
    rows, width = x_in.shape
    total = 4 * rows
    ff = weights[4].shape[0]
    hbm = pl.BlockSpec(memory_space=pl.ANY)
    vmem = pl.BlockSpec(memory_space=pltpu.VMEM)

    def shape(*dims, dtype=bf16):
        return jax.ShapeDtypeStruct(dims, dtype)

    outs = (
        shape(8, 256, 640),
        shape(8, 256, 512),
        shape(8, 256, ff),
        shape(8, 256, ff),
        shape(8, 256, ff),
        shape(total, width),
        shape(total, width),
        shape(total, 640),
        shape(total, 512),
        shape(total, 128, dtype=f32),
        shape(rows, width, dtype=f32),
        shape(total, width),
        shape(total, ff),
        shape(total, ff),
        shape(total, ff),
        shape(4, 256, 128, dtype=f32),
        shape(8, width, dtype=f32),
        shape(width, ff),
    )
    scratch = [
        pltpu.VMEM((rows, width), bf16),
        pltpu.VMEM((total, 128), f32),
        pltpu.VMEM((8, total), f32),
        pltpu.VMEM((8, 128), f32),
        pltpu.VMEM((16, 256), bf16),
        pltpu.VMEM((256, 640), bf16),
        pltpu.VMEM((256, 512), bf16),
        pltpu.VMEM((256, ff), bf16),
        pltpu.VMEM((256, ff), bf16),
        pltpu.VMEM((256, ff), bf16),
        pltpu.VMEM((128, 256), f32),
        pltpu.VMEM((256, 512), f32),
        pltpu.VMEM((512, 256), f32),
        pltpu.VMEM((-(-ff // 128) * 128, 256), f32),
        pltpu.VMEM((-(-ff // 128) * 128, 256), f32),
        pltpu.VMEM((total, width), bf16),
        pltpu.VMEM((total, width), bf16),
        pltpu.VMEM((width, 640), bf16),
        pltpu.VMEM((width, 512), bf16),
        pltpu.VMEM((width, ff), bf16),
        pltpu.VMEM((width, ff), bf16),
        pltpu.VMEM((total, 640), bf16),
        pltpu.VMEM((total, 128), bf16),
        pltpu.VMEM((total, 512), f32),
        pltpu.VMEM((total, 128), f32),
        pltpu.VMEM((total, 512), bf16),
        pltpu.VMEM((2, rows, width), bf16),
        pltpu.VMEM((2, rows, width), bf16),
        pltpu.VMEM((rows, width), bf16),
        pltpu.VMEM((rows, width), bf16),
        pltpu.VMEM((rows, width), f32),
        pltpu.VMEM((total, ff), bf16),
        pltpu.VMEM((total, ff), bf16),
        pltpu.VMEM((total, ff), bf16),
        pltpu.VMEM((8, 16, 256), bf16),
        pltpu.VMEM((8, width), f32),
        pltpu.VMEM((4, 176, 128), bf16),
        pltpu.VMEM((4, 176, 128), bf16),
        pltpu.VMEM((4, 176, 128), bf16),
        pltpu.VMEM((4, 176, 128), bf16),
        pltpu.VMEM((4, 256, 128), f32),
        pltpu.SemaphoreType.DMA((112,)),
        pltpu.SemaphoreType.DMA((112,)),
        pltpu.SemaphoreType.DMA((112,)),
    ]
    return pl.pallas_call(
        fwd_kernel,
        out_shape=outs,
        in_specs=[pl.BlockSpec(memory_space=pltpu.SMEM)] + [vmem] * 6 + [hbm] * 9,
        out_specs=(hbm,) * len(outs),
        scratch_shapes=scratch,
        compiler_params=pltpu.CompilerParams(
            collective_id=0, has_side_effects=True, vmem_limit_bytes=60 * 2**20
        ),
    )(lengths, *constants, gain_first, gain_second, x_in, *weights, c_in)


def backward_pass(lengths, constants, gains, s_in, den, gain_pair, x_in, x1, weights, c_all, acts):
    rows, width = x_in.shape
    total = 4 * rows
    ff = weights[2].shape[2]
    hbm = pl.BlockSpec(memory_space=pl.ANY)
    vmem = pl.BlockSpec(memory_space=pltpu.VMEM)

    def shape(*dims, dtype=f32):
        return jax.ShapeDtypeStruct(dims, dtype)

    outs = (
        shape(256, ff),
        shape(256, ff),
        shape(256, ff),
        shape(256, 1152),
        shape(rows, width, dtype=bf16),
        shape(rows, width),
        shape(8, 256),
        shape(width, ff, dtype=bf16),
    )
    scratch = [
        pltpu.VMEM((total, 128), f32),
        pltpu.VMEM((8, total), f32),
        pltpu.VMEM((8, 128), f32),
        pltpu.VMEM((3, 8, 256), f32),
        pltpu.VMEM((8, 256), f32),
        pltpu.VMEM((8, 256), f32),
        pltpu.VMEM((8, 256, ff), bf16),
        pltpu.VMEM((width, ff), bf16),
        pltpu.VMEM((width, ff), bf16),
        pltpu.VMEM((width, 512), bf16),
        pltpu.VMEM((2, 2, 256, ff), bf16),
        pltpu.VMEM((2, total, 256), bf16),
        pltpu.VMEM((total, width), bf16),
        pltpu.VMEM((total, ff), bf16),
        pltpu.VMEM((total, ff), bf16),
        pltpu.VMEM((2, 256, ff), bf16),
        pltpu.VMEM((total, 640), bf16),
        pltpu.VMEM((total, 128), bf16),
        pltpu.VMEM((total, 512), bf16),
        pltpu.VMEM((total, 512), bf16),
        pltpu.VMEM((total, 128), f32),
        pltpu.VMEM((4, 8, 256), f32),
        pltpu.VMEM((total, 640), bf16),
        pltpu.VMEM((total, 128), f32),
        pltpu.VMEM((total, 128), f32),
        pltpu.VMEM((8, 4, 256, 256), bf16),
        pltpu.VMEM((8, 2, 256, 256), bf16),
        pltpu.VMEM((8, 256, 256), bf16),
        pltpu.VMEM((rows, width), f32),
        pltpu.VMEM((rows, width), f32),
        pltpu.VMEM((256, ff), f32),
        pltpu.VMEM((4, 176, 128), bf16),
        pltpu.VMEM((4, 176, 128), bf16),
        pltpu.VMEM((4, 176, 128), bf16),
        pltpu.VMEM((4, 176, 128), bf16),
        pltpu.VMEM((4, 256, 128), f32),
        pltpu.VMEM((rows, width), bf16),
        pltpu.SemaphoreType.DMA((2, 2, 2)),
        pltpu.SemaphoreType.DMA((2, 2, 2, 7)),
        pltpu.SemaphoreType.DMA((6, 8)),
        pltpu.SemaphoreType.REGULAR((2,)),
        pltpu.SemaphoreType.DMA((16,)),
        pltpu.SemaphoreType.DMA((16,)),
        pltpu.SemaphoreType.DMA((80,)),
        pltpu.SemaphoreType.DMA((2, 2)),
    ]
    return pl.pallas_call(
        bwd_kernel,
        out_shape=outs,
        in_specs=[pl.BlockSpec(memory_space=pltpu.SMEM)] + [vmem] * 9 + [hbm] * 16,
        out_specs=(hbm,) * len(outs),
        scratch_shapes=scratch,
        compiler_params=pltpu.CompilerParams(
            collective_id=1, has_side_effects=True, vmem_limit_bytes=62 * 2**20
        ),
    )(lengths, *constants, gains, s_in, den, *gain_pair, x_in, x1, *weights, c_all, *acts)


def finish_kernel(
    d_in, g_in, u_in, oq_in, block_in, input_in,
    d_out, g_out, u_out, o_out, q_out, k_out, v_out, block_out, input_out,
    wide, turned, oq, oq_t, sems,
):
    keeper = Sems(sems)
    ff = d_in.shape[1]

    def copy(src, dst):
        made = pltpu.make_async_copy(src, dst, keeper.take())
        made.start()
        return made

    came = [copy(ref, wide.at[i]) for i, ref in enumerate((g_in, u_in, d_in))]
    came_oq = copy(oq_in, oq)
    kept = [
        copy(block_in, block_out),
        copy(input_in, input_out),
        copy(oq_in.at[:, pl.ds(640, 512)], v_out),
    ]
    came_oq.wait()
    oq_t[...] = oq[:, 0:640].T
    kept += [
        copy(oq_t.at[pl.ds(0, 512)], o_out),
        copy(oq_t.at[pl.ds(512, 64)], q_out),
        copy(oq_t.at[pl.ds(576, 64)], k_out),
    ]
    for i, out in enumerate((g_out, u_out, d_out)):
        came[i].wait()
        for at in range(0, ff, 128):
            at = min(at, ff - 128)
            turned[i, at : at + 128, :] = wide[i, :, at : at + 128].T
        kept.append(copy(turned.at[i], out))
    for made in kept:
        made.wait()


def finish(d, g, u, oq, block, grad_input):
    rows, width = block.shape
    ff = d.shape[1]
    hbm = pl.BlockSpec(memory_space=pl.ANY)

    def shape(*dims, dtype=f32):
        return jax.ShapeDtypeStruct(dims, dtype)

    outs = (
        shape(ff, 256), shape(ff, 256), shape(ff, 256), shape(512, 256), shape(64, 256),
        shape(64, 256), shape(256, 512), shape(rows, width, dtype=bf16), shape(rows, width),
    )
    return pl.pallas_call(
        finish_kernel,
        out_shape=outs,
        in_specs=[hbm] * 6,
        out_specs=(hbm,) * len(outs),
        scratch_shapes=[
            pltpu.VMEM((3, 256, ff), f32),
            pltpu.VMEM((3, ff, 256), f32),
            pltpu.VMEM((256, 1152), f32),
            pltpu.VMEM((640, 256), f32),
            pltpu.SemaphoreType.DMA((16,)),
        ],
        compiler_params=pltpu.CompilerParams(vmem_limit_bytes=40 * 2**20),
    )(d, g, u, oq, block, grad_input)


def on_device_rings(
    inputs, lengths, gain_attn, w_query, w_key, w_value, w_out, gain_mlp, w_gate, w_up, w_down,
    cotangent,
):
    first, second, lanes, mask = feature_tables(4)
    constants = (
        jnp.asarray(first, bf16), jnp.asarray(second, bf16), jnp.asarray(lanes), jnp.asarray(mask),
    )
    gain_pair = (gain_attn.reshape(1, -1), gain_mlp.reshape(1, -1))
    made = forward_pass(
        lengths, constants, *gain_pair, inputs,
        (w_query.T, w_key.T, w_value, w_out, w_gate.T, w_up.T, w_down), cotangent,
    )
    weights = made[:5]
    c_all, h1, qkv, yb, den, x1, h2, gate, up, mixed, s_in, gain_all, terms = made[5:]
    sum_down_t, sum_gate, sum_up, sum_oq, block, grad_input, gain_sums, _ = backward_pass(
        lengths, constants, gain_all, s_in, den, gain_pair, inputs, x1, weights, c_all,
        (h1, qkv, yb, h2, gate, up, mixed, terms),
    )
    d, g_t, u_t, o, q_t, k_t, v, block, grad_input = finish(
        sum_down_t, sum_gate, sum_up, sum_oq, block, grad_input
    )
    return (
        block,
        grad_input,
        gain_sums[0],
        q_t.T,
        k_t.T,
        v,
        o,
        gain_sums[1],
        g_t.T,
        u_t.T,
        d,
    )


def on_device(
    inputs,
    lengths,
    gain_attn,
    w_query,
    w_key,
    w_value,
    w_out,
    gain_mlp,
    w_gate,
    w_up,
    w_down,
    cotangent,
):
    seq_count = lax.axis_size("seq")
    tp_count = lax.axis_size("tp")
    seq_index = lax.axis_index("seq")
    rows_own, width = inputs.shape
    chunk = width // seq_count
    half = chunk // 2
    block_len = rows_own * tp_count
    anchor = seq_index * block_len
    relative = relative_list(seq_count)
    ring = ring_order(seq_count)
    place_of = [ring.index(s) for s in range(seq_count)]
    to_rel = jnp.array(
        [[ring[(place_of[s] - k) % seq_count] for k in relative] for s in range(seq_count)],
        jnp.int32,
    )[seq_index]
    to_abs = jnp.array(
        [
            [relative.index((place_of[s] - place_of[o]) % seq_count) for o in range(seq_count)]
            for s in range(seq_count)
        ],
        jnp.int32,
    )[seq_index]
    to_rel = [to_rel[j] for j in range(seq_count)]
    to_abs = [to_abs[j] for j in range(seq_count)]

    qk_cols, v_cols, ff_cols = w_query.shape[1], w_value.shape[1], w_gate.shape[1]
    gains = jnp.stack([gain_attn, gain_mlp]).astype(bf16)
    qkv_cols = 2 * qk_cols + v_cols
    qkv_own = jnp.concatenate([w_query, w_key, w_value], axis=1).astype(bf16)
    gain_rows = jnp.zeros((16, qkv_cols), bf16).at[:2, :chunk].set(gains)
    first_own = jnp.concatenate([qkv_own, gain_rows], axis=0)
    out_own = w_out.astype(bf16).T
    gate_up_own = jnp.concatenate([w_gate, w_up], axis=1).astype(bf16)
    down_own = w_down.astype(bf16).T

    first_got = ring_gather(first_own, half)
    out_got = ring_gather(out_own, half)
    gate_up_got = ring_gather(gate_up_own, half)
    down_got = ring_gather(down_own, half)
    w_qkv = jnp.concatenate([first_got[k][:chunk] for k in relative], axis=0)
    gain_first = jnp.concatenate([first_got[k][chunk, :chunk] for k in relative]).astype(f32)
    gain_second = jnp.concatenate([first_got[k][chunk + 1, :chunk] for k in relative]).astype(f32)
    w_out_t = jnp.concatenate([out_got[k] for k in relative], axis=0)
    w_gate_up = jnp.concatenate([gate_up_got[k] for k in relative], axis=0)
    w_down_t = jnp.concatenate([down_got[k] for k in relative], axis=0)

    at = jnp.arange(lengths.shape[0])
    starts = jnp.sum(jnp.where(at[None, :] < at[:, None], lengths[None, :], 0), axis=1)
    positions, row_ids, carry_in, after_last = segment_masks(anchor, starts, block_len)
    carry_mask = carry_in.astype(f32)
    last_mask = after_last.astype(f32)
    resets = (
        jnp.sum(
            ((starts // block_len)[None, :] == jnp.arange(seq_count)[:, None]).astype(jnp.int32),
            axis=1,
        )
        > 0
    ).astype(jnp.int32)

    inputs_own = to_relative(inputs, to_rel, chunk)
    grad_own = to_relative(cotangent, to_rel, chunk)
    inputs_full = tp_gather(inputs_own).astype(f32)
    grad_full = tp_gather(grad_own)
    inputs_own = inputs_own.astype(f32)
    hidden_first = (inputs_full * rms_scale(inputs_full) * gain_first).astype(bf16)
    qkv = dot(hidden_first, w_qkv).astype(bf16)
    queries = qkv[:, :qk_cols]
    key_flat = qkv[:, qk_cols : 2 * qk_cols]
    value_flat = qkv[:, 2 * qk_cols :]
    heads_local = qk_cols // FEAT
    query_heads = queries.reshape(block_len, heads_local, FEAT)
    key_heads = key_flat.reshape(block_len, heads_local, FEAT)
    value_heads = value_flat.reshape(block_len, heads_local, VHEAD)
    query_float = query_heads.astype(f32)
    key_float = key_heads.astype(f32)
    value_float = value_heads.astype(f32)
    key_feat = features(key_float) * last_mask[:, None, None]
    local_state = jnp.einsum("thn,thv->hnv", key_feat, value_float, precision=highest)
    local_sum = jnp.sum(key_feat, axis=0)
    carry_state, carry_sum = carried([local_state, local_sum], resets, 1)
    step_rows = 512
    query_feat = features(query_float)
    carry_weight = carry_mask[:, None]
    numer_parts = []
    denom_parts = []
    for first_row in range(0, block_len, step_rows):
        query_part = query_heads[first_row : first_row + step_rows]
        scores, allowed, kernel = pair_block(
            query_part, key_heads, row_ids, positions, first_row, step_rows
        )
        numer_parts.append(
            jnp.einsum("hts,shv->thv", kernel.astype(bf16), value_heads, preferred_element_type=f32)
        )
        denom_parts.append(jnp.sum(kernel, axis=-1).T)
    numerator = (
        jnp.concatenate(numer_parts, axis=0)
        + jnp.einsum("thn,hnv->thv", query_feat, carry_state, precision=highest)
        * carry_weight[:, :, None]
    )
    denominator = (
        jnp.concatenate(denom_parts, axis=0)
        + jnp.einsum("thn,hn->th", query_feat, carry_sum, precision=highest) * carry_weight
    )
    attended = numerator / denominator[:, :, None]
    attended_low = attended.reshape(block_len, heads_local * VHEAD).astype(bf16)
    attn_partial = dot_t(attended_low, w_out_t).astype(bf16)
    middle_own = inputs_own + tp_scatter(attn_partial)
    scale_second = rms_scale(middle_own)
    normed_second = middle_own * scale_second
    hidden_second = tp_gather((normed_second * gain_second).astype(bf16))
    gate_up = dot(hidden_second, w_gate_up)
    gate_value, upward = gate_up[:, :ff_cols], gate_up[:, ff_cols:]
    sigmoid_gate = jax.nn.sigmoid(gate_value)
    silu_gate = gate_value * sigmoid_gate
    mixed_rows = (silu_gate * upward).astype(bf16)
    grad_down_t = dot_tt(grad_full, mixed_rows).astype(bf16)

    def by_distance(stack):
        return {k: stack[j * chunk : (j + 1) * chunk] for j, k in enumerate(relative)}

    sum_down_t = ring_scatter(by_distance(grad_down_t))
    mlp_own = tp_scatter(dot_t(mixed_rows, w_down_t).astype(bf16))
    block_output = to_relative((middle_own + mlp_own).astype(bf16), to_abs, chunk)

    grad_mixed = dot(grad_full, w_down_t).astype(bf16).astype(f32)
    grad_gate = (
        grad_mixed * upward * sigmoid_gate * (1.0 + gate_value * (1.0 - sigmoid_gate))
    ).astype(bf16)
    grad_upward = (grad_mixed * silu_gate).astype(bf16)
    grad_gate_up = jnp.concatenate([grad_gate, grad_upward], axis=1)
    hidden_partial = dot_t(grad_gate_up, w_gate_up).astype(bf16)
    sum_gate_up = ring_scatter(by_distance(dot_tt(hidden_second, grad_gate_up).astype(bf16)))
    grad_hidden = tp_scatter(hidden_partial)
    grad_middle = grad_own.astype(f32) + norm_back(
        grad_hidden, normed_second, scale_second, gain_second
    )
    grad_branch = tp_gather(grad_middle.astype(bf16))
    sum_out_t = ring_scatter(by_distance(dot_tt(grad_branch, attended_low).astype(bf16)))
    grad_attended = dot(grad_branch, w_out_t).reshape(block_len, heads_local, VHEAD)
    grad_numer = (grad_attended / denominator[:, :, None]).astype(bf16)
    grad_denom = -jnp.sum(grad_attended * attended, axis=-1) / denominator
    grad_numer_carried = grad_numer.astype(f32) * carry_weight[:, :, None]
    grad_denom_carried = grad_denom * carry_weight
    grad_state_in = jnp.einsum("thn,thv->hnv", query_feat, grad_numer_carried, precision=highest)
    grad_sum_in = jnp.einsum("thn,th->hn", query_feat, grad_denom_carried, precision=highest)
    grad_query_feat = (
        jnp.einsum("thv,hnv->thn", grad_numer_carried, carry_state, precision=highest)
        + grad_denom_carried[:, :, None] * carry_sum[None]
    )
    grad_state_out, grad_sum_out = carried([grad_state_in, grad_sum_in], resets, -1)
    grad_key_feat = (
        jnp.einsum("thv,hnv->thn", value_float, grad_state_out, precision=highest)
        + grad_sum_out[None]
    ) * last_mask[:, None, None]
    grad_value_state = jnp.einsum("thn,hnv->thv", key_feat, grad_state_out, precision=highest)
    grad_query_parts = []
    grad_key_inner = jnp.zeros((block_len, heads_local, FEAT), f32)
    grad_value_inner = jnp.zeros((block_len, heads_local, VHEAD), f32)
    for first_row in range(0, block_len, step_rows):
        query_part = query_heads[first_row : first_row + step_rows]
        scores, allowed, kernel = pair_block(
            query_part, key_heads, row_ids, positions, first_row, step_rows
        )
        numer_grad_part = grad_numer[first_row : first_row + step_rows]
        grad_weights = jnp.einsum(
            "thv,shv->hts", numer_grad_part, value_heads, preferred_element_type=f32
        )
        grad_scores = (
            (grad_weights + grad_denom[first_row : first_row + step_rows].T[:, :, None])
            * allowed[None]
            * (1.0 + scores)
        ).astype(bf16)
        grad_query_parts.append(
            jnp.einsum("hts,shf->thf", grad_scores, key_heads, preferred_element_type=f32) * 0.25
        )
        grad_key_inner = (
            grad_key_inner
            + jnp.einsum("hts,thf->shf", grad_scores, query_part, preferred_element_type=f32) * 0.25
        )
        grad_value_inner = grad_value_inner + jnp.einsum(
            "hts,thv->shv", kernel.astype(bf16), numer_grad_part, preferred_element_type=f32
        )
    grad_query = (
        jnp.concatenate(grad_query_parts, axis=0) + feature_grad(query_float, grad_query_feat)
    ).astype(bf16)
    grad_key = (grad_key_inner + feature_grad(key_float, grad_key_feat)).astype(bf16)
    grad_value = (grad_value_inner + grad_value_state).astype(bf16)
    grad_qkv = jnp.concatenate(
        [
            grad_query.reshape(block_len, heads_local * FEAT),
            grad_key.reshape(block_len, heads_local * FEAT),
            grad_value.reshape(block_len, heads_local * VHEAD),
        ],
        axis=1,
    )
    sum_qkv = ring_scatter(by_distance(dot_tt(hidden_first, grad_qkv).astype(bf16)))
    grad_hidden_first = tp_scatter(dot_t(grad_qkv, w_qkv).astype(bf16))
    scale_first = rms_scale(inputs_own)
    normed_first = inputs_own * scale_first
    grad_input = to_relative(
        grad_middle + norm_back(grad_hidden_first, normed_first, scale_first, gain_first),
        to_abs,
        chunk,
    )

    gain_terms = jnp.stack(
        [
            jnp.sum(qkv_own.astype(f32) * sum_qkv, axis=1),
            jnp.sum(gate_up_own.astype(f32) * sum_gate_up, axis=1),
        ]
    )
    gain_sums = tp_sum(gain_terms) / gains.astype(f32)
    return (
        block_output,
        grad_input,
        gain_sums[0],
        sum_qkv[:, :qk_cols],
        sum_qkv[:, qk_cols : 2 * qk_cols],
        sum_qkv[:, 2 * qk_cols :],
        sum_out_t.T,
        gain_sums[1],
        sum_gate_up[:, :ff_cols],
        sum_gate_up[:, ff_cols:],
        sum_down_t.T,
    )


def solution(mesh):
    in_specs = (
        P(("seq", "tp"), None),
        P(),
        P("seq"),
        P("seq", "tp"),
        P("seq", "tp"),
        P("seq", "tp"),
        P("tp", "seq"),
        P("seq"),
        P("seq", "tp"),
        P("seq", "tp"),
        P("tp", "seq"),
        P(("seq", "tp"), None),
    )
    out_specs = (
        P(("seq", "tp"), None),
        P(("seq", "tp"), None),
        P("seq"),
        P("seq", "tp"),
        P("seq", "tp"),
        P("seq", "tp"),
        P("tp", "seq"),
        P("seq"),
        P("seq", "tp"),
        P("seq", "tp"),
        P("tp", "seq"),
    )
    small = mesh.shape["seq"] == 8 and mesh.shape["tp"] == 4
    body = on_device_rings if small else on_device
    return jax.shard_map(
        body, mesh=mesh, in_specs=in_specs, out_specs=out_specs, check_vma=False
    )
```

```python
import jax
import jax.numpy as jnp
import numpy as np
from jax import lax
from jax.experimental import pallas as pl
from jax.experimental.pallas import tpu as pltpu
from jax.sharding import PartitionSpec as P

FEAT = 16
VHEAD = 128


epsilon = 1e-05
linear_coef = 0.5
square_coef = 0.17677669529663687
highest = lax.Precision.HIGHEST
f32 = jnp.float32
bf16 = jnp.bfloat16


def ring_order(count):
    planes = 4 if count % 4 == 0 else 2
    columns = count // planes
    order = [z * columns for z in range(planes)]
    for z in reversed(range(planes)):
        xs = list(range(1, columns))
        if (planes - 1 - z) % 2:
            xs.reverse()
        order += [z * columns + x for x in xs]
    return order


def relative_list(count):
    half = count // 2
    out = []
    for j in range(1, half):
        out += [j, count - j]
    return out + [half, 0]


def ring_perms(count):
    ring = ring_order(count)
    fwd = [(ring[i], ring[(i + 1) % count]) for i in range(count)]
    return fwd, [(b, a) for a, b in fwd]


def ring_gather(own, half_rows):
    count = lax.axis_size("seq")
    fwd, bwd = ring_perms(count)
    half = count // 2
    got = {0: own}
    ahead = back = own
    for step in range(1, half):
        ahead = lax.ppermute(ahead, "seq", fwd)
        back = lax.ppermute(back, "seq", bwd)
        got[step] = ahead
        got[count - step] = back
    ahead = lax.ppermute(ahead[:half_rows], "seq", fwd)
    back = lax.ppermute(back[half_rows:], "seq", bwd)
    got[half] = jnp.concatenate([ahead, back], axis=0)
    return got


def ring_scatter(chunks):
    count = lax.axis_size("seq")
    fwd, bwd = ring_perms(count)
    half = chunks[0].shape[0] // 2
    ahead = chunks[1][:half]
    back = chunks[count - 1][half:]
    for step in range(count - 1):
        ahead = lax.ppermute(ahead, "seq", fwd).astype(f32)
        back = lax.ppermute(back, "seq", bwd).astype(f32)
        last = step == count - 2
        ahead = ahead + chunks[0 if last else 2 + step][:half].astype(f32)
        back = back + chunks[0 if last else count - 2 - step][half:].astype(f32)
        if not last:
            ahead = ahead.astype(bf16)
            back = back.astype(bf16)
    return jnp.concatenate([ahead, back], axis=0)


def to_relative(array, index_row, chunk):
    return jnp.concatenate(
        [lax.dynamic_slice_in_dim(array, i * chunk, chunk, 1) for i in index_row], axis=1
    )


def tp_perms(count):
    ys = count // 2
    core = [(i, i ^ 1) for i in range(count)]
    shift = [
        [(i, (((i // 2) + d) % ys) * 2 + i % 2) for i in range(count)] for d in range(ys)
    ]
    return core, shift


def tp_gather(own):
    count = lax.axis_size("tp")
    ys = count // 2
    place = lax.axis_index("tp")
    y, c = place // 2, place % 2
    core, shift = tp_perms(count)
    parts = [own] + [lax.ppermute(own, "tp", shift[d]) for d in range(1, ys)]
    mine = jnp.stack([lax.select_n((y - at + ys) % ys, *parts) for at in range(ys)])
    other = lax.ppermute(mine, "tp", core)
    full = jnp.stack([jnp.where(c == 0, mine, other), jnp.where(c == 0, other, mine)], axis=1)
    return full.reshape((count * own.shape[0],) + own.shape[1:])


def tp_scatter(partial):
    count = lax.axis_size("tp")
    ys = count // 2
    place = lax.axis_index("tp")
    y, c = place // 2, place % 2
    core, shift = tp_perms(count)
    blocks = partial.reshape((ys, 2, partial.shape[0] // count) + partial.shape[1:])
    sent = lax.dynamic_index_in_dim(blocks, 1 - c, 1, False)
    kept = lax.dynamic_index_in_dim(blocks, c, 1, False)
    pair = kept.astype(f32) + lax.ppermute(sent, "tp", core).astype(f32)
    low = pair.astype(bf16)
    own = lax.dynamic_index_in_dim(pair, y, 0, False)
    for d in range(1, ys):
        away = lax.dynamic_index_in_dim(low, (y + d) % ys, 0, False)
        own = own + lax.ppermute(away, "tp", shift[d]).astype(f32)
    return own


def tp_sum(vector):
    count = lax.axis_size("tp")
    core, shift = tp_perms(count)
    vector = vector + lax.ppermute(vector, "tp", core)
    return vector + sum(lax.ppermute(vector, "tp", shift[d]) for d in range(1, count // 2))


def carried(arrays, resets, step):
    count = lax.axis_size("seq")
    place = lax.axis_index("seq")

    def from_near(a, d):
        perm = [(i, i + d * step) for i in range(count) if 0 <= i + d * step < count]
        return lax.ppermute(a.astype(bf16), "seq", perm).astype(f32)

    def reset_within(d):
        at = jnp.arange(count)
        away = (place - at) * step
        return jnp.sum(jnp.where((away >= 1) & (away <= d), resets, 0)) > 0

    arrays = [from_near(a, 1) for a in arrays]
    d = 1
    while d < count - 1:
        keep = 1.0 - reset_within(d).astype(f32)
        arrays = [a + keep * from_near(a, d) for a in arrays]
        d *= 2
    return arrays


def features(vector):
    squares = (vector[..., :, None] * vector[..., None, :]).reshape(
        vector.shape[:-1] + (vector.shape[-1] * vector.shape[-1],)
    )
    return jnp.concatenate(
        [jnp.ones_like(vector[..., :1]), vector * linear_coef, squares * square_coef], axis=-1
    )


def feature_grad(vector, grad_feat):
    feat_width = vector.shape[-1]
    linear_part = grad_feat[..., 1 : 1 + feat_width]
    square_part = grad_feat[..., 1 + feat_width :].reshape(vector.shape + (feat_width,))
    mixed_part = jnp.sum(square_part * vector[..., None, :], axis=-1) + jnp.sum(
        square_part * vector[..., :, None], axis=-2
    )
    return linear_coef * linear_part + square_coef * mixed_part


def segment_masks(anchor, starts, length):
    positions = anchor + jnp.arange(length, dtype=jnp.int32)
    start_le = starts[None, :] <= positions[:, None]
    row_ids = jnp.sum(start_le.astype(jnp.int32), axis=1)
    inside = (starts >= anchor) & (starts < anchor + length)
    carry = jnp.sum(((starts[None, :] >= anchor) & start_le).astype(jnp.int32), axis=1) == 0
    after_last = (
        jnp.sum(
            ((starts[None, :] > positions[:, None]) & inside[None, :]).astype(jnp.int32), axis=1
        )
        == 0
    )
    return (positions, row_ids, carry, after_last)


def rms_scale(values):
    return lax.rsqrt(jnp.mean(values * values, axis=-1, keepdims=True) + epsilon)


def norm_back(grad_out, normed, scale, gain):
    grad_normed = grad_out * gain
    return scale * (grad_normed - normed * jnp.mean(grad_normed * normed, axis=-1, keepdims=True))


def pair_block(query_part, key_heads, row_ids, positions, first_row, span_rows):
    scores = (
        jnp.einsum("thf,shf->hts", query_part, key_heads, preferred_element_type=f32) * 0.25
    )
    rows_here = row_ids[first_row : first_row + span_rows]
    place_here = positions[first_row : first_row + span_rows]
    allowed = (
        (rows_here[:, None] == row_ids[None, :]) & (positions[None, :] <= place_here[:, None])
    ).astype(f32)
    kernel = (1.0 + scores + 0.5 * scores * scores) * allowed[None]
    return (scores, allowed, kernel)


def dot(a, b):
    return jnp.dot(a, b, preferred_element_type=f32)


def dot_t(a, b):
    return lax.dot_general(a, b, (((1,), (1,)), ((), ())), preferred_element_type=f32)


def dot_tt(a, b):
    return lax.dot_general(a, b, (((0,), (0,)), ((), ())), preferred_element_type=f32)


def ring_place(seq):
    z, x = seq // 2, seq % 2
    return z + x * (7 - 2 * z)


def ring_seq(place):
    place = lax.rem(place + 8, 8)
    far = place // 4
    return (1 - far) * 2 * place + far * (15 - 2 * place)


class Sems:
    def __init__(self, ref):
        self.ref, self.used = ref, 0

    def take(self):
        self.used += 1
        return self.ref.at[self.used - 1]


class Links:
    def __init__(self, send, recv):
        self.send, self.recv, self.sent = Sems(send), Sems(recv), []

    def copy(self, src, dst, **to):
        return pltpu.make_async_remote_copy(
            src_ref=src,
            dst_ref=dst,
            send_sem=self.send.take(),
            recv_sem=self.recv.take(),
            device_id=to,
            device_id_type=pl.DeviceIdType.MESH,
        )

    def start(self, src, dst, **to):
        made = self.copy(src, dst, **to)
        made.start()
        self.sent.append(made)
        return made

    def sent_now(self, some):
        for made in some:
            made.wait_send()
        self.sent = [made for made in self.sent if all(made is not other for other in some)]

    def finish(self):
        for made in self.sent:
            made.wait_send()


class Gather:
    def __init__(self, links, arrays, split, nearby, gangs):
        self.links, self.arrays, self.split, self.nearby = links, arrays, split, nearby
        self.at = {k: j for j, k in enumerate(relative_list(8))}
        self.flying, self.gangs, self.done = {}, gangs, 0
        self.gang_of = {a: i for i, gang in enumerate(gangs) for a in gang}
        self.events = [
            (a, step, way, part)
            for gang in gangs
            for step in (1, 2, 3, 4)
            for a in gang
            for part in (0, 1)
            for way in (0, 1)
            if step < 4 or way == part
        ]
        for a in gangs[0]:
            for part in (0, 1):
                for way in (0, 1):
                    self.go(a, 1, way, part)

    def rows(self, part):
        return pl.ds(part * self.split, self.split)

    def go(self, a, step, way, part):
        own, everyone = self.arrays[a]
        before, after = (step - 1, step) if way == 0 else ((9 - step) % 8, 8 - step)
        src = own if step == 1 else everyone.at[self.at[before]]
        self.flying[a, step, way, part] = self.links.start(
            src.at[self.rows(part)],
            everyone.at[self.at[after], self.rows(part)],
            seq=self.nearby[way],
        )

    def pump(self, upto):
        while self.done < min(upto, len(self.events)):
            a, step, way, part = self.events[self.done]
            self.flying[a, step, way, part].wait_recv()
            if step < 3 or (step == 3 and way == part):
                self.go(a, step + 1, way, part)
            i = self.gang_of[a]
            if step == 3 and i + 1 < len(self.gangs):
                mine, later = self.gangs[i].index(a), self.gangs[i + 1]
                last = mine == len(self.gangs[i]) - 1
                for other in later[mine:] if last else later[mine : mine + 1]:
                    self.go(other, 1, way, part)
            self.done += 1

    def pump_array(self, a):
        gang = self.gang_of[a]
        self.pump(14 * sum(len(g) for g in self.gangs[: gang + 1]))


def greet(peers):
    barrier = pltpu.get_barrier_semaphore()
    for peer in peers:
        pl.semaphore_signal(
            barrier, inc=1, device_id=peer, device_id_type=pl.DeviceIdType.MESH
        )
    pl.semaphore_wait(barrier, len(peers))


def places():
    seq, tp = lax.axis_index("seq"), lax.axis_index("tp")
    place = ring_place(seq)
    nearby = (ring_seq(place + 1), ring_seq(place - 1))
    over_y = lax.rem(tp + 2, 4)
    over_core = tp + 1 - 2 * (tp % 2)
    peers = [{"seq": ring_seq(place + k)} for k in range(1, 8)]
    peers += [{"tp": over_y}, {"tp": over_core}]
    return seq, tp, place, nearby, over_y, over_core, peers


class Rows:
    def __init__(self, links, own, everyone, tp, over_y, over_core, rows):
        self.links, self.all, self.tp = links, everyone, tp
        self.over_y, self.over_core, self.rows = over_y, over_core, rows
        half = rows // 2
        self.first = [
            links.start(
                own.at[pl.ds(i * half, half)], self.block(tp, i * half, half), tp=over_y
            )
            for i in (0, 1)
        ]
        self.near = links.start(own, self.block(tp, 0, rows), tp=over_core)
        self.last = []

    def block(self, owner, offset, size):
        return self.all.at[pl.ds(pl.multiple_of(owner * self.rows + offset, 16), size)]

    def forward(self, i):
        half = self.rows // 2
        self.first[i].wait_recv()
        came = self.block(self.over_y, i * half, half)
        self.last.append(self.links.start(came, came, tp=self.over_core))

    def finish(self):
        self.near.wait_recv()
        for made in self.last:
            made.wait_recv()


FEATS = 160


def fill_tables(lengths, seq, tok, line, coefs, step):
    total = tok.shape[0]
    anchor = seq * total
    starts, at = [], 0
    for i in range(lengths.shape[0]):
        starts.append(at)
        at = at + lengths[i]

    def places_of(shape, axis):
        pos = lax.broadcasted_iota(jnp.int32, shape, axis)
        low = jnp.zeros(shape, jnp.int32) - anchor
        last = jnp.ones(shape, f32)
        for start in starts:
            here = start - anchor
            low = jnp.maximum(low, jnp.where(pos >= here, here, -anchor))
            last = jnp.where((pos < here) & (here < total), 0.0, last)
        return pos.astype(f32), low, last

    lane = lax.broadcasted_iota(jnp.int32, (total, 128), 1)
    pos, low, last = places_of((total, 128), 0)
    began = jnp.where(low < 0, 1.0, 0.0)
    first = jnp.maximum(low, 0).astype(f32)
    tok[...] = jnp.where(
        lane == 0, first, jnp.where(lane == 1, began, jnp.where(lane == 2, last, pos))
    )
    pos, low, last = places_of((8, total), 1)
    row = lax.broadcasted_iota(jnp.int32, (8, total), 0)
    line[...] = jnp.where(row == 0, pos, jnp.maximum(low, 0).astype(f32))

    def clear(lo, hi):
        free = jnp.ones((1, 128), f32)
        for start in starts:
            at = jnp.zeros((1, 128), jnp.int32) + start
            free = jnp.where((at >= lo * total) & (at < (hi + 1) * total), 0.0, free)
        return free

    z = seq // 2
    one = jnp.ones((1, 128), f32)
    first, second = clear(2 * z, 2 * z), clear(2 * z + 1, 2 * z + 1)
    before = 2 * (z - step)
    rows = [second, first] if step > 0 else [first, second]
    rows += [first * second, clear(before, before + 1)]
    coefs[...] = jnp.concatenate(rows + [one * 0.0] * 4, axis=0)


class Exchange:
    def __init__(self, links, st, near, term, first, second, given, states, coefs, seq, step):
        z, x = seq // 2, seq % 2
        self.st, self.near, self.term, self.first, self.second = st, near, term, first, second
        self.given, self.states, self.coefs, self.x = given, states, coefs, x
        self.turn = z if step > 0 else 3 - z
        self.late = x if step > 0 else 1 - x
        over_x = seq + 1 - 2 * x
        self.half = links.start(st.at[pl.ds(2 * (1 - x), 2)], near, seq=over_x)
        self.hop = links.copy(term, first, seq=seq + 2 * step)
        self.on = links.copy(term, second, seq=seq + 2 * step)
        self.far = links.copy(term, second, seq=seq + 4 * step)
        self.links, self.over_x = links, over_x

    def coef(self, k):
        return self.coefs[k : k + 1, :]

    def pair(self):
        self.half.wait_recv()
        for i in (0, 1):
            mine, theirs = self.st[2 * self.x + i].astype(f32), self.near[i].astype(f32)
            early = jnp.where(self.late == 0, mine, theirs)
            later = jnp.where(self.late == 0, theirs, mine)
            self.term[i] = (later + self.coef(0) * early).astype(bf16)

        @pl.when(self.turn % 2 == 0)
        def _():
            self.hop.start()

    def planes(self):
        @pl.when(self.turn % 2 == 1)
        def _():
            self.hop.wait_recv()

        @pl.when(self.turn == 1)
        def _():
            for i in (0, 1):
                came = self.coef(2) * self.first[i].astype(f32)
                self.term[i] = (self.term[i].astype(f32) + came).astype(bf16)
            self.on.start()
            self.far.start()

    def give(self):
        x = self.x
        for i in (0, 1):
            self.states[2 * x + i] = jnp.zeros((256, 128), f32)
            self.states[2 * (1 - x) + i] = jnp.zeros((256, 128), f32)

        def enter(i):
            return self.states.at[2 * x + i, pl.ds(0, 176)]

        @pl.when(self.turn == 1)
        def _():
            for i in (0, 1):
                enter(i)[...] = self.first[i].astype(f32)

        @pl.when(self.turn == 2)
        def _():
            self.on.wait_recv()
            for i in (0, 1):
                enter(i)[...] = self.second[i].astype(f32)

        @pl.when(self.turn == 3)
        def _():
            self.far.wait_recv()
            for i in (0, 1):
                older = self.coef(3) * self.second[i].astype(f32)
                enter(i)[...] = self.first[i].astype(f32) + older

        for i in (0, 1):
            came = enter(i)[...]
            mine, theirs = self.st[2 * x + i].astype(f32), self.near[i].astype(f32)
            early = jnp.where(self.late == 0, mine, theirs)
            passed = early + self.coef(1) * came
            self.given[0, i] = jnp.where(self.late == 0, passed, came).astype(bf16)
            enter(i)[...] = jnp.where(self.late == 0, came, passed)
        self.back = self.links.start(self.given.at[0], self.given.at[1], seq=self.over_x)

    def take(self):
        self.back.wait_recv()
        for i in (0, 1):
            self.states[2 * (1 - self.x) + i, 0:176, :] = self.given[1, i].astype(f32)

    def finish(self):
        @pl.when(self.turn % 2 == 0)
        def _():
            self.hop.wait_send()

        @pl.when(self.turn == 1)
        def _():
            self.on.wait_send()
            self.far.wait_send()


def ring_columns(place):
    return [pl.ds(pl.multiple_of(ring_seq(place - k) * 256, 256), 256) for k in relative_list(8)]


def phi(heads, h, select_a, select_b, lanes):
    a = dot(heads, select_a[h]) + lanes[0:1, :]
    b = dot(heads, select_b[h]) + lanes[1:2, :]
    return a, b


def fwd_kernel(
    lengths, sa_ref, sb_ref, lanes_ref, hm_ref, gain_first, gain_second,
    x_in, wq_in, wk_in, wv_in, wo_in, wg_in, wu_in, wd_in, c_in,
    wq_all, wo_all, wg_all, wu_all, wd_all, c_all,
    h1_out, qkv_out, yb_out, den_out, x1_out, h2_out, gate_out, up_out, m_out, sin_out, gain_out, terms_out,
    x_ref, tok_ref, line_ref, coef_ref, gain_ref, q_own, o_own, g_own, u_own, d_own,
    w_small, w_v, w_o, w_d, w_g,
    xg, h1, wq, wo, wg, wu, qkv, kq, num, den, yb, sc, rc, sy, ry, x1, gate, up, mm,
    gains_all, gains, st, st_x, st_t, st_z, st_y, st_g, s_in,
    send, recv, local,
):
    seq, tp, place, nearby, over_y, over_core, peers = places()
    z, x = seq // 2, seq % 2
    at = {k: j for j, k in enumerate(relative_list(8))}
    rows = x_ref.shape[0]
    total = 4 * rows
    links = Links(send, recv)
    locs = Sems(local)
    pending = []

    def store(src, dst):
        made = pltpu.make_async_copy(src, dst, locs.take())
        made.start()
        pending.append(made)

    def load(src, dst):
        made = pltpu.make_async_copy(src, dst, locs.take())
        made.start()
        return made

    got_qk = [load(wq_in, w_small.at[0:64]), load(wk_in, w_small.at[64:128]), load(wv_in, w_v)]
    columns = ring_columns(place)
    got_x = [load(x_in.at[:, c], x_ref.at[:, col(j)]) for j, c in enumerate(columns)]
    c_rows = pl.ds(pl.multiple_of(tp * rows, rows), rows)
    got_c = [load(c_in.at[:, c], c_all.at[c_rows, col(j)]) for j, c in enumerate(columns)]
    got_o = load(wo_in, w_o)
    ff = wd_in.shape[0]
    got_g = load(wg_in, w_g.at[pl.ds(0, ff)])
    got_d = load(wd_in, w_d.at[pl.ds(0, ff)])

    def turn(src, dst):
        for i in range(0, ff, 128):
            size = min(128, ff - i)
            dst[:, i : i + size] = src[i : i + 128, :].T[:, :size].astype(bf16)

    gain_ref[...] = jnp.concatenate(
        [gain_first[...], gain_second[...], jnp.zeros((14, 256), f32)], axis=0
    ).astype(bf16)
    greet(peers)
    gain_flying = [
        links.start(gain_ref, gains_all.at[at[k]], seq=ring_seq(place + k)) for k in range(1, 8)
    ]
    for made in got_x:
        made.wait()
    xrows = Rows(links, x_ref, xg, tp, over_y, over_core, rows)
    for made in got_qk:
        made.wait()
    q_own[:, 0:128] = w_small[...].T.astype(bf16)
    q_own[:, 128:640] = w_v[...].astype(bf16)
    ring = Gather(
        links,
        [(q_own, wq_all), (o_own, wo_all), (g_own, wg_all), (u_own, wu_all), (d_own, wd_all)],
        128,
        nearby,
        [[0], [1], [2, 3], [4]],
    )
    own_in = [
        load(x_ref, xrows.block(tp, 0, rows)),
        load(gain_ref, gains_all.at[at[0]]),
    ]
    got_o.wait()
    o_own[...] = w_o[...].T.astype(bf16)
    ring.pump(2)
    got_g.wait()
    turn(w_g, g_own)
    got_u = load(wu_in, w_g.at[pl.ds(0, ff)])
    ring.pump(4)
    got_d.wait()
    turn(w_d, d_own)
    got_u.wait()
    turn(w_g, u_own)
    own_kept = [load(own, everyone.at[at[0]]) for own, everyone in ring.arrays]
    fill_tables(lengths, seq, tok_ref, line_ref, coef_ref, 1)

    ring.pump(6)
    xrows.forward(0)
    for made in gain_flying:
        made.wait_recv()
    for made in own_in:
        made.wait()
    for j in range(8):
        chunk = gains_all[j].astype(f32)
        gains[0:8, j * 256 : (j + 1) * 256] = chunk[0:8]
    ring.pump(10)
    xrows.forward(1)
    ring.pump_array(0)
    own_kept[0].wait()
    got = load_weights(load, wq_all, wq)
    xrows.finish()

    def norm_first(i, _):
        r = pl.ds(pl.multiple_of(i * 32, 32), 32)
        v = xg[r, :].astype(f32)
        s = lax.rsqrt(jnp.mean(v * v, axis=1, keepdims=True) + epsilon)
        h1[r, :] = (v * s * gains[0:1, :]).astype(bf16)
        return 0

    lax.fori_loop(0, total // 32, norm_first, 0)
    links.sent_now(xrows.last)
    kept_h1 = load(h1, h1_out)
    for made in got_c:
        made.wait()
    crows = Rows(links, c_all.at[c_rows], c_all, tp, over_y, over_core, rows)
    ring.pump(15)
    for made in got:
        made.wait()

    def project(i, _):
        r = pl.ds(pl.multiple_of(i * 256, 256), 256)
        res = dot(h1[r, :], wq[...])
        qkv[r, :] = res.astype(bf16)
        kq[r, :] = pltpu.roll(res[:, :128], 64, 1).astype(bf16)
        return 0

    lax.fori_loop(0, total // 256, project, 0)
    store(qkv, qkv_out)
    ring.pump(16)

    heads = 4

    def head_v(h):
        return slice(128 + h * 128, 256 + h * 128)

    for h in range(heads):

        def state(i, c, h=h):
            s, zz = c
            r = pl.ds(pl.multiple_of(i * 256, 256), 256)
            a, b = phi(kq[r, :], h, sa_ref, sb_ref, lanes_ref)
            f = a * b * lanes_ref[2:3, :] * tok_ref[r, 2:3]
            s = s + dot_tt(f.astype(bf16), qkv[r, head_v(h)])
            return s, zz + jnp.sum(f, axis=0, keepdims=True)

        s, zz = lax.fori_loop(
            0, total // 256, state, (jnp.zeros((256, 128), f32), jnp.zeros((1, 256), f32))
        )
        pack_state(st, h, s, zz)
        ring.pump(17 + h)
    moved = Exchange(links, st, st_x, st_t, st_z, st_y, st_g, s_in, coef_ref, seq, 1)

    def local_head(h):
        for i in range(total // 256):
            r = slice(i * 256, (i + 1) * 256)
            span = (i + 1) * 256
            qm = (qkv[r, :128].astype(f32) * hm_ref[h : h + 1, :]).astype(bf16)
            u = dot_t(qm, kq[:span, :])
            keep = (line_ref[0:1, :span] >= tok_ref[r, 0:1]) & (
                line_ref[0:1, :span] <= tok_ref[r, 3:4]
            )
            kap = jnp.where(keep, (0.5 * u + 1.0) * u + 1.0, 0.0)
            den[r, h : h + 1] = jnp.sum(kap, axis=1, keepdims=True)
            num[r, h * 128 : (h + 1) * 128] = dot(kap.astype(bf16), qkv[:span, head_v(h)])

    local_head(0)
    ring.pump(22)
    moved.pair()
    local_head(1)
    ring.pump(24)
    moved.planes()
    local_head(2)
    ring.pump(26)
    moved.give()
    local_head(3)
    ring.pump(28)
    moved.take()
    store(s_in, sin_out)
    for h in range(heads):
        z_row = jnp.concatenate([s_in[h, 160:161, :], s_in[h, 161:162, :]], axis=1)
        feat = jax.lax.broadcasted_iota(jnp.int32, (256, 128), 0)
        s_low = jnp.where(feat < FEATS, s_in[h], 0.0).astype(bf16)

        def carry(i, _, h=h, z_row=z_row, s_low=s_low):
            r = pl.ds(pl.multiple_of(i * 256, 256), 256)
            a, b = phi(qkv[r, 0:128], h, sa_ref, sb_ref, lanes_ref)
            f = a * b * lanes_ref[2:3, :] * tok_ref[r, 1:2]
            hv = slice(h * 128, (h + 1) * 128)
            top = num[r, hv] + dot(f.astype(bf16), s_low)
            low = den[r, h : h + 1] + jnp.sum(f * z_row, axis=1, keepdims=True)
            den[r, h : h + 1] = low
            y = top / low
            yb[r, hv] = y.astype(bf16)
            return 0

        lax.fori_loop(0, total // 256, carry, 0)
        ring.pump(28 + (h + 1) // 2)
    store(yb, yb_out)
    store(den, den_out)
    ring.pump_array(1)
    own_kept[1].wait()
    got = load_weights(load, wo_all, wo)
    for made in got:
        made.wait()

    y_at, c_at = tp // 2, tp % 2

    def out_rows(block):
        return yb[pl.ds(pl.multiple_of(block * rows, rows), rows), :]

    cols = 512
    to_core = []
    for yy in (0, 1):

        def core_cols(i, _, yy=yy):
            c = pl.ds(pl.multiple_of(i * cols, cols), cols)
            sc[yy, :, c] = dot_t(out_rows(yy * 2 + 1 - c_at), wo[c, :]).astype(bf16)
            return 0

        lax.fori_loop(0, 2048 // cols, core_cols, 0)
        to_core.append(links.start(sc.at[yy], rc.at[yy], tp=over_core))
    for made in to_core:
        made.wait_recv()
    ring.pump(32)

    def away_cols(i, _):
        c = pl.ds(pl.multiple_of(i * cols, cols), cols)
        part = dot_t(out_rows((1 - y_at) * 2 + c_at), wo[c, :])
        sy[:, c] = (part + rc[1 - y_at, :, c].astype(f32)).astype(bf16)
        return 0

    lax.fori_loop(0, 2048 // cols, away_cols, 0)
    to_y = links.start(sy, ry, tp=over_y)

    def own_cols(i, _):
        c = pl.ds(pl.multiple_of(i * cols, cols), cols)
        x1[:, c] = (
            dot_t(out_rows(tp), wo[c, :]) + rc[y_at, :, c].astype(f32) + x_ref[:, c].astype(f32)
        )
        return 0

    lax.fori_loop(0, 2048 // cols, own_cols, 0)
    ring.pump(34)
    to_y.wait_recv()
    ring.pump(37)

    links.sent_now(xrows.first + [xrows.near])
    ho = x_ref

    def norm_second(i, _):
        r = pl.ds(pl.multiple_of(i * 32, 32), 32)
        v = x1[r, :] + ry[r, :].astype(f32)
        x1[r, :] = v
        s = lax.rsqrt(jnp.mean(v * v, axis=1, keepdims=True) + epsilon)
        ho[r, :] = (v * s * gains[1:2, :]).astype(bf16)
        return 0

    lax.fori_loop(0, rows // 32, norm_second, 0)
    store(x1, x1_out)
    store(gains, gain_out)
    h2 = xg
    hrows = Rows(links, ho, h2, tp, over_y, over_core, rows)
    own_in = load(ho, hrows.block(tp, 0, rows))
    ring.pump(40)
    hrows.forward(0)
    ring.pump(43)
    hrows.forward(1)
    crows.forward(0)
    crows.forward(1)
    hrows.finish()
    crows.finish()
    own_in.wait()
    store(h2, h2_out)
    kept_h1.wait()
    got_c = load(c_all, h1)
    ring.pump_array(2)
    own_kept[2].wait()
    got = load_weights(load, wg_all, wg)
    ring.pump_array(3)
    own_kept[3].wait()
    got += load_weights(load, wu_all, wu)
    for made in got:
        made.wait()

    def gate_up(i, _):
        r = pl.ds(pl.multiple_of(i * 128, 128), 128)
        g = dot(h2[r, :], wg[...])
        uu = dot(h2[r, :], wu[...])
        gate[r, :] = g.astype(bf16)
        up[r, :] = uu.astype(bf16)
        mm[r, :] = (g * jax.nn.sigmoid(g) * uu).astype(bf16)
        return 0

    for quarter in range(4):
        lax.fori_loop(quarter * total // 512, (quarter + 1) * total // 512, gate_up, 0)
        ring.pump(58 + 2 * quarter)
    store(gate, gate_out)
    store(up, up_out)
    store(mm, m_out)
    got_c.wait()
    links.sent_now([ring.flying[a, 1, way, part] for a in (2, 3) for way in (0, 1) for part in (0, 1)])
    out_sems = [locs.take(), locs.take()]
    buffers = [g_own, u_own]

    def keep_terms(j, k):
        return pltpu.make_async_copy(buffers[k], terms_out.at[col(j)], out_sems[k])

    def grad_down(i, _):
        for k in (0, 1):
            pl.when(i > 0)(lambda k=k: keep_terms(2 * i - 2 + k, k).wait())
            buffers[k][...] = dot_tt(h1[:, col(2 * i + k)], mm[...]).astype(bf16)
            keep_terms(2 * i + k, k).start()
        return 0

    lax.fori_loop(0, 2, grad_down, 0)
    ring.pump(66)
    lax.fori_loop(2, 4, grad_down, 0)
    for k in (0, 1):
        keep_terms(6 + k, k).wait()
    ring.pump_array(4)
    own_kept[4].wait()
    for made in pending:
        made.wait()
    links.finish()
    moved.finish()


def pack_state(st, h, s, zz):
    st[h, 0:FEATS, :] = s[:FEATS].astype(bf16)
    tail = jnp.concatenate([zz[:, :128], zz[:, 128:], jnp.zeros((14, 128), f32)], axis=0)
    st[h, FEATS : FEATS + 16, :] = tail.astype(bf16)


def load_weights(load, everyone, flat):
    count, chunk = everyone.shape[0], everyone.shape[1]
    return [load(everyone.at[j], flat.at[pl.ds(j * chunk, chunk)]) for j in range(count)]


class Scatter:
    def __init__(self, slots, send, recv, nearby):
        self.slots, self.send, self.recv, self.nearby = slots, send, recv, nearby

    def copy(self, a, step, way, sub, src, slot, width):
        return pltpu.make_async_remote_copy(
            src_ref=src,
            dst_ref=self.piece(slot, way, sub, width),
            send_sem=self.send.at[a % 2, way, sub],
            recv_sem=self.recv.at[a % 2, way, sub, step],
            device_id={"seq": self.nearby[way]},
            device_id_type=pl.DeviceIdType.MESH,
        )

    def slot(self, a, step):
        return (a % 2) * 4 + (a // 2 * 7 + step) % 4

    def rows(self, way, sub, base=0):
        start = base + way * 128 + sub * 64
        return pl.ds(start if isinstance(start, int) else pl.multiple_of(start, 64), 64)

    def piece(self, slot, way, sub, width):
        return self.slots.at[slot, self.rows(way, sub), pl.ds(0, width)]

    def begin(self, a, own, width, column=0):
        for sub in (0, 1):
            for way in (0, 1):
                src = own.at[self.rows(way, sub, way * 256), pl.ds(column, width)]
                self.copy(a, 0, way, sub, src, self.slot(a, 0), width).start()

    def event(self, a, e, own, width, out, column=0):
        step, sub = e // 2, e % 2
        is_last = step // 6
        here = self.slot(a, step)
        far = (step + 1) // 4
        place0 = (1 - far) * 2 * (step + 1) + far * (11 - 2 * step) + is_last * 8
        far = (step + 2) // 4 - is_last
        place1 = (1 - far) * (3 + 2 * step) + far * (10 - 2 * step) + is_last * 9
        places = (place0, place1)
        for way in (0, 1):
            piece = self.piece(here, way, sub, width)
            came = self.copy(a, step, way, sub, piece, here, width)
            came.wait_recv()
            came.wait_send()

        def summed(way):
            mine = own[self.rows(way, sub, places[way] * 256), pl.ds(column, width)]
            came = self.slots[here, self.rows(way, sub), pl.ds(0, width)]
            return came.astype(f32) + mine.astype(f32)

        def on():
            for way in (0, 1):
                self.slots[here, self.rows(way, sub), pl.ds(0, width)] = summed(way).astype(bf16)
                piece = self.piece(here, way, sub, width)
                self.copy(a, step + 1, way, sub, piece, self.slot(a, step + 1), width).start()

        def end():
            for way in (0, 1):
                out[self.rows(way, sub), pl.ds(0, width)] = summed(way)

        if isinstance(e, int):
            if step < 6:
                on()
            else:
                end()
        else:
            pl.when(step < 6)(on)
            pl.when(step == 6)(end)


class TpSum:
    def __init__(self, part, from_core, from_y, sems, credits, tp, over_y, over_core):
        self.part, self.from_core, self.from_y = part, from_core, from_y
        self.sems, self.credits = sems, credits
        self.tp, self.over_y, self.over_core = tp, over_y, over_core
        self.y, self.c = tp // 2, tp % 2

    def to_core(self, i, yy):
        return pltpu.make_async_remote_copy(
            src_ref=self.part.at[i, yy * 2 + 1 - self.c],
            dst_ref=self.from_core.at[i, yy],
            send_sem=self.sems.at[yy, i],
            recv_sem=self.sems.at[2 + yy, i],
            device_id={"tp": self.over_core},
            device_id_type=pl.DeviceIdType.MESH,
        )

    def to_y(self, i):
        return pltpu.make_async_remote_copy(
            src_ref=self.part.at[i, (1 - self.y) * 2 + self.c],
            dst_ref=self.from_y.at[i],
            send_sem=self.sems.at[4, i],
            recv_sem=self.sems.at[5, i],
            device_id={"tp": self.over_y},
            device_id_type=pl.DeviceIdType.MESH,
        )

    def sent(self, i):
        self.to_core(i, 0).wait_send()
        self.to_core(i, 1).wait_send()
        self.to_y(i).wait_send()

    def offer(self, i, turn, value):
        if turn > 0:
            self.sent(i)
        for block in range(4):
            self.part[i, block] = value[block * 256 : (block + 1) * 256].astype(bf16)
        if turn > 0:
            pl.semaphore_wait(self.credits.at[0], 1)
        for yy in (0, 1):
            self.to_core(i, yy).start()

    def pass_on(self, i, turn):
        for yy in (0, 1):
            self.to_core(i, yy).wait_recv()
        away = (1 - self.y) * 2 + self.c
        self.part[i, away] = (
            self.part[i, away].astype(f32) + self.from_core[i, 1 - self.y].astype(f32)
        ).astype(bf16)
        if turn > 0:
            pl.semaphore_wait(self.credits.at[1], 1)
        self.to_y(i).start()

    def take(self, i, turn, use):
        self.to_y(i).wait_recv()
        use(
            self.part[i, self.tp].astype(f32)
            + self.from_core[i, self.y].astype(f32)
            + self.from_y[i].astype(f32)
        )
        if turn < 2:
            for k, peer in ((0, self.over_core), (1, self.over_y)):
                pl.semaphore_signal(
                    self.credits.at[k],
                    inc=1,
                    device_id={"tp": peer},
                    device_id_type=pl.DeviceIdType.MESH,
                )


def col(i, width=256):
    return pl.ds(i * width if isinstance(i, int) else pl.multiple_of(i * width, width), width)


def bwd_kernel(
    lengths, sa_ref, sb_ref, lanes_ref, hm_ref, gains, s_in, den, gain_first, gain_second,
    x_in, x1_in, wq_all, wo_all, wg_all, wu_all, wd_all, c_all, h1_all, qkv_all, yb_all, h2_all,
    gate_all, up_all, m_all, terms_all,
    d_out, g_out, u_out, oq_out, block_out, input_out, gain_out, u_kept,
    tok_ref, line_ref, coef_ref, terms, terms_core, terms_y,
    slots, s1, s2, wo, stream, hs, rows_all, mm, dup, tiles, qkv, kq, yb, dnum, dden, dden_t, dqkv,
    dq, dk, part, from_core, from_y, acc, x1, fout, st, st_x, st_t, st_z, st_y, st_g, s_back, own_rows,
    ring_send, ring_recv, tp_sems, credits, send, recv, local, tile_sems,
):
    seq, tp, place, nearby, over_y, over_core, peers = places()
    z, x = seq // 2, seq % 2
    rows, width = own_rows.shape
    total = 4 * rows
    ff = mm.shape[1]
    links = Links(send, recv)
    locs = Sems(local)

    def load(src, dst):
        made = pltpu.make_async_copy(src, dst, locs.take())
        made.start()
        return made

    def whole(everyone, flat):
        count, chunk = everyone.shape[0], everyone.shape[1]
        return [load(everyone.at[j], flat.at[pl.ds(j * chunk, chunk)]) for j in range(count)]

    got_m = load(m_all, mm)
    got_wd = whole(wd_all, s2)
    got_terms = load(terms_all, s1)
    got_c = load(c_all, rows_all)
    greet(peers)
    ring = Scatter(slots, ring_send, ring_recv, nearby)
    ring.begin(0, terms_all, ff)
    got_x1 = load(x1_in, x1)
    fill_tables(lengths, seq, tok_ref, line_ref, coef_ref, -1)
    columns = ring_columns(place)
    got_qkv = [load(qkv_all, qkv), load(yb_all, yb)]
    got_wo = whole(wo_all, wo)
    sums = TpSum(part, from_core, from_y, tp_sems, credits, tp, over_y, over_core)

    def run(n, body, pumps=None):
        def step(i, _):
            body(i)
            if pumps:
                a, first, count = pumps
                every = n // count
                pl.when((i + 1) % every == 0)(lambda: event(a, first + (i + 1) // every - 1))
            return 0

        lax.fori_loop(0, n, step, 0)

    plan = {0: (s1, ff, 0), 1: (s2, ff, 0), 2: (s1, ff, 0), 3: (s2, 1152, 0)}

    def event(a, e):
        own, wide, column = plan[a]
        ring.event(a, e, own, wide, fout, column)

    def begin(a):
        own, wide, column = plan[a]
        ring.begin(a, own, wide, column)

    def events(a, first, last):
        lax.fori_loop(first, last, lambda e, _: (event(a, e), 0)[1], 0)

    def both(a, first, b, second, count):
        def pair(i, _):
            event(a, first + i)
            event(b, second + i)
            return 0

        lax.fori_loop(0, count, pair, 0)

    def chunks_of(source, size, body, pumps=None, count=8):
        def copies(i, slot):
            return [
                pltpu.make_async_copy(a, b, tile_sems.at[k, slot])
                for k, (a, b) in enumerate(source(i, slot))
            ]

        for made in copies(0, 0):
            made.start()

        def step(i):
            slot = i % 2

            @pl.when(i + 1 < count)
            def _():
                for made in copies(i + 1, 1 - slot):
                    made.start()

            for made in copies(i, slot):
                made.wait()
            body(i, slot)

        run(count, step, pumps)

    got_m.wait()
    for made in got_wd:
        made.wait()
    got_terms.wait()

    def mlp(i):
        sums.offer(i, 0, dot_t(mm[...], s2[col(i), :]))
        pl.when(i > 0)(lambda: sums.pass_on(i - 1, 0))

    run(8, mlp, (0, 0, 2))
    sums.pass_on(7, 0)

    def gate_up_tiles(i, slot):
        r = col(i, 128)
        return [
            (gate_all.at[r], tiles.at[slot, pl.ds(0, 128)]),
            (up_all.at[r], tiles.at[slot, pl.ds(128, 128)]),
        ]

    def grad_gate_up(i, slot):
        r = col(i, 128)
        dm = dot(rows_all[r, :], s2[...]).astype(bf16).astype(f32)
        g = tiles[slot, 0:128].astype(f32)
        u = tiles[slot, 128:256].astype(f32)
        s = jax.nn.sigmoid(g)
        mm[r, :] = (dm * u * s * (1.0 + g * (1.0 - s))).astype(bf16)
        dup[r, :] = (dm * (g * s)).astype(bf16)

        pl.when(i >= 3)(lambda: take_block(i - 3))

    def take_block(i):
        def use(value):
            own_rows[:, col(i)] = (x1[:, col(i)] + value).astype(bf16)

        sums.take(i, 0, use)

    got_x1.wait()
    got_c.wait()
    chunks_of(gate_up_tiles, 8, grad_gate_up, (0, 2, 4))

    def w_tiles(i, slot):
        return [(wg_all.at[i], stream.at[slot, 0]), (wu_all.at[i], stream.at[slot, 1])]

    def grad_hidden(i, slot):
        pl.when(i < 3)(lambda: take_block(5 + i))
        value = dot_t(mm[...], stream[slot, 0]) + dot_t(dup[...], stream[slot, 1])
        sums.offer(i, 1, value)
        pl.when(i > 0)(lambda: sums.pass_on(i - 1, 1))

    chunks_of(w_tiles, 8, grad_hidden, (0, 6, 4))
    kept = [load(own_rows.at[:, col(j)], block_out.at[:, c]) for j, c in enumerate(columns)]
    pending = []
    sums.pass_on(7, 1)

    def h_tiles(everyone):
        return lambda i, slot: [(everyone.at[:, col(i)], hs.at[slot])]

    def keep_up(i, slot):
        return pltpu.make_async_copy(tiles.at[slot], u_kept.at[col(i)], tile_sems.at[1, slot])

    def grads(i, slot):
        s2[col(i), :] = dot_tt(hs[slot], mm[...]).astype(bf16)
        pl.when(i >= 2)(lambda: keep_up(i - 2, slot).wait())
        tiles[slot] = dot_tt(hs[slot], dup[...]).astype(bf16)
        keep_up(i, slot).start()
        pl.when(i == 1)(lambda: begin(1))

    chunks_of(h_tiles(h2_all), 8, grads, (0, 10, 2))
    keep_up(6, 0).wait()
    keep_up(7, 1).wait()

    def take_second(i):
        def use(value):
            acc[:, col(i)] = value

        sums.take(i, 1, use)

    run(2, take_second)
    both(1, 0, 0, 12, 2)
    done = load(fout.at[:, pl.ds(0, ff)], d_out)
    got_up = load(u_kept, s1)
    lax.fori_loop(2, 5, lambda i, _: (take_second(i), 0)[1], 0)
    events(1, 2, 3)
    got_up.wait()
    begin(2)
    lax.fori_loop(5, 8, lambda i, _: (take_second(i), 0)[1], 0)
    both(1, 3, 2, 0, 1)

    for made in kept:
        made.wait()

    def norm_back_second(i, _):
        r = pl.ds(pl.multiple_of(i * 32, 32), 32)
        v = x1[r, :]
        s = lax.rsqrt(jnp.mean(v * v, axis=1, keepdims=True) + epsilon)
        n = v * s
        dn = acc[r, :] * gains[1:2, :]
        own = pl.ds(pl.multiple_of(tp * rows + i * 32, 32), 32)
        back = rows_all[own, :].astype(f32) + s * (
            dn - n * jnp.mean(dn * n, axis=1, keepdims=True)
        )
        acc[r, :] = back
        own_rows[r, :] = back.astype(bf16)
        return 0

    lax.fori_loop(0, rows // 32, norm_back_second, 0)
    da = Rows(links, own_rows, rows_all, tp, over_y, over_core, rows)
    own_in = load(own_rows, da.block(tp, 0, rows))

    both(1, 4, 2, 1, 1)
    da.forward(0)
    both(1, 5, 2, 2, 1)
    da.forward(1)
    for made in got_qkv + got_wo:
        made.wait()
    da.finish()
    own_in.wait()
    links.sent_now(da.first + [da.near])
    got_x = [load(x_in.at[:, c], own_rows.at[:, col(j)]) for j, c in enumerate(columns)]

    def head_v(h):
        return slice(128 + h * 128, 256 + h * 128)

    def grad_attended(i):
        r = col(i, 256)
        dy = dot(rows_all[r, :], wo[...])
        kq[r, :] = pltpu.roll(qkv[r, 0:128].astype(f32), 64, 1).astype(bf16)
        columns = []
        for h in range(4):
            hv = slice(h * 128, (h + 1) * 128)
            under = 1.0 / den[r, h : h + 1]
            part_h = dy[:, hv]
            dnum[r, hv] = (part_h * under).astype(bf16)
            low = jnp.sum(part_h * yb[r, hv].astype(f32), axis=1, keepdims=True)
            columns.append(-low * under)
        lane = lax.broadcasted_iota(jnp.int32, (256, 128), 1)
        packed = jnp.zeros((256, 128), f32)
        for h in range(4):
            packed = jnp.where(lane == h, columns[h], packed)
        dden[r, :] = packed
        dden_t[i] = packed.T[0:8, :]

    run(4, grad_attended)
    both(1, 6, 2, 3, 1)

    for h in range(4):

        def state(i, c, h=h):
            s, zz = c
            r = col(i, 256)
            a, b = phi(qkv[r, 0:128], h, sa_ref, sb_ref, lanes_ref)
            f = a * b * lanes_ref[2:3, :] * tok_ref[r, 1:2]
            s = s + dot_tt(f.astype(bf16), dnum[r, h * 128 : (h + 1) * 128])
            return s, zz + jnp.sum(f * dden[r, h : h + 1], axis=0, keepdims=True)

        s, zz = lax.fori_loop(
            0, 4, state, (jnp.zeros((256, 128), f32), jnp.zeros((1, 256), f32))
        )
        pack_state(st, h, s, zz)
    moved = Exchange(links, st, st_x, st_t, st_z, st_y, st_g, s_back, coef_ref, seq, -1)
    both(1, 7, 2, 4, 1)

    dq[...] = jnp.zeros(dq.shape, f32)

    def local_head(h):
        hm = hm_ref[h : h + 1, :]
        hv = slice(h * 128, (h + 1) * 128)
        for j in range(total // 256):
            k_rows = slice(j * 256, (j + 1) * 256)
            dv_s = jnp.zeros((256, 128), f32)
            dk_s = jnp.zeros((256, 128), f32)
            for i in range(j, total // 256):
                q_rows = slice(i * 256, (i + 1) * 256)
                qm = (qkv[q_rows, 0:128].astype(f32) * hm).astype(bf16)
                u = dot_t(kq[k_rows, :], qm)
                keep = tok_ref[k_rows, 3:4] >= line_ref[1:2, q_rows]
                if i == j:
                    keep = keep & (tok_ref[k_rows, 3:4] <= line_ref[0:1, q_rows])
                kap = jnp.where(keep, (0.5 * u + 1.0) * u + 1.0, 0.0).astype(bf16)
                dn = dnum[q_rows, hv]
                grad = dot_t(qkv[k_rows, head_v(h)], dn) + dden_t[i, h : h + 1, :]
                du = jnp.where(keep, grad * (1.0 + u), 0.0).astype(bf16)
                dv_s = dv_s + dot(kap, dn)
                dk_s = dk_s + dot(du, qm)
                dq[q_rows, :] += dot_tt(du, kq[k_rows, :]) * hm
            dqkv[k_rows, head_v(h)] = dv_s.astype(bf16)
            if h == 0:
                dk[k_rows, :] = dk_s
            else:
                dk[k_rows, :] += dk_s

    local_head(0)
    moved.pair()
    both(1, 8, 2, 5, 1)
    local_head(1)
    moved.planes()
    both(1, 9, 2, 6, 1)
    local_head(2)
    moved.give()
    both(1, 10, 2, 7, 1)
    local_head(3)
    both(1, 11, 2, 8, 1)
    moved.take()

    def split_state(ref, h):
        z_row = jnp.concatenate([ref[h, 160:161, :], ref[h, 161:162, :]], axis=1)
        feat = lax.broadcasted_iota(jnp.int32, (256, 128), 0)
        return jnp.where(feat < FEATS, ref[h], 0.0).astype(bf16), z_row

    for h in range(4):
        s_q, z_q = split_state(s_in, h)
        s_k, z_k = split_state(s_back, h)
        hv = slice(h * 128, (h + 1) * 128)

        def through(grad, a, b, h=h):
            grad = grad * lanes_ref[2:3, :]
            return dot_t((grad * b).astype(bf16), sa_ref[h]) + dot_t(
                (grad * a).astype(bf16), sb_ref[h]
            )

        def carried_part(i, _, h=h, s_q=s_q, z_q=z_q, s_k=s_k, z_k=z_k, hv=hv, through=through):
            r = col(i, 256)
            a, b = phi(qkv[r, 0:128], h, sa_ref, sb_ref, lanes_ref)
            grad = dot_t(dnum[r, hv], s_q) + dden[r, h : h + 1] * z_q
            dq[r, :] += through(grad * tok_ref[r, 1:2], a, b)
            a, b = phi(kq[r, :], h, sa_ref, sb_ref, lanes_ref)
            last = tok_ref[r, 2:3]
            grad = dot_t(qkv[r, head_v(h)], s_k) + z_k
            dk[r, :] += through(grad * last, a, b)
            f = (a * b * lanes_ref[2:3, :] * last).astype(bf16)
            dqkv[r, head_v(h)] = (dqkv[r, head_v(h)].astype(f32) + dot(f, s_k)).astype(bf16)
            return 0

        lax.fori_loop(0, 4, carried_part, 0)

    def join(i):
        r = col(i, 256)
        dqkv[r, 0:128] = (dq[r, :] + pltpu.roll(dk[r, :], 64, 1)).astype(bf16)

    run(4, join)
    done.wait()
    both(1, 12, 2, 9, 2)
    done = load(fout.at[:, pl.ds(0, ff)], g_out)
    own_w = load(wg_all.at[7], stream.at[0, 0])
    own_w.wait()
    gain_two = jnp.sum(fout[:, 0:ff] * stream[0, 0].astype(f32), axis=1, keepdims=True)

    def wq_tiles(i, slot):
        return [(wq_all.at[i], stream.at[slot, 0, :, pl.ds(0, 640)])]

    def grad_hidden_first(i, slot):
        sums.offer(i, 2, dot_t(dqkv[...], stream[slot, 0, :, 0:640]))
        pl.when(i > 0)(lambda: sums.pass_on(i - 1, 2))

    chunks_of(wq_tiles, 8, grad_hidden_first, (2, 11, 1))
    sums.pass_on(7, 2)

    def grad_out_qkv(i, slot):
        s2[col(i), 0:512] = dot_tt(rows_all[:, col(i)], yb[...]).astype(bf16)
        s2[col(i), 512:1152] = dot_tt(hs[slot], dqkv[...]).astype(bf16)

        pl.when(i == 1)(lambda: begin(3))

    chunks_of(h_tiles(h1_all), 8, grad_out_qkv, (3, 0, 1))
    done.wait()
    both(2, 12, 3, 1, 2)
    done = load(fout.at[:, pl.ds(0, ff)], u_out)
    def take_first(i):
        def use(value):
            x1[:, col(i)] = value

        sums.take(i, 2, use)

    run(8, take_first, (3, 3, 4))
    for made in got_x:
        made.wait()

    def norm_back_first(i, _):
        r = pl.ds(pl.multiple_of(i * 32, 32), 32)
        v = own_rows[r, :].astype(f32)
        s = lax.rsqrt(jnp.mean(v * v, axis=1, keepdims=True) + epsilon)
        n = v * s
        dn = x1[r, :] * gains[0:1, :]
        acc[r, :] += s * (dn - n * jnp.mean(dn * n, axis=1, keepdims=True))
        return 0

    lax.fori_loop(0, rows // 32, norm_back_first, 0)
    pending += [load(acc.at[:, col(j)], input_out.at[:, c]) for j, c in enumerate(columns)]
    own_w = load(wu_all.at[7], stream.at[0, 0])
    own_q = load(wq_all.at[7], stream.at[1, 0, :, pl.ds(0, 640)])
    own_w.wait()
    own_q.wait()
    gain_two += jnp.sum(fout[:, 0:ff] * stream[0, 0].astype(f32), axis=1, keepdims=True)
    events(3, 7, 12)
    done.wait()
    events(3, 12, 14)
    pending.append(load(fout.at[:, pl.ds(0, 1152)], oq_out))
    gain_one = jnp.sum(fout[:, 512:1152] * stream[1, 0, :, 0:640].astype(f32), axis=1, keepdims=True)
    lane = lax.broadcasted_iota(jnp.int32, (256, 128), 1)
    both = jnp.where(lane == 0, gain_one, jnp.where(lane == 1, gain_two, 0.0)).T[0:8, :]
    terms[0] = both
    over = links.start(terms.at[0], terms_core, tp=over_core)
    over.wait_recv()
    both = both + terms_core[...]
    terms[1] = both
    over = links.start(terms.at[1], terms_y, tp=over_y)
    over.wait_recv()
    own_gains = jnp.concatenate(
        [gain_first[...], gain_second[...], jnp.ones((6, 256), f32)], axis=0
    ).astype(bf16)
    terms[2] = (both + terms_y[...]) / own_gains.astype(f32)
    pending.append(load(terms.at[2], gain_out))
    run(8, lambda i: sums.sent(i))
    for made in pending:
        made.wait()
    links.finish()
    moved.finish()


def feature_tables(heads):
    first = np.zeros((heads, 128, 256), np.float32)
    second = np.zeros((heads, 128, 256), np.float32)
    lanes = np.zeros((8, 256), np.float32)
    f = 0
    for i in range(FEAT):
        for j in range(i, FEAT):
            for h in range(heads):
                first[h, h * FEAT + i, f] = 1
                second[h, h * FEAT + j, f] = 1
            lanes[2, f] = square_coef if i == j else square_coef * 2**0.5
            f += 1
    for i in range(FEAT):
        for h in range(heads):
            first[h, h * FEAT + i, f] = 1
        lanes[1, f] = 1
        lanes[2, f] = linear_coef
        f += 1
    lanes[0, f] = lanes[1, f] = lanes[2, f] = 1
    mask = np.zeros((8, 128), np.float32)
    for h in range(heads):
        mask[h, h * FEAT : (h + 1) * FEAT] = 0.25
    return first, second, lanes, mask


def forward_pass(lengths, constants, gain_first, gain_second, x_in, weights, c_in):
    rows, width = x_in.shape
    total = 4 * rows
    ff = weights[4].shape[0]
    hbm = pl.BlockSpec(memory_space=pl.ANY)
    vmem = pl.BlockSpec(memory_space=pltpu.VMEM)

    def shape(*dims, dtype=bf16):
        return jax.ShapeDtypeStruct(dims, dtype)

    outs = (
        shape(8, 256, 640),
        shape(8, 256, 512),
        shape(8, 256, ff),
        shape(8, 256, ff),
        shape(8, 256, ff),
        shape(total, width),
        shape(total, width),
        shape(total, 640),
        shape(total, 512),
        shape(total, 128, dtype=f32),
        shape(rows, width, dtype=f32),
        shape(total, width),
        shape(total, ff),
        shape(total, ff),
        shape(total, ff),
        shape(4, 256, 128, dtype=f32),
        shape(8, width, dtype=f32),
        shape(width, ff),
    )
    scratch = [
        pltpu.VMEM((rows, width), bf16),
        pltpu.VMEM((total, 128), f32),
        pltpu.VMEM((8, total), f32),
        pltpu.VMEM((8, 128), f32),
        pltpu.VMEM((16, 256), bf16),
        pltpu.VMEM((256, 640), bf16),
        pltpu.VMEM((256, 512), bf16),
        pltpu.VMEM((256, ff), bf16),
        pltpu.VMEM((256, ff), bf16),
        pltpu.VMEM((256, ff), bf16),
        pltpu.VMEM((128, 256), f32),
        pltpu.VMEM((256, 512), f32),
        pltpu.VMEM((512, 256), f32),
        pltpu.VMEM((-(-ff // 128) * 128, 256), f32),
        pltpu.VMEM((-(-ff // 128) * 128, 256), f32),
        pltpu.VMEM((total, width), bf16),
        pltpu.VMEM((total, width), bf16),
        pltpu.VMEM((width, 640), bf16),
        pltpu.VMEM((width, 512), bf16),
        pltpu.VMEM((width, ff), bf16),
        pltpu.VMEM((width, ff), bf16),
        pltpu.VMEM((total, 640), bf16),
        pltpu.VMEM((total, 128), bf16),
        pltpu.VMEM((total, 512), f32),
        pltpu.VMEM((total, 128), f32),
        pltpu.VMEM((total, 512), bf16),
        pltpu.VMEM((2, rows, width), bf16),
        pltpu.VMEM((2, rows, width), bf16),
        pltpu.VMEM((rows, width), bf16),
        pltpu.VMEM((rows, width), bf16),
        pltpu.VMEM((rows, width), f32),
        pltpu.VMEM((total, ff), bf16),
        pltpu.VMEM((total, ff), bf16),
        pltpu.VMEM((total, ff), bf16),
        pltpu.VMEM((8, 16, 256), bf16),
        pltpu.VMEM((8, width), f32),
        pltpu.VMEM((4, 176, 128), bf16),
        pltpu.VMEM((2, 176, 128), bf16),
        pltpu.VMEM((2, 176, 128), bf16),
        pltpu.VMEM((2, 176, 128), bf16),
        pltpu.VMEM((2, 176, 128), bf16),
        pltpu.VMEM((2, 2, 176, 128), bf16),
        pltpu.VMEM((4, 256, 128), f32),
        pltpu.SemaphoreType.DMA((112,)),
        pltpu.SemaphoreType.DMA((112,)),
        pltpu.SemaphoreType.DMA((112,)),
    ]
    return pl.pallas_call(
        fwd_kernel,
        out_shape=outs,
        in_specs=[pl.BlockSpec(memory_space=pltpu.SMEM)] + [vmem] * 6 + [hbm] * 9,
        out_specs=(hbm,) * len(outs),
        scratch_shapes=scratch,
        compiler_params=pltpu.CompilerParams(
            collective_id=0, has_side_effects=True, vmem_limit_bytes=60 * 2**20
        ),
    )(lengths, *constants, gain_first, gain_second, x_in, *weights, c_in)


def backward_pass(lengths, constants, gains, s_in, den, gain_pair, x_in, x1, weights, c_all, acts):
    rows, width = x_in.shape
    total = 4 * rows
    ff = weights[2].shape[2]
    hbm = pl.BlockSpec(memory_space=pl.ANY)
    vmem = pl.BlockSpec(memory_space=pltpu.VMEM)

    def shape(*dims, dtype=f32):
        return jax.ShapeDtypeStruct(dims, dtype)

    outs = (
        shape(256, ff),
        shape(256, ff),
        shape(256, ff),
        shape(256, 1152),
        shape(rows, width, dtype=bf16),
        shape(rows, width),
        shape(8, 256),
        shape(width, ff, dtype=bf16),
    )
    scratch = [
        pltpu.VMEM((total, 128), f32),
        pltpu.VMEM((8, total), f32),
        pltpu.VMEM((8, 128), f32),
        pltpu.VMEM((3, 8, 256), f32),
        pltpu.VMEM((8, 256), f32),
        pltpu.VMEM((8, 256), f32),
        pltpu.VMEM((8, 256, ff), bf16),
        pltpu.VMEM((width, ff), bf16),
        pltpu.VMEM((width, ff), bf16),
        pltpu.VMEM((width, 512), bf16),
        pltpu.VMEM((2, 2, 256, ff), bf16),
        pltpu.VMEM((2, total, 256), bf16),
        pltpu.VMEM((total, width), bf16),
        pltpu.VMEM((total, ff), bf16),
        pltpu.VMEM((total, ff), bf16),
        pltpu.VMEM((2, 256, ff), bf16),
        pltpu.VMEM((total, 640), bf16),
        pltpu.VMEM((total, 128), bf16),
        pltpu.VMEM((total, 512), bf16),
        pltpu.VMEM((total, 512), bf16),
        pltpu.VMEM((total, 128), f32),
        pltpu.VMEM((4, 8, 256), f32),
        pltpu.VMEM((total, 640), bf16),
        pltpu.VMEM((total, 128), f32),
        pltpu.VMEM((total, 128), f32),
        pltpu.VMEM((8, 4, 256, 256), bf16),
        pltpu.VMEM((8, 2, 256, 256), bf16),
        pltpu.VMEM((8, 256, 256), bf16),
        pltpu.VMEM((rows, width), f32),
        pltpu.VMEM((rows, width), f32),
        pltpu.VMEM((256, ff), f32),
        pltpu.VMEM((4, 176, 128), bf16),
        pltpu.VMEM((2, 176, 128), bf16),
        pltpu.VMEM((2, 176, 128), bf16),
        pltpu.VMEM((2, 176, 128), bf16),
        pltpu.VMEM((2, 176, 128), bf16),
        pltpu.VMEM((2, 2, 176, 128), bf16),
        pltpu.VMEM((4, 256, 128), f32),
        pltpu.VMEM((rows, width), bf16),
        pltpu.SemaphoreType.DMA((2, 2, 2)),
        pltpu.SemaphoreType.DMA((2, 2, 2, 7)),
        pltpu.SemaphoreType.DMA((6, 8)),
        pltpu.SemaphoreType.REGULAR((2,)),
        pltpu.SemaphoreType.DMA((16,)),
        pltpu.SemaphoreType.DMA((16,)),
        pltpu.SemaphoreType.DMA((80,)),
        pltpu.SemaphoreType.DMA((2, 2)),
    ]
    return pl.pallas_call(
        bwd_kernel,
        out_shape=outs,
        in_specs=[pl.BlockSpec(memory_space=pltpu.SMEM)] + [vmem] * 9 + [hbm] * 16,
        out_specs=(hbm,) * len(outs),
        scratch_shapes=scratch,
        compiler_params=pltpu.CompilerParams(
            collective_id=1, has_side_effects=True, vmem_limit_bytes=62 * 2**20
        ),
    )(lengths, *constants, gains, s_in, den, *gain_pair, x_in, x1, *weights, c_all, *acts)


def finish_kernel(
    d_in, g_in, u_in, oq_in, block_in, input_in,
    d_out, g_out, u_out, o_out, q_out, k_out, v_out, block_out, input_out,
    wide, turned, oq, oq_t, sems,
):
    keeper = Sems(sems)
    ff = d_in.shape[1]

    def copy(src, dst):
        made = pltpu.make_async_copy(src, dst, keeper.take())
        made.start()
        return made

    came = [copy(ref, wide.at[i]) for i, ref in enumerate((g_in, u_in, d_in))]
    came_oq = copy(oq_in, oq)
    kept = [
        copy(block_in, block_out),
        copy(input_in, input_out),
        copy(oq_in.at[:, pl.ds(640, 512)], v_out),
    ]
    came_oq.wait()
    oq_t[...] = oq[:, 0:640].T
    kept += [
        copy(oq_t.at[pl.ds(0, 512)], o_out),
        copy(oq_t.at[pl.ds(512, 64)], q_out),
        copy(oq_t.at[pl.ds(576, 64)], k_out),
    ]
    for i, out in enumerate((g_out, u_out, d_out)):
        came[i].wait()
        for at in range(0, ff, 128):
            at = min(at, ff - 128)
            turned[i, at : at + 128, :] = wide[i, :, at : at + 128].T
        kept.append(copy(turned.at[i], out))
    for made in kept:
        made.wait()


def finish(d, g, u, oq, block, grad_input):
    rows, width = block.shape
    ff = d.shape[1]
    hbm = pl.BlockSpec(memory_space=pl.ANY)

    def shape(*dims, dtype=f32):
        return jax.ShapeDtypeStruct(dims, dtype)

    outs = (
        shape(ff, 256), shape(ff, 256), shape(ff, 256), shape(512, 256), shape(64, 256),
        shape(64, 256), shape(256, 512), shape(rows, width, dtype=bf16), shape(rows, width),
    )
    return pl.pallas_call(
        finish_kernel,
        out_shape=outs,
        in_specs=[hbm] * 6,
        out_specs=(hbm,) * len(outs),
        scratch_shapes=[
            pltpu.VMEM((3, 256, ff), f32),
            pltpu.VMEM((3, ff, 256), f32),
            pltpu.VMEM((256, 1152), f32),
            pltpu.VMEM((640, 256), f32),
            pltpu.SemaphoreType.DMA((16,)),
        ],
        compiler_params=pltpu.CompilerParams(vmem_limit_bytes=60 * 2**20),
    )(d, g, u, oq, block, grad_input)


def on_device_rings(
    inputs, lengths, gain_attn, w_query, w_key, w_value, w_out, gain_mlp, w_gate, w_up, w_down,
    cotangent,
):
    first, second, lanes, mask = feature_tables(4)
    constants = (
        jnp.asarray(first, bf16), jnp.asarray(second, bf16), jnp.asarray(lanes), jnp.asarray(mask),
    )
    gain_pair = (gain_attn.reshape(1, -1), gain_mlp.reshape(1, -1))
    made = forward_pass(
        lengths, constants, *gain_pair, inputs,
        (w_query.T, w_key.T, w_value, w_out, w_gate.T, w_up.T, w_down), cotangent,
    )
    weights = made[:5]
    c_all, h1, qkv, yb, den, x1, h2, gate, up, mixed, s_in, gain_all, terms = made[5:]
    sum_down_t, sum_gate, sum_up, sum_oq, block, grad_input, gain_sums, _ = backward_pass(
        lengths, constants, gain_all, s_in, den, gain_pair, inputs, x1, weights, c_all,
        (h1, qkv, yb, h2, gate, up, mixed, terms),
    )
    d, g_t, u_t, o, q_t, k_t, v, block, grad_input = finish(
        sum_down_t, sum_gate, sum_up, sum_oq, block, grad_input
    )
    return (
        block,
        grad_input,
        gain_sums[0],
        q_t.T,
        k_t.T,
        v,
        o,
        gain_sums[1],
        g_t.T,
        u_t.T,
        d,
    )


def on_device(
    inputs,
    lengths,
    gain_attn,
    w_query,
    w_key,
    w_value,
    w_out,
    gain_mlp,
    w_gate,
    w_up,
    w_down,
    cotangent,
):
    seq_count = lax.axis_size("seq")
    tp_count = lax.axis_size("tp")
    seq_index = lax.axis_index("seq")
    rows_own, width = inputs.shape
    chunk = width // seq_count
    half = chunk // 2
    block_len = rows_own * tp_count
    anchor = seq_index * block_len
    relative = relative_list(seq_count)
    ring = ring_order(seq_count)
    place_of = [ring.index(s) for s in range(seq_count)]
    to_rel = jnp.array(
        [[ring[(place_of[s] - k) % seq_count] for k in relative] for s in range(seq_count)],
        jnp.int32,
    )[seq_index]
    to_abs = jnp.array(
        [
            [relative.index((place_of[s] - place_of[o]) % seq_count) for o in range(seq_count)]
            for s in range(seq_count)
        ],
        jnp.int32,
    )[seq_index]
    to_rel = [to_rel[j] for j in range(seq_count)]
    to_abs = [to_abs[j] for j in range(seq_count)]

    qk_cols, v_cols, ff_cols = w_query.shape[1], w_value.shape[1], w_gate.shape[1]
    gains = jnp.stack([gain_attn, gain_mlp]).astype(bf16)
    qkv_cols = 2 * qk_cols + v_cols
    qkv_own = jnp.concatenate([w_query, w_key, w_value], axis=1).astype(bf16)
    gain_rows = jnp.zeros((16, qkv_cols), bf16).at[:2, :chunk].set(gains)
    first_own = jnp.concatenate([qkv_own, gain_rows], axis=0)
    out_own = w_out.astype(bf16).T
    gate_up_own = jnp.concatenate([w_gate, w_up], axis=1).astype(bf16)
    down_own = w_down.astype(bf16).T

    first_got = ring_gather(first_own, half)
    out_got = ring_gather(out_own, half)
    gate_up_got = ring_gather(gate_up_own, half)
    down_got = ring_gather(down_own, half)
    w_qkv = jnp.concatenate([first_got[k][:chunk] for k in relative], axis=0)
    gain_first = jnp.concatenate([first_got[k][chunk, :chunk] for k in relative]).astype(f32)
    gain_second = jnp.concatenate([first_got[k][chunk + 1, :chunk] for k in relative]).astype(f32)
    w_out_t = jnp.concatenate([out_got[k] for k in relative], axis=0)
    w_gate_up = jnp.concatenate([gate_up_got[k] for k in relative], axis=0)
    w_down_t = jnp.concatenate([down_got[k] for k in relative], axis=0)

    at = jnp.arange(lengths.shape[0])
    starts = jnp.sum(jnp.where(at[None, :] < at[:, None], lengths[None, :], 0), axis=1)
    positions, row_ids, carry_in, after_last = segment_masks(anchor, starts, block_len)
    carry_mask = carry_in.astype(f32)
    last_mask = after_last.astype(f32)
    resets = (
        jnp.sum(
            ((starts // block_len)[None, :] == jnp.arange(seq_count)[:, None]).astype(jnp.int32),
            axis=1,
        )
        > 0
    ).astype(jnp.int32)

    inputs_own = to_relative(inputs, to_rel, chunk)
    grad_own = to_relative(cotangent, to_rel, chunk)
    inputs_full = tp_gather(inputs_own).astype(f32)
    grad_full = tp_gather(grad_own)
    inputs_own = inputs_own.astype(f32)
    hidden_first = (inputs_full * rms_scale(inputs_full) * gain_first).astype(bf16)
    qkv = dot(hidden_first, w_qkv).astype(bf16)
    queries = qkv[:, :qk_cols]
    key_flat = qkv[:, qk_cols : 2 * qk_cols]
    value_flat = qkv[:, 2 * qk_cols :]
    heads_local = qk_cols // FEAT
    query_heads = queries.reshape(block_len, heads_local, FEAT)
    key_heads = key_flat.reshape(block_len, heads_local, FEAT)
    value_heads = value_flat.reshape(block_len, heads_local, VHEAD)
    query_float = query_heads.astype(f32)
    key_float = key_heads.astype(f32)
    value_float = value_heads.astype(f32)
    key_feat = features(key_float) * last_mask[:, None, None]
    local_state = jnp.einsum("thn,thv->hnv", key_feat, value_float, precision=highest)
    local_sum = jnp.sum(key_feat, axis=0)
    carry_state, carry_sum = carried([local_state, local_sum], resets, 1)
    step_rows = 512
    query_feat = features(query_float)
    carry_weight = carry_mask[:, None]
    numer_parts = []
    denom_parts = []
    for first_row in range(0, block_len, step_rows):
        query_part = query_heads[first_row : first_row + step_rows]
        scores, allowed, kernel = pair_block(
            query_part, key_heads, row_ids, positions, first_row, step_rows
        )
        numer_parts.append(
            jnp.einsum("hts,shv->thv", kernel.astype(bf16), value_heads, preferred_element_type=f32)
        )
        denom_parts.append(jnp.sum(kernel, axis=-1).T)
    numerator = (
        jnp.concatenate(numer_parts, axis=0)
        + jnp.einsum("thn,hnv->thv", query_feat, carry_state, precision=highest)
        * carry_weight[:, :, None]
    )
    denominator = (
        jnp.concatenate(denom_parts, axis=0)
        + jnp.einsum("thn,hn->th", query_feat, carry_sum, precision=highest) * carry_weight
    )
    attended = numerator / denominator[:, :, None]
    attended_low = attended.reshape(block_len, heads_local * VHEAD).astype(bf16)
    attn_partial = dot_t(attended_low, w_out_t).astype(bf16)
    middle_own = inputs_own + tp_scatter(attn_partial)
    scale_second = rms_scale(middle_own)
    normed_second = middle_own * scale_second
    hidden_second = tp_gather((normed_second * gain_second).astype(bf16))
    gate_up = dot(hidden_second, w_gate_up)
    gate_value, upward = gate_up[:, :ff_cols], gate_up[:, ff_cols:]
    sigmoid_gate = jax.nn.sigmoid(gate_value)
    silu_gate = gate_value * sigmoid_gate
    mixed_rows = (silu_gate * upward).astype(bf16)
    grad_down_t = dot_tt(grad_full, mixed_rows).astype(bf16)

    def by_distance(stack):
        return {k: stack[j * chunk : (j + 1) * chunk] for j, k in enumerate(relative)}

    sum_down_t = ring_scatter(by_distance(grad_down_t))
    mlp_own = tp_scatter(dot_t(mixed_rows, w_down_t).astype(bf16))
    block_output = to_relative((middle_own + mlp_own).astype(bf16), to_abs, chunk)

    grad_mixed = dot(grad_full, w_down_t).astype(bf16).astype(f32)
    grad_gate = (
        grad_mixed * upward * sigmoid_gate * (1.0 + gate_value * (1.0 - sigmoid_gate))
    ).astype(bf16)
    grad_upward = (grad_mixed * silu_gate).astype(bf16)
    grad_gate_up = jnp.concatenate([grad_gate, grad_upward], axis=1)
    hidden_partial = dot_t(grad_gate_up, w_gate_up).astype(bf16)
    sum_gate_up = ring_scatter(by_distance(dot_tt(hidden_second, grad_gate_up).astype(bf16)))
    grad_hidden = tp_scatter(hidden_partial)
    grad_middle = grad_own.astype(f32) + norm_back(
        grad_hidden, normed_second, scale_second, gain_second
    )
    grad_branch = tp_gather(grad_middle.astype(bf16))
    sum_out_t = ring_scatter(by_distance(dot_tt(grad_branch, attended_low).astype(bf16)))
    grad_attended = dot(grad_branch, w_out_t).reshape(block_len, heads_local, VHEAD)
    grad_numer = (grad_attended / denominator[:, :, None]).astype(bf16)
    grad_denom = -jnp.sum(grad_attended * attended, axis=-1) / denominator
    grad_numer_carried = grad_numer.astype(f32) * carry_weight[:, :, None]
    grad_denom_carried = grad_denom * carry_weight
    grad_state_in = jnp.einsum("thn,thv->hnv", query_feat, grad_numer_carried, precision=highest)
    grad_sum_in = jnp.einsum("thn,th->hn", query_feat, grad_denom_carried, precision=highest)
    grad_query_feat = (
        jnp.einsum("thv,hnv->thn", grad_numer_carried, carry_state, precision=highest)
        + grad_denom_carried[:, :, None] * carry_sum[None]
    )
    grad_state_out, grad_sum_out = carried([grad_state_in, grad_sum_in], resets, -1)
    grad_key_feat = (
        jnp.einsum("thv,hnv->thn", value_float, grad_state_out, precision=highest)
        + grad_sum_out[None]
    ) * last_mask[:, None, None]
    grad_value_state = jnp.einsum("thn,hnv->thv", key_feat, grad_state_out, precision=highest)
    grad_query_parts = []
    grad_key_inner = jnp.zeros((block_len, heads_local, FEAT), f32)
    grad_value_inner = jnp.zeros((block_len, heads_local, VHEAD), f32)
    for first_row in range(0, block_len, step_rows):
        query_part = query_heads[first_row : first_row + step_rows]
        scores, allowed, kernel = pair_block(
            query_part, key_heads, row_ids, positions, first_row, step_rows
        )
        numer_grad_part = grad_numer[first_row : first_row + step_rows]
        grad_weights = jnp.einsum(
            "thv,shv->hts", numer_grad_part, value_heads, preferred_element_type=f32
        )
        grad_scores = (
            (grad_weights + grad_denom[first_row : first_row + step_rows].T[:, :, None])
            * allowed[None]
            * (1.0 + scores)
        ).astype(bf16)
        grad_query_parts.append(
            jnp.einsum("hts,shf->thf", grad_scores, key_heads, preferred_element_type=f32) * 0.25
        )
        grad_key_inner = (
            grad_key_inner
            + jnp.einsum("hts,thf->shf", grad_scores, query_part, preferred_element_type=f32) * 0.25
        )
        grad_value_inner = grad_value_inner + jnp.einsum(
            "hts,thv->shv", kernel.astype(bf16), numer_grad_part, preferred_element_type=f32
        )
    grad_query = (
        jnp.concatenate(grad_query_parts, axis=0) + feature_grad(query_float, grad_query_feat)
    ).astype(bf16)
    grad_key = (grad_key_inner + feature_grad(key_float, grad_key_feat)).astype(bf16)
    grad_value = (grad_value_inner + grad_value_state).astype(bf16)
    grad_qkv = jnp.concatenate(
        [
            grad_query.reshape(block_len, heads_local * FEAT),
            grad_key.reshape(block_len, heads_local * FEAT),
            grad_value.reshape(block_len, heads_local * VHEAD),
        ],
        axis=1,
    )
    sum_qkv = ring_scatter(by_distance(dot_tt(hidden_first, grad_qkv).astype(bf16)))
    grad_hidden_first = tp_scatter(dot_t(grad_qkv, w_qkv).astype(bf16))
    scale_first = rms_scale(inputs_own)
    normed_first = inputs_own * scale_first
    grad_input = to_relative(
        grad_middle + norm_back(grad_hidden_first, normed_first, scale_first, gain_first),
        to_abs,
        chunk,
    )

    gain_terms = jnp.stack(
        [
            jnp.sum(qkv_own.astype(f32) * sum_qkv, axis=1),
            jnp.sum(gate_up_own.astype(f32) * sum_gate_up, axis=1),
        ]
    )
    gain_sums = tp_sum(gain_terms) / gains.astype(f32)
    return (
        block_output,
        grad_input,
        gain_sums[0],
        sum_qkv[:, :qk_cols],
        sum_qkv[:, qk_cols : 2 * qk_cols],
        sum_qkv[:, 2 * qk_cols :],
        sum_out_t.T,
        gain_sums[1],
        sum_gate_up[:, :ff_cols],
        sum_gate_up[:, ff_cols:],
        sum_down_t.T,
    )


def solution(mesh):
    in_specs = (
        P(("seq", "tp"), None),
        P(),
        P("seq"),
        P("seq", "tp"),
        P("seq", "tp"),
        P("seq", "tp"),
        P("tp", "seq"),
        P("seq"),
        P("seq", "tp"),
        P("seq", "tp"),
        P("tp", "seq"),
        P(("seq", "tp"), None),
    )
    out_specs = (
        P(("seq", "tp"), None),
        P(("seq", "tp"), None),
        P("seq"),
        P("seq", "tp"),
        P("seq", "tp"),
        P("seq", "tp"),
        P("tp", "seq"),
        P("seq"),
        P("seq", "tp"),
        P("seq", "tp"),
        P("tp", "seq"),
    )
    small = mesh.shape["seq"] == 8 and mesh.shape["tp"] == 4
    body = on_device_rings if small else on_device
    return jax.shard_map(
        body, mesh=mesh, in_specs=in_specs, out_specs=out_specs, check_vma=False
    )
```

```python
import jax
import jax.numpy as jnp
import numpy as np
from jax import lax
from jax.experimental import pallas as pl
from jax.experimental.pallas import tpu as pltpu
from jax.sharding import PartitionSpec as P

FEAT = 16
VHEAD = 128


epsilon = 1e-05
linear_coef = 0.5
square_coef = 0.17677669529663687
highest = lax.Precision.HIGHEST
f32 = jnp.float32
bf16 = jnp.bfloat16


def ring_order(count):
    planes = 4 if count % 4 == 0 else 2
    columns = count // planes
    order = [z * columns for z in range(planes)]
    for z in reversed(range(planes)):
        xs = list(range(1, columns))
        if (planes - 1 - z) % 2:
            xs.reverse()
        order += [z * columns + x for x in xs]
    return order


def relative_list(count):
    half = count // 2
    out = []
    for j in range(1, half):
        out += [j, count - j]
    return out + [half, 0]


def ring_perms(count):
    ring = ring_order(count)
    fwd = [(ring[i], ring[(i + 1) % count]) for i in range(count)]
    return fwd, [(b, a) for a, b in fwd]


def ring_gather(own, half_rows):
    count = lax.axis_size("seq")
    fwd, bwd = ring_perms(count)
    half = count // 2
    got = {0: own}
    ahead = back = own
    for step in range(1, half):
        ahead = lax.ppermute(ahead, "seq", fwd)
        back = lax.ppermute(back, "seq", bwd)
        got[step] = ahead
        got[count - step] = back
    ahead = lax.ppermute(ahead[:half_rows], "seq", fwd)
    back = lax.ppermute(back[half_rows:], "seq", bwd)
    got[half] = jnp.concatenate([ahead, back], axis=0)
    return got


def ring_scatter(chunks):
    count = lax.axis_size("seq")
    fwd, bwd = ring_perms(count)
    half = chunks[0].shape[0] // 2
    ahead = chunks[1][:half]
    back = chunks[count - 1][half:]
    for step in range(count - 1):
        ahead = lax.ppermute(ahead, "seq", fwd).astype(f32)
        back = lax.ppermute(back, "seq", bwd).astype(f32)
        last = step == count - 2
        ahead = ahead + chunks[0 if last else 2 + step][:half].astype(f32)
        back = back + chunks[0 if last else count - 2 - step][half:].astype(f32)
        if not last:
            ahead = ahead.astype(bf16)
            back = back.astype(bf16)
    return jnp.concatenate([ahead, back], axis=0)


def to_relative(array, index_row, chunk):
    return jnp.concatenate(
        [lax.dynamic_slice_in_dim(array, i * chunk, chunk, 1) for i in index_row], axis=1
    )


def tp_perms(count):
    ys = count // 2
    core = [(i, i ^ 1) for i in range(count)]
    shift = [
        [(i, (((i // 2) + d) % ys) * 2 + i % 2) for i in range(count)] for d in range(ys)
    ]
    return core, shift


def tp_gather(own):
    count = lax.axis_size("tp")
    ys = count // 2
    place = lax.axis_index("tp")
    y, c = place // 2, place % 2
    core, shift = tp_perms(count)
    parts = [own] + [lax.ppermute(own, "tp", shift[d]) for d in range(1, ys)]
    mine = jnp.stack([lax.select_n((y - at + ys) % ys, *parts) for at in range(ys)])
    other = lax.ppermute(mine, "tp", core)
    full = jnp.stack([jnp.where(c == 0, mine, other), jnp.where(c == 0, other, mine)], axis=1)
    return full.reshape((count * own.shape[0],) + own.shape[1:])


def tp_scatter(partial):
    count = lax.axis_size("tp")
    ys = count // 2
    place = lax.axis_index("tp")
    y, c = place // 2, place % 2
    core, shift = tp_perms(count)
    blocks = partial.reshape((ys, 2, partial.shape[0] // count) + partial.shape[1:])
    sent = lax.dynamic_index_in_dim(blocks, 1 - c, 1, False)
    kept = lax.dynamic_index_in_dim(blocks, c, 1, False)
    pair = kept.astype(f32) + lax.ppermute(sent, "tp", core).astype(f32)
    low = pair.astype(bf16)
    own = lax.dynamic_index_in_dim(pair, y, 0, False)
    for d in range(1, ys):
        away = lax.dynamic_index_in_dim(low, (y + d) % ys, 0, False)
        own = own + lax.ppermute(away, "tp", shift[d]).astype(f32)
    return own


def tp_sum(vector):
    count = lax.axis_size("tp")
    core, shift = tp_perms(count)
    vector = vector + lax.ppermute(vector, "tp", core)
    return vector + sum(lax.ppermute(vector, "tp", shift[d]) for d in range(1, count // 2))


def carried(arrays, resets, step):
    count = lax.axis_size("seq")
    place = lax.axis_index("seq")

    def from_near(a, d):
        perm = [(i, i + d * step) for i in range(count) if 0 <= i + d * step < count]
        return lax.ppermute(a.astype(bf16), "seq", perm).astype(f32)

    def reset_within(d):
        at = jnp.arange(count)
        away = (place - at) * step
        return jnp.sum(jnp.where((away >= 1) & (away <= d), resets, 0)) > 0

    arrays = [from_near(a, 1) for a in arrays]
    d = 1
    while d < count - 1:
        keep = 1.0 - reset_within(d).astype(f32)
        arrays = [a + keep * from_near(a, d) for a in arrays]
        d *= 2
    return arrays


def features(vector):
    squares = (vector[..., :, None] * vector[..., None, :]).reshape(
        vector.shape[:-1] + (vector.shape[-1] * vector.shape[-1],)
    )
    return jnp.concatenate(
        [jnp.ones_like(vector[..., :1]), vector * linear_coef, squares * square_coef], axis=-1
    )


def feature_grad(vector, grad_feat):
    feat_width = vector.shape[-1]
    linear_part = grad_feat[..., 1 : 1 + feat_width]
    square_part = grad_feat[..., 1 + feat_width :].reshape(vector.shape + (feat_width,))
    mixed_part = jnp.sum(square_part * vector[..., None, :], axis=-1) + jnp.sum(
        square_part * vector[..., :, None], axis=-2
    )
    return linear_coef * linear_part + square_coef * mixed_part


def segment_masks(anchor, starts, length):
    positions = anchor + jnp.arange(length, dtype=jnp.int32)
    start_le = starts[None, :] <= positions[:, None]
    row_ids = jnp.sum(start_le.astype(jnp.int32), axis=1)
    inside = (starts >= anchor) & (starts < anchor + length)
    carry = jnp.sum(((starts[None, :] >= anchor) & start_le).astype(jnp.int32), axis=1) == 0
    after_last = (
        jnp.sum(
            ((starts[None, :] > positions[:, None]) & inside[None, :]).astype(jnp.int32), axis=1
        )
        == 0
    )
    return (positions, row_ids, carry, after_last)


def rms_scale(values):
    return lax.rsqrt(jnp.mean(values * values, axis=-1, keepdims=True) + epsilon)


def norm_back(grad_out, normed, scale, gain):
    grad_normed = grad_out * gain
    return scale * (grad_normed - normed * jnp.mean(grad_normed * normed, axis=-1, keepdims=True))


def pair_block(query_part, key_heads, row_ids, positions, first_row, span_rows):
    scores = (
        jnp.einsum("thf,shf->hts", query_part, key_heads, preferred_element_type=f32) * 0.25
    )
    rows_here = row_ids[first_row : first_row + span_rows]
    place_here = positions[first_row : first_row + span_rows]
    allowed = (
        (rows_here[:, None] == row_ids[None, :]) & (positions[None, :] <= place_here[:, None])
    ).astype(f32)
    kernel = (1.0 + scores + 0.5 * scores * scores) * allowed[None]
    return (scores, allowed, kernel)


def dot(a, b):
    return jnp.dot(a, b, preferred_element_type=f32)


def dot_t(a, b):
    return lax.dot_general(a, b, (((1,), (1,)), ((), ())), preferred_element_type=f32)


def dot_tt(a, b):
    return lax.dot_general(a, b, (((0,), (0,)), ((), ())), preferred_element_type=f32)


def ring_place(seq):
    z, x = seq // 2, seq % 2
    return z + x * (7 - 2 * z)


def ring_seq(place):
    place = lax.rem(place + 8, 8)
    far = place // 4
    return (1 - far) * 2 * place + far * (15 - 2 * place)


class Sems:
    def __init__(self, ref):
        self.ref, self.used = ref, 0

    def take(self):
        self.used += 1
        return self.ref.at[self.used - 1]


class Links:
    def __init__(self, send, recv):
        self.send, self.recv, self.sent = Sems(send), Sems(recv), []

    def copy(self, src, dst, **to):
        return pltpu.make_async_remote_copy(
            src_ref=src,
            dst_ref=dst,
            send_sem=self.send.take(),
            recv_sem=self.recv.take(),
            device_id=to,
            device_id_type=pl.DeviceIdType.MESH,
        )

    def start(self, src, dst, **to):
        made = self.copy(src, dst, **to)
        made.start()
        self.sent.append(made)
        return made

    def sent_now(self, some):
        for made in some:
            made.wait_send()
        self.sent = [made for made in self.sent if all(made is not other for other in some)]

    def finish(self):
        for made in self.sent:
            made.wait_send()


class Gather:
    def __init__(self, links, arrays, split, nearby, gangs):
        self.links, self.arrays, self.split, self.nearby = links, arrays, split, nearby
        self.at = {k: j for j, k in enumerate(relative_list(8))}
        self.flying, self.gangs, self.done = {}, gangs, 0
        self.gang_of = {a: i for i, gang in enumerate(gangs) for a in gang}
        self.events = [
            (a, step, way, part)
            for gang in gangs
            for step in (1, 2, 3, 4)
            for a in gang
            for part in (0, 1)
            for way in (0, 1)
            if step < 4 or way == part
        ]
        for a in gangs[0]:
            for part in (0, 1):
                for way in (0, 1):
                    self.go(a, 1, way, part)

    def rows(self, part):
        return pl.ds(part * self.split, self.split)

    def go(self, a, step, way, part):
        own, everyone = self.arrays[a]
        before, after = (step - 1, step) if way == 0 else ((9 - step) % 8, 8 - step)
        src = own if step == 1 else everyone.at[self.at[before]]
        self.flying[a, step, way, part] = self.links.start(
            src.at[self.rows(part)],
            everyone.at[self.at[after], self.rows(part)],
            seq=self.nearby[way],
        )

    def pump(self, upto):
        while self.done < min(upto, len(self.events)):
            a, step, way, part = self.events[self.done]
            self.flying[a, step, way, part].wait_recv()
            if step < 3 or (step == 3 and way == part):
                self.go(a, step + 1, way, part)
            i = self.gang_of[a]
            if step == 3 and i + 1 < len(self.gangs):
                mine, later = self.gangs[i].index(a), self.gangs[i + 1]
                last = mine == len(self.gangs[i]) - 1
                for other in later[mine:] if last else later[mine : mine + 1]:
                    self.go(other, 1, way, part)
            self.done += 1

    def pump_array(self, a):
        gang = self.gang_of[a]
        self.pump(14 * sum(len(g) for g in self.gangs[: gang + 1]))


def greet(peers):
    barrier = pltpu.get_barrier_semaphore()
    for peer in peers:
        pl.semaphore_signal(
            barrier, inc=1, device_id=peer, device_id_type=pl.DeviceIdType.MESH
        )
    pl.semaphore_wait(barrier, len(peers))


def places():
    seq, tp = lax.axis_index("seq"), lax.axis_index("tp")
    place = ring_place(seq)
    nearby = (ring_seq(place + 1), ring_seq(place - 1))
    over_y = lax.rem(tp + 2, 4)
    over_core = tp + 1 - 2 * (tp % 2)
    peers = [{"seq": ring_seq(place + k)} for k in range(1, 8)]
    peers += [{"tp": over_y}, {"tp": over_core}]
    return seq, tp, place, nearby, over_y, over_core, peers


class Rows:
    def __init__(self, links, own, everyone, tp, over_y, over_core, rows):
        self.links, self.all, self.tp = links, everyone, tp
        self.over_y, self.over_core, self.rows = over_y, over_core, rows
        half = rows // 2
        self.first = [
            links.start(
                own.at[pl.ds(i * half, half)], self.block(tp, i * half, half), tp=over_y
            )
            for i in (0, 1)
        ]
        self.near = links.start(own, self.block(tp, 0, rows), tp=over_core)
        self.last = []

    def block(self, owner, offset, size):
        return self.all.at[pl.ds(pl.multiple_of(owner * self.rows + offset, 16), size)]

    def forward(self, i):
        half = self.rows // 2
        self.first[i].wait_recv()
        came = self.block(self.over_y, i * half, half)
        self.last.append(self.links.start(came, came, tp=self.over_core))

    def finish(self):
        self.near.wait_recv()
        for made in self.last:
            made.wait_recv()


FEATS = 160


def fill_tables(lengths, seq, tok, line, coefs, step):
    total = tok.shape[0]
    anchor = seq * total
    starts, at = [], 0
    for i in range(lengths.shape[0]):
        starts.append(at)
        at = at + lengths[i]

    def places_of(shape, axis):
        pos = lax.broadcasted_iota(jnp.int32, shape, axis)
        low = jnp.zeros(shape, jnp.int32) - anchor
        last = jnp.ones(shape, f32)
        for start in starts:
            here = start - anchor
            low = jnp.maximum(low, jnp.where(pos >= here, here, -anchor))
            last = jnp.where((pos < here) & (here < total), 0.0, last)
        return pos.astype(f32), low, last

    lane = lax.broadcasted_iota(jnp.int32, (total, 128), 1)
    pos, low, last = places_of((total, 128), 0)
    began = jnp.where(low < 0, 1.0, 0.0)
    first = jnp.maximum(low, 0).astype(f32)
    tok[...] = jnp.where(
        lane == 0, first, jnp.where(lane == 1, began, jnp.where(lane == 2, last, pos))
    )
    pos, low, last = places_of((8, total), 1)
    row = lax.broadcasted_iota(jnp.int32, (8, total), 0)
    line[...] = jnp.where(row == 0, pos, jnp.maximum(low, 0).astype(f32))

    def clear(lo, hi):
        free = jnp.ones((1, 128), f32)
        for start in starts:
            at = jnp.zeros((1, 128), jnp.int32) + start
            free = jnp.where((at >= lo * total) & (at < (hi + 1) * total), 0.0, free)
        return free

    z = seq // 2
    one = jnp.ones((1, 128), f32)
    first, second = clear(2 * z, 2 * z), clear(2 * z + 1, 2 * z + 1)
    before = 2 * (z - step)
    rows = [second, first] if step > 0 else [first, second]
    rows += [first * second, clear(before, before + 1)]
    coefs[...] = jnp.concatenate(rows + [one * 0.0] * 4, axis=0)


class Exchange:
    def __init__(self, links, st, near, term, first, second, given, states, coefs, seq, step):
        z, x = seq // 2, seq % 2
        self.st, self.near, self.term, self.first, self.second = st, near, term, first, second
        self.given, self.states, self.coefs, self.x = given, states, coefs, x
        self.turn = z if step > 0 else 3 - z
        self.late = x if step > 0 else 1 - x
        over_x = seq + 1 - 2 * x
        self.half = links.start(st.at[pl.ds(2 * (1 - x), 2)], near, seq=over_x)
        self.hop = links.copy(term, first, seq=seq + 2 * step)
        self.on = links.copy(term, second, seq=seq + 2 * step)
        self.far = links.copy(term, second, seq=seq + 4 * step)
        self.links, self.over_x = links, over_x

    def coef(self, k):
        return self.coefs[k : k + 1, :]

    def pair(self):
        self.half.wait_recv()
        for i in (0, 1):
            mine, theirs = self.st[2 * self.x + i].astype(f32), self.near[i].astype(f32)
            early = jnp.where(self.late == 0, mine, theirs)
            later = jnp.where(self.late == 0, theirs, mine)
            self.term[i] = (later + self.coef(0) * early).astype(bf16)

        @pl.when(self.turn % 2 == 0)
        def _():
            self.hop.start()

    def planes(self):
        @pl.when(self.turn % 2 == 1)
        def _():
            self.hop.wait_recv()

        @pl.when(self.turn == 1)
        def _():
            for i in (0, 1):
                came = self.coef(2) * self.first[i].astype(f32)
                self.term[i] = (self.term[i].astype(f32) + came).astype(bf16)
            self.on.start()
            self.far.start()

    def give(self):
        x = self.x
        for i in (0, 1):
            self.states[2 * x + i] = jnp.zeros((256, 128), f32)
            self.states[2 * (1 - x) + i] = jnp.zeros((256, 128), f32)

        def enter(i):
            return self.states.at[2 * x + i, pl.ds(0, 176)]

        @pl.when(self.turn == 1)
        def _():
            for i in (0, 1):
                enter(i)[...] = self.first[i].astype(f32)

        @pl.when(self.turn == 2)
        def _():
            self.on.wait_recv()
            for i in (0, 1):
                enter(i)[...] = self.second[i].astype(f32)

        @pl.when(self.turn == 3)
        def _():
            self.far.wait_recv()
            for i in (0, 1):
                older = self.coef(3) * self.second[i].astype(f32)
                enter(i)[...] = self.first[i].astype(f32) + older

        for i in (0, 1):
            came = enter(i)[...]
            mine, theirs = self.st[2 * x + i].astype(f32), self.near[i].astype(f32)
            early = jnp.where(self.late == 0, mine, theirs)
            passed = early + self.coef(1) * came
            self.given[0, i] = jnp.where(self.late == 0, passed, came).astype(bf16)
            enter(i)[...] = jnp.where(self.late == 0, came, passed)
        self.back = self.links.start(self.given.at[0], self.given.at[1], seq=self.over_x)

    def take(self):
        self.back.wait_recv()
        for i in (0, 1):
            self.states[2 * (1 - self.x) + i, 0:176, :] = self.given[1, i].astype(f32)

    def finish(self):
        @pl.when(self.turn % 2 == 0)
        def _():
            self.hop.wait_send()

        @pl.when(self.turn == 1)
        def _():
            self.on.wait_send()
            self.far.wait_send()


def ring_columns(place):
    return [pl.ds(pl.multiple_of(ring_seq(place - k) * 256, 256), 256) for k in relative_list(8)]


def phi(heads, h, select_a, select_b, lanes):
    a = dot(heads, select_a[h]) + lanes[0:1, :]
    b = dot(heads, select_b[h]) + lanes[1:2, :]
    return a, b


def fwd_kernel(
    lengths, sa_ref, sb_ref, lanes_ref, hm_ref, gain_first, gain_second,
    x_in, wq_in, wk_in, wv_in, wo_in, wg_in, wu_in, wd_in, c_in,
    wq_all, wo_all, wg_all, wu_all, wd_all, c_all,
    h1_out, qkv_out, yb_out, den_out, x1_out, h2_out, gate_out, up_out, m_out, sin_out, gain_out, terms_out,
    x_ref, tok_ref, line_ref, coef_ref, gain_ref, q_own, o_own, g_own, u_own, d_own,
    w_small, w_v, w_o, w_d, w_g, c_v,
    xg, h1, wq, wo, wg, wu, qkv, kq, num, den, yb, sc, rc, sy, ry, x1, gate, up, mm,
    gains_all, gains, st, st_x, st_t, st_z, st_y, st_g, s_in,
    send, recv, local,
):
    seq, tp, place, nearby, over_y, over_core, peers = places()
    z, x = seq // 2, seq % 2
    at = {k: j for j, k in enumerate(relative_list(8))}
    rows = x_ref.shape[0]
    total = 4 * rows
    links = Links(send, recv)
    locs = Sems(local)
    pending = []

    def store(src, dst):
        made = pltpu.make_async_copy(src, dst, locs.take())
        made.start()
        pending.append(made)

    def load(src, dst):
        made = pltpu.make_async_copy(src, dst, locs.take())
        made.start()
        return made

    got_qk = [load(wq_in, w_small.at[0:64]), load(wk_in, w_small.at[64:128]), load(wv_in, w_v)]
    columns = ring_columns(place)
    got_x = [load(x_in.at[:, c], x_ref.at[:, col(j)]) for j, c in enumerate(columns)]
    c_rows = pl.ds(pl.multiple_of(tp * rows, rows), rows)
    got_c = [load(c_in.at[:, c], c_v.at[:, col(j)]) for j, c in enumerate(columns)]
    got_o = load(wo_in, w_o)
    ff = wd_in.shape[0]
    got_g = load(wg_in, w_g.at[pl.ds(0, ff)])
    got_d = load(wd_in, w_d.at[pl.ds(0, ff)])

    def turn(src, dst):
        for i in range(0, ff, 128):
            size = min(128, ff - i)
            dst[:, i : i + size] = src[i : i + 128, :].T[:, :size].astype(bf16)

    gain_ref[...] = jnp.concatenate(
        [gain_first[...], gain_second[...], jnp.zeros((14, 256), f32)], axis=0
    ).astype(bf16)
    greet(peers)
    gain_flying = [
        links.start(gain_ref, gains_all.at[at[k]], seq=ring_seq(place + k)) for k in range(1, 8)
    ]
    for made in got_x:
        made.wait()
    xrows = Rows(links, x_ref, xg, tp, over_y, over_core, rows)
    for made in got_qk:
        made.wait()
    q_own[:, 0:128] = w_small[...].T.astype(bf16)
    q_own[:, 128:640] = w_v[...].astype(bf16)
    ring = Gather(
        links,
        [(q_own, wq_all), (o_own, wo_all), (g_own, wg_all), (u_own, wu_all), (d_own, wd_all)],
        128,
        nearby,
        [[0], [1], [2, 3], [4]],
    )
    own_in = [
        load(x_ref, xrows.block(tp, 0, rows)),
        load(gain_ref, gains_all.at[at[0]]),
    ]
    got_o.wait()
    o_own[...] = w_o[...].T.astype(bf16)
    ring.pump(2)
    got_g.wait()
    turn(w_g, g_own)
    got_u = load(wu_in, w_g.at[pl.ds(0, ff)])
    ring.pump(4)
    got_d.wait()
    turn(w_d, d_own)
    got_u.wait()
    turn(w_g, u_own)
    own_kept = [load(own, everyone.at[at[0]]) for own, everyone in ring.arrays]
    fill_tables(lengths, seq, tok_ref, line_ref, coef_ref, 1)

    ring.pump(6)
    xrows.forward(0)
    for made in gain_flying:
        made.wait_recv()
    for made in own_in:
        made.wait()
    for j in range(8):
        chunk = gains_all[j].astype(f32)
        gains[0:8, j * 256 : (j + 1) * 256] = chunk[0:8]
    ring.pump(10)
    xrows.forward(1)
    ring.pump_array(0)
    own_kept[0].wait()
    got = load_weights(load, wq_all, wq)
    xrows.finish()

    def norm_first(i, _):
        r = pl.ds(pl.multiple_of(i * 32, 32), 32)
        v = xg[r, :].astype(f32)
        s = lax.rsqrt(jnp.mean(v * v, axis=1, keepdims=True) + epsilon)
        h1[r, :] = (v * s * gains[0:1, :]).astype(bf16)
        return 0

    lax.fori_loop(0, total // 32, norm_first, 0)
    links.sent_now(xrows.last)
    kept_h1 = load(h1, h1_out)
    for made in got_c:
        made.wait()
    crows = Rows(links, c_v, c_all, tp, over_y, over_core, rows)
    kept_c = load(c_v, c_all.at[c_rows])
    ring.pump(15)
    for made in got:
        made.wait()

    def project(i, _):
        r = pl.ds(pl.multiple_of(i * 256, 256), 256)
        res = dot(h1[r, :], wq[...])
        qkv[r, :] = res.astype(bf16)
        kq[r, :] = pltpu.roll(res[:, :128], 64, 1).astype(bf16)
        return 0

    lax.fori_loop(0, total // 256, project, 0)
    store(qkv, qkv_out)
    ring.pump(16)

    heads = 4

    def head_v(h):
        return slice(128 + h * 128, 256 + h * 128)

    for h in range(heads):

        def state(i, c, h=h):
            s, zz = c
            r = pl.ds(pl.multiple_of(i * 256, 256), 256)
            a, b = phi(kq[r, :], h, sa_ref, sb_ref, lanes_ref)
            f = a * b * lanes_ref[2:3, :] * tok_ref[r, 2:3]
            s = s + dot_tt(f.astype(bf16), qkv[r, head_v(h)])
            return s, zz + jnp.sum(f, axis=0, keepdims=True)

        s, zz = lax.fori_loop(
            0, total // 256, state, (jnp.zeros((256, 128), f32), jnp.zeros((1, 256), f32))
        )
        pack_state(st, h, s, zz)
        ring.pump(17 + h)
    moved = Exchange(links, st, st_x, st_t, st_z, st_y, st_g, s_in, coef_ref, seq, 1)

    def local_head(h):
        for i in range(total // 256):
            r = slice(i * 256, (i + 1) * 256)
            span = (i + 1) * 256
            qm = (qkv[r, :128].astype(f32) * hm_ref[h : h + 1, :]).astype(bf16)
            u = dot_t(qm, kq[:span, :])
            keep = (line_ref[0:1, :span] >= tok_ref[r, 0:1]) & (
                line_ref[0:1, :span] <= tok_ref[r, 3:4]
            )
            kap = jnp.where(keep, (0.5 * u + 1.0) * u + 1.0, 0.0)
            den[r, h : h + 1] = jnp.sum(kap, axis=1, keepdims=True)
            num[r, h * 128 : (h + 1) * 128] = dot(kap.astype(bf16), qkv[:span, head_v(h)])

    local_head(0)
    ring.pump(22)
    moved.pair()
    local_head(1)
    ring.pump(24)
    moved.planes()
    local_head(2)
    ring.pump(26)
    moved.give()
    local_head(3)
    ring.pump(28)
    moved.take()
    store(s_in, sin_out)
    for h in range(heads):
        z_row = jnp.concatenate([s_in[h, 160:161, :], s_in[h, 161:162, :]], axis=1)
        feat = jax.lax.broadcasted_iota(jnp.int32, (256, 128), 0)
        s_low = jnp.where(feat < FEATS, s_in[h], 0.0).astype(bf16)

        def carry(i, _, h=h, z_row=z_row, s_low=s_low):
            r = pl.ds(pl.multiple_of(i * 256, 256), 256)
            a, b = phi(qkv[r, 0:128], h, sa_ref, sb_ref, lanes_ref)
            f = a * b * lanes_ref[2:3, :] * tok_ref[r, 1:2]
            hv = slice(h * 128, (h + 1) * 128)
            top = num[r, hv] + dot(f.astype(bf16), s_low)
            low = den[r, h : h + 1] + jnp.sum(f * z_row, axis=1, keepdims=True)
            den[r, h : h + 1] = low
            y = top / low
            yb[r, hv] = y.astype(bf16)
            return 0

        lax.fori_loop(0, total // 256, carry, 0)
        ring.pump(28 + (h + 1) // 2)
    store(yb, yb_out)
    store(den, den_out)
    ring.pump_array(1)
    own_kept[1].wait()
    got = load_weights(load, wo_all, wo)
    for made in got:
        made.wait()

    y_at, c_at = tp // 2, tp % 2

    def out_rows(block):
        return yb[pl.ds(pl.multiple_of(block * rows, rows), rows), :]

    cols = 512
    to_core = []
    for yy in (0, 1):

        def core_cols(i, _, yy=yy):
            c = pl.ds(pl.multiple_of(i * cols, cols), cols)
            sc[yy, :, c] = dot_t(out_rows(yy * 2 + 1 - c_at), wo[c, :]).astype(bf16)
            return 0

        lax.fori_loop(0, 2048 // cols, core_cols, 0)
        to_core.append(links.start(sc.at[yy], rc.at[yy], tp=over_core))
    for made in to_core:
        made.wait_recv()
    ring.pump(32)

    def away_cols(i, _):
        c = pl.ds(pl.multiple_of(i * cols, cols), cols)
        part = dot_t(out_rows((1 - y_at) * 2 + c_at), wo[c, :])
        sy[:, c] = (part + rc[1 - y_at, :, c].astype(f32)).astype(bf16)
        return 0

    lax.fori_loop(0, 2048 // cols, away_cols, 0)
    to_y = links.start(sy, ry, tp=over_y)

    def own_cols(i, _):
        c = pl.ds(pl.multiple_of(i * cols, cols), cols)
        x1[:, c] = (
            dot_t(out_rows(tp), wo[c, :]) + rc[y_at, :, c].astype(f32) + x_ref[:, c].astype(f32)
        )
        return 0

    lax.fori_loop(0, 2048 // cols, own_cols, 0)
    ring.pump(34)
    to_y.wait_recv()
    ring.pump(37)

    links.sent_now(xrows.first + [xrows.near])
    ho = x_ref

    def norm_second(i, _):
        r = pl.ds(pl.multiple_of(i * 32, 32), 32)
        v = x1[r, :] + ry[r, :].astype(f32)
        x1[r, :] = v
        s = lax.rsqrt(jnp.mean(v * v, axis=1, keepdims=True) + epsilon)
        ho[r, :] = (v * s * gains[1:2, :]).astype(bf16)
        return 0

    lax.fori_loop(0, rows // 32, norm_second, 0)
    store(x1, x1_out)
    store(gains, gain_out)
    h2 = xg
    hrows = Rows(links, ho, h2, tp, over_y, over_core, rows)
    own_in = load(ho, hrows.block(tp, 0, rows))
    ring.pump(40)
    hrows.forward(0)
    ring.pump(43)
    hrows.forward(1)
    crows.forward(0)
    crows.forward(1)
    hrows.finish()
    crows.finish()
    own_in.wait()
    store(h2, h2_out)
    kept_h1.wait()
    kept_c.wait()
    got_c = load(c_all, h1)
    ring.pump_array(2)
    own_kept[2].wait()
    got = load_weights(load, wg_all, wg)
    ring.pump_array(3)
    own_kept[3].wait()
    got += load_weights(load, wu_all, wu)
    for made in got:
        made.wait()

    def gate_up(i, _):
        r = pl.ds(pl.multiple_of(i * 128, 128), 128)
        g = dot(h2[r, :], wg[...])
        uu = dot(h2[r, :], wu[...])
        gate[r, :] = g.astype(bf16)
        up[r, :] = uu.astype(bf16)
        mm[r, :] = (g * jax.nn.sigmoid(g) * uu).astype(bf16)
        return 0

    for quarter in range(4):
        lax.fori_loop(quarter * total // 512, (quarter + 1) * total // 512, gate_up, 0)
        ring.pump(58 + 2 * quarter)
    store(gate, gate_out)
    store(up, up_out)
    store(mm, m_out)
    got_c.wait()
    links.sent_now([ring.flying[a, 1, way, part] for a in (2, 3) for way in (0, 1) for part in (0, 1)])
    out_sems = [locs.take(), locs.take()]
    buffers = [g_own, u_own]

    def keep_terms(j, k):
        return pltpu.make_async_copy(buffers[k], terms_out.at[col(j)], out_sems[k])

    def grad_down(i, _):
        for k in (0, 1):
            pl.when(i > 0)(lambda k=k: keep_terms(2 * i - 2 + k, k).wait())
            buffers[k][...] = dot_tt(h1[:, col(2 * i + k)], mm[...]).astype(bf16)
            keep_terms(2 * i + k, k).start()
        return 0

    lax.fori_loop(0, 2, grad_down, 0)
    ring.pump(66)
    lax.fori_loop(2, 4, grad_down, 0)
    for k in (0, 1):
        keep_terms(6 + k, k).wait()
    ring.pump_array(4)
    own_kept[4].wait()
    for made in pending:
        made.wait()
    links.finish()
    moved.finish()


def pack_state(st, h, s, zz):
    st[h, 0:FEATS, :] = s[:FEATS].astype(bf16)
    tail = jnp.concatenate([zz[:, :128], zz[:, 128:], jnp.zeros((14, 128), f32)], axis=0)
    st[h, FEATS : FEATS + 16, :] = tail.astype(bf16)


def load_weights(load, everyone, flat):
    count, chunk = everyone.shape[0], everyone.shape[1]
    return [load(everyone.at[j], flat.at[pl.ds(j * chunk, chunk)]) for j in range(count)]


class Scatter:
    def __init__(self, slots, send, recv, nearby):
        self.slots, self.send, self.recv, self.nearby = slots, send, recv, nearby

    def copy(self, a, step, way, sub, src, slot, width):
        return pltpu.make_async_remote_copy(
            src_ref=src,
            dst_ref=self.piece(slot, way, sub, width),
            send_sem=self.send.at[a % 2, way, sub],
            recv_sem=self.recv.at[a % 2, way, sub, step],
            device_id={"seq": self.nearby[way]},
            device_id_type=pl.DeviceIdType.MESH,
        )

    def slot(self, a, step):
        return (a % 2) * 4 + (a // 2 * 7 + step) % 4

    def rows(self, way, sub, base=0):
        start = base + way * 128 + sub * 64
        return pl.ds(start if isinstance(start, int) else pl.multiple_of(start, 64), 64)

    def piece(self, slot, way, sub, width):
        return self.slots.at[slot, self.rows(way, sub), pl.ds(0, width)]

    def begin(self, a, own, width, column=0):
        for sub in (0, 1):
            for way in (0, 1):
                src = own.at[self.rows(way, sub, way * 256), pl.ds(column, width)]
                self.copy(a, 0, way, sub, src, self.slot(a, 0), width).start()

    def event(self, a, e, own, width, out, column=0):
        step, sub = e // 2, e % 2
        is_last = step // 6
        here = self.slot(a, step)
        far = (step + 1) // 4
        place0 = (1 - far) * 2 * (step + 1) + far * (11 - 2 * step) + is_last * 8
        far = (step + 2) // 4 - is_last
        place1 = (1 - far) * (3 + 2 * step) + far * (10 - 2 * step) + is_last * 9
        places = (place0, place1)
        for way in (0, 1):
            piece = self.piece(here, way, sub, width)
            came = self.copy(a, step, way, sub, piece, here, width)
            came.wait_recv()
            came.wait_send()

        def summed(way):
            mine = own[self.rows(way, sub, places[way] * 256), pl.ds(column, width)]
            came = self.slots[here, self.rows(way, sub), pl.ds(0, width)]
            return came.astype(f32) + mine.astype(f32)

        def on():
            for way in (0, 1):
                self.slots[here, self.rows(way, sub), pl.ds(0, width)] = summed(way).astype(bf16)
                piece = self.piece(here, way, sub, width)
                self.copy(a, step + 1, way, sub, piece, self.slot(a, step + 1), width).start()

        def end():
            for way in (0, 1):
                out[self.rows(way, sub), pl.ds(0, width)] = summed(way)

        if isinstance(e, int):
            if step < 6:
                on()
            else:
                end()
        else:
            pl.when(step < 6)(on)
            pl.when(step == 6)(end)


class TpSum:
    def __init__(self, part, from_core, from_y, sems, credits, tp, over_y, over_core):
        self.part, self.from_core, self.from_y = part, from_core, from_y
        self.sems, self.credits = sems, credits
        self.tp, self.over_y, self.over_core = tp, over_y, over_core
        self.y, self.c = tp // 2, tp % 2

    def to_core(self, i, yy):
        return pltpu.make_async_remote_copy(
            src_ref=self.part.at[i, yy * 2 + 1 - self.c],
            dst_ref=self.from_core.at[i, yy],
            send_sem=self.sems.at[yy, i],
            recv_sem=self.sems.at[2 + yy, i],
            device_id={"tp": self.over_core},
            device_id_type=pl.DeviceIdType.MESH,
        )

    def to_y(self, i):
        return pltpu.make_async_remote_copy(
            src_ref=self.part.at[i, (1 - self.y) * 2 + self.c],
            dst_ref=self.from_y.at[i],
            send_sem=self.sems.at[4, i],
            recv_sem=self.sems.at[5, i],
            device_id={"tp": self.over_y},
            device_id_type=pl.DeviceIdType.MESH,
        )

    def sent(self, i):
        self.to_core(i, 0).wait_send()
        self.to_core(i, 1).wait_send()
        self.to_y(i).wait_send()

    def offer(self, i, turn, value):
        if turn > 0:
            self.sent(i)
        for block in range(4):
            self.part[i, block] = value[block * 256 : (block + 1) * 256].astype(bf16)
        if turn > 0:
            pl.semaphore_wait(self.credits.at[0], 1)
        for yy in (0, 1):
            self.to_core(i, yy).start()

    def pass_on(self, i, turn):
        for yy in (0, 1):
            self.to_core(i, yy).wait_recv()
        away = (1 - self.y) * 2 + self.c
        self.part[i, away] = (
            self.part[i, away].astype(f32) + self.from_core[i, 1 - self.y].astype(f32)
        ).astype(bf16)
        if turn > 0:
            pl.semaphore_wait(self.credits.at[1], 1)
        self.to_y(i).start()

    def take(self, i, turn, use):
        self.to_y(i).wait_recv()
        use(
            self.part[i, self.tp].astype(f32)
            + self.from_core[i, self.y].astype(f32)
            + self.from_y[i].astype(f32)
        )
        if turn < 2:
            for k, peer in ((0, self.over_core), (1, self.over_y)):
                pl.semaphore_signal(
                    self.credits.at[k],
                    inc=1,
                    device_id={"tp": peer},
                    device_id_type=pl.DeviceIdType.MESH,
                )


def col(i, width=256):
    return pl.ds(i * width if isinstance(i, int) else pl.multiple_of(i * width, width), width)


def bwd_kernel(
    lengths, sa_ref, sb_ref, lanes_ref, hm_ref, gains, s_in, den, gain_first, gain_second,
    x_in, x1_in, wq_all, wo_all, wg_all, wu_all, wd_all, c_all, h1_all, qkv_all, yb_all, h2_all,
    gate_all, up_all, m_all, terms_all,
    d_out, g_out, u_out, oq_out, block_out, input_out, gain_out, u_kept,
    tok_ref, line_ref, coef_ref, terms, terms_core, terms_y,
    slots, s1, s2, wo, stream, hs, rows_all, mm, dup, tiles, qkv, kq, yb, dnum, dden, dden_t, dqkv,
    dq, dk, part, from_core, from_y, acc, x1, fout, st, st_x, st_t, st_z, st_y, st_g, s_back, own_rows,
    ring_send, ring_recv, tp_sems, credits, send, recv, local, tile_sems,
):
    seq, tp, place, nearby, over_y, over_core, peers = places()
    z, x = seq // 2, seq % 2
    rows, width = own_rows.shape
    total = 4 * rows
    ff = mm.shape[1]
    links = Links(send, recv)
    locs = Sems(local)

    def load(src, dst):
        made = pltpu.make_async_copy(src, dst, locs.take())
        made.start()
        return made

    def whole(everyone, flat):
        count, chunk = everyone.shape[0], everyone.shape[1]
        return [load(everyone.at[j], flat.at[pl.ds(j * chunk, chunk)]) for j in range(count)]

    got_m = load(m_all, mm)
    got_wd = whole(wd_all, s2)
    got_terms = load(terms_all, s1)
    got_c = load(c_all, rows_all)
    greet(peers)
    ring = Scatter(slots, ring_send, ring_recv, nearby)
    ring.begin(0, terms_all, ff)
    got_x1 = load(x1_in, x1)
    fill_tables(lengths, seq, tok_ref, line_ref, coef_ref, -1)
    columns = ring_columns(place)
    got_qkv = [load(qkv_all, qkv), load(yb_all, yb)]
    got_wo = whole(wo_all, wo)
    sums = TpSum(part, from_core, from_y, tp_sems, credits, tp, over_y, over_core)

    def run(n, body, pumps=None):
        def step(i, _):
            body(i)
            if pumps:
                a, first, count = pumps
                every = n // count
                pl.when((i + 1) % every == 0)(lambda: event(a, first + (i + 1) // every - 1))
            return 0

        lax.fori_loop(0, n, step, 0)

    plan = {0: (s1, ff, 0), 1: (s2, ff, 0), 2: (s1, ff, 0), 3: (s2, 1152, 0)}

    def event(a, e):
        own, wide, column = plan[a]
        ring.event(a, e, own, wide, fout, column)

    def begin(a):
        own, wide, column = plan[a]
        ring.begin(a, own, wide, column)

    def events(a, first, last):
        lax.fori_loop(first, last, lambda e, _: (event(a, e), 0)[1], 0)

    def both(a, first, b, second, count):
        def pair(i, _):
            event(a, first + i)
            event(b, second + i)
            return 0

        lax.fori_loop(0, count, pair, 0)

    def chunks_of(source, size, body, pumps=None, count=8):
        def copies(i, slot):
            return [
                pltpu.make_async_copy(a, b, tile_sems.at[k, slot])
                for k, (a, b) in enumerate(source(i, slot))
            ]

        for made in copies(0, 0):
            made.start()

        def step(i):
            slot = i % 2

            @pl.when(i + 1 < count)
            def _():
                for made in copies(i + 1, 1 - slot):
                    made.start()

            for made in copies(i, slot):
                made.wait()
            body(i, slot)

        run(count, step, pumps)

    got_m.wait()
    for made in got_wd:
        made.wait()
    got_terms.wait()

    def mlp(i):
        sums.offer(i, 0, dot_t(mm[...], s2[col(i), :]))
        pl.when(i > 0)(lambda: sums.pass_on(i - 1, 0))

    run(8, mlp, (0, 0, 2))
    sums.pass_on(7, 0)

    def gate_up_tiles(i, slot):
        r = col(i, 128)
        return [
            (gate_all.at[r], tiles.at[slot, pl.ds(0, 128)]),
            (up_all.at[r], tiles.at[slot, pl.ds(128, 128)]),
        ]

    def grad_gate_up(i, slot):
        r = col(i, 128)
        dm = dot(rows_all[r, :], s2[...]).astype(bf16).astype(f32)
        g = tiles[slot, 0:128].astype(f32)
        u = tiles[slot, 128:256].astype(f32)
        s = jax.nn.sigmoid(g)
        mm[r, :] = (dm * u * s * (1.0 + g * (1.0 - s))).astype(bf16)
        dup[r, :] = (dm * (g * s)).astype(bf16)

        pl.when(i >= 3)(lambda: take_block(i - 3))

    def take_block(i):
        def use(value):
            own_rows[:, col(i)] = (x1[:, col(i)] + value).astype(bf16)

        sums.take(i, 0, use)

    got_x1.wait()
    got_c.wait()
    chunks_of(gate_up_tiles, 8, grad_gate_up, (0, 2, 4))

    def w_tiles(i, slot):
        return [(wg_all.at[i], stream.at[slot, 0]), (wu_all.at[i], stream.at[slot, 1])]

    def grad_hidden(i, slot):
        pl.when(i < 3)(lambda: take_block(5 + i))
        value = dot_t(mm[...], stream[slot, 0]) + dot_t(dup[...], stream[slot, 1])
        sums.offer(i, 1, value)
        pl.when(i > 0)(lambda: sums.pass_on(i - 1, 1))

    chunks_of(w_tiles, 8, grad_hidden, (0, 6, 4))
    kept = [load(own_rows.at[:, col(j)], block_out.at[:, c]) for j, c in enumerate(columns)]
    pending = []
    sums.pass_on(7, 1)

    def h_tiles(everyone):
        return lambda i, slot: [(everyone.at[:, col(i)], hs.at[slot])]

    def keep_up(i, slot):
        return pltpu.make_async_copy(tiles.at[slot], u_kept.at[col(i)], tile_sems.at[1, slot])

    def grads(i, slot):
        s2[col(i), :] = dot_tt(hs[slot], mm[...]).astype(bf16)
        pl.when(i >= 2)(lambda: keep_up(i - 2, slot).wait())
        tiles[slot] = dot_tt(hs[slot], dup[...]).astype(bf16)
        keep_up(i, slot).start()
        pl.when(i == 1)(lambda: begin(1))

    chunks_of(h_tiles(h2_all), 8, grads, (0, 10, 2))
    keep_up(6, 0).wait()
    keep_up(7, 1).wait()

    def take_second(i):
        def use(value):
            acc[:, col(i)] = value

        sums.take(i, 1, use)

    run(2, take_second)
    both(1, 0, 0, 12, 2)
    done = load(fout.at[:, pl.ds(0, ff)], d_out)
    got_up = load(u_kept, s1)
    lax.fori_loop(2, 5, lambda i, _: (take_second(i), 0)[1], 0)
    events(1, 2, 3)
    got_up.wait()
    begin(2)
    lax.fori_loop(5, 8, lambda i, _: (take_second(i), 0)[1], 0)
    both(1, 3, 2, 0, 1)

    for made in kept:
        made.wait()

    def norm_back_second(i, _):
        r = pl.ds(pl.multiple_of(i * 32, 32), 32)
        v = x1[r, :]
        s = lax.rsqrt(jnp.mean(v * v, axis=1, keepdims=True) + epsilon)
        n = v * s
        dn = acc[r, :] * gains[1:2, :]
        own = pl.ds(pl.multiple_of(tp * rows + i * 32, 32), 32)
        back = rows_all[own, :].astype(f32) + s * (
            dn - n * jnp.mean(dn * n, axis=1, keepdims=True)
        )
        acc[r, :] = back
        own_rows[r, :] = back.astype(bf16)
        return 0

    lax.fori_loop(0, rows // 32, norm_back_second, 0)
    da = Rows(links, own_rows, rows_all, tp, over_y, over_core, rows)
    own_in = load(own_rows, da.block(tp, 0, rows))

    both(1, 4, 2, 1, 1)
    da.forward(0)
    both(1, 5, 2, 2, 1)
    da.forward(1)
    for made in got_qkv + got_wo:
        made.wait()
    da.finish()
    own_in.wait()
    links.sent_now(da.first + [da.near])
    got_x = [load(x_in.at[:, c], own_rows.at[:, col(j)]) for j, c in enumerate(columns)]

    def head_v(h):
        return slice(128 + h * 128, 256 + h * 128)

    def grad_attended(i):
        r = col(i, 256)
        dy = dot(rows_all[r, :], wo[...])
        kq[r, :] = pltpu.roll(qkv[r, 0:128].astype(f32), 64, 1).astype(bf16)
        columns = []
        for h in range(4):
            hv = slice(h * 128, (h + 1) * 128)
            under = 1.0 / den[r, h : h + 1]
            part_h = dy[:, hv]
            dnum[r, hv] = (part_h * under).astype(bf16)
            low = jnp.sum(part_h * yb[r, hv].astype(f32), axis=1, keepdims=True)
            columns.append(-low * under)
        lane = lax.broadcasted_iota(jnp.int32, (256, 128), 1)
        packed = jnp.zeros((256, 128), f32)
        for h in range(4):
            packed = jnp.where(lane == h, columns[h], packed)
        dden[r, :] = packed
        dden_t[i] = packed.T[0:8, :]

    run(4, grad_attended)
    both(1, 6, 2, 3, 1)

    for h in range(4):

        def state(i, c, h=h):
            s, zz = c
            r = col(i, 256)
            a, b = phi(qkv[r, 0:128], h, sa_ref, sb_ref, lanes_ref)
            f = a * b * lanes_ref[2:3, :] * tok_ref[r, 1:2]
            s = s + dot_tt(f.astype(bf16), dnum[r, h * 128 : (h + 1) * 128])
            return s, zz + jnp.sum(f * dden[r, h : h + 1], axis=0, keepdims=True)

        s, zz = lax.fori_loop(
            0, 4, state, (jnp.zeros((256, 128), f32), jnp.zeros((1, 256), f32))
        )
        pack_state(st, h, s, zz)
    moved = Exchange(links, st, st_x, st_t, st_z, st_y, st_g, s_back, coef_ref, seq, -1)
    both(1, 7, 2, 4, 1)

    dq[...] = jnp.zeros(dq.shape, f32)

    def local_head(h):
        hm = hm_ref[h : h + 1, :]
        hv = slice(h * 128, (h + 1) * 128)
        for j in range(total // 256):
            k_rows = slice(j * 256, (j + 1) * 256)
            dv_s = jnp.zeros((256, 128), f32)
            dk_s = jnp.zeros((256, 128), f32)
            for i in range(j, total // 256):
                q_rows = slice(i * 256, (i + 1) * 256)
                qm = (qkv[q_rows, 0:128].astype(f32) * hm).astype(bf16)
                u = dot_t(kq[k_rows, :], qm)
                keep = tok_ref[k_rows, 3:4] >= line_ref[1:2, q_rows]
                if i == j:
                    keep = keep & (tok_ref[k_rows, 3:4] <= line_ref[0:1, q_rows])
                kap = jnp.where(keep, (0.5 * u + 1.0) * u + 1.0, 0.0).astype(bf16)
                dn = dnum[q_rows, hv]
                grad = dot_t(qkv[k_rows, head_v(h)], dn) + dden_t[i, h : h + 1, :]
                du = jnp.where(keep, grad * (1.0 + u), 0.0).astype(bf16)
                dv_s = dv_s + dot(kap, dn)
                dk_s = dk_s + dot(du, qm)
                dq[q_rows, :] += dot_tt(du, kq[k_rows, :]) * hm
            dqkv[k_rows, head_v(h)] = dv_s.astype(bf16)
            if h == 0:
                dk[k_rows, :] = dk_s
            else:
                dk[k_rows, :] += dk_s

    local_head(0)
    moved.pair()
    both(1, 8, 2, 5, 1)
    local_head(1)
    moved.planes()
    both(1, 9, 2, 6, 1)
    local_head(2)
    moved.give()
    both(1, 10, 2, 7, 1)
    local_head(3)
    both(1, 11, 2, 8, 1)
    moved.take()

    def split_state(ref, h):
        z_row = jnp.concatenate([ref[h, 160:161, :], ref[h, 161:162, :]], axis=1)
        feat = lax.broadcasted_iota(jnp.int32, (256, 128), 0)
        return jnp.where(feat < FEATS, ref[h], 0.0).astype(bf16), z_row

    for h in range(4):
        s_q, z_q = split_state(s_in, h)
        s_k, z_k = split_state(s_back, h)
        hv = slice(h * 128, (h + 1) * 128)

        def through(grad, a, b, h=h):
            grad = grad * lanes_ref[2:3, :]
            return dot_t((grad * b).astype(bf16), sa_ref[h]) + dot_t(
                (grad * a).astype(bf16), sb_ref[h]
            )

        def carried_part(i, _, h=h, s_q=s_q, z_q=z_q, s_k=s_k, z_k=z_k, hv=hv, through=through):
            r = col(i, 256)
            a, b = phi(qkv[r, 0:128], h, sa_ref, sb_ref, lanes_ref)
            grad = dot_t(dnum[r, hv], s_q) + dden[r, h : h + 1] * z_q
            dq[r, :] += through(grad * tok_ref[r, 1:2], a, b)
            a, b = phi(kq[r, :], h, sa_ref, sb_ref, lanes_ref)
            last = tok_ref[r, 2:3]
            grad = dot_t(qkv[r, head_v(h)], s_k) + z_k
            dk[r, :] += through(grad * last, a, b)
            f = (a * b * lanes_ref[2:3, :] * last).astype(bf16)
            dqkv[r, head_v(h)] = (dqkv[r, head_v(h)].astype(f32) + dot(f, s_k)).astype(bf16)
            return 0

        lax.fori_loop(0, 4, carried_part, 0)

    def join(i):
        r = col(i, 256)
        dqkv[r, 0:128] = (dq[r, :] + pltpu.roll(dk[r, :], 64, 1)).astype(bf16)

    run(4, join)
    done.wait()
    both(1, 12, 2, 9, 2)
    done = load(fout.at[:, pl.ds(0, ff)], g_out)
    own_w = load(wg_all.at[7], stream.at[0, 0])
    own_w.wait()
    gain_two = jnp.sum(fout[:, 0:ff] * stream[0, 0].astype(f32), axis=1, keepdims=True)

    def wq_tiles(i, slot):
        return [(wq_all.at[i], stream.at[slot, 0, :, pl.ds(0, 640)])]

    def grad_hidden_first(i, slot):
        sums.offer(i, 2, dot_t(dqkv[...], stream[slot, 0, :, 0:640]))
        pl.when(i > 0)(lambda: sums.pass_on(i - 1, 2))

    chunks_of(wq_tiles, 8, grad_hidden_first, (2, 11, 1))
    sums.pass_on(7, 2)

    def grad_out_qkv(i, slot):
        s2[col(i), 0:512] = dot_tt(rows_all[:, col(i)], yb[...]).astype(bf16)
        s2[col(i), 512:1152] = dot_tt(hs[slot], dqkv[...]).astype(bf16)

        pl.when(i == 1)(lambda: begin(3))

    chunks_of(h_tiles(h1_all), 8, grad_out_qkv, (3, 0, 1))
    done.wait()
    both(2, 12, 3, 1, 2)
    done = load(fout.at[:, pl.ds(0, ff)], u_out)
    def take_first(i):
        def use(value):
            x1[:, col(i)] = value

        sums.take(i, 2, use)

    run(8, take_first, (3, 3, 4))
    for made in got_x:
        made.wait()

    def norm_back_first(i, _):
        r = pl.ds(pl.multiple_of(i * 32, 32), 32)
        v = own_rows[r, :].astype(f32)
        s = lax.rsqrt(jnp.mean(v * v, axis=1, keepdims=True) + epsilon)
        n = v * s
        dn = x1[r, :] * gains[0:1, :]
        acc[r, :] += s * (dn - n * jnp.mean(dn * n, axis=1, keepdims=True))
        return 0

    lax.fori_loop(0, rows // 32, norm_back_first, 0)
    pending += [load(acc.at[:, col(j)], input_out.at[:, c]) for j, c in enumerate(columns)]
    own_w = load(wu_all.at[7], stream.at[0, 0])
    own_q = load(wq_all.at[7], stream.at[1, 0, :, pl.ds(0, 640)])
    own_w.wait()
    own_q.wait()
    gain_two += jnp.sum(fout[:, 0:ff] * stream[0, 0].astype(f32), axis=1, keepdims=True)
    events(3, 7, 12)
    done.wait()
    events(3, 12, 14)
    pending.append(load(fout.at[:, pl.ds(0, 1152)], oq_out))
    gain_one = jnp.sum(fout[:, 512:1152] * stream[1, 0, :, 0:640].astype(f32), axis=1, keepdims=True)
    lane = lax.broadcasted_iota(jnp.int32, (256, 128), 1)
    both = jnp.where(lane == 0, gain_one, jnp.where(lane == 1, gain_two, 0.0)).T[0:8, :]
    terms[0] = both
    over = links.start(terms.at[0], terms_core, tp=over_core)
    over.wait_recv()
    both = both + terms_core[...]
    terms[1] = both
    over = links.start(terms.at[1], terms_y, tp=over_y)
    over.wait_recv()
    own_gains = jnp.concatenate(
        [gain_first[...], gain_second[...], jnp.ones((6, 256), f32)], axis=0
    ).astype(bf16)
    terms[2] = (both + terms_y[...]) / own_gains.astype(f32)
    pending.append(load(terms.at[2], gain_out))
    run(8, lambda i: sums.sent(i))
    for made in pending:
        made.wait()
    links.finish()
    moved.finish()


def feature_tables(heads):
    first = np.zeros((heads, 128, 256), np.float32)
    second = np.zeros((heads, 128, 256), np.float32)
    lanes = np.zeros((8, 256), np.float32)
    f = 0
    for i in range(FEAT):
        for j in range(i, FEAT):
            for h in range(heads):
                first[h, h * FEAT + i, f] = 1
                second[h, h * FEAT + j, f] = 1
            lanes[2, f] = square_coef if i == j else square_coef * 2**0.5
            f += 1
    for i in range(FEAT):
        for h in range(heads):
            first[h, h * FEAT + i, f] = 1
        lanes[1, f] = 1
        lanes[2, f] = linear_coef
        f += 1
    lanes[0, f] = lanes[1, f] = lanes[2, f] = 1
    mask = np.zeros((8, 128), np.float32)
    for h in range(heads):
        mask[h, h * FEAT : (h + 1) * FEAT] = 0.25
    return first, second, lanes, mask


def forward_pass(lengths, constants, gain_first, gain_second, x_in, weights, c_in):
    rows, width = x_in.shape
    total = 4 * rows
    ff = weights[4].shape[0]
    hbm = pl.BlockSpec(memory_space=pl.ANY)
    vmem = pl.BlockSpec(memory_space=pltpu.VMEM)

    def shape(*dims, dtype=bf16):
        return jax.ShapeDtypeStruct(dims, dtype)

    outs = (
        shape(8, 256, 640),
        shape(8, 256, 512),
        shape(8, 256, ff),
        shape(8, 256, ff),
        shape(8, 256, ff),
        shape(total, width),
        shape(total, width),
        shape(total, 640),
        shape(total, 512),
        shape(total, 128, dtype=f32),
        shape(rows, width, dtype=f32),
        shape(total, width),
        shape(total, ff),
        shape(total, ff),
        shape(total, ff),
        shape(4, 256, 128, dtype=f32),
        shape(8, width, dtype=f32),
        shape(width, ff),
    )
    scratch = [
        pltpu.VMEM((rows, width), bf16),
        pltpu.VMEM((total, 128), f32),
        pltpu.VMEM((8, total), f32),
        pltpu.VMEM((8, 128), f32),
        pltpu.VMEM((16, 256), bf16),
        pltpu.VMEM((256, 640), bf16),
        pltpu.VMEM((256, 512), bf16),
        pltpu.VMEM((256, ff), bf16),
        pltpu.VMEM((256, ff), bf16),
        pltpu.VMEM((256, ff), bf16),
        pltpu.VMEM((128, 256), f32),
        pltpu.VMEM((256, 512), f32),
        pltpu.VMEM((512, 256), f32),
        pltpu.VMEM((-(-ff // 128) * 128, 256), f32),
        pltpu.VMEM((-(-ff // 128) * 128, 256), f32),
        pltpu.VMEM((rows, width), bf16),
        pltpu.VMEM((total, width), bf16),
        pltpu.VMEM((total, width), bf16),
        pltpu.VMEM((width, 640), bf16),
        pltpu.VMEM((width, 512), bf16),
        pltpu.VMEM((width, ff), bf16),
        pltpu.VMEM((width, ff), bf16),
        pltpu.VMEM((total, 640), bf16),
        pltpu.VMEM((total, 128), bf16),
        pltpu.VMEM((total, 512), f32),
        pltpu.VMEM((total, 128), f32),
        pltpu.VMEM((total, 512), bf16),
        pltpu.VMEM((2, rows, width), bf16),
        pltpu.VMEM((2, rows, width), bf16),
        pltpu.VMEM((rows, width), bf16),
        pltpu.VMEM((rows, width), bf16),
        pltpu.VMEM((rows, width), f32),
        pltpu.VMEM((total, ff), bf16),
        pltpu.VMEM((total, ff), bf16),
        pltpu.VMEM((total, ff), bf16),
        pltpu.VMEM((8, 16, 256), bf16),
        pltpu.VMEM((8, width), f32),
        pltpu.VMEM((4, 176, 128), bf16),
        pltpu.VMEM((2, 176, 128), bf16),
        pltpu.VMEM((2, 176, 128), bf16),
        pltpu.VMEM((2, 176, 128), bf16),
        pltpu.VMEM((2, 176, 128), bf16),
        pltpu.VMEM((2, 2, 176, 128), bf16),
        pltpu.VMEM((4, 256, 128), f32),
        pltpu.SemaphoreType.DMA((112,)),
        pltpu.SemaphoreType.DMA((112,)),
        pltpu.SemaphoreType.DMA((112,)),
    ]
    return pl.pallas_call(
        fwd_kernel,
        out_shape=outs,
        in_specs=[pl.BlockSpec(memory_space=pltpu.SMEM)] + [vmem] * 6 + [hbm] * 9,
        out_specs=(hbm,) * len(outs),
        scratch_shapes=scratch,
        compiler_params=pltpu.CompilerParams(
            collective_id=0, has_side_effects=True, vmem_limit_bytes=60 * 2**20
        ),
    )(lengths, *constants, gain_first, gain_second, x_in, *weights, c_in)


def backward_pass(lengths, constants, gains, s_in, den, gain_pair, x_in, x1, weights, c_all, acts):
    rows, width = x_in.shape
    total = 4 * rows
    ff = weights[2].shape[2]
    hbm = pl.BlockSpec(memory_space=pl.ANY)
    vmem = pl.BlockSpec(memory_space=pltpu.VMEM)

    def shape(*dims, dtype=f32):
        return jax.ShapeDtypeStruct(dims, dtype)

    outs = (
        shape(256, ff),
        shape(256, ff),
        shape(256, ff),
        shape(256, 1152),
        shape(rows, width, dtype=bf16),
        shape(rows, width),
        shape(8, 256),
        shape(width, ff, dtype=bf16),
    )
    scratch = [
        pltpu.VMEM((total, 128), f32),
        pltpu.VMEM((8, total), f32),
        pltpu.VMEM((8, 128), f32),
        pltpu.VMEM((3, 8, 256), f32),
        pltpu.VMEM((8, 256), f32),
        pltpu.VMEM((8, 256), f32),
        pltpu.VMEM((8, 256, ff), bf16),
        pltpu.VMEM((width, ff), bf16),
        pltpu.VMEM((width, ff), bf16),
        pltpu.VMEM((width, 512), bf16),
        pltpu.VMEM((2, 2, 256, ff), bf16),
        pltpu.VMEM((2, total, 256), bf16),
        pltpu.VMEM((total, width), bf16),
        pltpu.VMEM((total, ff), bf16),
        pltpu.VMEM((total, ff), bf16),
        pltpu.VMEM((2, 256, ff), bf16),
        pltpu.VMEM((total, 640), bf16),
        pltpu.VMEM((total, 128), bf16),
        pltpu.VMEM((total, 512), bf16),
        pltpu.VMEM((total, 512), bf16),
        pltpu.VMEM((total, 128), f32),
        pltpu.VMEM((4, 8, 256), f32),
        pltpu.VMEM((total, 640), bf16),
        pltpu.VMEM((total, 128), f32),
        pltpu.VMEM((total, 128), f32),
        pltpu.VMEM((8, 4, 256, 256), bf16),
        pltpu.VMEM((8, 2, 256, 256), bf16),
        pltpu.VMEM((8, 256, 256), bf16),
        pltpu.VMEM((rows, width), f32),
        pltpu.VMEM((rows, width), f32),
        pltpu.VMEM((256, ff), f32),
        pltpu.VMEM((4, 176, 128), bf16),
        pltpu.VMEM((2, 176, 128), bf16),
        pltpu.VMEM((2, 176, 128), bf16),
        pltpu.VMEM((2, 176, 128), bf16),
        pltpu.VMEM((2, 176, 128), bf16),
        pltpu.VMEM((2, 2, 176, 128), bf16),
        pltpu.VMEM((4, 256, 128), f32),
        pltpu.VMEM((rows, width), bf16),
        pltpu.SemaphoreType.DMA((2, 2, 2)),
        pltpu.SemaphoreType.DMA((2, 2, 2, 7)),
        pltpu.SemaphoreType.DMA((6, 8)),
        pltpu.SemaphoreType.REGULAR((2,)),
        pltpu.SemaphoreType.DMA((16,)),
        pltpu.SemaphoreType.DMA((16,)),
        pltpu.SemaphoreType.DMA((80,)),
        pltpu.SemaphoreType.DMA((2, 2)),
    ]
    return pl.pallas_call(
        bwd_kernel,
        out_shape=outs,
        in_specs=[pl.BlockSpec(memory_space=pltpu.SMEM)] + [vmem] * 9 + [hbm] * 16,
        out_specs=(hbm,) * len(outs),
        scratch_shapes=scratch,
        compiler_params=pltpu.CompilerParams(
            collective_id=1, has_side_effects=True, vmem_limit_bytes=62 * 2**20
        ),
    )(lengths, *constants, gains, s_in, den, *gain_pair, x_in, x1, *weights, c_all, *acts)


def finish_kernel(
    d_in, g_in, u_in, oq_in, block_in, input_in,
    d_out, g_out, u_out, o_out, q_out, k_out, v_out, block_out, input_out,
    wide, turned, oq, oq_t, block, grad, sems,
):
    keeper = Sems(sems)
    ff = d_in.shape[1]

    def copy(src, dst):
        made = pltpu.make_async_copy(src, dst, keeper.take())
        made.start()
        return made

    came = [copy(ref, wide.at[i]) for i, ref in enumerate((g_in, u_in, d_in))]
    came_oq = copy(oq_in, oq)
    came_block, came_grad = copy(block_in, block), copy(input_in, grad)
    came_oq.wait()
    oq_t[...] = oq[:, 0:640].T
    kept = [
        copy(oq.at[:, pl.ds(640, 512)], v_out),
        copy(oq_t.at[pl.ds(0, 512)], o_out),
        copy(oq_t.at[pl.ds(512, 64)], q_out),
        copy(oq_t.at[pl.ds(576, 64)], k_out),
    ]
    for i, out in enumerate((g_out, u_out, d_out)):
        came[i].wait()
        for at in range(0, ff, 128):
            at = min(at, ff - 128)
            turned[i, at : at + 128, :] = wide[i, :, at : at + 128].T
        kept.append(copy(turned.at[i], out))
    came_block.wait()
    kept.append(copy(block, block_out))
    came_grad.wait()
    kept.append(copy(grad, input_out))
    for made in kept:
        made.wait()


def finish(d, g, u, oq, block, grad_input):
    rows, width = block.shape
    ff = d.shape[1]
    hbm = pl.BlockSpec(memory_space=pl.ANY)

    def shape(*dims, dtype=f32):
        return jax.ShapeDtypeStruct(dims, dtype)

    outs = (
        shape(ff, 256), shape(ff, 256), shape(ff, 256), shape(512, 256), shape(64, 256),
        shape(64, 256), shape(256, 512), shape(rows, width, dtype=bf16), shape(rows, width),
    )
    return pl.pallas_call(
        finish_kernel,
        out_shape=outs,
        in_specs=[hbm] * 6,
        out_specs=(hbm,) * len(outs),
        scratch_shapes=[
            pltpu.VMEM((3, 256, ff), f32),
            pltpu.VMEM((3, ff, 256), f32),
            pltpu.VMEM((256, 1152), f32),
            pltpu.VMEM((640, 256), f32),
            pltpu.VMEM((rows, width), bf16),
            pltpu.VMEM((rows, width), f32),
            pltpu.SemaphoreType.DMA((24,)),
        ],
        compiler_params=pltpu.CompilerParams(vmem_limit_bytes=60 * 2**20),
    )(d, g, u, oq, block, grad_input)


def on_device_rings(
    inputs, lengths, gain_attn, w_query, w_key, w_value, w_out, gain_mlp, w_gate, w_up, w_down,
    cotangent,
):
    first, second, lanes, mask = feature_tables(4)
    constants = (
        jnp.asarray(first, bf16), jnp.asarray(second, bf16), jnp.asarray(lanes), jnp.asarray(mask),
    )
    gain_pair = (gain_attn.reshape(1, -1), gain_mlp.reshape(1, -1))
    made = forward_pass(
        lengths, constants, *gain_pair, inputs,
        (w_query.T, w_key.T, w_value, w_out, w_gate.T, w_up.T, w_down), cotangent,
    )
    weights = made[:5]
    c_all, h1, qkv, yb, den, x1, h2, gate, up, mixed, s_in, gain_all, terms = made[5:]
    sum_down_t, sum_gate, sum_up, sum_oq, block, grad_input, gain_sums, _ = backward_pass(
        lengths, constants, gain_all, s_in, den, gain_pair, inputs, x1, weights, c_all,
        (h1, qkv, yb, h2, gate, up, mixed, terms),
    )
    d, g_t, u_t, o, q_t, k_t, v, block, grad_input = finish(
        sum_down_t, sum_gate, sum_up, sum_oq, block, grad_input
    )
    return (
        block,
        grad_input,
        gain_sums[0],
        q_t.T,
        k_t.T,
        v,
        o,
        gain_sums[1],
        g_t.T,
        u_t.T,
        d,
    )


def on_device(
    inputs,
    lengths,
    gain_attn,
    w_query,
    w_key,
    w_value,
    w_out,
    gain_mlp,
    w_gate,
    w_up,
    w_down,
    cotangent,
):
    seq_count = lax.axis_size("seq")
    tp_count = lax.axis_size("tp")
    seq_index = lax.axis_index("seq")
    rows_own, width = inputs.shape
    chunk = width // seq_count
    half = chunk // 2
    block_len = rows_own * tp_count
    anchor = seq_index * block_len
    relative = relative_list(seq_count)
    ring = ring_order(seq_count)
    place_of = [ring.index(s) for s in range(seq_count)]
    to_rel = jnp.array(
        [[ring[(place_of[s] - k) % seq_count] for k in relative] for s in range(seq_count)],
        jnp.int32,
    )[seq_index]
    to_abs = jnp.array(
        [
            [relative.index((place_of[s] - place_of[o]) % seq_count) for o in range(seq_count)]
            for s in range(seq_count)
        ],
        jnp.int32,
    )[seq_index]
    to_rel = [to_rel[j] for j in range(seq_count)]
    to_abs = [to_abs[j] for j in range(seq_count)]

    qk_cols, v_cols, ff_cols = w_query.shape[1], w_value.shape[1], w_gate.shape[1]
    gains = jnp.stack([gain_attn, gain_mlp]).astype(bf16)
    qkv_cols = 2 * qk_cols + v_cols
    qkv_own = jnp.concatenate([w_query, w_key, w_value], axis=1).astype(bf16)
    gain_rows = jnp.zeros((16, qkv_cols), bf16).at[:2, :chunk].set(gains)
    first_own = jnp.concatenate([qkv_own, gain_rows], axis=0)
    out_own = w_out.astype(bf16).T
    gate_up_own = jnp.concatenate([w_gate, w_up], axis=1).astype(bf16)
    down_own = w_down.astype(bf16).T

    first_got = ring_gather(first_own, half)
    out_got = ring_gather(out_own, half)
    gate_up_got = ring_gather(gate_up_own, half)
    down_got = ring_gather(down_own, half)
    w_qkv = jnp.concatenate([first_got[k][:chunk] for k in relative], axis=0)
    gain_first = jnp.concatenate([first_got[k][chunk, :chunk] for k in relative]).astype(f32)
    gain_second = jnp.concatenate([first_got[k][chunk + 1, :chunk] for k in relative]).astype(f32)
    w_out_t = jnp.concatenate([out_got[k] for k in relative], axis=0)
    w_gate_up = jnp.concatenate([gate_up_got[k] for k in relative], axis=0)
    w_down_t = jnp.concatenate([down_got[k] for k in relative], axis=0)

    at = jnp.arange(lengths.shape[0])
    starts = jnp.sum(jnp.where(at[None, :] < at[:, None], lengths[None, :], 0), axis=1)
    positions, row_ids, carry_in, after_last = segment_masks(anchor, starts, block_len)
    carry_mask = carry_in.astype(f32)
    last_mask = after_last.astype(f32)
    resets = (
        jnp.sum(
            ((starts // block_len)[None, :] == jnp.arange(seq_count)[:, None]).astype(jnp.int32),
            axis=1,
        )
        > 0
    ).astype(jnp.int32)

    inputs_own = to_relative(inputs, to_rel, chunk)
    grad_own = to_relative(cotangent, to_rel, chunk)
    inputs_full = tp_gather(inputs_own).astype(f32)
    grad_full = tp_gather(grad_own)
    inputs_own = inputs_own.astype(f32)
    hidden_first = (inputs_full * rms_scale(inputs_full) * gain_first).astype(bf16)
    qkv = dot(hidden_first, w_qkv).astype(bf16)
    queries = qkv[:, :qk_cols]
    key_flat = qkv[:, qk_cols : 2 * qk_cols]
    value_flat = qkv[:, 2 * qk_cols :]
    heads_local = qk_cols // FEAT
    query_heads = queries.reshape(block_len, heads_local, FEAT)
    key_heads = key_flat.reshape(block_len, heads_local, FEAT)
    value_heads = value_flat.reshape(block_len, heads_local, VHEAD)
    query_float = query_heads.astype(f32)
    key_float = key_heads.astype(f32)
    value_float = value_heads.astype(f32)
    key_feat = features(key_float) * last_mask[:, None, None]
    local_state = jnp.einsum("thn,thv->hnv", key_feat, value_float, precision=highest)
    local_sum = jnp.sum(key_feat, axis=0)
    carry_state, carry_sum = carried([local_state, local_sum], resets, 1)
    step_rows = 512
    query_feat = features(query_float)
    carry_weight = carry_mask[:, None]
    numer_parts = []
    denom_parts = []
    for first_row in range(0, block_len, step_rows):
        query_part = query_heads[first_row : first_row + step_rows]
        scores, allowed, kernel = pair_block(
            query_part, key_heads, row_ids, positions, first_row, step_rows
        )
        numer_parts.append(
            jnp.einsum("hts,shv->thv", kernel.astype(bf16), value_heads, preferred_element_type=f32)
        )
        denom_parts.append(jnp.sum(kernel, axis=-1).T)
    numerator = (
        jnp.concatenate(numer_parts, axis=0)
        + jnp.einsum("thn,hnv->thv", query_feat, carry_state, precision=highest)
        * carry_weight[:, :, None]
    )
    denominator = (
        jnp.concatenate(denom_parts, axis=0)
        + jnp.einsum("thn,hn->th", query_feat, carry_sum, precision=highest) * carry_weight
    )
    attended = numerator / denominator[:, :, None]
    attended_low = attended.reshape(block_len, heads_local * VHEAD).astype(bf16)
    attn_partial = dot_t(attended_low, w_out_t).astype(bf16)
    middle_own = inputs_own + tp_scatter(attn_partial)
    scale_second = rms_scale(middle_own)
    normed_second = middle_own * scale_second
    hidden_second = tp_gather((normed_second * gain_second).astype(bf16))
    gate_up = dot(hidden_second, w_gate_up)
    gate_value, upward = gate_up[:, :ff_cols], gate_up[:, ff_cols:]
    sigmoid_gate = jax.nn.sigmoid(gate_value)
    silu_gate = gate_value * sigmoid_gate
    mixed_rows = (silu_gate * upward).astype(bf16)
    grad_down_t = dot_tt(grad_full, mixed_rows).astype(bf16)

    def by_distance(stack):
        return {k: stack[j * chunk : (j + 1) * chunk] for j, k in enumerate(relative)}

    sum_down_t = ring_scatter(by_distance(grad_down_t))
    mlp_own = tp_scatter(dot_t(mixed_rows, w_down_t).astype(bf16))
    block_output = to_relative((middle_own + mlp_own).astype(bf16), to_abs, chunk)

    grad_mixed = dot(grad_full, w_down_t).astype(bf16).astype(f32)
    grad_gate = (
        grad_mixed * upward * sigmoid_gate * (1.0 + gate_value * (1.0 - sigmoid_gate))
    ).astype(bf16)
    grad_upward = (grad_mixed * silu_gate).astype(bf16)
    grad_gate_up = jnp.concatenate([grad_gate, grad_upward], axis=1)
    hidden_partial = dot_t(grad_gate_up, w_gate_up).astype(bf16)
    sum_gate_up = ring_scatter(by_distance(dot_tt(hidden_second, grad_gate_up).astype(bf16)))
    grad_hidden = tp_scatter(hidden_partial)
    grad_middle = grad_own.astype(f32) + norm_back(
        grad_hidden, normed_second, scale_second, gain_second
    )
    grad_branch = tp_gather(grad_middle.astype(bf16))
    sum_out_t = ring_scatter(by_distance(dot_tt(grad_branch, attended_low).astype(bf16)))
    grad_attended = dot(grad_branch, w_out_t).reshape(block_len, heads_local, VHEAD)
    grad_numer = (grad_attended / denominator[:, :, None]).astype(bf16)
    grad_denom = -jnp.sum(grad_attended * attended, axis=-1) / denominator
    grad_numer_carried = grad_numer.astype(f32) * carry_weight[:, :, None]
    grad_denom_carried = grad_denom * carry_weight
    grad_state_in = jnp.einsum("thn,thv->hnv", query_feat, grad_numer_carried, precision=highest)
    grad_sum_in = jnp.einsum("thn,th->hn", query_feat, grad_denom_carried, precision=highest)
    grad_query_feat = (
        jnp.einsum("thv,hnv->thn", grad_numer_carried, carry_state, precision=highest)
        + grad_denom_carried[:, :, None] * carry_sum[None]
    )
    grad_state_out, grad_sum_out = carried([grad_state_in, grad_sum_in], resets, -1)
    grad_key_feat = (
        jnp.einsum("thv,hnv->thn", value_float, grad_state_out, precision=highest)
        + grad_sum_out[None]
    ) * last_mask[:, None, None]
    grad_value_state = jnp.einsum("thn,hnv->thv", key_feat, grad_state_out, precision=highest)
    grad_query_parts = []
    grad_key_inner = jnp.zeros((block_len, heads_local, FEAT), f32)
    grad_value_inner = jnp.zeros((block_len, heads_local, VHEAD), f32)
    for first_row in range(0, block_len, step_rows):
        query_part = query_heads[first_row : first_row + step_rows]
        scores, allowed, kernel = pair_block(
            query_part, key_heads, row_ids, positions, first_row, step_rows
        )
        numer_grad_part = grad_numer[first_row : first_row + step_rows]
        grad_weights = jnp.einsum(
            "thv,shv->hts", numer_grad_part, value_heads, preferred_element_type=f32
        )
        grad_scores = (
            (grad_weights + grad_denom[first_row : first_row + step_rows].T[:, :, None])
            * allowed[None]
            * (1.0 + scores)
        ).astype(bf16)
        grad_query_parts.append(
            jnp.einsum("hts,shf->thf", grad_scores, key_heads, preferred_element_type=f32) * 0.25
        )
        grad_key_inner = (
            grad_key_inner
            + jnp.einsum("hts,thf->shf", grad_scores, query_part, preferred_element_type=f32) * 0.25
        )
        grad_value_inner = grad_value_inner + jnp.einsum(
            "hts,thv->shv", kernel.astype(bf16), numer_grad_part, preferred_element_type=f32
        )
    grad_query = (
        jnp.concatenate(grad_query_parts, axis=0) + feature_grad(query_float, grad_query_feat)
    ).astype(bf16)
    grad_key = (grad_key_inner + feature_grad(key_float, grad_key_feat)).astype(bf16)
    grad_value = (grad_value_inner + grad_value_state).astype(bf16)
    grad_qkv = jnp.concatenate(
        [
            grad_query.reshape(block_len, heads_local * FEAT),
            grad_key.reshape(block_len, heads_local * FEAT),
            grad_value.reshape(block_len, heads_local * VHEAD),
        ],
        axis=1,
    )
    sum_qkv = ring_scatter(by_distance(dot_tt(hidden_first, grad_qkv).astype(bf16)))
    grad_hidden_first = tp_scatter(dot_t(grad_qkv, w_qkv).astype(bf16))
    scale_first = rms_scale(inputs_own)
    normed_first = inputs_own * scale_first
    grad_input = to_relative(
        grad_middle + norm_back(grad_hidden_first, normed_first, scale_first, gain_first),
        to_abs,
        chunk,
    )

    gain_terms = jnp.stack(
        [
            jnp.sum(qkv_own.astype(f32) * sum_qkv, axis=1),
            jnp.sum(gate_up_own.astype(f32) * sum_gate_up, axis=1),
        ]
    )
    gain_sums = tp_sum(gain_terms) / gains.astype(f32)
    return (
        block_output,
        grad_input,
        gain_sums[0],
        sum_qkv[:, :qk_cols],
        sum_qkv[:, qk_cols : 2 * qk_cols],
        sum_qkv[:, 2 * qk_cols :],
        sum_out_t.T,
        gain_sums[1],
        sum_gate_up[:, :ff_cols],
        sum_gate_up[:, ff_cols:],
        sum_down_t.T,
    )


def solution(mesh):
    in_specs = (
        P(("seq", "tp"), None),
        P(),
        P("seq"),
        P("seq", "tp"),
        P("seq", "tp"),
        P("seq", "tp"),
        P("tp", "seq"),
        P("seq"),
        P("seq", "tp"),
        P("seq", "tp"),
        P("tp", "seq"),
        P(("seq", "tp"), None),
    )
    out_specs = (
        P(("seq", "tp"), None),
        P(("seq", "tp"), None),
        P("seq"),
        P("seq", "tp"),
        P("seq", "tp"),
        P("seq", "tp"),
        P("tp", "seq"),
        P("seq"),
        P("seq", "tp"),
        P("seq", "tp"),
        P("tp", "seq"),
    )
    small = mesh.shape["seq"] == 8 and mesh.shape["tp"] == 4
    body = on_device_rings if small else on_device
    return jax.shard_map(
        body, mesh=mesh, in_specs=in_specs, out_specs=out_specs, check_vma=False
    )
```

```python
import jax
import jax.numpy as jnp
import numpy as np
from jax import lax
from jax.experimental import pallas as pl
from jax.experimental.pallas import tpu as pltpu
from jax.sharding import PartitionSpec as P

FEAT = 16
VHEAD = 128


epsilon = 1e-05
linear_coef = 0.5
square_coef = 0.17677669529663687
highest = lax.Precision.HIGHEST
f32 = jnp.float32
bf16 = jnp.bfloat16


def ring_order(count):
    planes = 4 if count % 4 == 0 else 2
    columns = count // planes
    order = [z * columns for z in range(planes)]
    for z in reversed(range(planes)):
        xs = list(range(1, columns))
        if (planes - 1 - z) % 2:
            xs.reverse()
        order += [z * columns + x for x in xs]
    return order


def relative_list(count):
    half = count // 2
    out = []
    for j in range(1, half):
        out += [j, count - j]
    return out + [half, 0]


def ring_perms(count):
    ring = ring_order(count)
    fwd = [(ring[i], ring[(i + 1) % count]) for i in range(count)]
    return fwd, [(b, a) for a, b in fwd]


def ring_gather(own, half_rows):
    count = lax.axis_size("seq")
    fwd, bwd = ring_perms(count)
    half = count // 2
    got = {0: own}
    ahead = back = own
    for step in range(1, half):
        ahead = lax.ppermute(ahead, "seq", fwd)
        back = lax.ppermute(back, "seq", bwd)
        got[step] = ahead
        got[count - step] = back
    ahead = lax.ppermute(ahead[:half_rows], "seq", fwd)
    back = lax.ppermute(back[half_rows:], "seq", bwd)
    got[half] = jnp.concatenate([ahead, back], axis=0)
    return got


def ring_scatter(chunks):
    count = lax.axis_size("seq")
    fwd, bwd = ring_perms(count)
    half = chunks[0].shape[0] // 2
    ahead = chunks[1][:half]
    back = chunks[count - 1][half:]
    for step in range(count - 1):
        ahead = lax.ppermute(ahead, "seq", fwd).astype(f32)
        back = lax.ppermute(back, "seq", bwd).astype(f32)
        last = step == count - 2
        ahead = ahead + chunks[0 if last else 2 + step][:half].astype(f32)
        back = back + chunks[0 if last else count - 2 - step][half:].astype(f32)
        if not last:
            ahead = ahead.astype(bf16)
            back = back.astype(bf16)
    return jnp.concatenate([ahead, back], axis=0)


def to_relative(array, index_row, chunk):
    return jnp.concatenate(
        [lax.dynamic_slice_in_dim(array, i * chunk, chunk, 1) for i in index_row], axis=1
    )


def tp_perms(count):
    ys = count // 2
    core = [(i, i ^ 1) for i in range(count)]
    shift = [
        [(i, (((i // 2) + d) % ys) * 2 + i % 2) for i in range(count)] for d in range(ys)
    ]
    return core, shift


def tp_gather(own):
    count = lax.axis_size("tp")
    ys = count // 2
    place = lax.axis_index("tp")
    y, c = place // 2, place % 2
    core, shift = tp_perms(count)
    parts = [own] + [lax.ppermute(own, "tp", shift[d]) for d in range(1, ys)]
    mine = jnp.stack([lax.select_n((y - at + ys) % ys, *parts) for at in range(ys)])
    other = lax.ppermute(mine, "tp", core)
    full = jnp.stack([jnp.where(c == 0, mine, other), jnp.where(c == 0, other, mine)], axis=1)
    return full.reshape((count * own.shape[0],) + own.shape[1:])


def tp_scatter(partial):
    count = lax.axis_size("tp")
    ys = count // 2
    place = lax.axis_index("tp")
    y, c = place // 2, place % 2
    core, shift = tp_perms(count)
    blocks = partial.reshape((ys, 2, partial.shape[0] // count) + partial.shape[1:])
    sent = lax.dynamic_index_in_dim(blocks, 1 - c, 1, False)
    kept = lax.dynamic_index_in_dim(blocks, c, 1, False)
    pair = kept.astype(f32) + lax.ppermute(sent, "tp", core).astype(f32)
    low = pair.astype(bf16)
    own = lax.dynamic_index_in_dim(pair, y, 0, False)
    for d in range(1, ys):
        away = lax.dynamic_index_in_dim(low, (y + d) % ys, 0, False)
        own = own + lax.ppermute(away, "tp", shift[d]).astype(f32)
    return own


def tp_sum(vector):
    count = lax.axis_size("tp")
    core, shift = tp_perms(count)
    vector = vector + lax.ppermute(vector, "tp", core)
    return vector + sum(lax.ppermute(vector, "tp", shift[d]) for d in range(1, count // 2))


def carried(arrays, resets, step):
    count = lax.axis_size("seq")
    place = lax.axis_index("seq")

    def from_near(a, d):
        perm = [(i, i + d * step) for i in range(count) if 0 <= i + d * step < count]
        return lax.ppermute(a.astype(bf16), "seq", perm).astype(f32)

    def reset_within(d):
        at = jnp.arange(count)
        away = (place - at) * step
        return jnp.sum(jnp.where((away >= 1) & (away <= d), resets, 0)) > 0

    arrays = [from_near(a, 1) for a in arrays]
    d = 1
    while d < count - 1:
        keep = 1.0 - reset_within(d).astype(f32)
        arrays = [a + keep * from_near(a, d) for a in arrays]
        d *= 2
    return arrays


def features(vector):
    squares = (vector[..., :, None] * vector[..., None, :]).reshape(
        vector.shape[:-1] + (vector.shape[-1] * vector.shape[-1],)
    )
    return jnp.concatenate(
        [jnp.ones_like(vector[..., :1]), vector * linear_coef, squares * square_coef], axis=-1
    )


def feature_grad(vector, grad_feat):
    feat_width = vector.shape[-1]
    linear_part = grad_feat[..., 1 : 1 + feat_width]
    square_part = grad_feat[..., 1 + feat_width :].reshape(vector.shape + (feat_width,))
    mixed_part = jnp.sum(square_part * vector[..., None, :], axis=-1) + jnp.sum(
        square_part * vector[..., :, None], axis=-2
    )
    return linear_coef * linear_part + square_coef * mixed_part


def segment_masks(anchor, starts, length):
    positions = anchor + jnp.arange(length, dtype=jnp.int32)
    start_le = starts[None, :] <= positions[:, None]
    row_ids = jnp.sum(start_le.astype(jnp.int32), axis=1)
    inside = (starts >= anchor) & (starts < anchor + length)
    carry = jnp.sum(((starts[None, :] >= anchor) & start_le).astype(jnp.int32), axis=1) == 0
    after_last = (
        jnp.sum(
            ((starts[None, :] > positions[:, None]) & inside[None, :]).astype(jnp.int32), axis=1
        )
        == 0
    )
    return (positions, row_ids, carry, after_last)


def rms_scale(values):
    return lax.rsqrt(jnp.mean(values * values, axis=-1, keepdims=True) + epsilon)


def norm_back(grad_out, normed, scale, gain):
    grad_normed = grad_out * gain
    return scale * (grad_normed - normed * jnp.mean(grad_normed * normed, axis=-1, keepdims=True))


def pair_block(query_part, key_heads, row_ids, positions, first_row, span_rows):
    scores = (
        jnp.einsum("thf,shf->hts", query_part, key_heads, preferred_element_type=f32) * 0.25
    )
    rows_here = row_ids[first_row : first_row + span_rows]
    place_here = positions[first_row : first_row + span_rows]
    allowed = (
        (rows_here[:, None] == row_ids[None, :]) & (positions[None, :] <= place_here[:, None])
    ).astype(f32)
    kernel = (1.0 + scores + 0.5 * scores * scores) * allowed[None]
    return (scores, allowed, kernel)


def dot(a, b):
    return jnp.dot(a, b, preferred_element_type=f32)


def dot_t(a, b):
    return lax.dot_general(a, b, (((1,), (1,)), ((), ())), preferred_element_type=f32)


def dot_tt(a, b):
    return lax.dot_general(a, b, (((0,), (0,)), ((), ())), preferred_element_type=f32)


def ring_place(seq):
    z, x = seq // 2, seq % 2
    return z + x * (7 - 2 * z)


def ring_seq(place):
    place = lax.rem(place + 8, 8)
    far = place // 4
    return (1 - far) * 2 * place + far * (15 - 2 * place)


class Sems:
    def __init__(self, ref):
        self.ref, self.used = ref, 0

    def take(self):
        self.used += 1
        assert self.used <= self.ref.shape[0]
        return self.ref.at[self.used - 1]


class Links:
    def __init__(self, send, recv):
        self.send, self.recv, self.sent = Sems(send), Sems(recv), []

    def copy(self, src, dst, **to):
        return pltpu.make_async_remote_copy(
            src_ref=src,
            dst_ref=dst,
            send_sem=self.send.take(),
            recv_sem=self.recv.take(),
            device_id=to,
            device_id_type=pl.DeviceIdType.MESH,
        )

    def start(self, src, dst, **to):
        made = self.copy(src, dst, **to)
        made.start()
        self.sent.append(made)
        return made

    def sent_now(self, some):
        for made in some:
            made.wait_send()
        self.sent = [made for made in self.sent if all(made is not other for other in some)]

    def finish(self):
        for made in self.sent:
            made.wait_send()


class Gather:
    def __init__(self, links, arrays, nearby, gangs):
        self.links, self.arrays, self.nearby = links, arrays, nearby
        self.at = {k: j for j, k in enumerate(relative_list(8))}
        self.flying, self.gangs, self.done = {}, gangs, 0
        self.gang_of = {a: i for i, gang in enumerate(gangs) for a in gang}
        self.events = [
            (a, step, way, part)
            for gang in gangs
            for step in (1, 2, 3, 4)
            for a in gang
            for part in (0, 1)
            for way in (0, 1)
            if step < 4 or way == part
        ]
        for a in gangs[0]:
            for part in (0, 1):
                for way in (0, 1):
                    self.go(a, 1, way, part)

    def rows(self, a, part):
        first, size = self.arrays[a][2:]
        return pl.ds(first + part * size, size)

    def go(self, a, step, way, part):
        own, everyone = self.arrays[a][:2]
        before, after = (step - 1, step) if way == 0 else ((9 - step) % 8, 8 - step)
        src = own if step == 1 else everyone.at[self.at[before]]
        self.flying[a, step, way, part] = self.links.start(
            src.at[self.rows(a, part)],
            everyone.at[self.at[after], self.rows(a, part)],
            seq=self.nearby[way],
        )

    def pump(self, upto):
        while self.done < min(upto, len(self.events)):
            a, step, way, part = self.events[self.done]
            self.flying[a, step, way, part].wait_recv()
            if step < 3 or (step == 3 and way == part):
                self.go(a, step + 1, way, part)
            i = self.gang_of[a]
            if step == 3 and i + 1 < len(self.gangs):
                mine, later = self.gangs[i].index(a), self.gangs[i + 1]
                last = mine == len(self.gangs[i]) - 1
                for other in later[mine:] if last else later[mine : mine + 1]:
                    self.go(other, 1, way, part)
            self.done += 1

    def pump_array(self, a):
        gang = self.gang_of[a]
        self.pump(14 * sum(len(g) for g in self.gangs[: gang + 1]))


def greet(peers):
    barrier = pltpu.get_barrier_semaphore()
    for peer in peers:
        pl.semaphore_signal(
            barrier, inc=1, device_id=peer, device_id_type=pl.DeviceIdType.MESH
        )
    pl.semaphore_wait(barrier, len(peers))


def places():
    seq, tp = lax.axis_index("seq"), lax.axis_index("tp")
    place = ring_place(seq)
    nearby = (ring_seq(place + 1), ring_seq(place - 1))
    over_y = lax.rem(tp + 2, 4)
    over_core = tp + 1 - 2 * (tp % 2)
    peers = [{"seq": ring_seq(place + k)} for k in range(1, 8)]
    peers += [{"tp": over_y}, {"tp": over_core}]
    return seq, tp, place, nearby, over_y, over_core, peers


class Rows:
    def __init__(self, links, own, everyone, tp, over_y, over_core, rows):
        self.links, self.all, self.tp = links, everyone, tp
        self.over_y, self.over_core, self.rows = over_y, over_core, rows
        half = rows // 2
        self.first = [
            links.start(
                own.at[pl.ds(i * half, half)], self.block(tp, i * half, half), tp=over_y
            )
            for i in (0, 1)
        ]
        self.near = links.start(own, self.block(tp, 0, rows), tp=over_core)
        self.last = []

    def block(self, owner, offset, size):
        return self.all.at[pl.ds(pl.multiple_of(owner * self.rows + offset, 16), size)]

    def forward(self, i):
        half = self.rows // 2
        self.first[i].wait_recv()
        came = self.block(self.over_y, i * half, half)
        self.last.append(self.links.start(came, came, tp=self.over_core))

    def finish(self):
        self.near.wait_recv()
        for made in self.last:
            made.wait_recv()


FEATS = 160


def fill_tables(lengths, seq, tok, line, coefs, step):
    total = tok.shape[0]
    anchor = seq * total
    starts, at = [], 0
    for i in range(lengths.shape[0]):
        starts.append(at)
        at = at + lengths[i]

    def places_of(shape, axis):
        pos = lax.broadcasted_iota(jnp.int32, shape, axis)
        low = jnp.zeros(shape, jnp.int32) - anchor
        last = jnp.ones(shape, f32)
        for start in starts:
            here = start - anchor
            low = jnp.maximum(low, jnp.where(pos >= here, here, -anchor))
            last = jnp.where((pos < here) & (here < total), 0.0, last)
        return pos.astype(f32), low, last

    lane = lax.broadcasted_iota(jnp.int32, (total, 128), 1)
    pos, low, last = places_of((total, 128), 0)
    began = jnp.where(low < 0, 1.0, 0.0)
    first = jnp.maximum(low, 0).astype(f32)
    tok[...] = jnp.where(
        lane == 0, first, jnp.where(lane == 1, began, jnp.where(lane == 2, last, pos))
    )
    pos, low, last = places_of((8, total), 1)
    row = lax.broadcasted_iota(jnp.int32, (8, total), 0)
    line[...] = jnp.where(row == 0, pos, jnp.maximum(low, 0).astype(f32))

    def clear(lo, hi):
        free = jnp.ones((1, 128), f32)
        for start in starts:
            at = jnp.zeros((1, 128), jnp.int32) + start
            free = jnp.where((at >= lo * total) & (at < (hi + 1) * total), 0.0, free)
        return free

    z = seq // 2
    one = jnp.ones((1, 128), f32)
    first, second = clear(2 * z, 2 * z), clear(2 * z + 1, 2 * z + 1)
    before = 2 * (z - step)
    rows = [second, first] if step > 0 else [first, second]
    rows += [first * second, clear(before, before + 1)]
    coefs[...] = jnp.concatenate(rows + [one * 0.0] * 4, axis=0)


class Exchange:
    def __init__(self, links, st, near, term, first, second, given, states, coefs, seq, step):
        z, x = seq // 2, seq % 2
        self.st, self.near, self.term, self.first, self.second = st, near, term, first, second
        self.given, self.states, self.coefs, self.x = given, states, coefs, x
        self.turn = z if step > 0 else 3 - z
        self.late = x if step > 0 else 1 - x
        over_x = seq + 1 - 2 * x
        self.half = links.start(st.at[pl.ds(2 * (1 - x), 2)], near, seq=over_x)
        self.hop = links.copy(term, first, seq=seq + 2 * step)
        self.on = links.copy(term, second, seq=seq + 2 * step)
        self.far = links.copy(term, second, seq=seq + 4 * step)
        self.links, self.over_x = links, over_x

    def coef(self, k):
        return self.coefs[k : k + 1, :]

    def pair(self):
        self.half.wait_recv()
        for i in (0, 1):
            mine, theirs = self.st[2 * self.x + i].astype(f32), self.near[i].astype(f32)
            early = jnp.where(self.late == 0, mine, theirs)
            later = jnp.where(self.late == 0, theirs, mine)
            self.term[i] = (later + self.coef(0) * early).astype(bf16)

        @pl.when(self.turn % 2 == 0)
        def _():
            self.hop.start()

    def planes(self):
        @pl.when(self.turn % 2 == 1)
        def _():
            self.hop.wait_recv()

        @pl.when(self.turn == 1)
        def _():
            for i in (0, 1):
                came = self.coef(2) * self.first[i].astype(f32)
                self.term[i] = (self.term[i].astype(f32) + came).astype(bf16)
            self.on.start()
            self.far.start()

    def give(self):
        x = self.x
        for i in (0, 1):
            self.states[2 * x + i] = jnp.zeros((256, 128), f32)
            self.states[2 * (1 - x) + i] = jnp.zeros((256, 128), f32)

        def enter(i):
            return self.states.at[2 * x + i, pl.ds(0, 176)]

        @pl.when(self.turn == 1)
        def _():
            for i in (0, 1):
                enter(i)[...] = self.first[i].astype(f32)

        @pl.when(self.turn == 2)
        def _():
            self.on.wait_recv()
            for i in (0, 1):
                enter(i)[...] = self.second[i].astype(f32)

        @pl.when(self.turn == 3)
        def _():
            self.far.wait_recv()
            for i in (0, 1):
                older = self.coef(3) * self.second[i].astype(f32)
                enter(i)[...] = self.first[i].astype(f32) + older

        for i in (0, 1):
            came = enter(i)[...]
            mine, theirs = self.st[2 * x + i].astype(f32), self.near[i].astype(f32)
            early = jnp.where(self.late == 0, mine, theirs)
            passed = early + self.coef(1) * came
            self.given[0, i] = jnp.where(self.late == 0, passed, came).astype(bf16)
            enter(i)[...] = jnp.where(self.late == 0, came, passed)
        self.back = self.links.start(self.given.at[0], self.given.at[1], seq=self.over_x)

    def take(self):
        self.back.wait_recv()
        for i in (0, 1):
            self.states[2 * (1 - self.x) + i, 0:176, :] = self.given[1, i].astype(f32)

    def finish(self):
        @pl.when(self.turn % 2 == 0)
        def _():
            self.hop.wait_send()

        @pl.when(self.turn == 1)
        def _():
            self.on.wait_send()
            self.far.wait_send()


def ring_columns(place):
    return [pl.ds(pl.multiple_of(ring_seq(place - k) * 256, 256), 256) for k in relative_list(8)]


def phi(heads, h, select_a, select_b, lanes):
    a = dot(heads, select_a[h]) + lanes[0:1, :]
    b = dot(heads, select_b[h]) + lanes[1:2, :]
    return a, b


def fwd_kernel(
    lengths, sa_ref, sb_ref, lanes_ref, hm_ref, gain_first, gain_second,
    x_in, wq_in, wk_in, wv_in, wo_in, wg_in, wu_in, wd_in, c_in,
    wq_all, wo_all, wg_all, wu_all, wd_all, c_all,
    h1_out, qkv_out, yb_out, den_out, x1_out, h2_out, gate_out, up_out, m_out, sin_out, gain_out, terms_out,
    x_ref, tok_ref, line_ref, coef_ref, gain_ref, q_own, o_own, g_own, u_own, d_own,
    w_small, w_v, w_o, w_d, w_g, c_v,
    xg, h1, wq, wo, wg, wu, qkv, kq, num, den, yb, sc, rc, sy, ry, x1, gate, up, mm,
    gains_all, gains, st, st_x, st_t, st_z, st_y, st_g, s_in,
    send, recv, local,
):
    seq, tp, place, nearby, over_y, over_core, peers = places()
    z, x = seq // 2, seq % 2
    at = {k: j for j, k in enumerate(relative_list(8))}
    rows = x_ref.shape[0]
    total = 4 * rows
    links = Links(send, recv)
    locs = Sems(local)
    pending = []

    def store(src, dst):
        made = pltpu.make_async_copy(src, dst, locs.take())
        made.start()
        pending.append(made)

    def load(src, dst):
        made = pltpu.make_async_copy(src, dst, locs.take())
        made.start()
        return made

    got_qk = [load(wq_in, w_small.at[0:64]), load(wk_in, w_small.at[64:128]), load(wv_in, w_v)]
    columns = ring_columns(place)
    got_x = [load(x_in.at[:, c], x_ref.at[:, col(j)]) for j, c in enumerate(columns)]
    c_rows = pl.ds(pl.multiple_of(tp * rows, rows), rows)
    got_c = [load(c_in.at[:, c], c_v.at[:, col(j)]) for j, c in enumerate(columns)]
    got_o = load(wo_in, w_o)
    ff = wd_in.shape[0]
    got_g = load(wg_in, w_g.at[pl.ds(0, ff)])
    got_d = load(wd_in, w_d.at[pl.ds(0, ff)])

    def turn(src, dst):
        for i in range(0, ff, 128):
            size = min(128, ff - i)
            dst[:, i : i + size] = src[i : i + 128, :].T[:, :size].astype(bf16)

    gain_ref[...] = jnp.concatenate(
        [gain_first[...], gain_second[...], jnp.zeros((14, 256), f32)], axis=0
    ).astype(bf16)
    greet(peers)
    gain_flying = [
        links.start(gain_ref, gains_all.at[at[k]], seq=ring_seq(place + k)) for k in range(1, 8)
    ]
    for made in got_x:
        made.wait()
    xrows = Rows(links, x_ref, xg, tp, over_y, over_core, rows)
    for made in got_qk:
        made.wait()
    q_own[:, 0:128] = w_small[...].T.astype(bf16)
    q_own[:, 128:640] = w_v[...].astype(bf16)
    ring = Gather(
        links,
        [
            (q_own, wq_all, 0, 128),
            (o_own, wo_all, 0, 128),
            (g_own, wg_all, 0, 64),
            (g_own, wg_all, 128, 64),
            (u_own, wu_all, 0, 64),
            (u_own, wu_all, 128, 64),
            (d_own, wd_all, 0, 128),
        ],
        nearby,
        [[0], [1], [2], [3, 4, 5], [6]],
    )
    own_in = [
        load(x_ref, xrows.block(tp, 0, rows)),
        load(gain_ref, gains_all.at[at[0]]),
    ]
    got_o.wait()
    o_own[...] = w_o[...].T.astype(bf16)
    ring.pump(2)
    got_g.wait()
    turn(w_g, g_own)
    got_u = load(wu_in, w_g.at[pl.ds(0, ff)])
    ring.pump(4)
    got_d.wait()
    turn(w_d, d_own)
    got_u.wait()
    turn(w_g, u_own)
    pairs = [(q_own, wq_all), (o_own, wo_all), (g_own, wg_all), (u_own, wu_all), (d_own, wd_all)]
    own_kept = [load(own, everyone.at[at[0]]) for own, everyone in pairs]
    fill_tables(lengths, seq, tok_ref, line_ref, coef_ref, 1)

    ring.pump(6)
    xrows.forward(0)
    for made in gain_flying:
        made.wait_recv()
    for made in own_in:
        made.wait()
    for j in range(8):
        chunk = gains_all[j].astype(f32)
        gains[0:8, j * 256 : (j + 1) * 256] = chunk[0:8]
    ring.pump(10)
    xrows.forward(1)
    ring.pump_array(0)
    own_kept[0].wait()
    got = load_weights(load, wq_all, wq)
    xrows.finish()

    def norm_first(i, _):
        r = pl.ds(pl.multiple_of(i * 32, 32), 32)
        v = xg[r, :].astype(f32)
        s = lax.rsqrt(jnp.mean(v * v, axis=1, keepdims=True) + epsilon)
        h1[r, :] = (v * s * gains[0:1, :]).astype(bf16)
        return 0

    lax.fori_loop(0, total // 32, norm_first, 0)
    links.sent_now(xrows.last)
    kept_h1 = load(h1, h1_out)
    for made in got_c:
        made.wait()
    crows = Rows(links, c_v, c_all, tp, over_y, over_core, rows)
    kept_c = load(c_v, c_all.at[c_rows])
    ring.pump(15)
    for made in got:
        made.wait()

    def project(i, _):
        r = pl.ds(pl.multiple_of(i * 256, 256), 256)
        res = dot(h1[r, :], wq[...])
        qkv[r, :] = res.astype(bf16)
        kq[r, :] = pltpu.roll(res[:, :128], 64, 1).astype(bf16)
        return 0

    lax.fori_loop(0, total // 256, project, 0)
    store(qkv, qkv_out)
    ring.pump(16)

    heads = 4

    def head_v(h):
        return slice(128 + h * 128, 256 + h * 128)

    for h in range(heads):

        def state(i, c, h=h):
            s, zz = c
            r = pl.ds(pl.multiple_of(i * 256, 256), 256)
            a, b = phi(kq[r, :], h, sa_ref, sb_ref, lanes_ref)
            f = a * b * lanes_ref[2:3, :] * tok_ref[r, 2:3]
            s = s + dot_tt(f.astype(bf16), qkv[r, head_v(h)])
            return s, zz + jnp.sum(f, axis=0, keepdims=True)

        s, zz = lax.fori_loop(
            0, total // 256, state, (jnp.zeros((256, 128), f32), jnp.zeros((1, 256), f32))
        )
        pack_state(st, h, s, zz)
        ring.pump(17 + h)
    moved = Exchange(links, st, st_x, st_t, st_z, st_y, st_g, s_in, coef_ref, seq, 1)

    def local_head(h):
        for i in range(total // 256):
            r = slice(i * 256, (i + 1) * 256)
            span = (i + 1) * 256
            qm = (qkv[r, :128].astype(f32) * hm_ref[h : h + 1, :]).astype(bf16)
            u = dot_t(qm, kq[:span, :])
            keep = (line_ref[0:1, :span] >= tok_ref[r, 0:1]) & (
                line_ref[0:1, :span] <= tok_ref[r, 3:4]
            )
            kap = jnp.where(keep, (0.5 * u + 1.0) * u + 1.0, 0.0)
            den[r, h : h + 1] = jnp.sum(kap, axis=1, keepdims=True)
            num[r, h * 128 : (h + 1) * 128] = dot(kap.astype(bf16), qkv[:span, head_v(h)])

    local_head(0)
    ring.pump(22)
    moved.pair()
    local_head(1)
    ring.pump(24)
    moved.planes()
    local_head(2)
    ring.pump(26)
    moved.give()
    local_head(3)
    ring.pump(28)
    moved.take()
    store(s_in, sin_out)
    for h in range(heads):
        z_row = jnp.concatenate([s_in[h, 160:161, :], s_in[h, 161:162, :]], axis=1)
        feat = jax.lax.broadcasted_iota(jnp.int32, (256, 128), 0)
        s_low = jnp.where(feat < FEATS, s_in[h], 0.0).astype(bf16)

        def carry(i, _, h=h, z_row=z_row, s_low=s_low):
            r = pl.ds(pl.multiple_of(i * 256, 256), 256)
            a, b = phi(qkv[r, 0:128], h, sa_ref, sb_ref, lanes_ref)
            f = a * b * lanes_ref[2:3, :] * tok_ref[r, 1:2]
            hv = slice(h * 128, (h + 1) * 128)
            top = num[r, hv] + dot(f.astype(bf16), s_low)
            low = den[r, h : h + 1] + jnp.sum(f * z_row, axis=1, keepdims=True)
            den[r, h : h + 1] = low
            y = top / low
            yb[r, hv] = y.astype(bf16)
            return 0

        lax.fori_loop(0, total // 256, carry, 0)
        ring.pump(31 + 2 * h)
    store(yb, yb_out)
    store(den, den_out)
    ring.pump_array(1)
    own_kept[1].wait()
    got = load_weights(load, wo_all, wo)
    for made in got:
        made.wait()

    y_at, c_at = tp // 2, tp % 2

    def out_rows(block):
        return yb[pl.ds(pl.multiple_of(block * rows, rows), rows), :]

    cols = 512
    to_core = []
    for yy in (0, 1):

        def core_cols(i, _, yy=yy):
            c = pl.ds(pl.multiple_of(i * cols, cols), cols)
            sc[yy, :, c] = dot_t(out_rows(yy * 2 + 1 - c_at), wo[c, :]).astype(bf16)
            return 0

        lax.fori_loop(0, 2048 // cols, core_cols, 0)
        to_core.append(links.start(sc.at[yy], rc.at[yy], tp=over_core))
    for made in to_core:
        made.wait_recv()
    ring.pump(40)

    def away_cols(i, _):
        c = pl.ds(pl.multiple_of(i * cols, cols), cols)
        part = dot_t(out_rows((1 - y_at) * 2 + c_at), wo[c, :])
        sy[:, c] = (part + rc[1 - y_at, :, c].astype(f32)).astype(bf16)
        return 0

    lax.fori_loop(0, 2048 // cols, away_cols, 0)
    to_y = links.start(sy, ry, tp=over_y)

    def own_cols(i, _):
        c = pl.ds(pl.multiple_of(i * cols, cols), cols)
        x1[:, c] = (
            dot_t(out_rows(tp), wo[c, :]) + rc[y_at, :, c].astype(f32) + x_ref[:, c].astype(f32)
        )
        return 0

    lax.fori_loop(0, 2048 // cols, own_cols, 0)
    ring.pump(44)
    to_y.wait_recv()
    ring.pump(54)

    links.sent_now(xrows.first + [xrows.near])
    ho = x_ref

    def norm_second(i, _):
        r = pl.ds(pl.multiple_of(i * 32, 32), 32)
        v = x1[r, :] + ry[r, :].astype(f32)
        x1[r, :] = v
        s = lax.rsqrt(jnp.mean(v * v, axis=1, keepdims=True) + epsilon)
        ho[r, :] = (v * s * gains[1:2, :]).astype(bf16)
        return 0

    lax.fori_loop(0, rows // 32, norm_second, 0)
    store(x1, x1_out)
    store(gains, gain_out)
    h2 = xg
    hrows = Rows(links, ho, h2, tp, over_y, over_core, rows)
    own_in = load(ho, hrows.block(tp, 0, rows))
    ring.pump(56)
    hrows.forward(0)
    ring.pump(63)
    hrows.forward(1)
    crows.forward(0)
    crows.forward(1)
    hrows.finish()
    crows.finish()
    own_in.wait()
    store(h2, h2_out)
    kept_h1.wait()
    kept_c.wait()
    got_c = load(c_all, h1)
    ring.pump_array(3)
    own_kept[2].wait()
    got = load_weights(load, wg_all, wg)
    own_kept[3].wait()
    got += load_weights(load, wu_all, wu)
    for made in got:
        made.wait()

    def gate_up(i, _):
        r = pl.ds(pl.multiple_of(i * 128, 128), 128)
        g = dot(h2[r, :], wg[...])
        uu = dot(h2[r, :], wu[...])
        gate[r, :] = g.astype(bf16)
        up[r, :] = uu.astype(bf16)
        mm[r, :] = (g * jax.nn.sigmoid(g) * uu).astype(bf16)
        return 0

    for quarter in range(4):
        lax.fori_loop(quarter * total // 512, (quarter + 1) * total // 512, gate_up, 0)
        ring.pump(86 + 2 * quarter)
    store(gate, gate_out)
    store(up, up_out)
    store(mm, m_out)
    got_c.wait()
    links.sent_now([ring.flying[a, 1, way, part] for a in (2, 3, 4, 5) for way in (0, 1) for part in (0, 1)])
    out_sems = [locs.take(), locs.take()]
    buffers = [g_own, u_own]

    def keep_terms(j, k):
        return pltpu.make_async_copy(buffers[k], terms_out.at[col(j)], out_sems[k])

    def grad_down(i, _):
        for k in (0, 1):
            pl.when(i > 0)(lambda k=k: keep_terms(2 * i - 2 + k, k).wait())
            buffers[k][...] = dot_tt(h1[:, col(2 * i + k)], mm[...]).astype(bf16)
            keep_terms(2 * i + k, k).start()
        return 0

    lax.fori_loop(0, 2, grad_down, 0)
    ring.pump(94)
    lax.fori_loop(2, 4, grad_down, 0)
    for k in (0, 1):
        keep_terms(6 + k, k).wait()
    ring.pump_array(6)
    own_kept[4].wait()
    for made in pending:
        made.wait()
    links.finish()
    moved.finish()


def pack_state(st, h, s, zz):
    st[h, 0:FEATS, :] = s[:FEATS].astype(bf16)
    tail = jnp.concatenate([zz[:, :128], zz[:, 128:], jnp.zeros((14, 128), f32)], axis=0)
    st[h, FEATS : FEATS + 16, :] = tail.astype(bf16)


def load_weights(load, everyone, flat):
    count, chunk = everyone.shape[0], everyone.shape[1]
    return [load(everyone.at[j], flat.at[pl.ds(j * chunk, chunk)]) for j in range(count)]


class Scatter:
    def __init__(self, slots, send, recv, nearby):
        self.slots, self.send, self.recv, self.nearby = slots, send, recv, nearby

    def copy(self, a, step, way, sub, src, slot, width):
        return pltpu.make_async_remote_copy(
            src_ref=src,
            dst_ref=self.piece(slot, way, sub, width),
            send_sem=self.send.at[a % 2, way, sub],
            recv_sem=self.recv.at[a % 2, way, sub, step],
            device_id={"seq": self.nearby[way]},
            device_id_type=pl.DeviceIdType.MESH,
        )

    def slot(self, a, step):
        return (a % 2) * 4 + (a // 2 * 7 + step) % 4

    def rows(self, way, sub, base=0):
        start = base + way * 128 + sub * 64
        return pl.ds(start if isinstance(start, int) else pl.multiple_of(start, 64), 64)

    def piece(self, slot, way, sub, width):
        return self.slots.at[slot, self.rows(way, sub), pl.ds(0, width)]

    def begin(self, a, own, width, column=0):
        for sub in (0, 1):
            for way in (0, 1):
                src = own.at[self.rows(way, sub, way * 256), pl.ds(column, width)]
                self.copy(a, 0, way, sub, src, self.slot(a, 0), width).start()

    def event(self, a, e, own, width, out, column=0):
        step, sub = e // 2, e % 2
        is_last = step // 6
        here = self.slot(a, step)
        far = (step + 1) // 4
        place0 = (1 - far) * 2 * (step + 1) + far * (11 - 2 * step) + is_last * 8
        far = (step + 2) // 4 - is_last
        place1 = (1 - far) * (3 + 2 * step) + far * (10 - 2 * step) + is_last * 9
        places = (place0, place1)
        for way in (0, 1):
            piece = self.piece(here, way, sub, width)
            came = self.copy(a, step, way, sub, piece, here, width)
            came.wait_recv()
            came.wait_send()

        def summed(way):
            mine = own[self.rows(way, sub, places[way] * 256), pl.ds(column, width)]
            came = self.slots[here, self.rows(way, sub), pl.ds(0, width)]
            return came.astype(f32) + mine.astype(f32)

        def on():
            for way in (0, 1):
                self.slots[here, self.rows(way, sub), pl.ds(0, width)] = summed(way).astype(bf16)
                piece = self.piece(here, way, sub, width)
                self.copy(a, step + 1, way, sub, piece, self.slot(a, step + 1), width).start()

        def end():
            for way in (0, 1):
                out[self.rows(way, sub), pl.ds(0, width)] = summed(way)

        if isinstance(e, int):
            if step < 6:
                on()
            else:
                end()
        else:
            pl.when(step < 6)(on)
            pl.when(step == 6)(end)


class TpSum:
    def __init__(self, part, from_core, from_y, sems, credits, tp, over_y, over_core):
        self.part, self.from_core, self.from_y = part, from_core, from_y
        self.sems, self.credits = sems, credits
        self.tp, self.over_y, self.over_core = tp, over_y, over_core
        self.y, self.c = tp // 2, tp % 2

    def to_core(self, i, yy):
        return pltpu.make_async_remote_copy(
            src_ref=self.part.at[i, yy * 2 + 1 - self.c],
            dst_ref=self.from_core.at[i, yy],
            send_sem=self.sems.at[yy, i],
            recv_sem=self.sems.at[2 + yy, i],
            device_id={"tp": self.over_core},
            device_id_type=pl.DeviceIdType.MESH,
        )

    def to_y(self, i):
        return pltpu.make_async_remote_copy(
            src_ref=self.part.at[i, (1 - self.y) * 2 + self.c],
            dst_ref=self.from_y.at[i],
            send_sem=self.sems.at[4, i],
            recv_sem=self.sems.at[5, i],
            device_id={"tp": self.over_y},
            device_id_type=pl.DeviceIdType.MESH,
        )

    def sent(self, i):
        self.to_core(i, 0).wait_send()
        self.to_core(i, 1).wait_send()
        self.to_y(i).wait_send()

    def offer(self, i, turn, value):
        if turn > 0:
            self.sent(i)
        for block in range(4):
            self.part[i, block] = value[block * 256 : (block + 1) * 256].astype(bf16)
        if turn > 0:
            pl.semaphore_wait(self.credits.at[0], 1)
        for yy in (0, 1):
            self.to_core(i, yy).start()

    def pass_on(self, i, turn):
        for yy in (0, 1):
            self.to_core(i, yy).wait_recv()
        away = (1 - self.y) * 2 + self.c
        self.part[i, away] = (
            self.part[i, away].astype(f32) + self.from_core[i, 1 - self.y].astype(f32)
        ).astype(bf16)
        if turn > 0:
            pl.semaphore_wait(self.credits.at[1], 1)
        self.to_y(i).start()

    def take(self, i, turn, use):
        self.to_y(i).wait_recv()
        use(
            self.part[i, self.tp].astype(f32)
            + self.from_core[i, self.y].astype(f32)
            + self.from_y[i].astype(f32)
        )
        if turn < 2:
            for k, peer in ((0, self.over_core), (1, self.over_y)):
                pl.semaphore_signal(
                    self.credits.at[k],
                    inc=1,
                    device_id={"tp": peer},
                    device_id_type=pl.DeviceIdType.MESH,
                )


def col(i, width=256):
    return pl.ds(i * width if isinstance(i, int) else pl.multiple_of(i * width, width), width)


def bwd_kernel(
    lengths, sa_ref, sb_ref, lanes_ref, hm_ref, gains, s_in, den, gain_first, gain_second,
    x_in, x1_in, wq_all, wo_all, wg_all, wu_all, wd_all, c_all, h1_all, qkv_all, yb_all, h2_all,
    gate_all, up_all, m_all, terms_all,
    d_out, g_out, u_out, oq_out, block_out, input_out, gain_out, u_kept,
    tok_ref, line_ref, coef_ref, terms, terms_core, terms_y,
    slots, s1, s2, wo, stream, hs, rows_all, mm, dup, tiles, qkv, kq, yb, dnum, dden, dden_t, dqkv,
    dq, dk, part, from_core, from_y, acc, x1, fout, st, st_x, st_t, st_z, st_y, st_g, s_back, own_rows,
    ring_send, ring_recv, tp_sems, credits, send, recv, local, tile_sems,
):
    seq, tp, place, nearby, over_y, over_core, peers = places()
    z, x = seq // 2, seq % 2
    rows, width = own_rows.shape
    total = 4 * rows
    ff = mm.shape[1]
    links = Links(send, recv)
    locs = Sems(local)

    def load(src, dst):
        made = pltpu.make_async_copy(src, dst, locs.take())
        made.start()
        return made

    def whole(everyone, flat):
        count, chunk = everyone.shape[0], everyone.shape[1]
        return [load(everyone.at[j], flat.at[pl.ds(j * chunk, chunk)]) for j in range(count)]

    got_m = load(m_all, mm)
    got_wd = whole(wd_all, s2)
    got_terms = load(terms_all, s1)
    got_c = load(c_all, rows_all)
    greet(peers)
    ring = Scatter(slots, ring_send, ring_recv, nearby)
    ring.begin(0, terms_all, ff)
    got_x1 = load(x1_in, x1)
    fill_tables(lengths, seq, tok_ref, line_ref, coef_ref, -1)
    columns = ring_columns(place)
    got_qkv = [load(qkv_all, qkv), load(yb_all, yb)]
    got_wo = whole(wo_all, wo)
    sums = TpSum(part, from_core, from_y, tp_sems, credits, tp, over_y, over_core)

    def run(n, body, pumps=None):
        def step(i, _):
            body(i)
            if pumps:
                a, first, count = pumps
                every = n // count
                pl.when((i + 1) % every == 0)(lambda: event(a, first + (i + 1) // every - 1))
            return 0

        lax.fori_loop(0, n, step, 0)

    plan = {0: (s1, ff, 0), 1: (s2, ff, 0), 2: (s1, ff, 0), 3: (s2, 1152, 0)}

    def event(a, e):
        own, wide, column = plan[a]
        ring.event(a, e, own, wide, fout, column)

    def begin(a):
        own, wide, column = plan[a]
        ring.begin(a, own, wide, column)

    def events(a, first, last):
        lax.fori_loop(first, last, lambda e, _: (event(a, e), 0)[1], 0)

    def both(a, first, b, second, count):
        def pair(i, _):
            event(a, first + i)
            event(b, second + i)
            return 0

        lax.fori_loop(0, count, pair, 0)

    def chunks_of(source, size, body, pumps=None, count=8):
        def copies(i, slot):
            return [
                pltpu.make_async_copy(a, b, tile_sems.at[k, slot])
                for k, (a, b) in enumerate(source(i, slot))
            ]

        for made in copies(0, 0):
            made.start()

        def step(i):
            slot = i % 2

            @pl.when(i + 1 < count)
            def _():
                for made in copies(i + 1, 1 - slot):
                    made.start()

            for made in copies(i, slot):
                made.wait()
            body(i, slot)

        run(count, step, pumps)

    got_m.wait()
    for made in got_wd:
        made.wait()
    got_terms.wait()

    def mlp(i):
        sums.offer(i, 0, dot_t(mm[...], s2[col(i), :]))
        pl.when(i > 0)(lambda: sums.pass_on(i - 1, 0))

    run(8, mlp, (0, 0, 2))
    sums.pass_on(7, 0)

    def gate_up_tiles(i, slot):
        r = col(i, 128)
        return [
            (gate_all.at[r], tiles.at[slot, pl.ds(0, 128)]),
            (up_all.at[r], tiles.at[slot, pl.ds(128, 128)]),
        ]

    def grad_gate_up(i, slot):
        r = col(i, 128)
        dm = dot(rows_all[r, :], s2[...]).astype(bf16).astype(f32)
        g = tiles[slot, 0:128].astype(f32)
        u = tiles[slot, 128:256].astype(f32)
        s = jax.nn.sigmoid(g)
        mm[r, :] = (dm * u * s * (1.0 + g * (1.0 - s))).astype(bf16)
        dup[r, :] = (dm * (g * s)).astype(bf16)

        pl.when(i >= 3)(lambda: take_block(i - 3))

    def take_block(i):
        def use(value):
            own_rows[:, col(i)] = (x1[:, col(i)] + value).astype(bf16)

        sums.take(i, 0, use)

    got_x1.wait()
    got_c.wait()
    chunks_of(gate_up_tiles, 8, grad_gate_up, (0, 2, 4))

    def w_tiles(i, slot):
        return [(wg_all.at[i], stream.at[slot, 0]), (wu_all.at[i], stream.at[slot, 1])]

    def grad_hidden(i, slot):
        pl.when(i < 3)(lambda: take_block(5 + i))
        value = dot_t(mm[...], stream[slot, 0]) + dot_t(dup[...], stream[slot, 1])
        sums.offer(i, 1, value)
        pl.when(i > 0)(lambda: sums.pass_on(i - 1, 1))

    chunks_of(w_tiles, 8, grad_hidden, (0, 6, 4))
    kept = [load(own_rows.at[:, col(j)], block_out.at[:, c]) for j, c in enumerate(columns)]
    pending = []
    sums.pass_on(7, 1)

    def h_tiles(everyone):
        return lambda i, slot: [(everyone.at[:, col(i)], hs.at[slot])]

    def keep_up(i, slot):
        return pltpu.make_async_copy(tiles.at[slot], u_kept.at[col(i)], tile_sems.at[1, slot])

    def grads(i, slot):
        s2[col(i), :] = dot_tt(hs[slot], mm[...]).astype(bf16)
        pl.when(i >= 2)(lambda: keep_up(i - 2, slot).wait())
        tiles[slot] = dot_tt(hs[slot], dup[...]).astype(bf16)
        keep_up(i, slot).start()
        pl.when(i == 1)(lambda: begin(1))

    chunks_of(h_tiles(h2_all), 8, grads, (0, 10, 2))
    keep_up(6, 0).wait()
    keep_up(7, 1).wait()

    def take_second(i):
        def use(value):
            acc[:, col(i)] = value

        sums.take(i, 1, use)

    run(2, take_second)
    both(1, 0, 0, 12, 2)
    done = load(fout.at[:, pl.ds(0, ff)], d_out)
    got_up = load(u_kept, s1)
    lax.fori_loop(2, 5, lambda i, _: (take_second(i), 0)[1], 0)
    events(1, 2, 3)
    lax.fori_loop(5, 8, lambda i, _: (take_second(i), 0)[1], 0)
    events(1, 3, 4)

    for made in kept:
        made.wait()

    def norm_back_second(i, _):
        r = pl.ds(pl.multiple_of(i * 32, 32), 32)
        v = x1[r, :]
        s = lax.rsqrt(jnp.mean(v * v, axis=1, keepdims=True) + epsilon)
        n = v * s
        dn = acc[r, :] * gains[1:2, :]
        own = pl.ds(pl.multiple_of(tp * rows + i * 32, 32), 32)
        back = rows_all[own, :].astype(f32) + s * (
            dn - n * jnp.mean(dn * n, axis=1, keepdims=True)
        )
        acc[r, :] = back
        own_rows[r, :] = back.astype(bf16)
        return 0

    lax.fori_loop(0, rows // 32, norm_back_second, 0)
    da = Rows(links, own_rows, rows_all, tp, over_y, over_core, rows)
    own_in = load(own_rows, da.block(tp, 0, rows))

    events(1, 4, 6)
    da.forward(0)
    events(1, 6, 8)
    da.forward(1)
    events(1, 8, 9)
    for made in got_qkv + got_wo:
        made.wait()
    da.finish()
    own_in.wait()
    links.sent_now(da.first + [da.near])
    got_x = [load(x_in.at[:, c], own_rows.at[:, col(j)]) for j, c in enumerate(columns)]

    def head_v(h):
        return slice(128 + h * 128, 256 + h * 128)

    def grad_attended(i):
        r = col(i, 256)
        dy = dot(rows_all[r, :], wo[...])
        kq[r, :] = pltpu.roll(qkv[r, 0:128].astype(f32), 64, 1).astype(bf16)
        columns = []
        for h in range(4):
            hv = slice(h * 128, (h + 1) * 128)
            under = 1.0 / den[r, h : h + 1]
            part_h = dy[:, hv]
            dnum[r, hv] = (part_h * under).astype(bf16)
            low = jnp.sum(part_h * yb[r, hv].astype(f32), axis=1, keepdims=True)
            columns.append(-low * under)
        lane = lax.broadcasted_iota(jnp.int32, (256, 128), 1)
        packed = jnp.zeros((256, 128), f32)
        for h in range(4):
            packed = jnp.where(lane == h, columns[h], packed)
        dden[r, :] = packed
        dden_t[i] = packed.T[0:8, :]

    run(4, grad_attended)
    events(1, 9, 10)

    for h in range(4):

        def state(i, c, h=h):
            s, zz = c
            r = col(i, 256)
            a, b = phi(qkv[r, 0:128], h, sa_ref, sb_ref, lanes_ref)
            f = a * b * lanes_ref[2:3, :] * tok_ref[r, 1:2]
            s = s + dot_tt(f.astype(bf16), dnum[r, h * 128 : (h + 1) * 128])
            return s, zz + jnp.sum(f * dden[r, h : h + 1], axis=0, keepdims=True)

        s, zz = lax.fori_loop(
            0, 4, state, (jnp.zeros((256, 128), f32), jnp.zeros((1, 256), f32))
        )
        pack_state(st, h, s, zz)
    moved = Exchange(links, st, st_x, st_t, st_z, st_y, st_g, s_back, coef_ref, seq, -1)
    events(1, 10, 11)

    dq[...] = jnp.zeros(dq.shape, f32)

    def local_head(h):
        hm = hm_ref[h : h + 1, :]
        hv = slice(h * 128, (h + 1) * 128)
        for j in range(total // 256):
            k_rows = slice(j * 256, (j + 1) * 256)
            dv_s = jnp.zeros((256, 128), f32)
            dk_s = jnp.zeros((256, 128), f32)
            for i in range(j, total // 256):
                q_rows = slice(i * 256, (i + 1) * 256)
                qm = (qkv[q_rows, 0:128].astype(f32) * hm).astype(bf16)
                u = dot_t(kq[k_rows, :], qm)
                keep = tok_ref[k_rows, 3:4] >= line_ref[1:2, q_rows]
                if i == j:
                    keep = keep & (tok_ref[k_rows, 3:4] <= line_ref[0:1, q_rows])
                kap = jnp.where(keep, (0.5 * u + 1.0) * u + 1.0, 0.0).astype(bf16)
                dn = dnum[q_rows, hv]
                grad = dot_t(qkv[k_rows, head_v(h)], dn) + dden_t[i, h : h + 1, :]
                du = jnp.where(keep, grad * (1.0 + u), 0.0).astype(bf16)
                dv_s = dv_s + dot(kap, dn)
                dk_s = dk_s + dot(du, qm)
                dq[q_rows, :] += dot_tt(du, kq[k_rows, :]) * hm
            dqkv[k_rows, head_v(h)] = dv_s.astype(bf16)
            if h == 0:
                dk[k_rows, :] = dk_s
            else:
                dk[k_rows, :] += dk_s

    local_head(0)
    moved.pair()
    events(1, 11, 12)
    got_up.wait()
    begin(2)
    local_head(1)
    moved.planes()
    done.wait()
    events(1, 12, 14)
    done = load(fout.at[:, pl.ds(0, ff)], g_out)
    local_head(2)
    moved.give()
    events(2, 0, 2)
    local_head(3)
    events(2, 2, 3)
    moved.take()

    def split_state(ref, h):
        z_row = jnp.concatenate([ref[h, 160:161, :], ref[h, 161:162, :]], axis=1)
        feat = lax.broadcasted_iota(jnp.int32, (256, 128), 0)
        return jnp.where(feat < FEATS, ref[h], 0.0).astype(bf16), z_row

    for h in range(4):
        s_q, z_q = split_state(s_in, h)
        s_k, z_k = split_state(s_back, h)
        hv = slice(h * 128, (h + 1) * 128)

        def through(grad, a, b, h=h):
            grad = grad * lanes_ref[2:3, :]
            return dot_t((grad * b).astype(bf16), sa_ref[h]) + dot_t(
                (grad * a).astype(bf16), sb_ref[h]
            )

        def carried_part(i, _, h=h, s_q=s_q, z_q=z_q, s_k=s_k, z_k=z_k, hv=hv, through=through):
            r = col(i, 256)
            a, b = phi(qkv[r, 0:128], h, sa_ref, sb_ref, lanes_ref)
            grad = dot_t(dnum[r, hv], s_q) + dden[r, h : h + 1] * z_q
            dq[r, :] += through(grad * tok_ref[r, 1:2], a, b)
            a, b = phi(kq[r, :], h, sa_ref, sb_ref, lanes_ref)
            last = tok_ref[r, 2:3]
            grad = dot_t(qkv[r, head_v(h)], s_k) + z_k
            dk[r, :] += through(grad * last, a, b)
            f = (a * b * lanes_ref[2:3, :] * last).astype(bf16)
            dqkv[r, head_v(h)] = (dqkv[r, head_v(h)].astype(f32) + dot(f, s_k)).astype(bf16)
            return 0

        lax.fori_loop(0, 4, carried_part, 0)

    def join(i):
        r = col(i, 256)
        dqkv[r, 0:128] = (dq[r, :] + pltpu.roll(dk[r, :], 64, 1)).astype(bf16)

    run(4, join)
    events(2, 3, 5)
    own_w = load(wg_all.at[7], stream.at[0, 0])
    own_w.wait()
    gain_two = jnp.sum(fout[:, 0:ff] * stream[0, 0].astype(f32), axis=1, keepdims=True)

    def wq_tiles(i, slot):
        return [(wq_all.at[i], stream.at[slot, 0, :, pl.ds(0, 640)])]

    def grad_hidden_first(i, slot):
        sums.offer(i, 2, dot_t(dqkv[...], stream[slot, 0, :, 0:640]))
        pl.when(i > 0)(lambda: sums.pass_on(i - 1, 2))

    chunks_of(wq_tiles, 8, grad_hidden_first, (2, 5, 2))
    sums.pass_on(7, 2)

    def grad_out_qkv(i, slot):
        s2[col(i), 0:512] = dot_tt(rows_all[:, col(i)], yb[...]).astype(bf16)
        s2[col(i), 512:1152] = dot_tt(hs[slot], dqkv[...]).astype(bf16)

        pl.when(i == 1)(lambda: begin(3))

    chunks_of(h_tiles(h1_all), 8, grad_out_qkv, (2, 7, 2))
    both(2, 9, 3, 0, 3)
    done.wait()
    both(2, 12, 3, 3, 2)
    done = load(fout.at[:, pl.ds(0, ff)], u_out)
    def take_first(i):
        def use(value):
            x1[:, col(i)] = value

        sums.take(i, 2, use)

    run(8, take_first, (3, 5, 4))
    for made in got_x:
        made.wait()

    def norm_back_first(i, _):
        r = pl.ds(pl.multiple_of(i * 32, 32), 32)
        v = own_rows[r, :].astype(f32)
        s = lax.rsqrt(jnp.mean(v * v, axis=1, keepdims=True) + epsilon)
        n = v * s
        dn = x1[r, :] * gains[0:1, :]
        acc[r, :] += s * (dn - n * jnp.mean(dn * n, axis=1, keepdims=True))
        return 0

    lax.fori_loop(0, rows // 32, norm_back_first, 0)
    pending += [load(acc.at[:, col(j)], input_out.at[:, c]) for j, c in enumerate(columns)]
    own_w = load(wu_all.at[7], stream.at[0, 0])
    own_q = load(wq_all.at[7], stream.at[1, 0, :, pl.ds(0, 640)])
    own_w.wait()
    own_q.wait()
    gain_two += jnp.sum(fout[:, 0:ff] * stream[0, 0].astype(f32), axis=1, keepdims=True)
    events(3, 9, 12)
    done.wait()
    events(3, 12, 14)
    pending.append(load(fout.at[:, pl.ds(0, 1152)], oq_out))
    gain_one = jnp.sum(fout[:, 512:1152] * stream[1, 0, :, 0:640].astype(f32), axis=1, keepdims=True)
    lane = lax.broadcasted_iota(jnp.int32, (256, 128), 1)
    both = jnp.where(lane == 0, gain_one, jnp.where(lane == 1, gain_two, 0.0)).T[0:8, :]
    terms[0] = both
    over = links.start(terms.at[0], terms_core, tp=over_core)
    over.wait_recv()
    both = both + terms_core[...]
    terms[1] = both
    over = links.start(terms.at[1], terms_y, tp=over_y)
    over.wait_recv()
    own_gains = jnp.concatenate(
        [gain_first[...], gain_second[...], jnp.ones((6, 256), f32)], axis=0
    ).astype(bf16)
    terms[2] = (both + terms_y[...]) / own_gains.astype(f32)
    pending.append(load(terms.at[2], gain_out))
    run(8, lambda i: sums.sent(i))
    for made in pending:
        made.wait()
    links.finish()
    moved.finish()


def feature_tables(heads):
    first = np.zeros((heads, 128, 256), np.float32)
    second = np.zeros((heads, 128, 256), np.float32)
    lanes = np.zeros((8, 256), np.float32)
    f = 0
    for i in range(FEAT):
        for j in range(i, FEAT):
            for h in range(heads):
                first[h, h * FEAT + i, f] = 1
                second[h, h * FEAT + j, f] = 1
            lanes[2, f] = square_coef if i == j else square_coef * 2**0.5
            f += 1
    for i in range(FEAT):
        for h in range(heads):
            first[h, h * FEAT + i, f] = 1
        lanes[1, f] = 1
        lanes[2, f] = linear_coef
        f += 1
    lanes[0, f] = lanes[1, f] = lanes[2, f] = 1
    mask = np.zeros((8, 128), np.float32)
    for h in range(heads):
        mask[h, h * FEAT : (h + 1) * FEAT] = 0.25
    return first, second, lanes, mask


def forward_pass(lengths, constants, gain_first, gain_second, x_in, weights, c_in):
    rows, width = x_in.shape
    total = 4 * rows
    ff = weights[4].shape[0]
    hbm = pl.BlockSpec(memory_space=pl.ANY)
    vmem = pl.BlockSpec(memory_space=pltpu.VMEM)

    def shape(*dims, dtype=bf16):
        return jax.ShapeDtypeStruct(dims, dtype)

    outs = (
        shape(8, 256, 640),
        shape(8, 256, 512),
        shape(8, 256, ff),
        shape(8, 256, ff),
        shape(8, 256, ff),
        shape(total, width),
        shape(total, width),
        shape(total, 640),
        shape(total, 512),
        shape(total, 128, dtype=f32),
        shape(rows, width, dtype=f32),
        shape(total, width),
        shape(total, ff),
        shape(total, ff),
        shape(total, ff),
        shape(4, 256, 128, dtype=f32),
        shape(8, width, dtype=f32),
        shape(width, ff),
    )
    scratch = [
        pltpu.VMEM((rows, width), bf16),
        pltpu.VMEM((total, 128), f32),
        pltpu.VMEM((8, total), f32),
        pltpu.VMEM((8, 128), f32),
        pltpu.VMEM((16, 256), bf16),
        pltpu.VMEM((256, 640), bf16),
        pltpu.VMEM((256, 512), bf16),
        pltpu.VMEM((256, ff), bf16),
        pltpu.VMEM((256, ff), bf16),
        pltpu.VMEM((256, ff), bf16),
        pltpu.VMEM((128, 256), f32),
        pltpu.VMEM((256, 512), f32),
        pltpu.VMEM((512, 256), f32),
        pltpu.VMEM((-(-ff // 128) * 128, 256), f32),
        pltpu.VMEM((-(-ff // 128) * 128, 256), f32),
        pltpu.VMEM((rows, width), bf16),
        pltpu.VMEM((total, width), bf16),
        pltpu.VMEM((total, width), bf16),
        pltpu.VMEM((width, 640), bf16),
        pltpu.VMEM((width, 512), bf16),
        pltpu.VMEM((width, ff), bf16),
        pltpu.VMEM((width, ff), bf16),
        pltpu.VMEM((total, 640), bf16),
        pltpu.VMEM((total, 128), bf16),
        pltpu.VMEM((total, 512), f32),
        pltpu.VMEM((total, 128), f32),
        pltpu.VMEM((total, 512), bf16),
        pltpu.VMEM((2, rows, width), bf16),
        pltpu.VMEM((2, rows, width), bf16),
        pltpu.VMEM((rows, width), bf16),
        pltpu.VMEM((rows, width), bf16),
        pltpu.VMEM((rows, width), f32),
        pltpu.VMEM((total, ff), bf16),
        pltpu.VMEM((total, ff), bf16),
        pltpu.VMEM((total, ff), bf16),
        pltpu.VMEM((8, 16, 256), bf16),
        pltpu.VMEM((8, width), f32),
        pltpu.VMEM((4, 176, 128), bf16),
        pltpu.VMEM((2, 176, 128), bf16),
        pltpu.VMEM((2, 176, 128), bf16),
        pltpu.VMEM((2, 176, 128), bf16),
        pltpu.VMEM((2, 176, 128), bf16),
        pltpu.VMEM((2, 2, 176, 128), bf16),
        pltpu.VMEM((4, 256, 128), f32),
        pltpu.SemaphoreType.DMA((144,)),
        pltpu.SemaphoreType.DMA((144,)),
        pltpu.SemaphoreType.DMA((144,)),
    ]
    return pl.pallas_call(
        fwd_kernel,
        out_shape=outs,
        in_specs=[pl.BlockSpec(memory_space=pltpu.SMEM)] + [vmem] * 6 + [hbm] * 9,
        out_specs=(hbm,) * len(outs),
        scratch_shapes=scratch,
        compiler_params=pltpu.CompilerParams(
            collective_id=0, has_side_effects=True, vmem_limit_bytes=60 * 2**20
        ),
    )(lengths, *constants, gain_first, gain_second, x_in, *weights, c_in)


def backward_pass(lengths, constants, gains, s_in, den, gain_pair, x_in, x1, weights, c_all, acts):
    rows, width = x_in.shape
    total = 4 * rows
    ff = weights[2].shape[2]
    hbm = pl.BlockSpec(memory_space=pl.ANY)
    vmem = pl.BlockSpec(memory_space=pltpu.VMEM)

    def shape(*dims, dtype=f32):
        return jax.ShapeDtypeStruct(dims, dtype)

    outs = (
        shape(256, ff),
        shape(256, ff),
        shape(256, ff),
        shape(256, 1152),
        shape(rows, width, dtype=bf16),
        shape(rows, width),
        shape(8, 256),
        shape(width, ff, dtype=bf16),
    )
    scratch = [
        pltpu.VMEM((total, 128), f32),
        pltpu.VMEM((8, total), f32),
        pltpu.VMEM((8, 128), f32),
        pltpu.VMEM((3, 8, 256), f32),
        pltpu.VMEM((8, 256), f32),
        pltpu.VMEM((8, 256), f32),
        pltpu.VMEM((8, 256, ff), bf16),
        pltpu.VMEM((width, ff), bf16),
        pltpu.VMEM((width, ff), bf16),
        pltpu.VMEM((width, 512), bf16),
        pltpu.VMEM((2, 2, 256, ff), bf16),
        pltpu.VMEM((2, total, 256), bf16),
        pltpu.VMEM((total, width), bf16),
        pltpu.VMEM((total, ff), bf16),
        pltpu.VMEM((total, ff), bf16),
        pltpu.VMEM((2, 256, ff), bf16),
        pltpu.VMEM((total, 640), bf16),
        pltpu.VMEM((total, 128), bf16),
        pltpu.VMEM((total, 512), bf16),
        pltpu.VMEM((total, 512), bf16),
        pltpu.VMEM((total, 128), f32),
        pltpu.VMEM((4, 8, 256), f32),
        pltpu.VMEM((total, 640), bf16),
        pltpu.VMEM((total, 128), f32),
        pltpu.VMEM((total, 128), f32),
        pltpu.VMEM((8, 4, 256, 256), bf16),
        pltpu.VMEM((8, 2, 256, 256), bf16),
        pltpu.VMEM((8, 256, 256), bf16),
        pltpu.VMEM((rows, width), f32),
        pltpu.VMEM((rows, width), f32),
        pltpu.VMEM((256, ff), f32),
        pltpu.VMEM((4, 176, 128), bf16),
        pltpu.VMEM((2, 176, 128), bf16),
        pltpu.VMEM((2, 176, 128), bf16),
        pltpu.VMEM((2, 176, 128), bf16),
        pltpu.VMEM((2, 176, 128), bf16),
        pltpu.VMEM((2, 2, 176, 128), bf16),
        pltpu.VMEM((4, 256, 128), f32),
        pltpu.VMEM((rows, width), bf16),
        pltpu.SemaphoreType.DMA((2, 2, 2)),
        pltpu.SemaphoreType.DMA((2, 2, 2, 7)),
        pltpu.SemaphoreType.DMA((6, 8)),
        pltpu.SemaphoreType.REGULAR((2,)),
        pltpu.SemaphoreType.DMA((16,)),
        pltpu.SemaphoreType.DMA((16,)),
        pltpu.SemaphoreType.DMA((80,)),
        pltpu.SemaphoreType.DMA((2, 2)),
    ]
    return pl.pallas_call(
        bwd_kernel,
        out_shape=outs,
        in_specs=[pl.BlockSpec(memory_space=pltpu.SMEM)] + [vmem] * 9 + [hbm] * 16,
        out_specs=(hbm,) * len(outs),
        scratch_shapes=scratch,
        compiler_params=pltpu.CompilerParams(
            collective_id=1, has_side_effects=True, vmem_limit_bytes=62 * 2**20
        ),
    )(lengths, *constants, gains, s_in, den, *gain_pair, x_in, x1, *weights, c_all, *acts)


def finish_kernel(
    d_in, g_in, u_in, oq_in, block_in, input_in,
    d_out, g_out, u_out, o_out, q_out, k_out, v_out, block_out, input_out,
    wide, turned, oq, oq_t, block, grad, sems,
):
    keeper = Sems(sems)
    ff = d_in.shape[1]

    def copy(src, dst):
        made = pltpu.make_async_copy(src, dst, keeper.take())
        made.start()
        return made

    came = [copy(ref, wide.at[i]) for i, ref in enumerate((g_in, u_in, d_in))]
    came_oq = copy(oq_in, oq)
    came_block, came_grad = copy(block_in, block), copy(input_in, grad)
    came_oq.wait()
    oq_t[...] = oq[:, 0:640].T
    kept = [
        copy(oq.at[:, pl.ds(640, 512)], v_out),
        copy(oq_t.at[pl.ds(0, 512)], o_out),
        copy(oq_t.at[pl.ds(512, 64)], q_out),
        copy(oq_t.at[pl.ds(576, 64)], k_out),
    ]
    for i, out in enumerate((g_out, u_out, d_out)):
        came[i].wait()
        for at in range(0, ff, 128):
            at = min(at, ff - 128)
            turned[i, at : at + 128, :] = wide[i, :, at : at + 128].T
        kept.append(copy(turned.at[i], out))
    came_block.wait()
    kept.append(copy(block, block_out))
    came_grad.wait()
    kept.append(copy(grad, input_out))
    for made in kept:
        made.wait()


def finish(d, g, u, oq, block, grad_input):
    rows, width = block.shape
    ff = d.shape[1]
    hbm = pl.BlockSpec(memory_space=pl.ANY)

    def shape(*dims, dtype=f32):
        return jax.ShapeDtypeStruct(dims, dtype)

    outs = (
        shape(ff, 256), shape(ff, 256), shape(ff, 256), shape(512, 256), shape(64, 256),
        shape(64, 256), shape(256, 512), shape(rows, width, dtype=bf16), shape(rows, width),
    )
    return pl.pallas_call(
        finish_kernel,
        out_shape=outs,
        in_specs=[hbm] * 6,
        out_specs=(hbm,) * len(outs),
        scratch_shapes=[
            pltpu.VMEM((3, 256, ff), f32),
            pltpu.VMEM((3, ff, 256), f32),
            pltpu.VMEM((256, 1152), f32),
            pltpu.VMEM((640, 256), f32),
            pltpu.VMEM((rows, width), bf16),
            pltpu.VMEM((rows, width), f32),
            pltpu.SemaphoreType.DMA((24,)),
        ],
        compiler_params=pltpu.CompilerParams(vmem_limit_bytes=60 * 2**20),
    )(d, g, u, oq, block, grad_input)


def on_device_rings(
    inputs, lengths, gain_attn, w_query, w_key, w_value, w_out, gain_mlp, w_gate, w_up, w_down,
    cotangent,
):
    first, second, lanes, mask = feature_tables(4)
    constants = (
        jnp.asarray(first, bf16), jnp.asarray(second, bf16), jnp.asarray(lanes), jnp.asarray(mask),
    )
    gain_pair = (gain_attn.reshape(1, -1), gain_mlp.reshape(1, -1))
    made = forward_pass(
        lengths, constants, *gain_pair, inputs,
        (w_query.T, w_key.T, w_value, w_out, w_gate.T, w_up.T, w_down), cotangent,
    )
    weights = made[:5]
    c_all, h1, qkv, yb, den, x1, h2, gate, up, mixed, s_in, gain_all, terms = made[5:]
    sum_down_t, sum_gate, sum_up, sum_oq, block, grad_input, gain_sums, _ = backward_pass(
        lengths, constants, gain_all, s_in, den, gain_pair, inputs, x1, weights, c_all,
        (h1, qkv, yb, h2, gate, up, mixed, terms),
    )
    d, g_t, u_t, o, q_t, k_t, v, block, grad_input = finish(
        sum_down_t, sum_gate, sum_up, sum_oq, block, grad_input
    )
    return (
        block,
        grad_input,
        gain_sums[0],
        q_t.T,
        k_t.T,
        v,
        o,
        gain_sums[1],
        g_t.T,
        u_t.T,
        d,
    )


def on_device(
    inputs,
    lengths,
    gain_attn,
    w_query,
    w_key,
    w_value,
    w_out,
    gain_mlp,
    w_gate,
    w_up,
    w_down,
    cotangent,
):
    seq_count = lax.axis_size("seq")
    tp_count = lax.axis_size("tp")
    seq_index = lax.axis_index("seq")
    rows_own, width = inputs.shape
    chunk = width // seq_count
    half = chunk // 2
    block_len = rows_own * tp_count
    anchor = seq_index * block_len
    relative = relative_list(seq_count)
    ring = ring_order(seq_count)
    place_of = [ring.index(s) for s in range(seq_count)]
    to_rel = jnp.array(
        [[ring[(place_of[s] - k) % seq_count] for k in relative] for s in range(seq_count)],
        jnp.int32,
    )[seq_index]
    to_abs = jnp.array(
        [
            [relative.index((place_of[s] - place_of[o]) % seq_count) for o in range(seq_count)]
            for s in range(seq_count)
        ],
        jnp.int32,
    )[seq_index]
    to_rel = [to_rel[j] for j in range(seq_count)]
    to_abs = [to_abs[j] for j in range(seq_count)]

    qk_cols, v_cols, ff_cols = w_query.shape[1], w_value.shape[1], w_gate.shape[1]
    gains = jnp.stack([gain_attn, gain_mlp]).astype(bf16)
    qkv_cols = 2 * qk_cols + v_cols
    qkv_own = jnp.concatenate([w_query, w_key, w_value], axis=1).astype(bf16)
    gain_rows = jnp.zeros((16, qkv_cols), bf16).at[:2, :chunk].set(gains)
    first_own = jnp.concatenate([qkv_own, gain_rows], axis=0)
    out_own = w_out.astype(bf16).T
    gate_up_own = jnp.concatenate([w_gate, w_up], axis=1).astype(bf16)
    down_own = w_down.astype(bf16).T

    first_got = ring_gather(first_own, half)
    out_got = ring_gather(out_own, half)
    gate_up_got = ring_gather(gate_up_own, half)
    down_got = ring_gather(down_own, half)
    w_qkv = jnp.concatenate([first_got[k][:chunk] for k in relative], axis=0)
    gain_first = jnp.concatenate([first_got[k][chunk, :chunk] for k in relative]).astype(f32)
    gain_second = jnp.concatenate([first_got[k][chunk + 1, :chunk] for k in relative]).astype(f32)
    w_out_t = jnp.concatenate([out_got[k] for k in relative], axis=0)
    w_gate_up = jnp.concatenate([gate_up_got[k] for k in relative], axis=0)
    w_down_t = jnp.concatenate([down_got[k] for k in relative], axis=0)

    at = jnp.arange(lengths.shape[0])
    starts = jnp.sum(jnp.where(at[None, :] < at[:, None], lengths[None, :], 0), axis=1)
    positions, row_ids, carry_in, after_last = segment_masks(anchor, starts, block_len)
    carry_mask = carry_in.astype(f32)
    last_mask = after_last.astype(f32)
    resets = (
        jnp.sum(
            ((starts // block_len)[None, :] == jnp.arange(seq_count)[:, None]).astype(jnp.int32),
            axis=1,
        )
        > 0
    ).astype(jnp.int32)

    inputs_own = to_relative(inputs, to_rel, chunk)
    grad_own = to_relative(cotangent, to_rel, chunk)
    inputs_full = tp_gather(inputs_own).astype(f32)
    grad_full = tp_gather(grad_own)
    inputs_own = inputs_own.astype(f32)
    hidden_first = (inputs_full * rms_scale(inputs_full) * gain_first).astype(bf16)
    qkv = dot(hidden_first, w_qkv).astype(bf16)
    queries = qkv[:, :qk_cols]
    key_flat = qkv[:, qk_cols : 2 * qk_cols]
    value_flat = qkv[:, 2 * qk_cols :]
    heads_local = qk_cols // FEAT
    query_heads = queries.reshape(block_len, heads_local, FEAT)
    key_heads = key_flat.reshape(block_len, heads_local, FEAT)
    value_heads = value_flat.reshape(block_len, heads_local, VHEAD)
    query_float = query_heads.astype(f32)
    key_float = key_heads.astype(f32)
    value_float = value_heads.astype(f32)
    key_feat = features(key_float) * last_mask[:, None, None]
    local_state = jnp.einsum("thn,thv->hnv", key_feat, value_float, precision=highest)
    local_sum = jnp.sum(key_feat, axis=0)
    carry_state, carry_sum = carried([local_state, local_sum], resets, 1)
    step_rows = 512
    query_feat = features(query_float)
    carry_weight = carry_mask[:, None]
    numer_parts = []
    denom_parts = []
    for first_row in range(0, block_len, step_rows):
        query_part = query_heads[first_row : first_row + step_rows]
        scores, allowed, kernel = pair_block(
            query_part, key_heads, row_ids, positions, first_row, step_rows
        )
        numer_parts.append(
            jnp.einsum("hts,shv->thv", kernel.astype(bf16), value_heads, preferred_element_type=f32)
        )
        denom_parts.append(jnp.sum(kernel, axis=-1).T)
    numerator = (
        jnp.concatenate(numer_parts, axis=0)
        + jnp.einsum("thn,hnv->thv", query_feat, carry_state, precision=highest)
        * carry_weight[:, :, None]
    )
    denominator = (
        jnp.concatenate(denom_parts, axis=0)
        + jnp.einsum("thn,hn->th", query_feat, carry_sum, precision=highest) * carry_weight
    )
    attended = numerator / denominator[:, :, None]
    attended_low = attended.reshape(block_len, heads_local * VHEAD).astype(bf16)
    attn_partial = dot_t(attended_low, w_out_t).astype(bf16)
    middle_own = inputs_own + tp_scatter(attn_partial)
    scale_second = rms_scale(middle_own)
    normed_second = middle_own * scale_second
    hidden_second = tp_gather((normed_second * gain_second).astype(bf16))
    gate_up = dot(hidden_second, w_gate_up)
    gate_value, upward = gate_up[:, :ff_cols], gate_up[:, ff_cols:]
    sigmoid_gate = jax.nn.sigmoid(gate_value)
    silu_gate = gate_value * sigmoid_gate
    mixed_rows = (silu_gate * upward).astype(bf16)
    grad_down_t = dot_tt(grad_full, mixed_rows).astype(bf16)

    def by_distance(stack):
        return {k: stack[j * chunk : (j + 1) * chunk] for j, k in enumerate(relative)}

    sum_down_t = ring_scatter(by_distance(grad_down_t))
    mlp_own = tp_scatter(dot_t(mixed_rows, w_down_t).astype(bf16))
    block_output = to_relative((middle_own + mlp_own).astype(bf16), to_abs, chunk)

    grad_mixed = dot(grad_full, w_down_t).astype(bf16).astype(f32)
    grad_gate = (
        grad_mixed * upward * sigmoid_gate * (1.0 + gate_value * (1.0 - sigmoid_gate))
    ).astype(bf16)
    grad_upward = (grad_mixed * silu_gate).astype(bf16)
    grad_gate_up = jnp.concatenate([grad_gate, grad_upward], axis=1)
    hidden_partial = dot_t(grad_gate_up, w_gate_up).astype(bf16)
    sum_gate_up = ring_scatter(by_distance(dot_tt(hidden_second, grad_gate_up).astype(bf16)))
    grad_hidden = tp_scatter(hidden_partial)
    grad_middle = grad_own.astype(f32) + norm_back(
        grad_hidden, normed_second, scale_second, gain_second
    )
    grad_branch = tp_gather(grad_middle.astype(bf16))
    sum_out_t = ring_scatter(by_distance(dot_tt(grad_branch, attended_low).astype(bf16)))
    grad_attended = dot(grad_branch, w_out_t).reshape(block_len, heads_local, VHEAD)
    grad_numer = (grad_attended / denominator[:, :, None]).astype(bf16)
    grad_denom = -jnp.sum(grad_attended * attended, axis=-1) / denominator
    grad_numer_carried = grad_numer.astype(f32) * carry_weight[:, :, None]
    grad_denom_carried = grad_denom * carry_weight
    grad_state_in = jnp.einsum("thn,thv->hnv", query_feat, grad_numer_carried, precision=highest)
    grad_sum_in = jnp.einsum("thn,th->hn", query_feat, grad_denom_carried, precision=highest)
    grad_query_feat = (
        jnp.einsum("thv,hnv->thn", grad_numer_carried, carry_state, precision=highest)
        + grad_denom_carried[:, :, None] * carry_sum[None]
    )
    grad_state_out, grad_sum_out = carried([grad_state_in, grad_sum_in], resets, -1)
    grad_key_feat = (
        jnp.einsum("thv,hnv->thn", value_float, grad_state_out, precision=highest)
        + grad_sum_out[None]
    ) * last_mask[:, None, None]
    grad_value_state = jnp.einsum("thn,hnv->thv", key_feat, grad_state_out, precision=highest)
    grad_query_parts = []
    grad_key_inner = jnp.zeros((block_len, heads_local, FEAT), f32)
    grad_value_inner = jnp.zeros((block_len, heads_local, VHEAD), f32)
    for first_row in range(0, block_len, step_rows):
        query_part = query_heads[first_row : first_row + step_rows]
        scores, allowed, kernel = pair_block(
            query_part, key_heads, row_ids, positions, first_row, step_rows
        )
        numer_grad_part = grad_numer[first_row : first_row + step_rows]
        grad_weights = jnp.einsum(
            "thv,shv->hts", numer_grad_part, value_heads, preferred_element_type=f32
        )
        grad_scores = (
            (grad_weights + grad_denom[first_row : first_row + step_rows].T[:, :, None])
            * allowed[None]
            * (1.0 + scores)
        ).astype(bf16)
        grad_query_parts.append(
            jnp.einsum("hts,shf->thf", grad_scores, key_heads, preferred_element_type=f32) * 0.25
        )
        grad_key_inner = (
            grad_key_inner
            + jnp.einsum("hts,thf->shf", grad_scores, query_part, preferred_element_type=f32) * 0.25
        )
        grad_value_inner = grad_value_inner + jnp.einsum(
            "hts,thv->shv", kernel.astype(bf16), numer_grad_part, preferred_element_type=f32
        )
    grad_query = (
        jnp.concatenate(grad_query_parts, axis=0) + feature_grad(query_float, grad_query_feat)
    ).astype(bf16)
    grad_key = (grad_key_inner + feature_grad(key_float, grad_key_feat)).astype(bf16)
    grad_value = (grad_value_inner + grad_value_state).astype(bf16)
    grad_qkv = jnp.concatenate(
        [
            grad_query.reshape(block_len, heads_local * FEAT),
            grad_key.reshape(block_len, heads_local * FEAT),
            grad_value.reshape(block_len, heads_local * VHEAD),
        ],
        axis=1,
    )
    sum_qkv = ring_scatter(by_distance(dot_tt(hidden_first, grad_qkv).astype(bf16)))
    grad_hidden_first = tp_scatter(dot_t(grad_qkv, w_qkv).astype(bf16))
    scale_first = rms_scale(inputs_own)
    normed_first = inputs_own * scale_first
    grad_input = to_relative(
        grad_middle + norm_back(grad_hidden_first, normed_first, scale_first, gain_first),
        to_abs,
        chunk,
    )

    gain_terms = jnp.stack(
        [
            jnp.sum(qkv_own.astype(f32) * sum_qkv, axis=1),
            jnp.sum(gate_up_own.astype(f32) * sum_gate_up, axis=1),
        ]
    )
    gain_sums = tp_sum(gain_terms) / gains.astype(f32)
    return (
        block_output,
        grad_input,
        gain_sums[0],
        sum_qkv[:, :qk_cols],
        sum_qkv[:, qk_cols : 2 * qk_cols],
        sum_qkv[:, 2 * qk_cols :],
        sum_out_t.T,
        gain_sums[1],
        sum_gate_up[:, :ff_cols],
        sum_gate_up[:, ff_cols:],
        sum_down_t.T,
    )


def solution(mesh):
    in_specs = (
        P(("seq", "tp"), None),
        P(),
        P("seq"),
        P("seq", "tp"),
        P("seq", "tp"),
        P("seq", "tp"),
        P("tp", "seq"),
        P("seq"),
        P("seq", "tp"),
        P("seq", "tp"),
        P("tp", "seq"),
        P(("seq", "tp"), None),
    )
    out_specs = (
        P(("seq", "tp"), None),
        P(("seq", "tp"), None),
        P("seq"),
        P("seq", "tp"),
        P("seq", "tp"),
        P("seq", "tp"),
        P("tp", "seq"),
        P("seq"),
        P("seq", "tp"),
        P("seq", "tp"),
        P("tp", "seq"),
    )
    small = mesh.shape["seq"] == 8 and mesh.shape["tp"] == 4
    body = on_device_rings if small else on_device
    return jax.shard_map(
        body, mesh=mesh, in_specs=in_specs, out_specs=out_specs, check_vma=False
    )
```

```python
import jax
import jax.numpy as jnp
import numpy as np
from jax import lax
from jax.experimental import pallas as pl
from jax.experimental.pallas import tpu as pltpu
from jax.sharding import PartitionSpec as P

FEAT = 16
VHEAD = 128


epsilon = 1e-05
linear_coef = 0.5
square_coef = 0.17677669529663687
highest = lax.Precision.HIGHEST
f32 = jnp.float32
bf16 = jnp.bfloat16


def ring_order(count):
    planes = 4 if count % 4 == 0 else 2
    columns = count // planes
    order = [z * columns for z in range(planes)]
    for z in reversed(range(planes)):
        xs = list(range(1, columns))
        if (planes - 1 - z) % 2:
            xs.reverse()
        order += [z * columns + x for x in xs]
    return order


def relative_list(count):
    half = count // 2
    out = []
    for j in range(1, half):
        out += [j, count - j]
    return out + [half, 0]


def ring_perms(count):
    ring = ring_order(count)
    fwd = [(ring[i], ring[(i + 1) % count]) for i in range(count)]
    return fwd, [(b, a) for a, b in fwd]


def ring_gather(own, half_rows):
    count = lax.axis_size("seq")
    fwd, bwd = ring_perms(count)
    half = count // 2
    got = {0: own}
    ahead = back = own
    for step in range(1, half):
        ahead = lax.ppermute(ahead, "seq", fwd)
        back = lax.ppermute(back, "seq", bwd)
        got[step] = ahead
        got[count - step] = back
    ahead = lax.ppermute(ahead[:half_rows], "seq", fwd)
    back = lax.ppermute(back[half_rows:], "seq", bwd)
    got[half] = jnp.concatenate([ahead, back], axis=0)
    return got


def ring_scatter(chunks):
    count = lax.axis_size("seq")
    fwd, bwd = ring_perms(count)
    half = chunks[0].shape[0] // 2
    ahead = chunks[1][:half]
    back = chunks[count - 1][half:]
    for step in range(count - 1):
        ahead = lax.ppermute(ahead, "seq", fwd).astype(f32)
        back = lax.ppermute(back, "seq", bwd).astype(f32)
        last = step == count - 2
        ahead = ahead + chunks[0 if last else 2 + step][:half].astype(f32)
        back = back + chunks[0 if last else count - 2 - step][half:].astype(f32)
        if not last:
            ahead = ahead.astype(bf16)
            back = back.astype(bf16)
    return jnp.concatenate([ahead, back], axis=0)


def to_relative(array, index_row, chunk):
    return jnp.concatenate(
        [lax.dynamic_slice_in_dim(array, i * chunk, chunk, 1) for i in index_row], axis=1
    )


def tp_perms(count):
    ys = count // 2
    core = [(i, i ^ 1) for i in range(count)]
    shift = [
        [(i, (((i // 2) + d) % ys) * 2 + i % 2) for i in range(count)] for d in range(ys)
    ]
    return core, shift


def tp_gather(own):
    count = lax.axis_size("tp")
    ys = count // 2
    place = lax.axis_index("tp")
    y, c = place // 2, place % 2
    core, shift = tp_perms(count)
    parts = [own] + [lax.ppermute(own, "tp", shift[d]) for d in range(1, ys)]
    mine = jnp.stack([lax.select_n((y - at + ys) % ys, *parts) for at in range(ys)])
    other = lax.ppermute(mine, "tp", core)
    full = jnp.stack([jnp.where(c == 0, mine, other), jnp.where(c == 0, other, mine)], axis=1)
    return full.reshape((count * own.shape[0],) + own.shape[1:])


def tp_scatter(partial):
    count = lax.axis_size("tp")
    ys = count // 2
    place = lax.axis_index("tp")
    y, c = place // 2, place % 2
    core, shift = tp_perms(count)
    blocks = partial.reshape((ys, 2, partial.shape[0] // count) + partial.shape[1:])
    sent = lax.dynamic_index_in_dim(blocks, 1 - c, 1, False)
    kept = lax.dynamic_index_in_dim(blocks, c, 1, False)
    pair = kept.astype(f32) + lax.ppermute(sent, "tp", core).astype(f32)
    low = pair.astype(bf16)
    own = lax.dynamic_index_in_dim(pair, y, 0, False)
    for d in range(1, ys):
        away = lax.dynamic_index_in_dim(low, (y + d) % ys, 0, False)
        own = own + lax.ppermute(away, "tp", shift[d]).astype(f32)
    return own


def tp_sum(vector):
    count = lax.axis_size("tp")
    core, shift = tp_perms(count)
    vector = vector + lax.ppermute(vector, "tp", core)
    return vector + sum(lax.ppermute(vector, "tp", shift[d]) for d in range(1, count // 2))


def carried(arrays, resets, step):
    count = lax.axis_size("seq")
    place = lax.axis_index("seq")

    def from_near(a, d):
        perm = [(i, i + d * step) for i in range(count) if 0 <= i + d * step < count]
        return lax.ppermute(a.astype(bf16), "seq", perm).astype(f32)

    def reset_within(d):
        at = jnp.arange(count)
        away = (place - at) * step
        return jnp.sum(jnp.where((away >= 1) & (away <= d), resets, 0)) > 0

    arrays = [from_near(a, 1) for a in arrays]
    d = 1
    while d < count - 1:
        keep = 1.0 - reset_within(d).astype(f32)
        arrays = [a + keep * from_near(a, d) for a in arrays]
        d *= 2
    return arrays


def features(vector):
    squares = (vector[..., :, None] * vector[..., None, :]).reshape(
        vector.shape[:-1] + (vector.shape[-1] * vector.shape[-1],)
    )
    return jnp.concatenate(
        [jnp.ones_like(vector[..., :1]), vector * linear_coef, squares * square_coef], axis=-1
    )


def feature_grad(vector, grad_feat):
    feat_width = vector.shape[-1]
    linear_part = grad_feat[..., 1 : 1 + feat_width]
    square_part = grad_feat[..., 1 + feat_width :].reshape(vector.shape + (feat_width,))
    mixed_part = jnp.sum(square_part * vector[..., None, :], axis=-1) + jnp.sum(
        square_part * vector[..., :, None], axis=-2
    )
    return linear_coef * linear_part + square_coef * mixed_part


def segment_masks(anchor, starts, length):
    positions = anchor + jnp.arange(length, dtype=jnp.int32)
    start_le = starts[None, :] <= positions[:, None]
    row_ids = jnp.sum(start_le.astype(jnp.int32), axis=1)
    inside = (starts >= anchor) & (starts < anchor + length)
    carry = jnp.sum(((starts[None, :] >= anchor) & start_le).astype(jnp.int32), axis=1) == 0
    after_last = (
        jnp.sum(
            ((starts[None, :] > positions[:, None]) & inside[None, :]).astype(jnp.int32), axis=1
        )
        == 0
    )
    return (positions, row_ids, carry, after_last)


def rms_scale(values):
    return lax.rsqrt(jnp.mean(values * values, axis=-1, keepdims=True) + epsilon)


def norm_back(grad_out, normed, scale, gain):
    grad_normed = grad_out * gain
    return scale * (grad_normed - normed * jnp.mean(grad_normed * normed, axis=-1, keepdims=True))


def pair_block(query_part, key_heads, row_ids, positions, first_row, span_rows):
    scores = (
        jnp.einsum("thf,shf->hts", query_part, key_heads, preferred_element_type=f32) * 0.25
    )
    rows_here = row_ids[first_row : first_row + span_rows]
    place_here = positions[first_row : first_row + span_rows]
    allowed = (
        (rows_here[:, None] == row_ids[None, :]) & (positions[None, :] <= place_here[:, None])
    ).astype(f32)
    kernel = (1.0 + scores + 0.5 * scores * scores) * allowed[None]
    return (scores, allowed, kernel)


def dot(a, b):
    return jnp.dot(a, b, preferred_element_type=f32)


def dot_t(a, b):
    return lax.dot_general(a, b, (((1,), (1,)), ((), ())), preferred_element_type=f32)


def dot_tt(a, b):
    return lax.dot_general(a, b, (((0,), (0,)), ((), ())), preferred_element_type=f32)


def ring_place(seq):
    z, x = seq // 2, seq % 2
    return z + x * (7 - 2 * z)


def ring_seq(place):
    place = lax.rem(place + 8, 8)
    far = place // 4
    return (1 - far) * 2 * place + far * (15 - 2 * place)


class Sems:
    def __init__(self, ref):
        self.ref, self.used = ref, 0

    def take(self):
        self.used += 1
        assert self.used <= self.ref.shape[0]
        return self.ref.at[self.used - 1]


class Links:
    def __init__(self, send, recv):
        self.send, self.recv, self.sent = Sems(send), Sems(recv), []

    def copy(self, src, dst, **to):
        return pltpu.make_async_remote_copy(
            src_ref=src,
            dst_ref=dst,
            send_sem=self.send.take(),
            recv_sem=self.recv.take(),
            device_id=to,
            device_id_type=pl.DeviceIdType.MESH,
        )

    def start(self, src, dst, **to):
        made = self.copy(src, dst, **to)
        made.start()
        self.sent.append(made)
        return made

    def sent_now(self, some):
        for made in some:
            made.wait_send()
        self.sent = [made for made in self.sent if all(made is not other for other in some)]

    def finish(self):
        for made in self.sent:
            made.wait_send()


class Gather:
    def __init__(self, links, arrays, nearby, gangs):
        self.links, self.arrays, self.nearby = links, arrays, nearby
        self.at = {k: j for j, k in enumerate(relative_list(8))}
        self.flying, self.gangs, self.done = {}, gangs, 0
        self.gang_of = {a: i for i, gang in enumerate(gangs) for a in gang}
        self.events = [
            (a, step, way, part)
            for gang in gangs
            for step in (1, 2, 3, 4)
            for a in gang
            for part in (0, 1)
            for way in (0, 1)
            if step < 4 or way == part
        ]
        for a in gangs[0]:
            for part in (0, 1):
                for way in (0, 1):
                    self.go(a, 1, way, part)

    def rows(self, a, part):
        first, size = self.arrays[a][2:]
        return pl.ds(first + part * size, size)

    def go(self, a, step, way, part):
        own, everyone = self.arrays[a][:2]
        before, after = (step - 1, step) if way == 0 else ((9 - step) % 8, 8 - step)
        src = own if step == 1 else everyone.at[self.at[before]]
        self.flying[a, step, way, part] = self.links.start(
            src.at[self.rows(a, part)],
            everyone.at[self.at[after], self.rows(a, part)],
            seq=self.nearby[way],
        )

    def pump(self, upto):
        while self.done < min(upto, len(self.events)):
            a, step, way, part = self.events[self.done]
            self.flying[a, step, way, part].wait_recv()
            if step < 3 or (step == 3 and way == part):
                self.go(a, step + 1, way, part)
            i = self.gang_of[a]
            if step == 3 and i + 1 < len(self.gangs):
                mine, later = self.gangs[i].index(a), self.gangs[i + 1]
                last = mine == len(self.gangs[i]) - 1
                for other in later[mine:] if last else later[mine : mine + 1]:
                    self.go(other, 1, way, part)
            self.done += 1

    def pump_array(self, a):
        gang = self.gang_of[a]
        self.pump(14 * sum(len(g) for g in self.gangs[: gang + 1]))


def greet(peers):
    barrier = pltpu.get_barrier_semaphore()
    for peer in peers:
        pl.semaphore_signal(
            barrier, inc=1, device_id=peer, device_id_type=pl.DeviceIdType.MESH
        )
    pl.semaphore_wait(barrier, len(peers))


def places():
    seq, tp = lax.axis_index("seq"), lax.axis_index("tp")
    place = ring_place(seq)
    nearby = (ring_seq(place + 1), ring_seq(place - 1))
    over_y = lax.rem(tp + 2, 4)
    over_core = tp + 1 - 2 * (tp % 2)
    peers = [{"seq": ring_seq(place + k)} for k in range(1, 8)]
    peers += [{"tp": over_y}, {"tp": over_core}]
    return seq, tp, place, nearby, over_y, over_core, peers


class Rows:
    def __init__(self, links, own, everyone, tp, over_y, over_core, rows):
        self.links, self.all, self.tp = links, everyone, tp
        self.over_y, self.over_core, self.rows = over_y, over_core, rows
        half = rows // 2
        self.first = [
            links.start(
                own.at[pl.ds(i * half, half)], self.block(tp, i * half, half), tp=over_y
            )
            for i in (0, 1)
        ]
        self.near = links.start(own, self.block(tp, 0, rows), tp=over_core)
        self.last = []

    def block(self, owner, offset, size):
        return self.all.at[pl.ds(pl.multiple_of(owner * self.rows + offset, 16), size)]

    def forward(self, i):
        half = self.rows // 2
        self.first[i].wait_recv()
        came = self.block(self.over_y, i * half, half)
        self.last.append(self.links.start(came, came, tp=self.over_core))

    def finish(self):
        self.near.wait_recv()
        for made in self.last:
            made.wait_recv()


FEATS = 160


def fill_tables(lengths, seq, tok, line, coefs, step):
    total = tok.shape[0]
    anchor = seq * total
    starts, at = [], 0
    for i in range(lengths.shape[0]):
        starts.append(at)
        at = at + lengths[i]

    def places_of(shape, axis):
        pos = lax.broadcasted_iota(jnp.int32, shape, axis)
        low = jnp.zeros(shape, jnp.int32) - anchor
        last = jnp.ones(shape, f32)
        for start in starts:
            here = start - anchor
            low = jnp.maximum(low, jnp.where(pos >= here, here, -anchor))
            last = jnp.where((pos < here) & (here < total), 0.0, last)
        return pos.astype(f32), low, last

    lane = lax.broadcasted_iota(jnp.int32, (total, 128), 1)
    pos, low, last = places_of((total, 128), 0)
    began = jnp.where(low < 0, 1.0, 0.0)
    first = jnp.maximum(low, 0).astype(f32)
    tok[...] = jnp.where(
        lane == 0, first, jnp.where(lane == 1, began, jnp.where(lane == 2, last, pos))
    )
    pos, low, last = places_of((8, total), 1)
    row = lax.broadcasted_iota(jnp.int32, (8, total), 0)
    line[...] = jnp.where(row == 0, pos, jnp.maximum(low, 0).astype(f32))

    def clear(lo, hi):
        free = jnp.ones((1, 128), f32)
        for start in starts:
            at = jnp.zeros((1, 128), jnp.int32) + start
            free = jnp.where((at >= lo * total) & (at < (hi + 1) * total), 0.0, free)
        return free

    z = seq // 2
    one = jnp.ones((1, 128), f32)
    first, second = clear(2 * z, 2 * z), clear(2 * z + 1, 2 * z + 1)
    before = 2 * (z - step)
    rows = [second, first] if step > 0 else [first, second]
    rows += [first * second, clear(before, before + 1)]
    coefs[...] = jnp.concatenate(rows + [one * 0.0] * 4, axis=0)


class Exchange:
    def __init__(self, links, st, near, term, first, second, given, states, coefs, seq, step):
        z, x = seq // 2, seq % 2
        self.st, self.near, self.term, self.first, self.second = st, near, term, first, second
        self.given, self.states, self.coefs, self.x = given, states, coefs, x
        self.turn = z if step > 0 else 3 - z
        self.late = x if step > 0 else 1 - x
        over_x = seq + 1 - 2 * x
        self.half = links.start(st.at[pl.ds(2 * (1 - x), 2)], near, seq=over_x)
        self.hop = links.copy(term, first, seq=seq + 2 * step)
        self.on = links.copy(term, second, seq=seq + 2 * step)
        self.far = links.copy(term, second, seq=seq + 4 * step)
        self.links, self.over_x = links, over_x

    def coef(self, k):
        return self.coefs[k : k + 1, :]

    def pair(self):
        self.half.wait_recv()
        for i in (0, 1):
            mine, theirs = self.st[2 * self.x + i].astype(f32), self.near[i].astype(f32)
            early = jnp.where(self.late == 0, mine, theirs)
            later = jnp.where(self.late == 0, theirs, mine)
            self.term[i] = (later + self.coef(0) * early).astype(bf16)

        @pl.when(self.turn % 2 == 0)
        def _():
            self.hop.start()

    def planes(self):
        @pl.when(self.turn % 2 == 1)
        def _():
            self.hop.wait_recv()

        @pl.when(self.turn == 1)
        def _():
            for i in (0, 1):
                came = self.coef(2) * self.first[i].astype(f32)
                self.term[i] = (self.term[i].astype(f32) + came).astype(bf16)
            self.on.start()
            self.far.start()

    def give(self):
        x = self.x
        for i in (0, 1):
            self.states[2 * x + i] = jnp.zeros((256, 128), f32)
            self.states[2 * (1 - x) + i] = jnp.zeros((256, 128), f32)

        def enter(i):
            return self.states.at[2 * x + i, pl.ds(0, 176)]

        @pl.when(self.turn == 1)
        def _():
            for i in (0, 1):
                enter(i)[...] = self.first[i].astype(f32)

        @pl.when(self.turn == 2)
        def _():
            self.on.wait_recv()
            for i in (0, 1):
                enter(i)[...] = self.second[i].astype(f32)

        @pl.when(self.turn == 3)
        def _():
            self.far.wait_recv()
            for i in (0, 1):
                older = self.coef(3) * self.second[i].astype(f32)
                enter(i)[...] = self.first[i].astype(f32) + older

        for i in (0, 1):
            came = enter(i)[...]
            mine, theirs = self.st[2 * x + i].astype(f32), self.near[i].astype(f32)
            early = jnp.where(self.late == 0, mine, theirs)
            passed = early + self.coef(1) * came
            self.given[0, i] = jnp.where(self.late == 0, passed, came).astype(bf16)
            enter(i)[...] = jnp.where(self.late == 0, came, passed)
        self.back = self.links.start(self.given.at[0], self.given.at[1], seq=self.over_x)

    def take(self):
        self.back.wait_recv()
        for i in (0, 1):
            self.states[2 * (1 - self.x) + i, 0:176, :] = self.given[1, i].astype(f32)

    def finish(self):
        @pl.when(self.turn % 2 == 0)
        def _():
            self.hop.wait_send()

        @pl.when(self.turn == 1)
        def _():
            self.on.wait_send()
            self.far.wait_send()


def ring_columns(place):
    return [pl.ds(pl.multiple_of(ring_seq(place - k) * 256, 256), 256) for k in relative_list(8)]


def phi(heads, h, select_a, select_b, lanes):
    a = dot(heads, select_a[h]) + lanes[0:1, :]
    b = dot(heads, select_b[h]) + lanes[1:2, :]
    return a, b


def fwd_kernel(
    lengths, sa_ref, sb_ref, lanes_ref, hm_ref, gain_first, gain_second,
    x_in, wq_in, wk_in, wv_in, wo_in, wg_in, wu_in, wd_in, c_in,
    wq_all, wo_all, wg_all, wu_all, wd_all, c_all,
    h1_out, qkv_out, yb_out, den_out, x1_out, h2_out, gate_out, up_out, m_out, sin_out, gain_out, terms_out,
    x_ref, tok_ref, line_ref, coef_ref, gain_ref, q_own, o_own, g_own, u_own, d_own,
    w_small, w_v, w_o, w_d, w_g, c_v,
    xg, h1, wq, wo, wg, wu, qkv, kq, num, den, yb, sc, rc, sy, ry, x1, gate, up, mm,
    gains_all, gains, st, st_x, st_t, st_z, st_y, st_g, s_in,
    send, recv, local,
):
    seq, tp, place, nearby, over_y, over_core, peers = places()
    z, x = seq // 2, seq % 2
    at = {k: j for j, k in enumerate(relative_list(8))}
    rows = x_ref.shape[0]
    total = 4 * rows
    links = Links(send, recv)
    locs = Sems(local)
    pending = []

    def store(src, dst):
        made = pltpu.make_async_copy(src, dst, locs.take())
        made.start()
        pending.append(made)

    def load(src, dst):
        made = pltpu.make_async_copy(src, dst, locs.take())
        made.start()
        return made

    got_qk = [load(wq_in, w_small.at[0:64]), load(wk_in, w_small.at[64:128]), load(wv_in, w_v)]
    columns = ring_columns(place)
    got_x = [load(x_in.at[:, c], x_ref.at[:, col(j)]) for j, c in enumerate(columns)]
    c_rows = pl.ds(pl.multiple_of(tp * rows, rows), rows)
    got_c = [load(c_in.at[:, c], c_v.at[:, col(j)]) for j, c in enumerate(columns)]
    got_o = load(wo_in, w_o)
    ff = wd_in.shape[0]
    got_g = load(wg_in, w_g.at[pl.ds(0, ff)])
    got_d = load(wd_in, w_d.at[pl.ds(0, ff)])

    def turn(src, dst):
        for i in range(0, ff, 128):
            size = min(128, ff - i)
            dst[:, i : i + size] = src[i : i + 128, :].T[:, :size].astype(bf16)

    gain_ref[...] = jnp.concatenate(
        [gain_first[...], gain_second[...], jnp.zeros((14, 256), f32)], axis=0
    ).astype(bf16)
    greet(peers)
    gain_flying = [
        links.start(gain_ref, gains_all.at[at[k]], seq=ring_seq(place + k)) for k in range(1, 8)
    ]
    for made in got_x:
        made.wait()
    xrows = Rows(links, x_ref, xg, tp, over_y, over_core, rows)
    for made in got_qk:
        made.wait()
    q_own[:, 0:128] = w_small[...].T.astype(bf16)
    q_own[:, 128:640] = w_v[...].astype(bf16)
    ring = Gather(
        links,
        [
            (q_own, wq_all, 0, 128),
            (o_own, wo_all, 0, 128),
            (g_own, wg_all, 0, 64),
            (g_own, wg_all, 128, 64),
            (u_own, wu_all, 0, 64),
            (u_own, wu_all, 128, 64),
            (d_own, wd_all, 0, 128),
        ],
        nearby,
        [[0], [1], [2], [3, 4, 5], [6]],
    )
    own_in = [
        load(x_ref, xrows.block(tp, 0, rows)),
        load(gain_ref, gains_all.at[at[0]]),
    ]
    got_o.wait()
    o_own[...] = w_o[...].T.astype(bf16)
    ring.pump(2)
    got_g.wait()
    turn(w_g, g_own)
    got_u = load(wu_in, w_g.at[pl.ds(0, ff)])
    ring.pump(4)
    got_d.wait()
    turn(w_d, d_own)
    got_u.wait()
    turn(w_g, u_own)
    pairs = [(q_own, wq_all), (o_own, wo_all), (g_own, wg_all), (u_own, wu_all), (d_own, wd_all)]
    own_kept = [load(own, everyone.at[at[0]]) for own, everyone in pairs]
    fill_tables(lengths, seq, tok_ref, line_ref, coef_ref, 1)

    ring.pump(6)
    xrows.forward(0)
    for made in gain_flying:
        made.wait_recv()
    for made in own_in:
        made.wait()
    for j in range(8):
        chunk = gains_all[j].astype(f32)
        gains[0:8, j * 256 : (j + 1) * 256] = chunk[0:8]
    ring.pump(10)
    xrows.forward(1)
    ring.pump_array(0)
    own_kept[0].wait()
    got = load_weights(load, wq_all, wq)
    xrows.finish()

    def norm_first(i, _):
        r = pl.ds(pl.multiple_of(i * 32, 32), 32)
        v = xg[r, :].astype(f32)
        s = lax.rsqrt(jnp.mean(v * v, axis=1, keepdims=True) + epsilon)
        h1[r, :] = (v * s * gains[0:1, :]).astype(bf16)
        return 0

    lax.fori_loop(0, total // 32, norm_first, 0)
    links.sent_now(xrows.last)
    kept_h1 = load(h1, h1_out)
    for made in got_c:
        made.wait()
    crows = Rows(links, c_v, c_all, tp, over_y, over_core, rows)
    kept_c = load(c_v, c_all.at[c_rows])
    ring.pump(15)
    for made in got:
        made.wait()

    def project(i, _):
        r = pl.ds(pl.multiple_of(i * 256, 256), 256)
        res = dot(h1[r, :], wq[...])
        qkv[r, :] = res.astype(bf16)
        kq[r, :] = pltpu.roll(res[:, :128], 64, 1).astype(bf16)
        return 0

    lax.fori_loop(0, total // 256, project, 0)
    store(qkv, qkv_out)
    ring.pump(16)

    heads = 4

    def head_v(h):
        return slice(128 + h * 128, 256 + h * 128)

    for h in range(heads):

        def state(i, c, h=h):
            s, zz = c
            r = pl.ds(pl.multiple_of(i * 256, 256), 256)
            a, b = phi(kq[r, :], h, sa_ref, sb_ref, lanes_ref)
            f = a * b * lanes_ref[2:3, :] * tok_ref[r, 2:3]
            s = s + dot_tt(f.astype(bf16), qkv[r, head_v(h)])
            return s, zz + jnp.sum(f, axis=0, keepdims=True)

        s, zz = lax.fori_loop(
            0, total // 256, state, (jnp.zeros((256, 128), f32), jnp.zeros((1, 256), f32))
        )
        pack_state(st, h, s, zz)
        ring.pump(17 + h)
    moved = Exchange(links, st, st_x, st_t, st_z, st_y, st_g, s_in, coef_ref, seq, 1)

    def local_head(h):
        for i in range(total // 256):
            r = slice(i * 256, (i + 1) * 256)
            span = (i + 1) * 256
            qm = (qkv[r, :128].astype(f32) * hm_ref[h : h + 1, :]).astype(bf16)
            u = dot_t(qm, kq[:span, :])
            keep = (line_ref[0:1, :span] >= tok_ref[r, 0:1]) & (
                line_ref[0:1, :span] <= tok_ref[r, 3:4]
            )
            kap = jnp.where(keep, (0.5 * u + 1.0) * u + 1.0, 0.0)
            den[r, h : h + 1] = jnp.sum(kap, axis=1, keepdims=True)
            num[r, h * 128 : (h + 1) * 128] = dot(kap.astype(bf16), qkv[:span, head_v(h)])

    local_head(0)
    ring.pump(22)
    moved.pair()
    local_head(1)
    ring.pump(24)
    moved.planes()
    local_head(2)
    ring.pump(26)
    moved.give()
    local_head(3)
    ring.pump(28)
    moved.take()
    store(s_in, sin_out)
    for h in range(heads):
        z_row = jnp.concatenate([s_in[h, 160:161, :], s_in[h, 161:162, :]], axis=1)
        feat = jax.lax.broadcasted_iota(jnp.int32, (256, 128), 0)
        s_low = jnp.where(feat < FEATS, s_in[h], 0.0).astype(bf16)

        def carry(i, _, h=h, z_row=z_row, s_low=s_low):
            r = pl.ds(pl.multiple_of(i * 256, 256), 256)
            a, b = phi(qkv[r, 0:128], h, sa_ref, sb_ref, lanes_ref)
            f = a * b * lanes_ref[2:3, :] * tok_ref[r, 1:2]
            hv = slice(h * 128, (h + 1) * 128)
            top = num[r, hv] + dot(f.astype(bf16), s_low)
            low = den[r, h : h + 1] + jnp.sum(f * z_row, axis=1, keepdims=True)
            den[r, h : h + 1] = low
            y = top / low
            yb[r, hv] = y.astype(bf16)
            return 0

        lax.fori_loop(0, total // 256, carry, 0)
        ring.pump(31 + 2 * h)
    store(yb, yb_out)
    store(den, den_out)
    ring.pump_array(1)
    own_kept[1].wait()
    got = load_weights(load, wo_all, wo)
    for made in got:
        made.wait()

    y_at, c_at = tp // 2, tp % 2

    def out_rows(block):
        return yb[pl.ds(pl.multiple_of(block * rows, rows), rows), :]

    cols = 512
    to_core = []
    for yy in (0, 1):

        def core_cols(i, _, yy=yy):
            c = pl.ds(pl.multiple_of(i * cols, cols), cols)
            sc[yy, :, c] = dot_t(out_rows(yy * 2 + 1 - c_at), wo[c, :]).astype(bf16)
            return 0

        lax.fori_loop(0, 2048 // cols, core_cols, 0)
        to_core.append(links.start(sc.at[yy], rc.at[yy], tp=over_core))
    for made in to_core:
        made.wait_recv()
    ring.pump(40)

    def away_cols(i, _):
        c = pl.ds(pl.multiple_of(i * cols, cols), cols)
        part = dot_t(out_rows((1 - y_at) * 2 + c_at), wo[c, :])
        sy[:, c] = (part + rc[1 - y_at, :, c].astype(f32)).astype(bf16)
        return 0

    lax.fori_loop(0, 2048 // cols, away_cols, 0)
    to_y = links.start(sy, ry, tp=over_y)

    def own_cols(i, _):
        c = pl.ds(pl.multiple_of(i * cols, cols), cols)
        x1[:, c] = (
            dot_t(out_rows(tp), wo[c, :]) + rc[y_at, :, c].astype(f32) + x_ref[:, c].astype(f32)
        )
        return 0

    lax.fori_loop(0, 2048 // cols, own_cols, 0)
    ring.pump(44)
    to_y.wait_recv()
    ring.pump(54)

    links.sent_now(xrows.first + [xrows.near])
    ho = x_ref

    def norm_second(i, _):
        r = pl.ds(pl.multiple_of(i * 32, 32), 32)
        v = x1[r, :] + ry[r, :].astype(f32)
        x1[r, :] = v
        s = lax.rsqrt(jnp.mean(v * v, axis=1, keepdims=True) + epsilon)
        ho[r, :] = (v * s * gains[1:2, :]).astype(bf16)
        return 0

    lax.fori_loop(0, rows // 32, norm_second, 0)
    store(x1, x1_out)
    store(gains, gain_out)
    h2 = xg
    hrows = Rows(links, ho, h2, tp, over_y, over_core, rows)
    own_in = load(ho, hrows.block(tp, 0, rows))
    ring.pump(56)
    hrows.forward(0)
    ring.pump(63)
    hrows.forward(1)
    crows.forward(0)
    crows.forward(1)
    hrows.finish()
    crows.finish()
    own_in.wait()
    store(h2, h2_out)
    kept_h1.wait()
    kept_c.wait()
    got_c = load(c_all, h1)
    ring.pump_array(3)
    own_kept[2].wait()
    got = load_weights(load, wg_all, wg)
    own_kept[3].wait()
    got += load_weights(load, wu_all, wu)
    for made in got:
        made.wait()

    def gate_up(i, _):
        r = pl.ds(pl.multiple_of(i * 128, 128), 128)
        g = dot(h2[r, :], wg[...])
        uu = dot(h2[r, :], wu[...])
        gate[r, :] = g.astype(bf16)
        up[r, :] = uu.astype(bf16)
        mm[r, :] = (g * jax.nn.sigmoid(g) * uu).astype(bf16)
        return 0

    for quarter in range(4):
        lax.fori_loop(quarter * total // 512, (quarter + 1) * total // 512, gate_up, 0)
        ring.pump(86 + 2 * quarter)
    store(gate, gate_out)
    store(up, up_out)
    store(mm, m_out)
    got_c.wait()
    links.sent_now([ring.flying[a, 1, way, part] for a in (2, 3, 4, 5) for way in (0, 1) for part in (0, 1)])
    out_sems = [locs.take(), locs.take()]
    buffers = [g_own, u_own]

    def keep_terms(j, k):
        return pltpu.make_async_copy(buffers[k], terms_out.at[col(j)], out_sems[k])

    def grad_down(i, _):
        for k in (0, 1):
            pl.when(i > 0)(lambda k=k: keep_terms(2 * i - 2 + k, k).wait())
            buffers[k][...] = dot_tt(h1[:, col(2 * i + k)], mm[...]).astype(bf16)
            keep_terms(2 * i + k, k).start()
        return 0

    lax.fori_loop(0, 2, grad_down, 0)
    ring.pump(94)
    lax.fori_loop(2, 4, grad_down, 0)
    for k in (0, 1):
        keep_terms(6 + k, k).wait()
    ring.pump_array(6)
    own_kept[4].wait()
    for made in pending:
        made.wait()
    links.finish()
    moved.finish()


def pack_state(st, h, s, zz):
    st[h, 0:FEATS, :] = s[:FEATS].astype(bf16)
    tail = jnp.concatenate([zz[:, :128], zz[:, 128:], jnp.zeros((14, 128), f32)], axis=0)
    st[h, FEATS : FEATS + 16, :] = tail.astype(bf16)


def load_weights(load, everyone, flat):
    count, chunk = everyone.shape[0], everyone.shape[1]
    return [load(everyone.at[j], flat.at[pl.ds(j * chunk, chunk)]) for j in range(count)]


class Scatter:
    def __init__(self, slots, send, recv, nearby):
        self.slots, self.send, self.recv, self.nearby = slots, send, recv, nearby

    def copy(self, a, step, way, sub, src, slot, width):
        return pltpu.make_async_remote_copy(
            src_ref=src,
            dst_ref=self.piece(slot, way, sub, width),
            send_sem=self.send.at[a % 2, way, sub],
            recv_sem=self.recv.at[a % 2, way, sub, step],
            device_id={"seq": self.nearby[way]},
            device_id_type=pl.DeviceIdType.MESH,
        )

    def slot(self, a, step):
        return (a % 2) * 4 + (a // 2 * 7 + step) % 4

    def rows(self, way, sub, base=0):
        start = base + way * 128 + sub * 64
        return pl.ds(start if isinstance(start, int) else pl.multiple_of(start, 64), 64)

    def piece(self, slot, way, sub, width):
        return self.slots.at[slot, self.rows(way, sub), pl.ds(0, width)]

    def begin(self, a, own, width, column=0):
        for sub in (0, 1):
            for way in (0, 1):
                src = own.at[self.rows(way, sub, way * 256), pl.ds(column, width)]
                self.copy(a, 0, way, sub, src, self.slot(a, 0), width).start()

    def event(self, a, e, own, width, out, column=0):
        step, sub = e // 2, e % 2
        is_last = step // 6
        here = self.slot(a, step)
        far = (step + 1) // 4
        place0 = (1 - far) * 2 * (step + 1) + far * (11 - 2 * step) + is_last * 8
        far = (step + 2) // 4 - is_last
        place1 = (1 - far) * (3 + 2 * step) + far * (10 - 2 * step) + is_last * 9
        places = (place0, place1)
        for way in (0, 1):
            piece = self.piece(here, way, sub, width)
            came = self.copy(a, step, way, sub, piece, here, width)
            came.wait_recv()
            came.wait_send()

        def summed(way):
            mine = own[self.rows(way, sub, places[way] * 256), pl.ds(column, width)]
            came = self.slots[here, self.rows(way, sub), pl.ds(0, width)]
            return came.astype(f32) + mine.astype(f32)

        def on():
            for way in (0, 1):
                self.slots[here, self.rows(way, sub), pl.ds(0, width)] = summed(way).astype(bf16)
                piece = self.piece(here, way, sub, width)
                self.copy(a, step + 1, way, sub, piece, self.slot(a, step + 1), width).start()

        def end():
            for way in (0, 1):
                out[self.rows(way, sub), pl.ds(0, width)] = summed(way)

        if isinstance(e, int):
            if step < 6:
                on()
            else:
                end()
        else:
            pl.when(step < 6)(on)
            pl.when(step == 6)(end)


class TpSum:
    def __init__(self, part, from_core, from_y, sems, credits, tp, over_y, over_core):
        self.part, self.from_core, self.from_y = part, from_core, from_y
        self.sems, self.credits = sems, credits
        self.tp, self.over_y, self.over_core = tp, over_y, over_core
        self.y, self.c = tp // 2, tp % 2

    def to_core(self, i, yy):
        return pltpu.make_async_remote_copy(
            src_ref=self.part.at[i, yy * 2 + 1 - self.c],
            dst_ref=self.from_core.at[i, yy],
            send_sem=self.sems.at[yy, i],
            recv_sem=self.sems.at[2 + yy, i],
            device_id={"tp": self.over_core},
            device_id_type=pl.DeviceIdType.MESH,
        )

    def to_y(self, i):
        return pltpu.make_async_remote_copy(
            src_ref=self.part.at[i, (1 - self.y) * 2 + self.c],
            dst_ref=self.from_y.at[i],
            send_sem=self.sems.at[4, i],
            recv_sem=self.sems.at[5, i],
            device_id={"tp": self.over_y},
            device_id_type=pl.DeviceIdType.MESH,
        )

    def sent(self, i):
        self.to_core(i, 0).wait_send()
        self.to_core(i, 1).wait_send()
        self.to_y(i).wait_send()

    def offer(self, i, turn, value):
        if turn > 0:
            self.sent(i)
        for block in range(4):
            self.part[i, block] = value[block * 256 : (block + 1) * 256].astype(bf16)
        if turn > 0:
            pl.semaphore_wait(self.credits.at[0], 1)
        for yy in (0, 1):
            self.to_core(i, yy).start()

    def pass_on(self, i, turn):
        for yy in (0, 1):
            self.to_core(i, yy).wait_recv()
        away = (1 - self.y) * 2 + self.c
        self.part[i, away] = (
            self.part[i, away].astype(f32) + self.from_core[i, 1 - self.y].astype(f32)
        ).astype(bf16)
        if turn > 0:
            pl.semaphore_wait(self.credits.at[1], 1)
        self.to_y(i).start()

    def take(self, i, turn, use):
        self.to_y(i).wait_recv()
        use(
            self.part[i, self.tp].astype(f32)
            + self.from_core[i, self.y].astype(f32)
            + self.from_y[i].astype(f32)
        )
        if turn < 2:
            for k, peer in ((0, self.over_core), (1, self.over_y)):
                pl.semaphore_signal(
                    self.credits.at[k],
                    inc=1,
                    device_id={"tp": peer},
                    device_id_type=pl.DeviceIdType.MESH,
                )


def col(i, width=256):
    return pl.ds(i * width if isinstance(i, int) else pl.multiple_of(i * width, width), width)


def bwd_kernel(
    lengths, sa_ref, sb_ref, lanes_ref, hm_ref, gains, s_in, den, gain_first, gain_second,
    x_in, x1_in, wq_all, wo_all, wg_all, wu_all, wd_all, c_all, h1_all, qkv_all, yb_all, h2_all,
    gate_all, up_all, m_all, terms_all,
    d_out, g_out, u_out, oq_out, block_out, input_out, gain_out, u_kept,
    tok_ref, line_ref, coef_ref, terms, terms_core, terms_y,
    slots, s1, s2, wo, stream, hs, rows_all, mm, dup, tiles, qkv, kq, yb, dnum, dden, dden_t, dqkv,
    dq, dk, part, from_core, from_y, acc, x1, fout, st, st_x, st_t, st_z, st_y, st_g, s_back, own_rows,
    ring_send, ring_recv, tp_sems, credits, send, recv, local, tile_sems,
):
    seq, tp, place, nearby, over_y, over_core, peers = places()
    z, x = seq // 2, seq % 2
    rows, width = own_rows.shape
    total = 4 * rows
    ff = mm.shape[1]
    links = Links(send, recv)
    locs = Sems(local)

    def load(src, dst):
        made = pltpu.make_async_copy(src, dst, locs.take())
        made.start()
        return made

    def whole(everyone, flat):
        count, chunk = everyone.shape[0], everyone.shape[1]
        return [load(everyone.at[j], flat.at[pl.ds(j * chunk, chunk)]) for j in range(count)]

    got_m = load(m_all, mm)
    got_wd = whole(wd_all, s2)
    got_terms = load(terms_all, s1)
    got_c = load(c_all, rows_all)
    greet(peers)
    ring = Scatter(slots, ring_send, ring_recv, nearby)
    ring.begin(0, terms_all, ff)
    got_x1 = load(x1_in, x1)
    fill_tables(lengths, seq, tok_ref, line_ref, coef_ref, -1)
    columns = ring_columns(place)
    got_qkv = [load(qkv_all, qkv), load(yb_all, yb)]
    got_wo = whole(wo_all, wo)
    sums = TpSum(part, from_core, from_y, tp_sems, credits, tp, over_y, over_core)

    def run(n, body, pumps=None):
        def step(i, _):
            body(i)
            if pumps:
                a, first, count = pumps
                every = n // count
                pl.when((i + 1) % every == 0)(lambda: event(a, first + (i + 1) // every - 1))
            return 0

        lax.fori_loop(0, n, step, 0)

    plan = {0: (s1, ff, 0), 1: (s2, ff, 0), 2: (s1, ff, 0), 3: (s2, 1152, 0)}

    def event(a, e):
        own, wide, column = plan[a]
        ring.event(a, e, own, wide, fout, column)

    def begin(a):
        own, wide, column = plan[a]
        ring.begin(a, own, wide, column)

    def events(a, first, last):
        lax.fori_loop(first, last, lambda e, _: (event(a, e), 0)[1], 0)

    def both(a, first, b, second, count):
        def pair(i, _):
            event(a, first + i)
            event(b, second + i)
            return 0

        lax.fori_loop(0, count, pair, 0)

    def chunks_of(source, size, body, pumps=None, count=8):
        def copies(i, slot):
            return [
                pltpu.make_async_copy(a, b, tile_sems.at[k, slot])
                for k, (a, b) in enumerate(source(i, slot))
            ]

        for made in copies(0, 0):
            made.start()

        def step(i):
            slot = i % 2

            @pl.when(i + 1 < count)
            def _():
                for made in copies(i + 1, 1 - slot):
                    made.start()

            for made in copies(i, slot):
                made.wait()
            body(i, slot)

        run(count, step, pumps)

    got_m.wait()
    for made in got_wd:
        made.wait()
    got_terms.wait()

    def mlp(i):
        sums.offer(i, 0, dot_t(mm[...], s2[col(i), :]))
        pl.when(i > 0)(lambda: sums.pass_on(i - 1, 0))

    run(8, mlp, (0, 0, 2))
    sums.pass_on(7, 0)

    def gate_up_tiles(i, slot):
        r = col(i, 128)
        return [
            (gate_all.at[r], tiles.at[slot, pl.ds(0, 128)]),
            (up_all.at[r], tiles.at[slot, pl.ds(128, 128)]),
        ]

    def grad_gate_up(i, slot):
        r = col(i, 128)
        dm = dot(rows_all[r, :], s2[...]).astype(bf16).astype(f32)
        g = tiles[slot, 0:128].astype(f32)
        u = tiles[slot, 128:256].astype(f32)
        s = jax.nn.sigmoid(g)
        mm[r, :] = (dm * u * s * (1.0 + g * (1.0 - s))).astype(bf16)
        dup[r, :] = (dm * (g * s)).astype(bf16)

        pl.when(i >= 3)(lambda: take_block(i - 3))

    def take_block(i):
        def use(value):
            own_rows[:, col(i)] = (x1[:, col(i)] + value).astype(bf16)

        sums.take(i, 0, use)

    got_x1.wait()
    got_c.wait()
    chunks_of(gate_up_tiles, 8, grad_gate_up, (0, 2, 4))

    def w_tiles(i, slot):
        return [(wg_all.at[i], stream.at[slot, 0]), (wu_all.at[i], stream.at[slot, 1])]

    def grad_hidden(i, slot):
        pl.when(i < 3)(lambda: take_block(5 + i))
        value = dot_t(mm[...], stream[slot, 0]) + dot_t(dup[...], stream[slot, 1])
        sums.offer(i, 1, value)
        pl.when(i > 0)(lambda: sums.pass_on(i - 1, 1))

    chunks_of(w_tiles, 8, grad_hidden, (0, 6, 4))
    kept = [load(own_rows.at[:, col(j)], block_out.at[:, c]) for j, c in enumerate(columns)]
    pending = []
    sums.pass_on(7, 1)

    def h_tiles(everyone):
        return lambda i, slot: [(everyone.at[:, col(i)], hs.at[slot])]

    def keep_up(i, slot):
        return pltpu.make_async_copy(tiles.at[slot], u_kept.at[col(i)], tile_sems.at[1, slot])

    def grads(i, slot):
        s2[col(i), :] = dot_tt(hs[slot], mm[...]).astype(bf16)
        pl.when(i >= 2)(lambda: keep_up(i - 2, slot).wait())
        tiles[slot] = dot_tt(hs[slot], dup[...]).astype(bf16)
        keep_up(i, slot).start()
        pl.when(i == 1)(lambda: begin(1))

    chunks_of(h_tiles(h2_all), 8, grads, (0, 10, 2))
    keep_up(6, 0).wait()
    keep_up(7, 1).wait()

    def take_second(i):
        def use(value):
            acc[:, col(i)] = value

        sums.take(i, 1, use)

    run(2, take_second)
    both(1, 0, 0, 12, 2)
    done = load(fout.at[:, pl.ds(0, ff)], d_out)
    got_up = load(u_kept, s1)
    lax.fori_loop(2, 5, lambda i, _: (take_second(i), 0)[1], 0)
    events(1, 2, 3)
    got_up.wait()
    begin(2)
    lax.fori_loop(5, 8, lambda i, _: (take_second(i), 0)[1], 0)
    both(1, 3, 2, 0, 1)

    for made in kept:
        made.wait()

    def norm_back_second(i, _):
        r = pl.ds(pl.multiple_of(i * 32, 32), 32)
        v = x1[r, :]
        s = lax.rsqrt(jnp.mean(v * v, axis=1, keepdims=True) + epsilon)
        n = v * s
        dn = acc[r, :] * gains[1:2, :]
        own = pl.ds(pl.multiple_of(tp * rows + i * 32, 32), 32)
        back = rows_all[own, :].astype(f32) + s * (
            dn - n * jnp.mean(dn * n, axis=1, keepdims=True)
        )
        acc[r, :] = back
        own_rows[r, :] = back.astype(bf16)
        return 0

    lax.fori_loop(0, rows // 32, norm_back_second, 0)
    da = Rows(links, own_rows, rows_all, tp, over_y, over_core, rows)
    own_in = load(own_rows, da.block(tp, 0, rows))

    both(1, 4, 2, 1, 1)
    da.forward(0)
    both(1, 5, 2, 2, 1)
    da.forward(1)
    for made in got_qkv + got_wo:
        made.wait()
    da.finish()
    own_in.wait()
    links.sent_now(da.first + [da.near])
    got_x = [load(x_in.at[:, c], own_rows.at[:, col(j)]) for j, c in enumerate(columns)]

    def head_v(h):
        return slice(128 + h * 128, 256 + h * 128)

    def grad_attended(i):
        r = col(i, 256)
        dy = dot(rows_all[r, :], wo[...])
        kq[r, :] = pltpu.roll(qkv[r, 0:128].astype(f32), 64, 1).astype(bf16)
        columns = []
        for h in range(4):
            hv = slice(h * 128, (h + 1) * 128)
            under = 1.0 / den[r, h : h + 1]
            part_h = dy[:, hv]
            dnum[r, hv] = (part_h * under).astype(bf16)
            low = jnp.sum(part_h * yb[r, hv].astype(f32), axis=1, keepdims=True)
            columns.append(-low * under)
        lane = lax.broadcasted_iota(jnp.int32, (256, 128), 1)
        packed = jnp.zeros((256, 128), f32)
        for h in range(4):
            packed = jnp.where(lane == h, columns[h], packed)
        dden[r, :] = packed
        dden_t[i] = packed.T[0:8, :]

    run(4, grad_attended)
    both(1, 6, 2, 3, 1)

    for h in range(4):

        def state(i, c, h=h):
            s, zz = c
            r = col(i, 256)
            a, b = phi(qkv[r, 0:128], h, sa_ref, sb_ref, lanes_ref)
            f = a * b * lanes_ref[2:3, :] * tok_ref[r, 1:2]
            s = s + dot_tt(f.astype(bf16), dnum[r, h * 128 : (h + 1) * 128])
            return s, zz + jnp.sum(f * dden[r, h : h + 1], axis=0, keepdims=True)

        s, zz = lax.fori_loop(
            0, 4, state, (jnp.zeros((256, 128), f32), jnp.zeros((1, 256), f32))
        )
        pack_state(st, h, s, zz)
    moved = Exchange(links, st, st_x, st_t, st_z, st_y, st_g, s_back, coef_ref, seq, -1)
    both(1, 7, 2, 4, 1)

    dq[...] = jnp.zeros(dq.shape, f32)

    def local_head(h):
        hm = hm_ref[h : h + 1, :]
        hv = slice(h * 128, (h + 1) * 128)
        for j in range(total // 256):
            k_rows = slice(j * 256, (j + 1) * 256)
            dv_s = jnp.zeros((256, 128), f32)
            dk_s = jnp.zeros((256, 128), f32)
            for i in range(j, total // 256):
                q_rows = slice(i * 256, (i + 1) * 256)
                qm = (qkv[q_rows, 0:128].astype(f32) * hm).astype(bf16)
                u = dot_t(kq[k_rows, :], qm)
                keep = tok_ref[k_rows, 3:4] >= line_ref[1:2, q_rows]
                if i == j:
                    keep = keep & (tok_ref[k_rows, 3:4] <= line_ref[0:1, q_rows])
                kap = jnp.where(keep, (0.5 * u + 1.0) * u + 1.0, 0.0).astype(bf16)
                dn = dnum[q_rows, hv]
                grad = dot_t(qkv[k_rows, head_v(h)], dn) + dden_t[i, h : h + 1, :]
                du = jnp.where(keep, grad * (1.0 + u), 0.0).astype(bf16)
                dv_s = dv_s + dot(kap, dn)
                dk_s = dk_s + dot(du, qm)
                dq[q_rows, :] += dot_tt(du, kq[k_rows, :]) * hm
            dqkv[k_rows, head_v(h)] = dv_s.astype(bf16)
            if h == 0:
                dk[k_rows, :] = dk_s
            else:
                dk[k_rows, :] += dk_s

    local_head(0)
    moved.pair()
    both(1, 8, 2, 5, 1)
    local_head(1)
    moved.planes()
    both(1, 9, 2, 6, 1)
    local_head(2)
    moved.give()
    both(1, 10, 2, 7, 1)
    local_head(3)
    both(1, 11, 2, 8, 1)
    moved.take()

    def split_state(ref, h):
        z_row = jnp.concatenate([ref[h, 160:161, :], ref[h, 161:162, :]], axis=1)
        feat = lax.broadcasted_iota(jnp.int32, (256, 128), 0)
        return jnp.where(feat < FEATS, ref[h], 0.0).astype(bf16), z_row

    for h in range(4):
        s_q, z_q = split_state(s_in, h)
        s_k, z_k = split_state(s_back, h)
        hv = slice(h * 128, (h + 1) * 128)

        def through(grad, a, b, h=h):
            grad = grad * lanes_ref[2:3, :]
            return dot_t((grad * b).astype(bf16), sa_ref[h]) + dot_t(
                (grad * a).astype(bf16), sb_ref[h]
            )

        def carried_part(i, _, h=h, s_q=s_q, z_q=z_q, s_k=s_k, z_k=z_k, hv=hv, through=through):
            r = col(i, 256)
            a, b = phi(qkv[r, 0:128], h, sa_ref, sb_ref, lanes_ref)
            grad = dot_t(dnum[r, hv], s_q) + dden[r, h : h + 1] * z_q
            dq[r, :] += through(grad * tok_ref[r, 1:2], a, b)
            a, b = phi(kq[r, :], h, sa_ref, sb_ref, lanes_ref)
            last = tok_ref[r, 2:3]
            grad = dot_t(qkv[r, head_v(h)], s_k) + z_k
            dk[r, :] += through(grad * last, a, b)
            f = (a * b * lanes_ref[2:3, :] * last).astype(bf16)
            dqkv[r, head_v(h)] = (dqkv[r, head_v(h)].astype(f32) + dot(f, s_k)).astype(bf16)
            return 0

        lax.fori_loop(0, 4, carried_part, 0)

    def join(i):
        r = col(i, 256)
        dqkv[r, 0:128] = (dq[r, :] + pltpu.roll(dk[r, :], 64, 1)).astype(bf16)

    run(4, join)
    done.wait()
    both(1, 12, 2, 9, 2)
    done = load(fout.at[:, pl.ds(0, ff)], g_out)
    own_w = load(wg_all.at[7], stream.at[0, 0])

    def grad_out_qkv(i, slot):
        s2[col(i), 0:512] = dot_tt(rows_all[:, col(i)], yb[...]).astype(bf16)
        s2[col(i), 512:1152] = dot_tt(hs[slot], dqkv[...]).astype(bf16)
        pl.when(i == 1)(lambda: begin(3))

    chunks_of(h_tiles(h1_all), 8, grad_out_qkv, (2, 11, 1))

    own_w.wait()
    gain_two = jnp.sum(fout[:, 0:ff] * stream[0, 0].astype(f32), axis=1, keepdims=True)

    def wq_tiles(i, slot):
        return [(wq_all.at[i], stream.at[slot, 0, :, pl.ds(0, 640)])]

    def grad_hidden_first(i, slot):
        sums.offer(i, 2, dot_t(dqkv[...], stream[slot, 0, :, 0:640]))
        pl.when(i > 0)(lambda: sums.pass_on(i - 1, 2))

    chunks_of(wq_tiles, 8, grad_hidden_first, (3, 0, 1))
    sums.pass_on(7, 2)
    done.wait()
    both(2, 12, 3, 1, 2)
    done = load(fout.at[:, pl.ds(0, ff)], u_out)

    def take_first(i):
        def use(value):
            x1[:, col(i)] = value

        sums.take(i, 2, use)

    run(8, take_first, (3, 3, 4))
    for made in got_x:
        made.wait()

    def norm_back_first(i, _):
        r = pl.ds(pl.multiple_of(i * 32, 32), 32)
        v = own_rows[r, :].astype(f32)
        s = lax.rsqrt(jnp.mean(v * v, axis=1, keepdims=True) + epsilon)
        n = v * s
        dn = x1[r, :] * gains[0:1, :]
        acc[r, :] += s * (dn - n * jnp.mean(dn * n, axis=1, keepdims=True))
        return 0

    lax.fori_loop(0, rows // 32, norm_back_first, 0)
    pending += [load(acc.at[:, col(j)], input_out.at[:, c]) for j, c in enumerate(columns)]
    own_w = load(wu_all.at[7], stream.at[0, 0])
    own_q = load(wq_all.at[7], stream.at[1, 0, :, pl.ds(0, 640)])
    own_w.wait()
    own_q.wait()
    gain_two += jnp.sum(fout[:, 0:ff] * stream[0, 0].astype(f32), axis=1, keepdims=True)
    events(3, 7, 12)
    done.wait()
    events(3, 12, 14)
    pending.append(load(fout.at[:, pl.ds(0, 1152)], oq_out))
    gain_one = jnp.sum(fout[:, 512:1152] * stream[1, 0, :, 0:640].astype(f32), axis=1, keepdims=True)
    lane = lax.broadcasted_iota(jnp.int32, (256, 128), 1)
    both = jnp.where(lane == 0, gain_one, jnp.where(lane == 1, gain_two, 0.0)).T[0:8, :]
    terms[0] = both
    over = links.start(terms.at[0], terms_core, tp=over_core)
    over.wait_recv()
    both = both + terms_core[...]
    terms[1] = both
    over = links.start(terms.at[1], terms_y, tp=over_y)
    over.wait_recv()
    own_gains = jnp.concatenate(
        [gain_first[...], gain_second[...], jnp.ones((6, 256), f32)], axis=0
    ).astype(bf16)
    terms[2] = (both + terms_y[...]) / own_gains.astype(f32)
    pending.append(load(terms.at[2], gain_out))
    run(8, lambda i: sums.sent(i))
    for made in pending:
        made.wait()
    links.finish()
    moved.finish()


def feature_tables(heads):
    first = np.zeros((heads, 128, 256), np.float32)
    second = np.zeros((heads, 128, 256), np.float32)
    lanes = np.zeros((8, 256), np.float32)
    f = 0
    for i in range(FEAT):
        for j in range(i, FEAT):
            for h in range(heads):
                first[h, h * FEAT + i, f] = 1
                second[h, h * FEAT + j, f] = 1
            lanes[2, f] = square_coef if i == j else square_coef * 2**0.5
            f += 1
    for i in range(FEAT):
        for h in range(heads):
            first[h, h * FEAT + i, f] = 1
        lanes[1, f] = 1
        lanes[2, f] = linear_coef
        f += 1
    lanes[0, f] = lanes[1, f] = lanes[2, f] = 1
    mask = np.zeros((8, 128), np.float32)
    for h in range(heads):
        mask[h, h * FEAT : (h + 1) * FEAT] = 0.25
    return first, second, lanes, mask


def forward_pass(lengths, constants, gain_first, gain_second, x_in, weights, c_in):
    rows, width = x_in.shape
    total = 4 * rows
    ff = weights[4].shape[0]
    hbm = pl.BlockSpec(memory_space=pl.ANY)
    vmem = pl.BlockSpec(memory_space=pltpu.VMEM)

    def shape(*dims, dtype=bf16):
        return jax.ShapeDtypeStruct(dims, dtype)

    outs = (
        shape(8, 256, 640),
        shape(8, 256, 512),
        shape(8, 256, ff),
        shape(8, 256, ff),
        shape(8, 256, ff),
        shape(total, width),
        shape(total, width),
        shape(total, 640),
        shape(total, 512),
        shape(total, 128, dtype=f32),
        shape(rows, width, dtype=f32),
        shape(total, width),
        shape(total, ff),
        shape(total, ff),
        shape(total, ff),
        shape(4, 256, 128, dtype=f32),
        shape(8, width, dtype=f32),
        shape(width, ff),
    )
    scratch = [
        pltpu.VMEM((rows, width), bf16),
        pltpu.VMEM((total, 128), f32),
        pltpu.VMEM((8, total), f32),
        pltpu.VMEM((8, 128), f32),
        pltpu.VMEM((16, 256), bf16),
        pltpu.VMEM((256, 640), bf16),
        pltpu.VMEM((256, 512), bf16),
        pltpu.VMEM((256, ff), bf16),
        pltpu.VMEM((256, ff), bf16),
        pltpu.VMEM((256, ff), bf16),
        pltpu.VMEM((128, 256), f32),
        pltpu.VMEM((256, 512), f32),
        pltpu.VMEM((512, 256), f32),
        pltpu.VMEM((-(-ff // 128) * 128, 256), f32),
        pltpu.VMEM((-(-ff // 128) * 128, 256), f32),
        pltpu.VMEM((rows, width), bf16),
        pltpu.VMEM((total, width), bf16),
        pltpu.VMEM((total, width), bf16),
        pltpu.VMEM((width, 640), bf16),
        pltpu.VMEM((width, 512), bf16),
        pltpu.VMEM((width, ff), bf16),
        pltpu.VMEM((width, ff), bf16),
        pltpu.VMEM((total, 640), bf16),
        pltpu.VMEM((total, 128), bf16),
        pltpu.VMEM((total, 512), f32),
        pltpu.VMEM((total, 128), f32),
        pltpu.VMEM((total, 512), bf16),
        pltpu.VMEM((2, rows, width), bf16),
        pltpu.VMEM((2, rows, width), bf16),
        pltpu.VMEM((rows, width), bf16),
        pltpu.VMEM((rows, width), bf16),
        pltpu.VMEM((rows, width), f32),
        pltpu.VMEM((total, ff), bf16),
        pltpu.VMEM((total, ff), bf16),
        pltpu.VMEM((total, ff), bf16),
        pltpu.VMEM((8, 16, 256), bf16),
        pltpu.VMEM((8, width), f32),
        pltpu.VMEM((4, 176, 128), bf16),
        pltpu.VMEM((2, 176, 128), bf16),
        pltpu.VMEM((2, 176, 128), bf16),
        pltpu.VMEM((2, 176, 128), bf16),
        pltpu.VMEM((2, 176, 128), bf16),
        pltpu.VMEM((2, 2, 176, 128), bf16),
        pltpu.VMEM((4, 256, 128), f32),
        pltpu.SemaphoreType.DMA((144,)),
        pltpu.SemaphoreType.DMA((144,)),
        pltpu.SemaphoreType.DMA((144,)),
    ]
    return pl.pallas_call(
        fwd_kernel,
        out_shape=outs,
        in_specs=[pl.BlockSpec(memory_space=pltpu.SMEM)] + [vmem] * 6 + [hbm] * 9,
        out_specs=(hbm,) * len(outs),
        scratch_shapes=scratch,
        compiler_params=pltpu.CompilerParams(
            collective_id=0, has_side_effects=True, vmem_limit_bytes=60 * 2**20
        ),
    )(lengths, *constants, gain_first, gain_second, x_in, *weights, c_in)


def backward_pass(lengths, constants, gains, s_in, den, gain_pair, x_in, x1, weights, c_all, acts):
    rows, width = x_in.shape
    total = 4 * rows
    ff = weights[2].shape[2]
    hbm = pl.BlockSpec(memory_space=pl.ANY)
    vmem = pl.BlockSpec(memory_space=pltpu.VMEM)

    def shape(*dims, dtype=f32):
        return jax.ShapeDtypeStruct(dims, dtype)

    outs = (
        shape(256, ff),
        shape(256, ff),
        shape(256, ff),
        shape(256, 1152),
        shape(rows, width, dtype=bf16),
        shape(rows, width),
        shape(8, 256),
        shape(width, ff, dtype=bf16),
    )
    scratch = [
        pltpu.VMEM((total, 128), f32),
        pltpu.VMEM((8, total), f32),
        pltpu.VMEM((8, 128), f32),
        pltpu.VMEM((3, 8, 256), f32),
        pltpu.VMEM((8, 256), f32),
        pltpu.VMEM((8, 256), f32),
        pltpu.VMEM((8, 256, ff), bf16),
        pltpu.VMEM((width, ff), bf16),
        pltpu.VMEM((width, ff), bf16),
        pltpu.VMEM((width, 512), bf16),
        pltpu.VMEM((2, 2, 256, ff), bf16),
        pltpu.VMEM((2, total, 256), bf16),
        pltpu.VMEM((total, width), bf16),
        pltpu.VMEM((total, ff), bf16),
        pltpu.VMEM((total, ff), bf16),
        pltpu.VMEM((2, 256, ff), bf16),
        pltpu.VMEM((total, 640), bf16),
        pltpu.VMEM((total, 128), bf16),
        pltpu.VMEM((total, 512), bf16),
        pltpu.VMEM((total, 512), bf16),
        pltpu.VMEM((total, 128), f32),
        pltpu.VMEM((4, 8, 256), f32),
        pltpu.VMEM((total, 640), bf16),
        pltpu.VMEM((total, 128), f32),
        pltpu.VMEM((total, 128), f32),
        pltpu.VMEM((8, 4, 256, 256), bf16),
        pltpu.VMEM((8, 2, 256, 256), bf16),
        pltpu.VMEM((8, 256, 256), bf16),
        pltpu.VMEM((rows, width), f32),
        pltpu.VMEM((rows, width), f32),
        pltpu.VMEM((256, ff), f32),
        pltpu.VMEM((4, 176, 128), bf16),
        pltpu.VMEM((2, 176, 128), bf16),
        pltpu.VMEM((2, 176, 128), bf16),
        pltpu.VMEM((2, 176, 128), bf16),
        pltpu.VMEM((2, 176, 128), bf16),
        pltpu.VMEM((2, 2, 176, 128), bf16),
        pltpu.VMEM((4, 256, 128), f32),
        pltpu.VMEM((rows, width), bf16),
        pltpu.SemaphoreType.DMA((2, 2, 2)),
        pltpu.SemaphoreType.DMA((2, 2, 2, 7)),
        pltpu.SemaphoreType.DMA((6, 8)),
        pltpu.SemaphoreType.REGULAR((2,)),
        pltpu.SemaphoreType.DMA((16,)),
        pltpu.SemaphoreType.DMA((16,)),
        pltpu.SemaphoreType.DMA((80,)),
        pltpu.SemaphoreType.DMA((2, 2)),
    ]
    return pl.pallas_call(
        bwd_kernel,
        out_shape=outs,
        in_specs=[pl.BlockSpec(memory_space=pltpu.SMEM)] + [vmem] * 9 + [hbm] * 16,
        out_specs=(hbm,) * len(outs),
        scratch_shapes=scratch,
        compiler_params=pltpu.CompilerParams(
            collective_id=1, has_side_effects=True, vmem_limit_bytes=62 * 2**20
        ),
    )(lengths, *constants, gains, s_in, den, *gain_pair, x_in, x1, *weights, c_all, *acts)


def finish_kernel(
    d_in, g_in, u_in, oq_in, block_in, input_in,
    d_out, g_out, u_out, o_out, q_out, k_out, v_out, block_out, input_out,
    wide, turned, oq, oq_t, block, grad, sems,
):
    keeper = Sems(sems)
    ff = d_in.shape[1]

    def copy(src, dst):
        made = pltpu.make_async_copy(src, dst, keeper.take())
        made.start()
        return made

    came = [copy(ref, wide.at[i]) for i, ref in enumerate((g_in, u_in, d_in))]
    came_oq = copy(oq_in, oq)
    came_block, came_grad = copy(block_in, block), copy(input_in, grad)
    came_oq.wait()
    oq_t[...] = oq[:, 0:640].T
    kept = [
        copy(oq.at[:, pl.ds(640, 512)], v_out),
        copy(oq_t.at[pl.ds(0, 512)], o_out),
        copy(oq_t.at[pl.ds(512, 64)], q_out),
        copy(oq_t.at[pl.ds(576, 64)], k_out),
    ]
    for i, out in enumerate((g_out, u_out, d_out)):
        came[i].wait()
        for at in range(0, ff, 128):
            at = min(at, ff - 128)
            turned[i, at : at + 128, :] = wide[i, :, at : at + 128].T
        kept.append(copy(turned.at[i], out))
    came_block.wait()
    kept.append(copy(block, block_out))
    came_grad.wait()
    kept.append(copy(grad, input_out))
    for made in kept:
        made.wait()


def finish(d, g, u, oq, block, grad_input):
    rows, width = block.shape
    ff = d.shape[1]
    hbm = pl.BlockSpec(memory_space=pl.ANY)

    def shape(*dims, dtype=f32):
        return jax.ShapeDtypeStruct(dims, dtype)

    outs = (
        shape(ff, 256), shape(ff, 256), shape(ff, 256), shape(512, 256), shape(64, 256),
        shape(64, 256), shape(256, 512), shape(rows, width, dtype=bf16), shape(rows, width),
    )
    return pl.pallas_call(
        finish_kernel,
        out_shape=outs,
        in_specs=[hbm] * 6,
        out_specs=(hbm,) * len(outs),
        scratch_shapes=[
            pltpu.VMEM((3, 256, ff), f32),
            pltpu.VMEM((3, ff, 256), f32),
            pltpu.VMEM((256, 1152), f32),
            pltpu.VMEM((640, 256), f32),
            pltpu.VMEM((rows, width), bf16),
            pltpu.VMEM((rows, width), f32),
            pltpu.SemaphoreType.DMA((24,)),
        ],
        compiler_params=pltpu.CompilerParams(vmem_limit_bytes=60 * 2**20),
    )(d, g, u, oq, block, grad_input)


def on_device_rings(
    inputs, lengths, gain_attn, w_query, w_key, w_value, w_out, gain_mlp, w_gate, w_up, w_down,
    cotangent,
):
    first, second, lanes, mask = feature_tables(4)
    constants = (
        jnp.asarray(first, bf16), jnp.asarray(second, bf16), jnp.asarray(lanes), jnp.asarray(mask),
    )
    gain_pair = (gain_attn.reshape(1, -1), gain_mlp.reshape(1, -1))
    made = forward_pass(
        lengths, constants, *gain_pair, inputs,
        (w_query.T, w_key.T, w_value, w_out, w_gate.T, w_up.T, w_down), cotangent,
    )
    weights = made[:5]
    c_all, h1, qkv, yb, den, x1, h2, gate, up, mixed, s_in, gain_all, terms = made[5:]
    sum_down_t, sum_gate, sum_up, sum_oq, block, grad_input, gain_sums, _ = backward_pass(
        lengths, constants, gain_all, s_in, den, gain_pair, inputs, x1, weights, c_all,
        (h1, qkv, yb, h2, gate, up, mixed, terms),
    )
    d, g_t, u_t, o, q_t, k_t, v, block, grad_input = finish(
        sum_down_t, sum_gate, sum_up, sum_oq, block, grad_input
    )
    return (
        block,
        grad_input,
        gain_sums[0],
        q_t.T,
        k_t.T,
        v,
        o,
        gain_sums[1],
        g_t.T,
        u_t.T,
        d,
    )


def on_device(
    inputs,
    lengths,
    gain_attn,
    w_query,
    w_key,
    w_value,
    w_out,
    gain_mlp,
    w_gate,
    w_up,
    w_down,
    cotangent,
):
    seq_count = lax.axis_size("seq")
    tp_count = lax.axis_size("tp")
    seq_index = lax.axis_index("seq")
    rows_own, width = inputs.shape
    chunk = width // seq_count
    half = chunk // 2
    block_len = rows_own * tp_count
    anchor = seq_index * block_len
    relative = relative_list(seq_count)
    ring = ring_order(seq_count)
    place_of = [ring.index(s) for s in range(seq_count)]
    to_rel = jnp.array(
        [[ring[(place_of[s] - k) % seq_count] for k in relative] for s in range(seq_count)],
        jnp.int32,
    )[seq_index]
    to_abs = jnp.array(
        [
            [relative.index((place_of[s] - place_of[o]) % seq_count) for o in range(seq_count)]
            for s in range(seq_count)
        ],
        jnp.int32,
    )[seq_index]
    to_rel = [to_rel[j] for j in range(seq_count)]
    to_abs = [to_abs[j] for j in range(seq_count)]

    qk_cols, v_cols, ff_cols = w_query.shape[1], w_value.shape[1], w_gate.shape[1]
    gains = jnp.stack([gain_attn, gain_mlp]).astype(bf16)
    qkv_cols = 2 * qk_cols + v_cols
    qkv_own = jnp.concatenate([w_query, w_key, w_value], axis=1).astype(bf16)
    gain_rows = jnp.zeros((16, qkv_cols), bf16).at[:2, :chunk].set(gains)
    first_own = jnp.concatenate([qkv_own, gain_rows], axis=0)
    out_own = w_out.astype(bf16).T
    gate_up_own = jnp.concatenate([w_gate, w_up], axis=1).astype(bf16)
    down_own = w_down.astype(bf16).T

    first_got = ring_gather(first_own, half)
    out_got = ring_gather(out_own, half)
    gate_up_got = ring_gather(gate_up_own, half)
    down_got = ring_gather(down_own, half)
    w_qkv = jnp.concatenate([first_got[k][:chunk] for k in relative], axis=0)
    gain_first = jnp.concatenate([first_got[k][chunk, :chunk] for k in relative]).astype(f32)
    gain_second = jnp.concatenate([first_got[k][chunk + 1, :chunk] for k in relative]).astype(f32)
    w_out_t = jnp.concatenate([out_got[k] for k in relative], axis=0)
    w_gate_up = jnp.concatenate([gate_up_got[k] for k in relative], axis=0)
    w_down_t = jnp.concatenate([down_got[k] for k in relative], axis=0)

    at = jnp.arange(lengths.shape[0])
    starts = jnp.sum(jnp.where(at[None, :] < at[:, None], lengths[None, :], 0), axis=1)
    positions, row_ids, carry_in, after_last = segment_masks(anchor, starts, block_len)
    carry_mask = carry_in.astype(f32)
    last_mask = after_last.astype(f32)
    resets = (
        jnp.sum(
            ((starts // block_len)[None, :] == jnp.arange(seq_count)[:, None]).astype(jnp.int32),
            axis=1,
        )
        > 0
    ).astype(jnp.int32)

    inputs_own = to_relative(inputs, to_rel, chunk)
    grad_own = to_relative(cotangent, to_rel, chunk)
    inputs_full = tp_gather(inputs_own).astype(f32)
    grad_full = tp_gather(grad_own)
    inputs_own = inputs_own.astype(f32)
    hidden_first = (inputs_full * rms_scale(inputs_full) * gain_first).astype(bf16)
    qkv = dot(hidden_first, w_qkv).astype(bf16)
    queries = qkv[:, :qk_cols]
    key_flat = qkv[:, qk_cols : 2 * qk_cols]
    value_flat = qkv[:, 2 * qk_cols :]
    heads_local = qk_cols // FEAT
    query_heads = queries.reshape(block_len, heads_local, FEAT)
    key_heads = key_flat.reshape(block_len, heads_local, FEAT)
    value_heads = value_flat.reshape(block_len, heads_local, VHEAD)
    query_float = query_heads.astype(f32)
    key_float = key_heads.astype(f32)
    value_float = value_heads.astype(f32)
    key_feat = features(key_float) * last_mask[:, None, None]
    local_state = jnp.einsum("thn,thv->hnv", key_feat, value_float, precision=highest)
    local_sum = jnp.sum(key_feat, axis=0)
    carry_state, carry_sum = carried([local_state, local_sum], resets, 1)
    step_rows = 512
    query_feat = features(query_float)
    carry_weight = carry_mask[:, None]
    numer_parts = []
    denom_parts = []
    for first_row in range(0, block_len, step_rows):
        query_part = query_heads[first_row : first_row + step_rows]
        scores, allowed, kernel = pair_block(
            query_part, key_heads, row_ids, positions, first_row, step_rows
        )
        numer_parts.append(
            jnp.einsum("hts,shv->thv", kernel.astype(bf16), value_heads, preferred_element_type=f32)
        )
        denom_parts.append(jnp.sum(kernel, axis=-1).T)
    numerator = (
        jnp.concatenate(numer_parts, axis=0)
        + jnp.einsum("thn,hnv->thv", query_feat, carry_state, precision=highest)
        * carry_weight[:, :, None]
    )
    denominator = (
        jnp.concatenate(denom_parts, axis=0)
        + jnp.einsum("thn,hn->th", query_feat, carry_sum, precision=highest) * carry_weight
    )
    attended = numerator / denominator[:, :, None]
    attended_low = attended.reshape(block_len, heads_local * VHEAD).astype(bf16)
    attn_partial = dot_t(attended_low, w_out_t).astype(bf16)
    middle_own = inputs_own + tp_scatter(attn_partial)
    scale_second = rms_scale(middle_own)
    normed_second = middle_own * scale_second
    hidden_second = tp_gather((normed_second * gain_second).astype(bf16))
    gate_up = dot(hidden_second, w_gate_up)
    gate_value, upward = gate_up[:, :ff_cols], gate_up[:, ff_cols:]
    sigmoid_gate = jax.nn.sigmoid(gate_value)
    silu_gate = gate_value * sigmoid_gate
    mixed_rows = (silu_gate * upward).astype(bf16)
    grad_down_t = dot_tt(grad_full, mixed_rows).astype(bf16)

    def by_distance(stack):
        return {k: stack[j * chunk : (j + 1) * chunk] for j, k in enumerate(relative)}

    sum_down_t = ring_scatter(by_distance(grad_down_t))
    mlp_own = tp_scatter(dot_t(mixed_rows, w_down_t).astype(bf16))
    block_output = to_relative((middle_own + mlp_own).astype(bf16), to_abs, chunk)

    grad_mixed = dot(grad_full, w_down_t).astype(bf16).astype(f32)
    grad_gate = (
        grad_mixed * upward * sigmoid_gate * (1.0 + gate_value * (1.0 - sigmoid_gate))
    ).astype(bf16)
    grad_upward = (grad_mixed * silu_gate).astype(bf16)
    grad_gate_up = jnp.concatenate([grad_gate, grad_upward], axis=1)
    hidden_partial = dot_t(grad_gate_up, w_gate_up).astype(bf16)
    sum_gate_up = ring_scatter(by_distance(dot_tt(hidden_second, grad_gate_up).astype(bf16)))
    grad_hidden = tp_scatter(hidden_partial)
    grad_middle = grad_own.astype(f32) + norm_back(
        grad_hidden, normed_second, scale_second, gain_second
    )
    grad_branch = tp_gather(grad_middle.astype(bf16))
    sum_out_t = ring_scatter(by_distance(dot_tt(grad_branch, attended_low).astype(bf16)))
    grad_attended = dot(grad_branch, w_out_t).reshape(block_len, heads_local, VHEAD)
    grad_numer = (grad_attended / denominator[:, :, None]).astype(bf16)
    grad_denom = -jnp.sum(grad_attended * attended, axis=-1) / denominator
    grad_numer_carried = grad_numer.astype(f32) * carry_weight[:, :, None]
    grad_denom_carried = grad_denom * carry_weight
    grad_state_in = jnp.einsum("thn,thv->hnv", query_feat, grad_numer_carried, precision=highest)
    grad_sum_in = jnp.einsum("thn,th->hn", query_feat, grad_denom_carried, precision=highest)
    grad_query_feat = (
        jnp.einsum("thv,hnv->thn", grad_numer_carried, carry_state, precision=highest)
        + grad_denom_carried[:, :, None] * carry_sum[None]
    )
    grad_state_out, grad_sum_out = carried([grad_state_in, grad_sum_in], resets, -1)
    grad_key_feat = (
        jnp.einsum("thv,hnv->thn", value_float, grad_state_out, precision=highest)
        + grad_sum_out[None]
    ) * last_mask[:, None, None]
    grad_value_state = jnp.einsum("thn,hnv->thv", key_feat, grad_state_out, precision=highest)
    grad_query_parts = []
    grad_key_inner = jnp.zeros((block_len, heads_local, FEAT), f32)
    grad_value_inner = jnp.zeros((block_len, heads_local, VHEAD), f32)
    for first_row in range(0, block_len, step_rows):
        query_part = query_heads[first_row : first_row + step_rows]
        scores, allowed, kernel = pair_block(
            query_part, key_heads, row_ids, positions, first_row, step_rows
        )
        numer_grad_part = grad_numer[first_row : first_row + step_rows]
        grad_weights = jnp.einsum(
            "thv,shv->hts", numer_grad_part, value_heads, preferred_element_type=f32
        )
        grad_scores = (
            (grad_weights + grad_denom[first_row : first_row + step_rows].T[:, :, None])
            * allowed[None]
            * (1.0 + scores)
        ).astype(bf16)
        grad_query_parts.append(
            jnp.einsum("hts,shf->thf", grad_scores, key_heads, preferred_element_type=f32) * 0.25
        )
        grad_key_inner = (
            grad_key_inner
            + jnp.einsum("hts,thf->shf", grad_scores, query_part, preferred_element_type=f32) * 0.25
        )
        grad_value_inner = grad_value_inner + jnp.einsum(
            "hts,thv->shv", kernel.astype(bf16), numer_grad_part, preferred_element_type=f32
        )
    grad_query = (
        jnp.concatenate(grad_query_parts, axis=0) + feature_grad(query_float, grad_query_feat)
    ).astype(bf16)
    grad_key = (grad_key_inner + feature_grad(key_float, grad_key_feat)).astype(bf16)
    grad_value = (grad_value_inner + grad_value_state).astype(bf16)
    grad_qkv = jnp.concatenate(
        [
            grad_query.reshape(block_len, heads_local * FEAT),
            grad_key.reshape(block_len, heads_local * FEAT),
            grad_value.reshape(block_len, heads_local * VHEAD),
        ],
        axis=1,
    )
    sum_qkv = ring_scatter(by_distance(dot_tt(hidden_first, grad_qkv).astype(bf16)))
    grad_hidden_first = tp_scatter(dot_t(grad_qkv, w_qkv).astype(bf16))
    scale_first = rms_scale(inputs_own)
    normed_first = inputs_own * scale_first
    grad_input = to_relative(
        grad_middle + norm_back(grad_hidden_first, normed_first, scale_first, gain_first),
        to_abs,
        chunk,
    )

    gain_terms = jnp.stack(
        [
            jnp.sum(qkv_own.astype(f32) * sum_qkv, axis=1),
            jnp.sum(gate_up_own.astype(f32) * sum_gate_up, axis=1),
        ]
    )
    gain_sums = tp_sum(gain_terms) / gains.astype(f32)
    return (
        block_output,
        grad_input,
        gain_sums[0],
        sum_qkv[:, :qk_cols],
        sum_qkv[:, qk_cols : 2 * qk_cols],
        sum_qkv[:, 2 * qk_cols :],
        sum_out_t.T,
        gain_sums[1],
        sum_gate_up[:, :ff_cols],
        sum_gate_up[:, ff_cols:],
        sum_down_t.T,
    )


def solution(mesh):
    in_specs = (
        P(("seq", "tp"), None),
        P(),
        P("seq"),
        P("seq", "tp"),
        P("seq", "tp"),
        P("seq", "tp"),
        P("tp", "seq"),
        P("seq"),
        P("seq", "tp"),
        P("seq", "tp"),
        P("tp", "seq"),
        P(("seq", "tp"), None),
    )
    out_specs = (
        P(("seq", "tp"), None),
        P(("seq", "tp"), None),
        P("seq"),
        P("seq", "tp"),
        P("seq", "tp"),
        P("seq", "tp"),
        P("tp", "seq"),
        P("seq"),
        P("seq", "tp"),
        P("seq", "tp"),
        P("tp", "seq"),
    )
    small = mesh.shape["seq"] == 8 and mesh.shape["tp"] == 4
    body = on_device_rings if small else on_device
    return jax.shard_map(
        body, mesh=mesh, in_specs=in_specs, out_specs=out_specs, check_vma=False
    )
```

```python
import jax
import jax.numpy as jnp
import numpy as np
from jax import lax
from jax.experimental import pallas as pl
from jax.experimental.pallas import tpu as pltpu
from jax.sharding import PartitionSpec as P

FEAT = 16
VHEAD = 128


epsilon = 1e-05
linear_coef = 0.5
square_coef = 0.17677669529663687
highest = lax.Precision.HIGHEST
f32 = jnp.float32
bf16 = jnp.bfloat16


def ring_order(count):
    planes = 4 if count % 4 == 0 else 2
    columns = count // planes
    order = [z * columns for z in range(planes)]
    for z in reversed(range(planes)):
        xs = list(range(1, columns))
        if (planes - 1 - z) % 2:
            xs.reverse()
        order += [z * columns + x for x in xs]
    return order


def relative_list(count):
    half = count // 2
    out = []
    for j in range(1, half):
        out += [j, count - j]
    return out + [half, 0]


def ring_perms(count):
    ring = ring_order(count)
    fwd = [(ring[i], ring[(i + 1) % count]) for i in range(count)]
    return fwd, [(b, a) for a, b in fwd]


def ring_gather(own, half_rows):
    count = lax.axis_size("seq")
    fwd, bwd = ring_perms(count)
    half = count // 2
    got = {0: own}
    ahead = back = own
    for step in range(1, half):
        ahead = lax.ppermute(ahead, "seq", fwd)
        back = lax.ppermute(back, "seq", bwd)
        got[step] = ahead
        got[count - step] = back
    ahead = lax.ppermute(ahead[:half_rows], "seq", fwd)
    back = lax.ppermute(back[half_rows:], "seq", bwd)
    got[half] = jnp.concatenate([ahead, back], axis=0)
    return got


def ring_scatter(chunks):
    count = lax.axis_size("seq")
    fwd, bwd = ring_perms(count)
    half = chunks[0].shape[0] // 2
    ahead = chunks[1][:half]
    back = chunks[count - 1][half:]
    for step in range(count - 1):
        ahead = lax.ppermute(ahead, "seq", fwd).astype(f32)
        back = lax.ppermute(back, "seq", bwd).astype(f32)
        last = step == count - 2
        ahead = ahead + chunks[0 if last else 2 + step][:half].astype(f32)
        back = back + chunks[0 if last else count - 2 - step][half:].astype(f32)
        if not last:
            ahead = ahead.astype(bf16)
            back = back.astype(bf16)
    return jnp.concatenate([ahead, back], axis=0)


def to_relative(array, index_row, chunk):
    return jnp.concatenate(
        [lax.dynamic_slice_in_dim(array, i * chunk, chunk, 1) for i in index_row], axis=1
    )


def tp_perms(count):
    ys = count // 2
    core = [(i, i ^ 1) for i in range(count)]
    shift = [
        [(i, (((i // 2) + d) % ys) * 2 + i % 2) for i in range(count)] for d in range(ys)
    ]
    return core, shift


def tp_gather(own):
    count = lax.axis_size("tp")
    ys = count // 2
    place = lax.axis_index("tp")
    y, c = place // 2, place % 2
    core, shift = tp_perms(count)
    parts = [own] + [lax.ppermute(own, "tp", shift[d]) for d in range(1, ys)]
    mine = jnp.stack([lax.select_n((y - at + ys) % ys, *parts) for at in range(ys)])
    other = lax.ppermute(mine, "tp", core)
    full = jnp.stack([jnp.where(c == 0, mine, other), jnp.where(c == 0, other, mine)], axis=1)
    return full.reshape((count * own.shape[0],) + own.shape[1:])


def tp_scatter(partial):
    count = lax.axis_size("tp")
    ys = count // 2
    place = lax.axis_index("tp")
    y, c = place // 2, place % 2
    core, shift = tp_perms(count)
    blocks = partial.reshape((ys, 2, partial.shape[0] // count) + partial.shape[1:])
    sent = lax.dynamic_index_in_dim(blocks, 1 - c, 1, False)
    kept = lax.dynamic_index_in_dim(blocks, c, 1, False)
    pair = kept.astype(f32) + lax.ppermute(sent, "tp", core).astype(f32)
    low = pair.astype(bf16)
    own = lax.dynamic_index_in_dim(pair, y, 0, False)
    for d in range(1, ys):
        away = lax.dynamic_index_in_dim(low, (y + d) % ys, 0, False)
        own = own + lax.ppermute(away, "tp", shift[d]).astype(f32)
    return own


def tp_sum(vector):
    count = lax.axis_size("tp")
    core, shift = tp_perms(count)
    vector = vector + lax.ppermute(vector, "tp", core)
    return vector + sum(lax.ppermute(vector, "tp", shift[d]) for d in range(1, count // 2))


def carried(arrays, resets, step):
    count = lax.axis_size("seq")
    place = lax.axis_index("seq")

    def from_near(a, d):
        perm = [(i, i + d * step) for i in range(count) if 0 <= i + d * step < count]
        return lax.ppermute(a.astype(bf16), "seq", perm).astype(f32)

    def reset_within(d):
        at = jnp.arange(count)
        away = (place - at) * step
        return jnp.sum(jnp.where((away >= 1) & (away <= d), resets, 0)) > 0

    arrays = [from_near(a, 1) for a in arrays]
    d = 1
    while d < count - 1:
        keep = 1.0 - reset_within(d).astype(f32)
        arrays = [a + keep * from_near(a, d) for a in arrays]
        d *= 2
    return arrays


def features(vector):
    squares = (vector[..., :, None] * vector[..., None, :]).reshape(
        vector.shape[:-1] + (vector.shape[-1] * vector.shape[-1],)
    )
    return jnp.concatenate(
        [jnp.ones_like(vector[..., :1]), vector * linear_coef, squares * square_coef], axis=-1
    )


def feature_grad(vector, grad_feat):
    feat_width = vector.shape[-1]
    linear_part = grad_feat[..., 1 : 1 + feat_width]
    square_part = grad_feat[..., 1 + feat_width :].reshape(vector.shape + (feat_width,))
    mixed_part = jnp.sum(square_part * vector[..., None, :], axis=-1) + jnp.sum(
        square_part * vector[..., :, None], axis=-2
    )
    return linear_coef * linear_part + square_coef * mixed_part


def segment_masks(anchor, starts, length):
    positions = anchor + jnp.arange(length, dtype=jnp.int32)
    start_le = starts[None, :] <= positions[:, None]
    row_ids = jnp.sum(start_le.astype(jnp.int32), axis=1)
    inside = (starts >= anchor) & (starts < anchor + length)
    carry = jnp.sum(((starts[None, :] >= anchor) & start_le).astype(jnp.int32), axis=1) == 0
    after_last = (
        jnp.sum(
            ((starts[None, :] > positions[:, None]) & inside[None, :]).astype(jnp.int32), axis=1
        )
        == 0
    )
    return (positions, row_ids, carry, after_last)


def rms_scale(values):
    return lax.rsqrt(jnp.mean(values * values, axis=-1, keepdims=True) + epsilon)


def norm_back(grad_out, normed, scale, gain):
    grad_normed = grad_out * gain
    return scale * (grad_normed - normed * jnp.mean(grad_normed * normed, axis=-1, keepdims=True))


def pair_block(query_part, key_heads, row_ids, positions, first_row, span_rows):
    scores = (
        jnp.einsum("thf,shf->hts", query_part, key_heads, preferred_element_type=f32) * 0.25
    )
    rows_here = row_ids[first_row : first_row + span_rows]
    place_here = positions[first_row : first_row + span_rows]
    allowed = (
        (rows_here[:, None] == row_ids[None, :]) & (positions[None, :] <= place_here[:, None])
    ).astype(f32)
    kernel = (1.0 + scores + 0.5 * scores * scores) * allowed[None]
    return (scores, allowed, kernel)


def dot(a, b):
    return jnp.dot(a, b, preferred_element_type=f32)


def dot_t(a, b):
    return lax.dot_general(a, b, (((1,), (1,)), ((), ())), preferred_element_type=f32)


def dot_tt(a, b):
    return lax.dot_general(a, b, (((0,), (0,)), ((), ())), preferred_element_type=f32)


def ring_place(seq):
    z, x = seq // 2, seq % 2
    return z + x * (7 - 2 * z)


def ring_seq(place):
    place = lax.rem(place + 8, 8)
    far = place // 4
    return (1 - far) * 2 * place + far * (15 - 2 * place)


class Sems:
    def __init__(self, ref):
        self.ref, self.used = ref, 0

    def take(self):
        self.used += 1
        assert self.used <= self.ref.shape[0]
        return self.ref.at[self.used - 1]


class Links:
    def __init__(self, send, recv):
        self.send, self.recv, self.sent = Sems(send), Sems(recv), []

    def copy(self, src, dst, **to):
        return pltpu.make_async_remote_copy(
            src_ref=src,
            dst_ref=dst,
            send_sem=self.send.take(),
            recv_sem=self.recv.take(),
            device_id=to,
            device_id_type=pl.DeviceIdType.MESH,
        )

    def start(self, src, dst, **to):
        made = self.copy(src, dst, **to)
        made.start()
        self.sent.append(made)
        return made

    def sent_now(self, some):
        for made in some:
            made.wait_send()
        self.sent = [made for made in self.sent if all(made is not other for other in some)]

    def finish(self):
        for made in self.sent:
            made.wait_send()


class Gather:
    def __init__(self, links, arrays, nearby, gangs):
        self.links, self.arrays, self.nearby = links, arrays, nearby
        self.at = {k: j for j, k in enumerate(relative_list(8))}
        self.flying, self.gangs, self.done = {}, gangs, 0
        self.gang_of = {a: i for i, gang in enumerate(gangs) for a in gang}
        self.events = [
            (a, step, way, part)
            for gang in gangs
            for step in (1, 2, 3, 4)
            for a in gang
            for part in (0, 1)
            for way in (0, 1)
            if step < 4 or way == part
        ]
        for a in gangs[0]:
            for part in (0, 1):
                for way in (0, 1):
                    self.go(a, 1, way, part)

    def rows(self, a, part):
        first, size = self.arrays[a][2:]
        return pl.ds(first + part * size, size)

    def go(self, a, step, way, part):
        own, everyone = self.arrays[a][:2]
        before, after = (step - 1, step) if way == 0 else ((9 - step) % 8, 8 - step)
        src = own if step == 1 else everyone.at[self.at[before]]
        self.flying[a, step, way, part] = self.links.start(
            src.at[self.rows(a, part)],
            everyone.at[self.at[after], self.rows(a, part)],
            seq=self.nearby[way],
        )

    def pump(self, upto):
        while self.done < min(upto, len(self.events)):
            a, step, way, part = self.events[self.done]
            self.flying[a, step, way, part].wait_recv()
            if step < 3 or (step == 3 and way == part):
                self.go(a, step + 1, way, part)
            i = self.gang_of[a]
            if step == 3 and i + 1 < len(self.gangs):
                mine, later = self.gangs[i].index(a), self.gangs[i + 1]
                last = mine == len(self.gangs[i]) - 1
                for other in later[mine:] if last else later[mine : mine + 1]:
                    self.go(other, 1, way, part)
            self.done += 1

    def pump_array(self, a):
        gang = self.gang_of[a]
        self.pump(14 * sum(len(g) for g in self.gangs[: gang + 1]))


def greet(peers):
    barrier = pltpu.get_barrier_semaphore()
    for peer in peers:
        pl.semaphore_signal(
            barrier, inc=1, device_id=peer, device_id_type=pl.DeviceIdType.MESH
        )
    pl.semaphore_wait(barrier, len(peers))


def places():
    seq, tp = lax.axis_index("seq"), lax.axis_index("tp")
    place = ring_place(seq)
    nearby = (ring_seq(place + 1), ring_seq(place - 1))
    over_y = lax.rem(tp + 2, 4)
    over_core = tp + 1 - 2 * (tp % 2)
    peers = [{"seq": ring_seq(place + k)} for k in range(1, 8)]
    peers += [{"tp": over_y}, {"tp": over_core}]
    return seq, tp, place, nearby, over_y, over_core, peers


class Rows:
    def __init__(self, links, own, everyone, tp, over_y, over_core, rows):
        self.links, self.all, self.tp = links, everyone, tp
        self.over_y, self.over_core, self.rows = over_y, over_core, rows
        half = rows // 2
        self.first = [
            links.start(
                own.at[pl.ds(i * half, half)], self.block(tp, i * half, half), tp=over_y
            )
            for i in (0, 1)
        ]
        self.near = links.start(own, self.block(tp, 0, rows), tp=over_core)
        self.last = []

    def block(self, owner, offset, size):
        return self.all.at[pl.ds(pl.multiple_of(owner * self.rows + offset, 16), size)]

    def forward(self, i):
        half = self.rows // 2
        self.first[i].wait_recv()
        came = self.block(self.over_y, i * half, half)
        self.last.append(self.links.start(came, came, tp=self.over_core))

    def finish(self):
        self.near.wait_recv()
        for made in self.last:
            made.wait_recv()


FEATS = 160


def fill_tables(lengths, seq, tok, line, coefs, step):
    total = tok.shape[0]
    anchor = seq * total
    starts, at = [], 0
    for i in range(lengths.shape[0]):
        starts.append(at)
        at = at + lengths[i]

    def places_of(shape, axis):
        pos = lax.broadcasted_iota(jnp.int32, shape, axis)
        low = jnp.zeros(shape, jnp.int32) - anchor
        last = jnp.ones(shape, f32)
        for start in starts:
            here = start - anchor
            low = jnp.maximum(low, jnp.where(pos >= here, here, -anchor))
            last = jnp.where((pos < here) & (here < total), 0.0, last)
        return pos.astype(f32), low, last

    lane = lax.broadcasted_iota(jnp.int32, (total, 128), 1)
    pos, low, last = places_of((total, 128), 0)
    began = jnp.where(low < 0, 1.0, 0.0)
    first = jnp.maximum(low, 0).astype(f32)
    tok[...] = jnp.where(
        lane == 0, first, jnp.where(lane == 1, began, jnp.where(lane == 2, last, pos))
    )
    pos, low, last = places_of((8, total), 1)
    row = lax.broadcasted_iota(jnp.int32, (8, total), 0)
    line[...] = jnp.where(row == 0, pos, jnp.maximum(low, 0).astype(f32))

    def clear(lo, hi):
        free = jnp.ones((1, 128), f32)
        for start in starts:
            at = jnp.zeros((1, 128), jnp.int32) + start
            free = jnp.where((at >= lo * total) & (at < (hi + 1) * total), 0.0, free)
        return free

    z = seq // 2
    one = jnp.ones((1, 128), f32)
    first, second = clear(2 * z, 2 * z), clear(2 * z + 1, 2 * z + 1)
    before = 2 * (z - step)
    rows = [second, first] if step > 0 else [first, second]
    rows += [first * second, clear(before, before + 1)]
    coefs[...] = jnp.concatenate(rows + [one * 0.0] * 4, axis=0)


class Exchange:
    def __init__(self, links, st, near, term, first, second, given, states, coefs, seq, step):
        z, x = seq // 2, seq % 2
        self.st, self.near, self.term, self.first, self.second = st, near, term, first, second
        self.given, self.states, self.coefs, self.x = given, states, coefs, x
        self.turn = z if step > 0 else 3 - z
        self.late = x if step > 0 else 1 - x
        over_x = seq + 1 - 2 * x
        self.half = links.start(st.at[pl.ds(2 * (1 - x), 2)], near, seq=over_x)
        self.hop = links.copy(term, first, seq=seq + 2 * step)
        self.on = links.copy(term, second, seq=seq + 2 * step)
        self.far = links.copy(term, second, seq=seq + 4 * step)
        self.links, self.over_x = links, over_x

    def coef(self, k):
        return self.coefs[k : k + 1, :]

    def pair(self):
        self.half.wait_recv()
        for i in (0, 1):
            mine, theirs = self.st[2 * self.x + i].astype(f32), self.near[i].astype(f32)
            early = jnp.where(self.late == 0, mine, theirs)
            later = jnp.where(self.late == 0, theirs, mine)
            self.term[i] = (later + self.coef(0) * early).astype(bf16)

        @pl.when(self.turn % 2 == 0)
        def _():
            self.hop.start()

    def planes(self):
        @pl.when(self.turn % 2 == 1)
        def _():
            self.hop.wait_recv()

        @pl.when(self.turn == 1)
        def _():
            for i in (0, 1):
                came = self.coef(2) * self.first[i].astype(f32)
                self.term[i] = (self.term[i].astype(f32) + came).astype(bf16)
            self.on.start()
            self.far.start()

    def give(self):
        x = self.x
        for i in (0, 1):
            self.states[2 * x + i] = jnp.zeros((256, 128), f32)
            self.states[2 * (1 - x) + i] = jnp.zeros((256, 128), f32)

        def enter(i):
            return self.states.at[2 * x + i, pl.ds(0, 176)]

        @pl.when(self.turn == 1)
        def _():
            for i in (0, 1):
                enter(i)[...] = self.first[i].astype(f32)

        @pl.when(self.turn == 2)
        def _():
            self.on.wait_recv()
            for i in (0, 1):
                enter(i)[...] = self.second[i].astype(f32)

        @pl.when(self.turn == 3)
        def _():
            self.far.wait_recv()
            for i in (0, 1):
                older = self.coef(3) * self.second[i].astype(f32)
                enter(i)[...] = self.first[i].astype(f32) + older

        for i in (0, 1):
            came = enter(i)[...]
            mine, theirs = self.st[2 * x + i].astype(f32), self.near[i].astype(f32)
            early = jnp.where(self.late == 0, mine, theirs)
            passed = early + self.coef(1) * came
            self.given[0, i] = jnp.where(self.late == 0, passed, came).astype(bf16)
            enter(i)[...] = jnp.where(self.late == 0, came, passed)
        self.back = self.links.start(self.given.at[0], self.given.at[1], seq=self.over_x)

    def take(self):
        self.back.wait_recv()
        for i in (0, 1):
            self.states[2 * (1 - self.x) + i, 0:176, :] = self.given[1, i].astype(f32)

    def finish(self):
        @pl.when(self.turn % 2 == 0)
        def _():
            self.hop.wait_send()

        @pl.when(self.turn == 1)
        def _():
            self.on.wait_send()
            self.far.wait_send()


def ring_columns(place):
    return [pl.ds(pl.multiple_of(ring_seq(place - k) * 256, 256), 256) for k in relative_list(8)]


def phi(heads, h, select_a, select_b, lanes):
    a = dot(heads, select_a[h]) + lanes[0:1, :]
    b = dot(heads, select_b[h]) + lanes[1:2, :]
    return a, b


def fwd_kernel(
    lengths, sa_ref, sb_ref, lanes_ref, hm_ref, gain_first, gain_second,
    x_in, wq_in, wk_in, wv_in, wo_in, wg_in, wu_in, wd_in, c_in,
    wq_all, wo_all, wg_all, wu_all, wd_all, c_all,
    h1_out, qkv_out, yb_out, den_out, x1_out, h2_out, gate_out, up_out, m_out, sin_out, gain_out, terms_out,
    x_ref, tok_ref, line_ref, coef_ref, gain_ref, q_own, o_own, g_own, u_own, d_own,
    w_small, w_v, w_o, w_d, w_g, c_v,
    xg, h1, wq, wo, wg, wu, qkv, kq, num, den, yb, sc, rc, sy, ry, x1, gate, up, mm,
    gains_all, gains, st, st_x, st_t, st_z, st_y, st_g, s_in,
    send, recv, local,
):
    seq, tp, place, nearby, over_y, over_core, peers = places()
    z, x = seq // 2, seq % 2
    at = {k: j for j, k in enumerate(relative_list(8))}
    rows = x_ref.shape[0]
    total = 4 * rows
    links = Links(send, recv)
    locs = Sems(local)
    pending = []

    def store(src, dst):
        made = pltpu.make_async_copy(src, dst, locs.take())
        made.start()
        pending.append(made)

    def load(src, dst):
        made = pltpu.make_async_copy(src, dst, locs.take())
        made.start()
        return made

    got_qk = [load(wq_in, w_small.at[0:64]), load(wk_in, w_small.at[64:128]), load(wv_in, w_v)]
    columns = ring_columns(place)
    got_x = [load(x_in.at[:, c], x_ref.at[:, col(j)]) for j, c in enumerate(columns)]
    c_rows = pl.ds(pl.multiple_of(tp * rows, rows), rows)
    got_c = [load(c_in.at[:, c], c_v.at[:, col(j)]) for j, c in enumerate(columns)]
    got_o = load(wo_in, w_o)
    ff = wd_in.shape[0]
    got_g = load(wg_in, w_g.at[pl.ds(0, ff)])
    got_d = load(wd_in, w_d.at[pl.ds(0, ff)])

    def turn(src, dst):
        for i in range(0, ff, 128):
            size = min(128, ff - i)
            dst[:, i : i + size] = src[i : i + 128, :].T[:, :size].astype(bf16)

    gain_ref[...] = jnp.concatenate(
        [gain_first[...], gain_second[...], jnp.zeros((14, 256), f32)], axis=0
    ).astype(bf16)
    greet(peers)
    gain_flying = [
        links.start(gain_ref, gains_all.at[at[k]], seq=ring_seq(place + k)) for k in range(1, 8)
    ]
    for made in got_x:
        made.wait()
    xrows = Rows(links, x_ref, xg, tp, over_y, over_core, rows)
    for made in got_qk:
        made.wait()
    q_own[:, 0:128] = w_small[...].T.astype(bf16)
    q_own[:, 128:640] = w_v[...].astype(bf16)
    ring = Gather(
        links,
        [
            (q_own, wq_all, 0, 128),
            (o_own, wo_all, 0, 128),
            (g_own, wg_all, 0, 64),
            (g_own, wg_all, 128, 64),
            (u_own, wu_all, 0, 64),
            (u_own, wu_all, 128, 64),
            (d_own, wd_all, 0, 128),
        ],
        nearby,
        [[0], [1], [2], [3, 4, 5], [6]],
    )
    own_in = [
        load(x_ref, xrows.block(tp, 0, rows)),
        load(gain_ref, gains_all.at[at[0]]),
    ]
    got_o.wait()
    o_own[...] = w_o[...].T.astype(bf16)
    ring.pump(2)
    got_g.wait()
    turn(w_g, g_own)
    got_u = load(wu_in, w_g.at[pl.ds(0, ff)])
    ring.pump(4)
    got_d.wait()
    turn(w_d, d_own)
    got_u.wait()
    turn(w_g, u_own)
    pairs = [(q_own, wq_all), (o_own, wo_all), (g_own, wg_all), (u_own, wu_all), (d_own, wd_all)]
    own_kept = [load(own, everyone.at[at[0]]) for own, everyone in pairs]
    fill_tables(lengths, seq, tok_ref, line_ref, coef_ref, 1)

    ring.pump(6)
    xrows.forward(0)
    for made in gain_flying:
        made.wait_recv()
    for made in own_in:
        made.wait()
    for j in range(8):
        chunk = gains_all[j].astype(f32)
        gains[0:8, j * 256 : (j + 1) * 256] = chunk[0:8]
    ring.pump(10)
    xrows.forward(1)
    ring.pump_array(0)
    own_kept[0].wait()
    got = load_weights(load, wq_all, wq)
    xrows.finish()

    def norm_first(i, _):
        r = pl.ds(pl.multiple_of(i * 32, 32), 32)
        v = xg[r, :].astype(f32)
        s = lax.rsqrt(jnp.mean(v * v, axis=1, keepdims=True) + epsilon)
        h1[r, :] = (v * s * gains[0:1, :]).astype(bf16)
        return 0

    lax.fori_loop(0, total // 32, norm_first, 0)
    links.sent_now(xrows.last)
    kept_h1 = load(h1, h1_out)
    for made in got_c:
        made.wait()
    crows = Rows(links, c_v, c_all, tp, over_y, over_core, rows)
    kept_c = load(c_v, c_all.at[c_rows])
    ring.pump(15)
    for made in got:
        made.wait()

    def project(i, _):
        r = pl.ds(pl.multiple_of(i * 256, 256), 256)
        res = dot(h1[r, :], wq[...])
        qkv[r, :] = res.astype(bf16)
        kq[r, :] = pltpu.roll(res[:, :128], 64, 1).astype(bf16)
        return 0

    lax.fori_loop(0, total // 256, project, 0)
    store(qkv, qkv_out)
    ring.pump(16)

    heads = 4

    def head_v(h):
        return slice(128 + h * 128, 256 + h * 128)

    for h in range(heads):

        def state(i, c, h=h):
            s, zz = c
            r = pl.ds(pl.multiple_of(i * 256, 256), 256)
            a, b = phi(kq[r, :], h, sa_ref, sb_ref, lanes_ref)
            f = a * b * lanes_ref[2:3, :] * tok_ref[r, 2:3]
            s = s + dot_tt(f.astype(bf16), qkv[r, head_v(h)])
            return s, zz + jnp.sum(f, axis=0, keepdims=True)

        s, zz = lax.fori_loop(
            0, total // 256, state, (jnp.zeros((256, 128), f32), jnp.zeros((1, 256), f32))
        )
        pack_state(st, h, s, zz)
        ring.pump(17 + h)
    moved = Exchange(links, st, st_x, st_t, st_z, st_y, st_g, s_in, coef_ref, seq, 1)

    def local_head(h):
        for i in range(total // 256):
            r = slice(i * 256, (i + 1) * 256)
            span = (i + 1) * 256
            qm = (qkv[r, :128].astype(f32) * hm_ref[h : h + 1, :]).astype(bf16)
            u = dot_t(qm, kq[:span, :])
            keep = (line_ref[0:1, :span] >= tok_ref[r, 0:1]) & (
                line_ref[0:1, :span] <= tok_ref[r, 3:4]
            )
            kap = jnp.where(keep, (0.5 * u + 1.0) * u + 1.0, 0.0)
            den[r, h : h + 1] = jnp.sum(kap, axis=1, keepdims=True)
            num[r, h * 128 : (h + 1) * 128] = dot(kap.astype(bf16), qkv[:span, head_v(h)])

    local_head(0)
    ring.pump(22)
    moved.pair()
    local_head(1)
    ring.pump(24)
    moved.planes()
    local_head(2)
    ring.pump(26)
    moved.give()
    local_head(3)
    ring.pump(28)
    moved.take()
    store(s_in, sin_out)
    for h in range(heads):
        z_row = jnp.concatenate([s_in[h, 160:161, :], s_in[h, 161:162, :]], axis=1)
        feat = jax.lax.broadcasted_iota(jnp.int32, (256, 128), 0)
        s_low = jnp.where(feat < FEATS, s_in[h], 0.0).astype(bf16)

        def carry(i, _, h=h, z_row=z_row, s_low=s_low):
            r = pl.ds(pl.multiple_of(i * 256, 256), 256)
            a, b = phi(qkv[r, 0:128], h, sa_ref, sb_ref, lanes_ref)
            f = a * b * lanes_ref[2:3, :] * tok_ref[r, 1:2]
            hv = slice(h * 128, (h + 1) * 128)
            top = num[r, hv] + dot(f.astype(bf16), s_low)
            low = den[r, h : h + 1] + jnp.sum(f * z_row, axis=1, keepdims=True)
            den[r, h : h + 1] = low
            y = top / low
            yb[r, hv] = y.astype(bf16)
            return 0

        lax.fori_loop(0, total // 256, carry, 0)
        ring.pump(31 + 2 * h)
    store(yb, yb_out)
    store(den, den_out)
    ring.pump_array(1)
    own_kept[1].wait()
    got = load_weights(load, wo_all, wo)
    for made in got:
        made.wait()

    y_at, c_at = tp // 2, tp % 2

    def out_rows(block):
        return yb[pl.ds(pl.multiple_of(block * rows, rows), rows), :]

    cols = 512
    to_core = []
    for yy in (0, 1):

        def core_cols(i, _, yy=yy):
            c = pl.ds(pl.multiple_of(i * cols, cols), cols)
            sc[yy, :, c] = dot_t(out_rows(yy * 2 + 1 - c_at), wo[c, :]).astype(bf16)
            return 0

        lax.fori_loop(0, 2048 // cols, core_cols, 0)
        to_core.append(links.start(sc.at[yy], rc.at[yy], tp=over_core))
    for made in to_core:
        made.wait_recv()
    ring.pump(40)

    def away_cols(i, _):
        c = pl.ds(pl.multiple_of(i * cols, cols), cols)
        part = dot_t(out_rows((1 - y_at) * 2 + c_at), wo[c, :])
        sy[:, c] = (part + rc[1 - y_at, :, c].astype(f32)).astype(bf16)
        return 0

    lax.fori_loop(0, 2048 // cols, away_cols, 0)
    to_y = links.start(sy, ry, tp=over_y)

    def own_cols(i, _):
        c = pl.ds(pl.multiple_of(i * cols, cols), cols)
        x1[:, c] = (
            dot_t(out_rows(tp), wo[c, :]) + rc[y_at, :, c].astype(f32) + x_ref[:, c].astype(f32)
        )
        return 0

    lax.fori_loop(0, 2048 // cols, own_cols, 0)
    ring.pump(44)
    to_y.wait_recv()
    ring.pump(54)

    links.sent_now(xrows.first + [xrows.near])
    ho = x_ref

    def norm_second(i, _):
        r = pl.ds(pl.multiple_of(i * 32, 32), 32)
        v = x1[r, :] + ry[r, :].astype(f32)
        x1[r, :] = v
        s = lax.rsqrt(jnp.mean(v * v, axis=1, keepdims=True) + epsilon)
        ho[r, :] = (v * s * gains[1:2, :]).astype(bf16)
        return 0

    lax.fori_loop(0, rows // 32, norm_second, 0)
    store(x1, x1_out)
    store(gains, gain_out)
    h2 = xg
    hrows = Rows(links, ho, h2, tp, over_y, over_core, rows)
    own_in = load(ho, hrows.block(tp, 0, rows))
    ring.pump(56)
    hrows.forward(0)
    ring.pump(63)
    hrows.forward(1)
    crows.forward(0)
    crows.forward(1)
    hrows.finish()
    crows.finish()
    own_in.wait()
    store(h2, h2_out)
    kept_h1.wait()
    kept_c.wait()
    got_c = load(c_all, h1)
    ring.pump_array(3)
    own_kept[2].wait()
    got = load_weights(load, wg_all, wg)
    own_kept[3].wait()
    got += load_weights(load, wu_all, wu)
    for made in got:
        made.wait()

    def gate_up(i, _):
        r = pl.ds(pl.multiple_of(i * 128, 128), 128)
        g = dot(h2[r, :], wg[...])
        uu = dot(h2[r, :], wu[...])
        gate[r, :] = g.astype(bf16)
        up[r, :] = uu.astype(bf16)
        mm[r, :] = (g * jax.nn.sigmoid(g) * uu).astype(bf16)
        return 0

    for quarter in range(4):
        lax.fori_loop(quarter * total // 512, (quarter + 1) * total // 512, gate_up, 0)
        ring.pump(86 + 2 * quarter)
    store(gate, gate_out)
    store(up, up_out)
    store(mm, m_out)
    got_c.wait()
    links.sent_now([ring.flying[a, 1, way, part] for a in (2, 3, 4, 5) for way in (0, 1) for part in (0, 1)])
    out_sems = [locs.take(), locs.take()]
    buffers = [g_own, u_own]

    def keep_terms(j, k):
        return pltpu.make_async_copy(buffers[k], terms_out.at[col(j)], out_sems[k])

    def grad_down(i, _):
        for k in (0, 1):
            pl.when(i > 0)(lambda k=k: keep_terms(2 * i - 2 + k, k).wait())
            buffers[k][...] = dot_tt(h1[:, col(2 * i + k)], mm[...]).astype(bf16)
            keep_terms(2 * i + k, k).start()
        return 0

    lax.fori_loop(0, 2, grad_down, 0)
    ring.pump(94)
    lax.fori_loop(2, 4, grad_down, 0)
    for k in (0, 1):
        keep_terms(6 + k, k).wait()
    ring.pump_array(6)
    own_kept[4].wait()
    for made in pending:
        made.wait()
    links.finish()
    moved.finish()


def pack_state(st, h, s, zz):
    st[h, 0:FEATS, :] = s[:FEATS].astype(bf16)
    tail = jnp.concatenate([zz[:, :128], zz[:, 128:], jnp.zeros((14, 128), f32)], axis=0)
    st[h, FEATS : FEATS + 16, :] = tail.astype(bf16)


def load_weights(load, everyone, flat):
    count, chunk = everyone.shape[0], everyone.shape[1]
    return [load(everyone.at[j], flat.at[pl.ds(j * chunk, chunk)]) for j in range(count)]


class Scatter:
    def __init__(self, slots, send, recv, nearby):
        self.slots, self.send, self.recv, self.nearby = slots, send, recv, nearby

    def copy(self, a, step, way, sub, src, slot, width):
        return pltpu.make_async_remote_copy(
            src_ref=src,
            dst_ref=self.piece(slot, way, sub, width),
            send_sem=self.send.at[a % 2, way, sub],
            recv_sem=self.recv.at[a % 2, way, sub, step],
            device_id={"seq": self.nearby[way]},
            device_id_type=pl.DeviceIdType.MESH,
        )

    def slot(self, a, step):
        return (a % 2) * 4 + (a // 2 * 7 + step) % 4

    def rows(self, way, sub, base=0):
        start = base + way * 128 + sub * 64
        return pl.ds(start if isinstance(start, int) else pl.multiple_of(start, 64), 64)

    def piece(self, slot, way, sub, width):
        return self.slots.at[slot, self.rows(way, sub), pl.ds(0, width)]

    def begin(self, a, own, width, column=0):
        for sub in (0, 1):
            for way in (0, 1):
                src = own.at[self.rows(way, sub, way * 256), pl.ds(column, width)]
                self.copy(a, 0, way, sub, src, self.slot(a, 0), width).start()

    def event(self, a, e, own, width, out, column=0):
        step, sub = e // 2, e % 2
        is_last = step // 6
        here = self.slot(a, step)
        far = (step + 1) // 4
        place0 = (1 - far) * 2 * (step + 1) + far * (11 - 2 * step) + is_last * 8
        far = (step + 2) // 4 - is_last
        place1 = (1 - far) * (3 + 2 * step) + far * (10 - 2 * step) + is_last * 9
        places = (place0, place1)
        for way in (0, 1):
            piece = self.piece(here, way, sub, width)
            came = self.copy(a, step, way, sub, piece, here, width)
            came.wait_recv()
            came.wait_send()

        def summed(way):
            mine = own[self.rows(way, sub, places[way] * 256), pl.ds(column, width)]
            came = self.slots[here, self.rows(way, sub), pl.ds(0, width)]
            return came.astype(f32) + mine.astype(f32)

        def on():
            for way in (0, 1):
                self.slots[here, self.rows(way, sub), pl.ds(0, width)] = summed(way).astype(bf16)
                piece = self.piece(here, way, sub, width)
                self.copy(a, step + 1, way, sub, piece, self.slot(a, step + 1), width).start()

        def end():
            for way in (0, 1):
                out[self.rows(way, sub), pl.ds(0, width)] = summed(way)

        if isinstance(e, int):
            if step < 6:
                on()
            else:
                end()
        else:
            pl.when(step < 6)(on)
            pl.when(step == 6)(end)


class TpSum:
    def __init__(self, part, from_core, from_y, sems, credits, tp, over_y, over_core):
        self.part, self.from_core, self.from_y = part, from_core, from_y
        self.sems, self.credits = sems, credits
        self.tp, self.over_y, self.over_core = tp, over_y, over_core
        self.y, self.c = tp // 2, tp % 2

    def to_core(self, i, yy):
        return pltpu.make_async_remote_copy(
            src_ref=self.part.at[i, yy * 2 + 1 - self.c],
            dst_ref=self.from_core.at[i, yy],
            send_sem=self.sems.at[yy, i],
            recv_sem=self.sems.at[2 + yy, i],
            device_id={"tp": self.over_core},
            device_id_type=pl.DeviceIdType.MESH,
        )

    def to_y(self, i):
        return pltpu.make_async_remote_copy(
            src_ref=self.part.at[i, (1 - self.y) * 2 + self.c],
            dst_ref=self.from_y.at[i],
            send_sem=self.sems.at[4, i],
            recv_sem=self.sems.at[5, i],
            device_id={"tp": self.over_y},
            device_id_type=pl.DeviceIdType.MESH,
        )

    def sent(self, i):
        self.to_core(i, 0).wait_send()
        self.to_core(i, 1).wait_send()
        self.to_y(i).wait_send()

    def offer(self, i, turn, value):
        if turn > 0:
            self.sent(i)
        for block in range(4):
            self.part[i, block] = value[block * 256 : (block + 1) * 256].astype(bf16)
        if turn > 0:
            pl.semaphore_wait(self.credits.at[0], 1)
        for yy in (0, 1):
            self.to_core(i, yy).start()

    def pass_on(self, i, turn):
        for yy in (0, 1):
            self.to_core(i, yy).wait_recv()
        away = (1 - self.y) * 2 + self.c
        self.part[i, away] = (
            self.part[i, away].astype(f32) + self.from_core[i, 1 - self.y].astype(f32)
        ).astype(bf16)
        if turn > 0:
            pl.semaphore_wait(self.credits.at[1], 1)
        self.to_y(i).start()

    def take(self, i, turn, use):
        self.to_y(i).wait_recv()
        use(
            self.part[i, self.tp].astype(f32)
            + self.from_core[i, self.y].astype(f32)
            + self.from_y[i].astype(f32)
        )
        if turn < 2:
            for k, peer in ((0, self.over_core), (1, self.over_y)):
                pl.semaphore_signal(
                    self.credits.at[k],
                    inc=1,
                    device_id={"tp": peer},
                    device_id_type=pl.DeviceIdType.MESH,
                )


def col(i, width=256):
    return pl.ds(i * width if isinstance(i, int) else pl.multiple_of(i * width, width), width)


def bwd_kernel(
    lengths, sa_ref, sb_ref, lanes_ref, hm_ref, gains, s_in, den, gain_first, gain_second,
    x_in, x1_in, wq_all, wo_all, wg_all, wu_all, wd_all, c_all, h1_all, qkv_all, yb_all, h2_all,
    gate_all, up_all, m_all, terms_all,
    d_out, g_out, u_out, oq_out, block_out, input_out, gain_out, u_kept,
    tok_ref, line_ref, coef_ref, terms, terms_core, terms_y,
    slots, s1, s2, wo, stream, hs, rows_all, mm, dup, tiles, qkv, kq, yb, dnum, dden, dden_t, dqkv,
    dq, dk, part, from_core, from_y, acc, x1, fout, st, st_x, st_t, st_z, st_y, st_g, s_back, own_rows,
    ring_send, ring_recv, tp_sems, credits, send, recv, local, tile_sems,
):
    seq, tp, place, nearby, over_y, over_core, peers = places()
    z, x = seq // 2, seq % 2
    rows, width = own_rows.shape
    total = 4 * rows
    ff = mm.shape[1]
    links = Links(send, recv)
    locs = Sems(local)

    def load(src, dst):
        made = pltpu.make_async_copy(src, dst, locs.take())
        made.start()
        return made

    def whole(everyone, flat):
        count, chunk = everyone.shape[0], everyone.shape[1]
        return [load(everyone.at[j], flat.at[pl.ds(j * chunk, chunk)]) for j in range(count)]

    got_m = load(m_all, mm)
    got_wd = whole(wd_all, s2)
    got_terms = load(terms_all, s1)
    got_c = load(c_all, rows_all)
    greet(peers)
    ring = Scatter(slots, ring_send, ring_recv, nearby)
    ring.begin(0, terms_all, ff)
    got_x1 = load(x1_in, x1)
    fill_tables(lengths, seq, tok_ref, line_ref, coef_ref, -1)
    columns = ring_columns(place)
    got_qkv = [load(qkv_all, qkv), load(yb_all, yb)]
    got_wo = whole(wo_all, wo)
    sums = TpSum(part, from_core, from_y, tp_sems, credits, tp, over_y, over_core)

    def run(n, body, pumps=None):
        def step(i, _):
            body(i)
            if pumps:
                a, first, count = pumps
                every = n // count
                pl.when((i + 1) % every == 0)(lambda: event(a, first + (i + 1) // every - 1))
            return 0

        lax.fori_loop(0, n, step, 0)

    plan = {0: (s1, ff, 0), 1: (s2, ff, 0), 2: (s1, ff, 0), 3: (s2, 512, 0), 4: (s2, 640, 512)}

    def event(a, e):
        own, wide, column = plan[a]
        ring.event(a, e, own, wide, fout, column)

    def begin(a):
        own, wide, column = plan[a]
        ring.begin(a, own, wide, column)

    def events(a, first, last):
        lax.fori_loop(first, last, lambda e, _: (event(a, e), 0)[1], 0)

    def both(a, first, b, second, count):
        def pair(i, _):
            event(a, first + i)
            event(b, second + i)
            return 0

        lax.fori_loop(0, count, pair, 0)

    def chunks_of(source, size, body, pumps=None, count=8):
        def copies(i, slot):
            return [
                pltpu.make_async_copy(a, b, tile_sems.at[k, slot])
                for k, (a, b) in enumerate(source(i, slot))
            ]

        for made in copies(0, 0):
            made.start()

        def step(i):
            slot = i % 2

            @pl.when(i + 1 < count)
            def _():
                for made in copies(i + 1, 1 - slot):
                    made.start()

            for made in copies(i, slot):
                made.wait()
            body(i, slot)

        run(count, step, pumps)

    got_m.wait()
    for made in got_wd:
        made.wait()
    got_terms.wait()

    def mlp(i):
        sums.offer(i, 0, dot_t(mm[...], s2[col(i), :]))
        pl.when(i > 0)(lambda: sums.pass_on(i - 1, 0))

    run(8, mlp, (0, 0, 2))
    sums.pass_on(7, 0)

    def gate_up_tiles(i, slot):
        r = col(i, 128)
        return [
            (gate_all.at[r], tiles.at[slot, pl.ds(0, 128)]),
            (up_all.at[r], tiles.at[slot, pl.ds(128, 128)]),
        ]

    def grad_gate_up(i, slot):
        r = col(i, 128)
        dm = dot(rows_all[r, :], s2[...]).astype(bf16).astype(f32)
        g = tiles[slot, 0:128].astype(f32)
        u = tiles[slot, 128:256].astype(f32)
        s = jax.nn.sigmoid(g)
        mm[r, :] = (dm * u * s * (1.0 + g * (1.0 - s))).astype(bf16)
        dup[r, :] = (dm * (g * s)).astype(bf16)

        pl.when(i >= 3)(lambda: take_block(i - 3))

    def take_block(i):
        def use(value):
            own_rows[:, col(i)] = (x1[:, col(i)] + value).astype(bf16)

        sums.take(i, 0, use)

    got_x1.wait()
    got_c.wait()
    chunks_of(gate_up_tiles, 8, grad_gate_up, (0, 2, 4))

    def w_tiles(i, slot):
        return [(wg_all.at[i], stream.at[slot, 0]), (wu_all.at[i], stream.at[slot, 1])]

    def grad_hidden(i, slot):
        pl.when(i < 3)(lambda: take_block(5 + i))
        value = dot_t(mm[...], stream[slot, 0]) + dot_t(dup[...], stream[slot, 1])
        sums.offer(i, 1, value)
        pl.when(i > 0)(lambda: sums.pass_on(i - 1, 1))

    chunks_of(w_tiles, 8, grad_hidden, (0, 6, 4))
    kept = [load(own_rows.at[:, col(j)], block_out.at[:, c]) for j, c in enumerate(columns)]
    pending = []
    sums.pass_on(7, 1)

    def h_tiles(everyone):
        return lambda i, slot: [(everyone.at[:, col(i)], hs.at[slot])]

    def keep_up(i, slot):
        return pltpu.make_async_copy(tiles.at[slot], u_kept.at[col(i)], tile_sems.at[1, slot])

    def grads(i, slot):
        s2[col(i), :] = dot_tt(hs[slot], mm[...]).astype(bf16)
        pl.when(i >= 2)(lambda: keep_up(i - 2, slot).wait())
        tiles[slot] = dot_tt(hs[slot], dup[...]).astype(bf16)
        keep_up(i, slot).start()
        pl.when(i == 1)(lambda: begin(1))

    chunks_of(h_tiles(h2_all), 8, grads, (0, 10, 2))
    keep_up(6, 0).wait()
    keep_up(7, 1).wait()

    def take_second(i):
        def use(value):
            acc[:, col(i)] = value

        sums.take(i, 1, use)

    run(2, take_second)
    both(1, 0, 0, 12, 2)
    done = load(fout.at[:, pl.ds(0, ff)], d_out)
    got_up = load(u_kept, s1)
    lax.fori_loop(2, 5, lambda i, _: (take_second(i), 0)[1], 0)
    events(1, 2, 3)
    got_up.wait()
    begin(2)
    lax.fori_loop(5, 8, lambda i, _: (take_second(i), 0)[1], 0)
    both(1, 3, 2, 0, 1)

    for made in kept:
        made.wait()

    def norm_back_second(i, _):
        r = pl.ds(pl.multiple_of(i * 32, 32), 32)
        v = x1[r, :]
        s = lax.rsqrt(jnp.mean(v * v, axis=1, keepdims=True) + epsilon)
        n = v * s
        dn = acc[r, :] * gains[1:2, :]
        own = pl.ds(pl.multiple_of(tp * rows + i * 32, 32), 32)
        back = rows_all[own, :].astype(f32) + s * (
            dn - n * jnp.mean(dn * n, axis=1, keepdims=True)
        )
        acc[r, :] = back
        own_rows[r, :] = back.astype(bf16)
        return 0

    lax.fori_loop(0, rows // 32, norm_back_second, 0)
    da = Rows(links, own_rows, rows_all, tp, over_y, over_core, rows)
    own_in = load(own_rows, da.block(tp, 0, rows))

    both(1, 4, 2, 1, 1)
    da.forward(0)
    both(1, 5, 2, 2, 1)
    da.forward(1)
    for made in got_qkv + got_wo:
        made.wait()
    da.finish()
    own_in.wait()
    links.sent_now(da.first + [da.near])
    got_x = [load(x_in.at[:, c], own_rows.at[:, col(j)]) for j, c in enumerate(columns)]

    def head_v(h):
        return slice(128 + h * 128, 256 + h * 128)

    def grad_attended(i):
        r = col(i, 256)
        dy = dot(rows_all[r, :], wo[...])
        kq[r, :] = pltpu.roll(qkv[r, 0:128].astype(f32), 64, 1).astype(bf16)
        columns = []
        for h in range(4):
            hv = slice(h * 128, (h + 1) * 128)
            under = 1.0 / den[r, h : h + 1]
            part_h = dy[:, hv]
            dnum[r, hv] = (part_h * under).astype(bf16)
            low = jnp.sum(part_h * yb[r, hv].astype(f32), axis=1, keepdims=True)
            columns.append(-low * under)
        lane = lax.broadcasted_iota(jnp.int32, (256, 128), 1)
        packed = jnp.zeros((256, 128), f32)
        for h in range(4):
            packed = jnp.where(lane == h, columns[h], packed)
        dden[r, :] = packed
        dden_t[i] = packed.T[0:8, :]

    run(4, grad_attended)
    both(1, 6, 2, 3, 1)

    for h in range(4):

        def state(i, c, h=h):
            s, zz = c
            r = col(i, 256)
            a, b = phi(qkv[r, 0:128], h, sa_ref, sb_ref, lanes_ref)
            f = a * b * lanes_ref[2:3, :] * tok_ref[r, 1:2]
            s = s + dot_tt(f.astype(bf16), dnum[r, h * 128 : (h + 1) * 128])
            return s, zz + jnp.sum(f * dden[r, h : h + 1], axis=0, keepdims=True)

        s, zz = lax.fori_loop(
            0, 4, state, (jnp.zeros((256, 128), f32), jnp.zeros((1, 256), f32))
        )
        pack_state(st, h, s, zz)
    moved = Exchange(links, st, st_x, st_t, st_z, st_y, st_g, s_back, coef_ref, seq, -1)
    both(1, 7, 2, 4, 1)

    dq[...] = jnp.zeros(dq.shape, f32)

    def local_head(h):
        hm = hm_ref[h : h + 1, :]
        hv = slice(h * 128, (h + 1) * 128)
        for j in range(total // 256):
            k_rows = slice(j * 256, (j + 1) * 256)
            dv_s = jnp.zeros((256, 128), f32)
            dk_s = jnp.zeros((256, 128), f32)
            for i in range(j, total // 256):
                q_rows = slice(i * 256, (i + 1) * 256)
                qm = (qkv[q_rows, 0:128].astype(f32) * hm).astype(bf16)
                u = dot_t(kq[k_rows, :], qm)
                keep = tok_ref[k_rows, 3:4] >= line_ref[1:2, q_rows]
                if i == j:
                    keep = keep & (tok_ref[k_rows, 3:4] <= line_ref[0:1, q_rows])
                kap = jnp.where(keep, (0.5 * u + 1.0) * u + 1.0, 0.0).astype(bf16)
                dn = dnum[q_rows, hv]
                grad = dot_t(qkv[k_rows, head_v(h)], dn) + dden_t[i, h : h + 1, :]
                du = jnp.where(keep, grad * (1.0 + u), 0.0).astype(bf16)
                dv_s = dv_s + dot(kap, dn)
                dk_s = dk_s + dot(du, qm)
                dq[q_rows, :] += dot_tt(du, kq[k_rows, :]) * hm
            dqkv[k_rows, head_v(h)] = dv_s.astype(bf16)
            if h == 0:
                dk[k_rows, :] = dk_s
            else:
                dk[k_rows, :] += dk_s

    local_head(0)
    moved.pair()
    both(1, 8, 2, 5, 1)
    local_head(1)
    moved.planes()
    both(1, 9, 2, 6, 1)
    local_head(2)
    moved.give()
    both(1, 10, 2, 7, 1)
    local_head(3)
    both(1, 11, 2, 8, 1)
    done.wait()
    both(1, 12, 2, 9, 2)
    done = load(fout.at[:, pl.ds(0, ff)], g_out)

    def grad_out(i):
        s2[col(i), 0:512] = dot_tt(rows_all[:, col(i)], yb[...]).astype(bf16)

    run(8, grad_out)
    begin(3)
    moved.take()

    def split_state(ref, h):
        z_row = jnp.concatenate([ref[h, 160:161, :], ref[h, 161:162, :]], axis=1)
        feat = lax.broadcasted_iota(jnp.int32, (256, 128), 0)
        return jnp.where(feat < FEATS, ref[h], 0.0).astype(bf16), z_row

    for h in range(4):
        s_q, z_q = split_state(s_in, h)
        s_k, z_k = split_state(s_back, h)
        hv = slice(h * 128, (h + 1) * 128)

        def through(grad, a, b, h=h):
            grad = grad * lanes_ref[2:3, :]
            return dot_t((grad * b).astype(bf16), sa_ref[h]) + dot_t(
                (grad * a).astype(bf16), sb_ref[h]
            )

        def carried_part(i, _, h=h, s_q=s_q, z_q=z_q, s_k=s_k, z_k=z_k, hv=hv, through=through):
            r = col(i, 256)
            a, b = phi(qkv[r, 0:128], h, sa_ref, sb_ref, lanes_ref)
            grad = dot_t(dnum[r, hv], s_q) + dden[r, h : h + 1] * z_q
            dq[r, :] += through(grad * tok_ref[r, 1:2], a, b)
            a, b = phi(kq[r, :], h, sa_ref, sb_ref, lanes_ref)
            last = tok_ref[r, 2:3]
            grad = dot_t(qkv[r, head_v(h)], s_k) + z_k
            dk[r, :] += through(grad * last, a, b)
            f = (a * b * lanes_ref[2:3, :] * last).astype(bf16)
            dqkv[r, head_v(h)] = (dqkv[r, head_v(h)].astype(f32) + dot(f, s_k)).astype(bf16)
            return 0

        lax.fori_loop(0, 4, carried_part, 0)

    def join(i):
        r = col(i, 256)
        dqkv[r, 0:128] = (dq[r, :] + pltpu.roll(dk[r, :], 64, 1)).astype(bf16)

    both(2, 11, 3, 0, 1)
    run(4, join)
    own_w = load(wg_all.at[7], stream.at[0, 0])

    def grad_out_qkv(i, slot):
        s2[col(i), 512:1152] = dot_tt(hs[slot], dqkv[...]).astype(bf16)

    chunks_of(h_tiles(h1_all), 8, grad_out_qkv, (3, 1, 1))

    own_w.wait()
    gain_two = jnp.sum(fout[:, 0:ff] * stream[0, 0].astype(f32), axis=1, keepdims=True)

    done.wait()
    both(2, 12, 3, 2, 2)
    done = load(fout.at[:, pl.ds(0, ff)], u_out)
    begin(4)

    def wq_tiles(i, slot):
        return [(wq_all.at[i], stream.at[slot, 0, :, pl.ds(0, 640)])]

    def grad_hidden_first(i, slot):
        sums.offer(i, 2, dot_t(dqkv[...], stream[slot, 0, :, 0:640]))
        pl.when(i > 0)(lambda: sums.pass_on(i - 1, 2))

    chunks_of(wq_tiles, 8, grad_hidden_first, (3, 4, 2))
    sums.pass_on(7, 2)
    both(3, 6, 4, 0, 4)

    def take_first(i):
        def use(value):
            x1[:, col(i)] = value

        sums.take(i, 2, use)

    run(8, take_first, (4, 4, 2))
    for made in got_x:
        made.wait()

    def norm_back_first(i, _):
        r = pl.ds(pl.multiple_of(i * 32, 32), 32)
        v = own_rows[r, :].astype(f32)
        s = lax.rsqrt(jnp.mean(v * v, axis=1, keepdims=True) + epsilon)
        n = v * s
        dn = x1[r, :] * gains[0:1, :]
        acc[r, :] += s * (dn - n * jnp.mean(dn * n, axis=1, keepdims=True))
        return 0

    lax.fori_loop(0, rows // 32, norm_back_first, 0)
    pending += [load(acc.at[:, col(j)], input_out.at[:, c]) for j, c in enumerate(columns)]
    own_w = load(wu_all.at[7], stream.at[0, 0])
    own_q = load(wq_all.at[7], stream.at[1, 0, :, pl.ds(0, 640)])
    own_w.wait()
    own_q.wait()
    gain_two += jnp.sum(fout[:, 0:ff] * stream[0, 0].astype(f32), axis=1, keepdims=True)
    both(3, 10, 4, 6, 2)
    done.wait()
    events(3, 12, 14)
    done = load(fout.at[:, pl.ds(0, 512)], oq_out.at[:, pl.ds(0, 512)])
    events(4, 8, 12)
    done.wait()
    events(4, 12, 14)
    pending.append(load(fout.at[:, pl.ds(0, 640)], oq_out.at[:, pl.ds(512, 640)]))
    gain_one = jnp.sum(fout[:, 0:640] * stream[1, 0, :, 0:640].astype(f32), axis=1, keepdims=True)
    lane = lax.broadcasted_iota(jnp.int32, (256, 128), 1)
    both = jnp.where(lane == 0, gain_one, jnp.where(lane == 1, gain_two, 0.0)).T[0:8, :]
    terms[0] = both
    over = links.start(terms.at[0], terms_core, tp=over_core)
    over.wait_recv()
    both = both + terms_core[...]
    terms[1] = both
    over = links.start(terms.at[1], terms_y, tp=over_y)
    over.wait_recv()
    own_gains = jnp.concatenate(
        [gain_first[...], gain_second[...], jnp.ones((6, 256), f32)], axis=0
    ).astype(bf16)
    terms[2] = (both + terms_y[...]) / own_gains.astype(f32)
    pending.append(load(terms.at[2], gain_out))
    run(8, lambda i: sums.sent(i))
    for made in pending:
        made.wait()
    links.finish()
    moved.finish()


def feature_tables(heads):
    first = np.zeros((heads, 128, 256), np.float32)
    second = np.zeros((heads, 128, 256), np.float32)
    lanes = np.zeros((8, 256), np.float32)
    f = 0
    for i in range(FEAT):
        for j in range(i, FEAT):
            for h in range(heads):
                first[h, h * FEAT + i, f] = 1
                second[h, h * FEAT + j, f] = 1
            lanes[2, f] = square_coef if i == j else square_coef * 2**0.5
            f += 1
    for i in range(FEAT):
        for h in range(heads):
            first[h, h * FEAT + i, f] = 1
        lanes[1, f] = 1
        lanes[2, f] = linear_coef
        f += 1
    lanes[0, f] = lanes[1, f] = lanes[2, f] = 1
    mask = np.zeros((8, 128), np.float32)
    for h in range(heads):
        mask[h, h * FEAT : (h + 1) * FEAT] = 0.25
    return first, second, lanes, mask


def forward_pass(lengths, constants, gain_first, gain_second, x_in, weights, c_in):
    rows, width = x_in.shape
    total = 4 * rows
    ff = weights[4].shape[0]
    hbm = pl.BlockSpec(memory_space=pl.ANY)
    vmem = pl.BlockSpec(memory_space=pltpu.VMEM)

    def shape(*dims, dtype=bf16):
        return jax.ShapeDtypeStruct(dims, dtype)

    outs = (
        shape(8, 256, 640),
        shape(8, 256, 512),
        shape(8, 256, ff),
        shape(8, 256, ff),
        shape(8, 256, ff),
        shape(total, width),
        shape(total, width),
        shape(total, 640),
        shape(total, 512),
        shape(total, 128, dtype=f32),
        shape(rows, width, dtype=f32),
        shape(total, width),
        shape(total, ff),
        shape(total, ff),
        shape(total, ff),
        shape(4, 256, 128, dtype=f32),
        shape(8, width, dtype=f32),
        shape(width, ff),
    )
    scratch = [
        pltpu.VMEM((rows, width), bf16),
        pltpu.VMEM((total, 128), f32),
        pltpu.VMEM((8, total), f32),
        pltpu.VMEM((8, 128), f32),
        pltpu.VMEM((16, 256), bf16),
        pltpu.VMEM((256, 640), bf16),
        pltpu.VMEM((256, 512), bf16),
        pltpu.VMEM((256, ff), bf16),
        pltpu.VMEM((256, ff), bf16),
        pltpu.VMEM((256, ff), bf16),
        pltpu.VMEM((128, 256), f32),
        pltpu.VMEM((256, 512), f32),
        pltpu.VMEM((512, 256), f32),
        pltpu.VMEM((-(-ff // 128) * 128, 256), f32),
        pltpu.VMEM((-(-ff // 128) * 128, 256), f32),
        pltpu.VMEM((rows, width), bf16),
        pltpu.VMEM((total, width), bf16),
        pltpu.VMEM((total, width), bf16),
        pltpu.VMEM((width, 640), bf16),
        pltpu.VMEM((width, 512), bf16),
        pltpu.VMEM((width, ff), bf16),
        pltpu.VMEM((width, ff), bf16),
        pltpu.VMEM((total, 640), bf16),
        pltpu.VMEM((total, 128), bf16),
        pltpu.VMEM((total, 512), f32),
        pltpu.VMEM((total, 128), f32),
        pltpu.VMEM((total, 512), bf16),
        pltpu.VMEM((2, rows, width), bf16),
        pltpu.VMEM((2, rows, width), bf16),
        pltpu.VMEM((rows, width), bf16),
        pltpu.VMEM((rows, width), bf16),
        pltpu.VMEM((rows, width), f32),
        pltpu.VMEM((total, ff), bf16),
        pltpu.VMEM((total, ff), bf16),
        pltpu.VMEM((total, ff), bf16),
        pltpu.VMEM((8, 16, 256), bf16),
        pltpu.VMEM((8, width), f32),
        pltpu.VMEM((4, 176, 128), bf16),
        pltpu.VMEM((2, 176, 128), bf16),
        pltpu.VMEM((2, 176, 128), bf16),
        pltpu.VMEM((2, 176, 128), bf16),
        pltpu.VMEM((2, 176, 128), bf16),
        pltpu.VMEM((2, 2, 176, 128), bf16),
        pltpu.VMEM((4, 256, 128), f32),
        pltpu.SemaphoreType.DMA((144,)),
        pltpu.SemaphoreType.DMA((144,)),
        pltpu.SemaphoreType.DMA((144,)),
    ]
    return pl.pallas_call(
        fwd_kernel,
        out_shape=outs,
        in_specs=[pl.BlockSpec(memory_space=pltpu.SMEM)] + [vmem] * 6 + [hbm] * 9,
        out_specs=(hbm,) * len(outs),
        scratch_shapes=scratch,
        compiler_params=pltpu.CompilerParams(
            collective_id=0, has_side_effects=True, vmem_limit_bytes=60 * 2**20
        ),
    )(lengths, *constants, gain_first, gain_second, x_in, *weights, c_in)


def backward_pass(lengths, constants, gains, s_in, den, gain_pair, x_in, x1, weights, c_all, acts):
    rows, width = x_in.shape
    total = 4 * rows
    ff = weights[2].shape[2]
    hbm = pl.BlockSpec(memory_space=pl.ANY)
    vmem = pl.BlockSpec(memory_space=pltpu.VMEM)

    def shape(*dims, dtype=f32):
        return jax.ShapeDtypeStruct(dims, dtype)

    outs = (
        shape(256, ff),
        shape(256, ff),
        shape(256, ff),
        shape(256, 1152),
        shape(rows, width, dtype=bf16),
        shape(rows, width),
        shape(8, 256),
        shape(width, ff, dtype=bf16),
    )
    scratch = [
        pltpu.VMEM((total, 128), f32),
        pltpu.VMEM((8, total), f32),
        pltpu.VMEM((8, 128), f32),
        pltpu.VMEM((3, 8, 256), f32),
        pltpu.VMEM((8, 256), f32),
        pltpu.VMEM((8, 256), f32),
        pltpu.VMEM((8, 256, ff), bf16),
        pltpu.VMEM((width, ff), bf16),
        pltpu.VMEM((width, ff), bf16),
        pltpu.VMEM((width, 512), bf16),
        pltpu.VMEM((2, 2, 256, ff), bf16),
        pltpu.VMEM((2, total, 256), bf16),
        pltpu.VMEM((total, width), bf16),
        pltpu.VMEM((total, ff), bf16),
        pltpu.VMEM((total, ff), bf16),
        pltpu.VMEM((2, 256, ff), bf16),
        pltpu.VMEM((total, 640), bf16),
        pltpu.VMEM((total, 128), bf16),
        pltpu.VMEM((total, 512), bf16),
        pltpu.VMEM((total, 512), bf16),
        pltpu.VMEM((total, 128), f32),
        pltpu.VMEM((4, 8, 256), f32),
        pltpu.VMEM((total, 640), bf16),
        pltpu.VMEM((total, 128), f32),
        pltpu.VMEM((total, 128), f32),
        pltpu.VMEM((8, 4, 256, 256), bf16),
        pltpu.VMEM((8, 2, 256, 256), bf16),
        pltpu.VMEM((8, 256, 256), bf16),
        pltpu.VMEM((rows, width), f32),
        pltpu.VMEM((rows, width), f32),
        pltpu.VMEM((256, ff), f32),
        pltpu.VMEM((4, 176, 128), bf16),
        pltpu.VMEM((2, 176, 128), bf16),
        pltpu.VMEM((2, 176, 128), bf16),
        pltpu.VMEM((2, 176, 128), bf16),
        pltpu.VMEM((2, 176, 128), bf16),
        pltpu.VMEM((2, 2, 176, 128), bf16),
        pltpu.VMEM((4, 256, 128), f32),
        pltpu.VMEM((rows, width), bf16),
        pltpu.SemaphoreType.DMA((2, 2, 2)),
        pltpu.SemaphoreType.DMA((2, 2, 2, 7)),
        pltpu.SemaphoreType.DMA((6, 8)),
        pltpu.SemaphoreType.REGULAR((2,)),
        pltpu.SemaphoreType.DMA((16,)),
        pltpu.SemaphoreType.DMA((16,)),
        pltpu.SemaphoreType.DMA((80,)),
        pltpu.SemaphoreType.DMA((2, 2)),
    ]
    return pl.pallas_call(
        bwd_kernel,
        out_shape=outs,
        in_specs=[pl.BlockSpec(memory_space=pltpu.SMEM)] + [vmem] * 9 + [hbm] * 16,
        out_specs=(hbm,) * len(outs),
        scratch_shapes=scratch,
        compiler_params=pltpu.CompilerParams(
            collective_id=1, has_side_effects=True, vmem_limit_bytes=62 * 2**20
        ),
    )(lengths, *constants, gains, s_in, den, *gain_pair, x_in, x1, *weights, c_all, *acts)


def finish_kernel(
    d_in, g_in, u_in, oq_in, block_in, input_in,
    d_out, g_out, u_out, o_out, q_out, k_out, v_out, block_out, input_out,
    wide, turned, oq, oq_t, block, grad, sems,
):
    keeper = Sems(sems)
    ff = d_in.shape[1]

    def copy(src, dst):
        made = pltpu.make_async_copy(src, dst, keeper.take())
        made.start()
        return made

    came = [copy(ref, wide.at[i]) for i, ref in enumerate((g_in, u_in, d_in))]
    came_oq = copy(oq_in, oq)
    came_block, came_grad = copy(block_in, block), copy(input_in, grad)
    came_oq.wait()
    oq_t[...] = oq[:, 0:640].T
    kept = [
        copy(oq.at[:, pl.ds(640, 512)], v_out),
        copy(oq_t.at[pl.ds(0, 512)], o_out),
        copy(oq_t.at[pl.ds(512, 64)], q_out),
        copy(oq_t.at[pl.ds(576, 64)], k_out),
    ]
    for i, out in enumerate((g_out, u_out, d_out)):
        came[i].wait()
        for at in range(0, ff, 128):
            at = min(at, ff - 128)
            turned[i, at : at + 128, :] = wide[i, :, at : at + 128].T
        kept.append(copy(turned.at[i], out))
    came_block.wait()
    kept.append(copy(block, block_out))
    came_grad.wait()
    kept.append(copy(grad, input_out))
    for made in kept:
        made.wait()


def finish(d, g, u, oq, block, grad_input):
    rows, width = block.shape
    ff = d.shape[1]
    hbm = pl.BlockSpec(memory_space=pl.ANY)

    def shape(*dims, dtype=f32):
        return jax.ShapeDtypeStruct(dims, dtype)

    outs = (
        shape(ff, 256), shape(ff, 256), shape(ff, 256), shape(512, 256), shape(64, 256),
        shape(64, 256), shape(256, 512), shape(rows, width, dtype=bf16), shape(rows, width),
    )
    return pl.pallas_call(
        finish_kernel,
        out_shape=outs,
        in_specs=[hbm] * 6,
        out_specs=(hbm,) * len(outs),
        scratch_shapes=[
            pltpu.VMEM((3, 256, ff), f32),
            pltpu.VMEM((3, ff, 256), f32),
            pltpu.VMEM((256, 1152), f32),
            pltpu.VMEM((640, 256), f32),
            pltpu.VMEM((rows, width), bf16),
            pltpu.VMEM((rows, width), f32),
            pltpu.SemaphoreType.DMA((24,)),
        ],
        compiler_params=pltpu.CompilerParams(vmem_limit_bytes=60 * 2**20),
    )(d, g, u, oq, block, grad_input)


def on_device_rings(
    inputs, lengths, gain_attn, w_query, w_key, w_value, w_out, gain_mlp, w_gate, w_up, w_down,
    cotangent,
):
    first, second, lanes, mask = feature_tables(4)
    constants = (
        jnp.asarray(first, bf16), jnp.asarray(second, bf16), jnp.asarray(lanes), jnp.asarray(mask),
    )
    gain_pair = (gain_attn.reshape(1, -1), gain_mlp.reshape(1, -1))
    made = forward_pass(
        lengths, constants, *gain_pair, inputs,
        (w_query.T, w_key.T, w_value, w_out, w_gate.T, w_up.T, w_down), cotangent,
    )
    weights = made[:5]
    c_all, h1, qkv, yb, den, x1, h2, gate, up, mixed, s_in, gain_all, terms = made[5:]
    sum_down_t, sum_gate, sum_up, sum_oq, block, grad_input, gain_sums, _ = backward_pass(
        lengths, constants, gain_all, s_in, den, gain_pair, inputs, x1, weights, c_all,
        (h1, qkv, yb, h2, gate, up, mixed, terms),
    )
    d, g_t, u_t, o, q_t, k_t, v, block, grad_input = finish(
        sum_down_t, sum_gate, sum_up, sum_oq, block, grad_input
    )
    return (
        block,
        grad_input,
        gain_sums[0],
        q_t.T,
        k_t.T,
        v,
        o,
        gain_sums[1],
        g_t.T,
        u_t.T,
        d,
    )


def on_device(
    inputs,
    lengths,
    gain_attn,
    w_query,
    w_key,
    w_value,
    w_out,
    gain_mlp,
    w_gate,
    w_up,
    w_down,
    cotangent,
):
    seq_count = lax.axis_size("seq")
    tp_count = lax.axis_size("tp")
    seq_index = lax.axis_index("seq")
    rows_own, width = inputs.shape
    chunk = width // seq_count
    half = chunk // 2
    block_len = rows_own * tp_count
    anchor = seq_index * block_len
    relative = relative_list(seq_count)
    ring = ring_order(seq_count)
    place_of = [ring.index(s) for s in range(seq_count)]
    to_rel = jnp.array(
        [[ring[(place_of[s] - k) % seq_count] for k in relative] for s in range(seq_count)],
        jnp.int32,
    )[seq_index]
    to_abs = jnp.array(
        [
            [relative.index((place_of[s] - place_of[o]) % seq_count) for o in range(seq_count)]
            for s in range(seq_count)
        ],
        jnp.int32,
    )[seq_index]
    to_rel = [to_rel[j] for j in range(seq_count)]
    to_abs = [to_abs[j] for j in range(seq_count)]

    qk_cols, v_cols, ff_cols = w_query.shape[1], w_value.shape[1], w_gate.shape[1]
    gains = jnp.stack([gain_attn, gain_mlp]).astype(bf16)
    qkv_cols = 2 * qk_cols + v_cols
    qkv_own = jnp.concatenate([w_query, w_key, w_value], axis=1).astype(bf16)
    gain_rows = jnp.zeros((16, qkv_cols), bf16).at[:2, :chunk].set(gains)
    first_own = jnp.concatenate([qkv_own, gain_rows], axis=0)
    out_own = w_out.astype(bf16).T
    gate_up_own = jnp.concatenate([w_gate, w_up], axis=1).astype(bf16)
    down_own = w_down.astype(bf16).T

    first_got = ring_gather(first_own, half)
    out_got = ring_gather(out_own, half)
    gate_up_got = ring_gather(gate_up_own, half)
    down_got = ring_gather(down_own, half)
    w_qkv = jnp.concatenate([first_got[k][:chunk] for k in relative], axis=0)
    gain_first = jnp.concatenate([first_got[k][chunk, :chunk] for k in relative]).astype(f32)
    gain_second = jnp.concatenate([first_got[k][chunk + 1, :chunk] for k in relative]).astype(f32)
    w_out_t = jnp.concatenate([out_got[k] for k in relative], axis=0)
    w_gate_up = jnp.concatenate([gate_up_got[k] for k in relative], axis=0)
    w_down_t = jnp.concatenate([down_got[k] for k in relative], axis=0)

    at = jnp.arange(lengths.shape[0])
    starts = jnp.sum(jnp.where(at[None, :] < at[:, None], lengths[None, :], 0), axis=1)
    positions, row_ids, carry_in, after_last = segment_masks(anchor, starts, block_len)
    carry_mask = carry_in.astype(f32)
    last_mask = after_last.astype(f32)
    resets = (
        jnp.sum(
            ((starts // block_len)[None, :] == jnp.arange(seq_count)[:, None]).astype(jnp.int32),
            axis=1,
        )
        > 0
    ).astype(jnp.int32)

    inputs_own = to_relative(inputs, to_rel, chunk)
    grad_own = to_relative(cotangent, to_rel, chunk)
    inputs_full = tp_gather(inputs_own).astype(f32)
    grad_full = tp_gather(grad_own)
    inputs_own = inputs_own.astype(f32)
    hidden_first = (inputs_full * rms_scale(inputs_full) * gain_first).astype(bf16)
    qkv = dot(hidden_first, w_qkv).astype(bf16)
    queries = qkv[:, :qk_cols]
    key_flat = qkv[:, qk_cols : 2 * qk_cols]
    value_flat = qkv[:, 2 * qk_cols :]
    heads_local = qk_cols // FEAT
    query_heads = queries.reshape(block_len, heads_local, FEAT)
    key_heads = key_flat.reshape(block_len, heads_local, FEAT)
    value_heads = value_flat.reshape(block_len, heads_local, VHEAD)
    query_float = query_heads.astype(f32)
    key_float = key_heads.astype(f32)
    value_float = value_heads.astype(f32)
    key_feat = features(key_float) * last_mask[:, None, None]
    local_state = jnp.einsum("thn,thv->hnv", key_feat, value_float, precision=highest)
    local_sum = jnp.sum(key_feat, axis=0)
    carry_state, carry_sum = carried([local_state, local_sum], resets, 1)
    step_rows = 512
    query_feat = features(query_float)
    carry_weight = carry_mask[:, None]
    numer_parts = []
    denom_parts = []
    for first_row in range(0, block_len, step_rows):
        query_part = query_heads[first_row : first_row + step_rows]
        scores, allowed, kernel = pair_block(
            query_part, key_heads, row_ids, positions, first_row, step_rows
        )
        numer_parts.append(
            jnp.einsum("hts,shv->thv", kernel.astype(bf16), value_heads, preferred_element_type=f32)
        )
        denom_parts.append(jnp.sum(kernel, axis=-1).T)
    numerator = (
        jnp.concatenate(numer_parts, axis=0)
        + jnp.einsum("thn,hnv->thv", query_feat, carry_state, precision=highest)
        * carry_weight[:, :, None]
    )
    denominator = (
        jnp.concatenate(denom_parts, axis=0)
        + jnp.einsum("thn,hn->th", query_feat, carry_sum, precision=highest) * carry_weight
    )
    attended = numerator / denominator[:, :, None]
    attended_low = attended.reshape(block_len, heads_local * VHEAD).astype(bf16)
    attn_partial = dot_t(attended_low, w_out_t).astype(bf16)
    middle_own = inputs_own + tp_scatter(attn_partial)
    scale_second = rms_scale(middle_own)
    normed_second = middle_own * scale_second
    hidden_second = tp_gather((normed_second * gain_second).astype(bf16))
    gate_up = dot(hidden_second, w_gate_up)
    gate_value, upward = gate_up[:, :ff_cols], gate_up[:, ff_cols:]
    sigmoid_gate = jax.nn.sigmoid(gate_value)
    silu_gate = gate_value * sigmoid_gate
    mixed_rows = (silu_gate * upward).astype(bf16)
    grad_down_t = dot_tt(grad_full, mixed_rows).astype(bf16)

    def by_distance(stack):
        return {k: stack[j * chunk : (j + 1) * chunk] for j, k in enumerate(relative)}

    sum_down_t = ring_scatter(by_distance(grad_down_t))
    mlp_own = tp_scatter(dot_t(mixed_rows, w_down_t).astype(bf16))
    block_output = to_relative((middle_own + mlp_own).astype(bf16), to_abs, chunk)

    grad_mixed = dot(grad_full, w_down_t).astype(bf16).astype(f32)
    grad_gate = (
        grad_mixed * upward * sigmoid_gate * (1.0 + gate_value * (1.0 - sigmoid_gate))
    ).astype(bf16)
    grad_upward = (grad_mixed * silu_gate).astype(bf16)
    grad_gate_up = jnp.concatenate([grad_gate, grad_upward], axis=1)
    hidden_partial = dot_t(grad_gate_up, w_gate_up).astype(bf16)
    sum_gate_up = ring_scatter(by_distance(dot_tt(hidden_second, grad_gate_up).astype(bf16)))
    grad_hidden = tp_scatter(hidden_partial)
    grad_middle = grad_own.astype(f32) + norm_back(
        grad_hidden, normed_second, scale_second, gain_second
    )
    grad_branch = tp_gather(grad_middle.astype(bf16))
    sum_out_t = ring_scatter(by_distance(dot_tt(grad_branch, attended_low).astype(bf16)))
    grad_attended = dot(grad_branch, w_out_t).reshape(block_len, heads_local, VHEAD)
    grad_numer = (grad_attended / denominator[:, :, None]).astype(bf16)
    grad_denom = -jnp.sum(grad_attended * attended, axis=-1) / denominator
    grad_numer_carried = grad_numer.astype(f32) * carry_weight[:, :, None]
    grad_denom_carried = grad_denom * carry_weight
    grad_state_in = jnp.einsum("thn,thv->hnv", query_feat, grad_numer_carried, precision=highest)
    grad_sum_in = jnp.einsum("thn,th->hn", query_feat, grad_denom_carried, precision=highest)
    grad_query_feat = (
        jnp.einsum("thv,hnv->thn", grad_numer_carried, carry_state, precision=highest)
        + grad_denom_carried[:, :, None] * carry_sum[None]
    )
    grad_state_out, grad_sum_out = carried([grad_state_in, grad_sum_in], resets, -1)
    grad_key_feat = (
        jnp.einsum("thv,hnv->thn", value_float, grad_state_out, precision=highest)
        + grad_sum_out[None]
    ) * last_mask[:, None, None]
    grad_value_state = jnp.einsum("thn,hnv->thv", key_feat, grad_state_out, precision=highest)
    grad_query_parts = []
    grad_key_inner = jnp.zeros((block_len, heads_local, FEAT), f32)
    grad_value_inner = jnp.zeros((block_len, heads_local, VHEAD), f32)
    for first_row in range(0, block_len, step_rows):
        query_part = query_heads[first_row : first_row + step_rows]
        scores, allowed, kernel = pair_block(
            query_part, key_heads, row_ids, positions, first_row, step_rows
        )
        numer_grad_part = grad_numer[first_row : first_row + step_rows]
        grad_weights = jnp.einsum(
            "thv,shv->hts", numer_grad_part, value_heads, preferred_element_type=f32
        )
        grad_scores = (
            (grad_weights + grad_denom[first_row : first_row + step_rows].T[:, :, None])
            * allowed[None]
            * (1.0 + scores)
        ).astype(bf16)
        grad_query_parts.append(
            jnp.einsum("hts,shf->thf", grad_scores, key_heads, preferred_element_type=f32) * 0.25
        )
        grad_key_inner = (
            grad_key_inner
            + jnp.einsum("hts,thf->shf", grad_scores, query_part, preferred_element_type=f32) * 0.25
        )
        grad_value_inner = grad_value_inner + jnp.einsum(
            "hts,thv->shv", kernel.astype(bf16), numer_grad_part, preferred_element_type=f32
        )
    grad_query = (
        jnp.concatenate(grad_query_parts, axis=0) + feature_grad(query_float, grad_query_feat)
    ).astype(bf16)
    grad_key = (grad_key_inner + feature_grad(key_float, grad_key_feat)).astype(bf16)
    grad_value = (grad_value_inner + grad_value_state).astype(bf16)
    grad_qkv = jnp.concatenate(
        [
            grad_query.reshape(block_len, heads_local * FEAT),
            grad_key.reshape(block_len, heads_local * FEAT),
            grad_value.reshape(block_len, heads_local * VHEAD),
        ],
        axis=1,
    )
    sum_qkv = ring_scatter(by_distance(dot_tt(hidden_first, grad_qkv).astype(bf16)))
    grad_hidden_first = tp_scatter(dot_t(grad_qkv, w_qkv).astype(bf16))
    scale_first = rms_scale(inputs_own)
    normed_first = inputs_own * scale_first
    grad_input = to_relative(
        grad_middle + norm_back(grad_hidden_first, normed_first, scale_first, gain_first),
        to_abs,
        chunk,
    )

    gain_terms = jnp.stack(
        [
            jnp.sum(qkv_own.astype(f32) * sum_qkv, axis=1),
            jnp.sum(gate_up_own.astype(f32) * sum_gate_up, axis=1),
        ]
    )
    gain_sums = tp_sum(gain_terms) / gains.astype(f32)
    return (
        block_output,
        grad_input,
        gain_sums[0],
        sum_qkv[:, :qk_cols],
        sum_qkv[:, qk_cols : 2 * qk_cols],
        sum_qkv[:, 2 * qk_cols :],
        sum_out_t.T,
        gain_sums[1],
        sum_gate_up[:, :ff_cols],
        sum_gate_up[:, ff_cols:],
        sum_down_t.T,
    )


def solution(mesh):
    in_specs = (
        P(("seq", "tp"), None),
        P(),
        P("seq"),
        P("seq", "tp"),
        P("seq", "tp"),
        P("seq", "tp"),
        P("tp", "seq"),
        P("seq"),
        P("seq", "tp"),
        P("seq", "tp"),
        P("tp", "seq"),
        P(("seq", "tp"), None),
    )
    out_specs = (
        P(("seq", "tp"), None),
        P(("seq", "tp"), None),
        P("seq"),
        P("seq", "tp"),
        P("seq", "tp"),
        P("seq", "tp"),
        P("tp", "seq"),
        P("seq"),
        P("seq", "tp"),
        P("seq", "tp"),
        P("tp", "seq"),
    )
    small = mesh.shape["seq"] == 8 and mesh.shape["tp"] == 4
    body = on_device_rings if small else on_device
    return jax.shard_map(
        body, mesh=mesh, in_specs=in_specs, out_specs=out_specs, check_vma=False
    )
```
